32 devices in a mesh: dp: 16 (over z, y, core), tensor: 2 (over x).
Axes of the slice: x: 2, y: 2, z: 4, core: 2. Of those that a mesh axis runs over, the one named last changes fastest.
Arguments:
- tokens: bfloat16 [32, 2048, 1024], P('dp', 'tensor'), may hold values from -6 to 6
- gain_attn: bfloat16 [1024], P('dp'), may hold values from 0.5 to 1.5
- w_query: bfloat16 [1024, 1024], P('dp', 'tensor'), may hold values from -0.375 to 0.375
- w_key: bfloat16 [1024, 1024], P('dp', 'tensor'), may hold values from -0.1875 to 0.1875
- w_value: bfloat16 [1024, 1024], P('dp', 'tensor'), may hold values from -0.1875 to 0.1875
- w_out: bfloat16 [1024, 1024], P('tensor', 'dp'), may hold values from -1 to 1
- gain_ffn: bfloat16 [1024], P('dp'), may hold values from 0.5 to 1.5
- w_gate: bfloat16 [1024, 2816], P('dp', 'tensor'), may hold values from -0.1875 to 0.1875
- w_up: bfloat16 [1024, 2816], P('dp', 'tensor'), may hold values from -0.1875 to 0.1875
- w_down: bfloat16 [2816, 1024], P('tensor', 'dp'), may hold values from -0.21875 to 0.21875
- cache_keys: bfloat16 [32, 1024, 1024], P('dp', None, 'tensor'), may hold values from -6 to 6
- cache_values: bfloat16 [32, 1024, 1024], P('dp', None, 'tensor'), may hold values from -6 to 6
- prefix: int32 [32], P('dp'), may hold values from 204 to 1024, as said below
- partner: int32 [32], P('dp'), may hold values from 0 to 31, each once
- own_blocks: int32 [32, 16, 4], P('dp'), may hold values from 0 to 15, all different within a row
- partner_blocks: int32 [32, 16, 4], P('dp'), may hold values from 0 to 15, all different within a row
- grad_out: bfloat16 [32, 2048, 1024], P('dp', 'tensor'), may hold values from -6 to 6
Outputs:
- out: bfloat16 [32, 2048, 1024], P('dp', 'tensor')
- grad_tokens: float32 [32, 2048, 1024], P('dp', 'tensor')
- grad_gain_attn: float32 [1024], replicated
- grad_w_query: float32 [1024, 1024], P('dp', 'tensor')
- grad_w_key: float32 [1024, 1024], P('dp', 'tensor')
- grad_w_value: float32 [1024, 1024], P('dp', 'tensor')
- grad_w_out: float32 [1024, 1024], P('tensor', 'dp')
- grad_gain_ffn: float32 [1024], replicated
- grad_w_gate: float32 [1024, 2816], P('dp', 'tensor')
- grad_w_up: float32 [1024, 2816], P('dp', 'tensor')
- grad_w_down: float32 [2816, 1024], P('tensor', 'dp')
The draws below stay inside these ranges and needn't reach their ends.
Inputs may be any that keep to these rules, and one draw needn't show every extreme that they name: prefix[s] leading positions of sequence s see each other both ways; both the smallest and the largest allowed value occur. `partner`: every sequence number occurs exactly once. `own_blocks`: the 4 block numbers of one query block are distinct. `partner_blocks`: the 4 block numbers of one query block are distinct.
All inputs are finite; a program needn't handle non-finite values.
Results may differ from the reference program's by a relative error of at most 0.02.
Values may be sent and summed in bfloat16 or wider, within the bound.
A program may use at most 384 MiB of HBM per device.

```python
import jax
import jax.numpy as jnp
from jax import lax

D = 1024
HEADS = 8
HD = 128
FF = 2816
L = 2048
CACHE_LEN = 1024
QBLOCK = 128
CBLOCK = 64
KR = 4
QROWS = 512
SEQS = 32


def draw_prefix(key, part):
    first, second = jax.random.split(key)
    values = jax.random.randint(first, (SEQS,), L // 10, L // 2 + 1, dtype=jnp.int32)
    spots = jax.random.permutation(second, SEQS)
    values = values.at[spots[0]].set(L // 2)
    values = values.at[spots[1]].set(L // 10)
    return values


def block_levels(own_key, dims, cuts, least, top_value):
    factor_of = 1.0
    for position, blocks in cuts:
        heights = jax.random.uniform(jax.random.fold_in(jax.random.fold_in(own_key, 6), position), (blocks,), jnp.float32, least / len(cuts), top_value / len(cuts))
        factor_of = factor_of * jnp.repeat(jnp.exp(heights), dims[position] // blocks).reshape((-1,) + (1,) * (len(dims) - 1 - position))
    return factor_of


def different_ones(stream_key, rows, number_of, top, lift):
    order = jax.random.permutation(jax.random.fold_in(stream_key, 1), number_of)
    favour = order
    for power in range(3):
        favour = favour * favour // number_of
    favour = favour * lift // number_of
    tickets = jax.random.randint(jax.random.fold_in(stream_key, 2), (rows, number_of), 0, 4096) + favour
    holders = jax.random.permutation(jax.random.fold_in(stream_key, 3), rows)[jnp.arange(number_of) % rows]
    tickets = jnp.where(jnp.arange(rows)[:, None] == holders[None, :], 1 << 14, tickets)
    score = tickets * number_of + jnp.arange(number_of)
    return lax.top_k(score.astype(jnp.int32), top)[1].astype(jnp.int32)


def centred(own_key, extent, scale, bound, shards=(), kind=jnp.bfloat16):
    array = scale * jax.random.normal(own_key, extent, jnp.float32)
    if shards:
        array = array * block_levels(own_key, extent, shards, -0.22, 0.18)
    return jnp.clip(array, -bound, bound).astype(kind)


def setup_inputs(seed: int = 0) -> dict:
    seeds = jax.random.split(jax.random.key(seed), 18)
    return {
        "tokens": centred(seeds[0], (SEQS, L, D), 1.0, 6.0, ((0, 16), (1, 2))),
        "gain_attn": jnp.clip(1.0 + 0.1 * jax.random.normal(seeds[1], (D,), jnp.float32), 0.5, 1.5).astype(jnp.bfloat16),
        "w_query": centred(seeds[2], (D, HEADS * HD), (D // 4) ** -0.5, 0.375, ((0, 16), (1, 2))),
        "w_key": centred(seeds[3], (D, HEADS * HD), D ** -0.5, 0.1875, ((0, 16), (1, 2))),
        "w_value": centred(seeds[4], (D, HEADS * HD), D ** -0.5, 0.1875, ((0, 16), (1, 2))),
        "w_out": centred(seeds[5], (HEADS * HD, D), (HD // 4) ** -0.5, 1.0, ((0, 2), (1, 16))),
        "gain_ffn": jnp.clip(1.0 + 0.1 * jax.random.normal(seeds[6], (D,), jnp.float32), 0.5, 1.5).astype(jnp.bfloat16),
        "w_gate": centred(seeds[7], (D, FF), D ** -0.5, 0.1875, ((0, 16), (1, 2))),
        "w_up": centred(seeds[8], (D, FF), D ** -0.5, 0.1875, ((0, 16), (1, 2))),
        "w_down": centred(seeds[9], (FF, D), (FF // 4) ** -0.5, 0.21875, ((0, 2), (1, 16))),
        "cache_keys": centred(seeds[10], (SEQS, CACHE_LEN, HEADS * HD), 1.0, 6.0, ((0, 16), (2, 2))),
        "cache_values": centred(seeds[11], (SEQS, CACHE_LEN, HEADS * HD), 1.0, 6.0, ((0, 16), (2, 2))),
        "prefix": draw_prefix(jax.random.fold_in(seeds[17], 71), 0),
        "partner": jax.random.permutation(seeds[13], SEQS).astype(jnp.int32),
        "own_blocks": different_ones(seeds[14], SEQS * (L // QBLOCK), CACHE_LEN // CBLOCK, KR, 0).reshape((SEQS, L // QBLOCK, KR)),
        "partner_blocks": different_ones(seeds[15], SEQS * (L // QBLOCK), CACHE_LEN // CBLOCK, KR, 0).reshape((SEQS, L // QBLOCK, KR)),
        "grad_out": centred(seeds[16], (SEQS, L, D), 1.0, 6.0, ((0, 16), (1, 2))),
    }


EPS = 1e-05
HIGH = lax.Precision.HIGHEST

@jax.custom_vjp
def low(v):
    return lax.optimization_barrier(v.astype(jnp.bfloat16)).astype(jnp.float32)

@jax.custom_vjp
def low_back(v):
    return v

def low_keep(v):
    return (low(v), None)

def low_pass(kept, grad):
    return (grad,)

def back_keep(v):
    return (v, None)

def back_low(kept, grad):
    return (low(grad),)
low.defvjp(low_keep, low_pass)
low_back.defvjp(back_keep, back_low)

def rounded_both(value):
    return low_back(low(value))

def norm_rows(values, gain):
    return values * lax.rsqrt(lax.optimization_barrier(jnp.mean(values * values, axis=-1, keepdims=True)) + EPS) * gain

def attend(query, keys, values, mem_keys, mem_values, limit):
    groups = QROWS // QBLOCK
    scale = HD ** (-0.5)
    key_ids = jnp.arange(L, dtype=jnp.int32)

    def one_block(index):
        first = index * QROWS
        query_block = lax.dynamic_slice_in_dim(query, first, QROWS, 0)
        local = low_back(jnp.einsum('qhd,khd->hqk', query_block, keys, precision=HIGH) * scale)
        row_ids = first + jnp.arange(QROWS, dtype=jnp.int32)
        allowed = (key_ids[None, :] <= row_ids[:, None]) | (row_ids[:, None] < limit) & (key_ids[None, :] < limit)
        local = jnp.where(allowed[None], local, -1e+30)
        mem_k = lax.dynamic_slice_in_dim(mem_keys, index * groups, groups, 0)
        mem_v = lax.dynamic_slice_in_dim(mem_values, index * groups, groups, 0)
        grouped = query_block.reshape(groups, QBLOCK, HEADS, HD)
        remote = jnp.einsum('bqhd,bkhd->hbqk', grouped, mem_k, precision=HIGH) * scale
        remote = low_back(remote).reshape(HEADS, QROWS, -1)
        top = jnp.maximum(lax.optimization_barrier(jnp.max(local, axis=-1)), lax.optimization_barrier(jnp.max(remote, axis=-1)))
        e_local = jnp.exp(local - top[..., None])
        e_remote = jnp.exp(remote - top[..., None])
        total = lax.optimization_barrier(jnp.sum(e_local, axis=-1)) + lax.optimization_barrier(jnp.sum(e_remote, axis=-1))
        p_local = low(e_local / total[..., None])
        p_remote = low(e_remote / total[..., None]).reshape(HEADS, groups, QBLOCK, -1)
        part = jnp.einsum('hqk,khd->qhd', p_local, values, precision=HIGH)
        extra = jnp.einsum('hbqk,bkhd->bqhd', p_remote, mem_v, precision=HIGH)
        return part + extra.reshape(QROWS, HEADS, HD)
    blocks = lax.map(jax.checkpoint(one_block), jnp.arange(L // QROWS, dtype=jnp.int32))
    return blocks.reshape(L, HEADS, HD)

def layer(params, token_rows, limit, mem_keys, mem_values):
    gain_attn, w_query, w_key, w_value, w_out, gain_ffn, w_gate, w_up, w_down = params
    normed = low(norm_rows(token_rows, gain_attn))
    query = rounded_both(jnp.dot(normed, w_query, precision=HIGH)).reshape(L, HEADS, HD)
    keys = rounded_both(jnp.dot(normed, w_key, precision=HIGH)).reshape(L, HEADS, HD)
    values = rounded_both(jnp.dot(normed, w_value, precision=HIGH)).reshape(L, HEADS, HD)
    context = rounded_both(attend(query, keys, values, mem_keys, mem_values, limit).reshape(L, HEADS * HD))
    mixed = token_rows + low_back(jnp.dot(context, w_out, precision=HIGH))
    normed_two = low(norm_rows(mixed, gain_ffn))
    gate = low_back(jnp.dot(normed_two, w_gate, precision=HIGH))
    upward = low_back(jnp.dot(normed_two, w_up, precision=HIGH))
    hidden = low(jax.nn.silu(gate) * upward)
    return mixed + low_back(jnp.dot(hidden, w_down, precision=HIGH))

def memory_rows(cache, owner, chosen):
    shaped = cache[owner].reshape(CACHE_LEN // CBLOCK, CBLOCK, HEADS, HD)
    return jnp.take(shaped, chosen, axis=0)

def reference(tokens, gain_attn, w_query, w_key, w_value, w_out, gain_ffn, w_gate, w_up, w_down, cache_keys, cache_values, prefix, partner, own_blocks, partner_blocks, grad_out):
    params = tuple((p.astype(jnp.float32) for p in (gain_attn, w_query, w_key, w_value, w_out, gain_ffn, w_gate, w_up, w_down)))
    keys_all = cache_keys.astype(jnp.float32)
    values_all = cache_values.astype(jnp.float32)
    qblocks = L // QBLOCK

    def run(token_all, weights):

        def one_seq(carry, index):
            other = partner[index]
            mem_k = jnp.concatenate([memory_rows(keys_all, index, own_blocks[index]), memory_rows(keys_all, other, partner_blocks[index])], axis=1)
            mem_v = jnp.concatenate([memory_rows(values_all, index, own_blocks[index]), memory_rows(values_all, other, partner_blocks[index])], axis=1)
            mem_k = mem_k.reshape(qblocks, 2 * KR * CBLOCK, HEADS, HD)
            mem_v = mem_v.reshape(qblocks, 2 * KR * CBLOCK, HEADS, HD)
            result = jax.checkpoint(layer)(weights, token_all[index], prefix[index], mem_k, mem_v)
            return (carry, result)
        unused, outs = lax.scan(one_seq, None, jnp.arange(SEQS, dtype=jnp.int32))
        return outs
    result, pull = jax.vjp(run, tokens.astype(jnp.float32), params)
    grad_tokens, grads = pull(grad_out.astype(jnp.float32))
    return (result.astype(jnp.bfloat16), grad_tokens, grads[0], grads[1], grads[2], grads[3], grads[4], grads[5], grads[6], grads[7], grads[8])
```

```python
import functools

import jax
import jax.numpy as jnp
from jax import lax
from jax.experimental import pallas as pl
from jax.experimental.pallas import tpu as pltpu
from jax.sharding import PartitionSpec as P

HD = 128
L = 2048
CACHE_LEN = 1024
QBLOCK = 128
CBLOCK = 64
KR = 4
QROWS = 512


EPS = 1e-05
NEGATIVE = -1e30


def norm_rows(values, gain):
    scale_rows = lax.rsqrt(jnp.mean(values * values, axis=-1, keepdims=True) + EPS)
    return (values * scale_rows * gain, scale_rows)


def norm_back(grad_normed, values, scale_rows, gain):
    unit = values * scale_rows
    grad_unit = grad_normed * gain
    grad_values = scale_rows * (
        grad_unit - unit * jnp.mean(grad_unit * unit, axis=-1, keepdims=True)
    )
    return (grad_values, jnp.sum(grad_normed * unit, axis=0))


def inner_rows(left, right):
    return lax.dot_general(
        left, right, (((0,), (0,)), ((), ())), preferred_element_type=jnp.float32
    )


def outer_cols(left, right):
    return lax.dot_general(
        left, right, (((1,), (1,)), ((), ())), preferred_element_type=jnp.float32
    )


def memory_rows(cache_one, chosen, width):
    shaped = cache_one.reshape(CACHE_LEN // CBLOCK, CBLOCK, width)
    return jnp.take(shaped, chosen, axis=0)


def block_scores(query_block, keys_part, mem_part, first_row, limit):
    rows_here, heads_here, size = query_block.shape
    extent = keys_part.shape[0]
    local = jnp.einsum(
        "qhd,khd->hqk", query_block, keys_part, preferred_element_type=jnp.float32
    ) * size ** (-0.5)
    row_ids = first_row + jnp.arange(rows_here, dtype=jnp.int32)[:, None]
    key_ids = jnp.arange(extent, dtype=jnp.int32)[None, :]
    allowed = (key_ids <= row_ids) | (row_ids < limit) & (key_ids < limit)
    local = jnp.where(allowed[None], local, NEGATIVE)
    groups = mem_part.shape[0]
    grouped = query_block.reshape(groups, rows_here // groups, heads_here, size)
    remote = jnp.einsum(
        "bqhd,bkhd->hbqk", grouped, mem_part, preferred_element_type=jnp.float32
    ) * size ** (-0.5)
    return (local, remote.reshape(heads_here, rows_here, -1))


def attention_forward(query, keys, values, mem_keys, mem_values, limit):
    groups = QROWS // QBLOCK
    heads_here = query.shape[1]
    context_parts = []
    lse_parts = []
    for index in range(L // QROWS):
        first = index * QROWS
        extent = max(first + QROWS, L // 2)
        query_block = query[first : first + QROWS]
        mem_k = mem_keys[index * groups : (index + 1) * groups]
        mem_v = mem_values[index * groups : (index + 1) * groups]
        local, remote = block_scores(query_block, keys[:extent], mem_k, first, limit)
        top = jnp.maximum(jnp.max(local, axis=-1), jnp.max(remote, axis=-1))
        e_local = jnp.exp(local - top[..., None])
        e_remote = jnp.exp(remote - top[..., None])
        total = jnp.sum(e_local, axis=-1) + jnp.sum(e_remote, axis=-1)
        p_local = (e_local / total[..., None]).astype(jnp.bfloat16)
        p_remote = (
            (e_remote / total[..., None])
            .astype(jnp.bfloat16)
            .reshape(heads_here, groups, QBLOCK, -1)
        )
        part = jnp.einsum(
            "hqk,khd->qhd", p_local, values[:extent], preferred_element_type=jnp.float32
        )
        extra = jnp.einsum("hbqk,bkhd->bqhd", p_remote, mem_v, preferred_element_type=jnp.float32)
        context_parts.append(part + extra.reshape(part.shape))
        lse_parts.append(top + jnp.log(total))
    return (jnp.concatenate(context_parts, axis=0), lse_parts)


def attention_backward(query, keys, values, mem_keys, mem_values, limit, lse_parts, grad_context):
    groups = QROWS // QBLOCK
    length, heads_here, size = query.shape
    scale = size ** (-0.5)
    grad_query_parts = []
    grad_keys = jnp.zeros(query.shape, jnp.float32)
    grad_values = jnp.zeros(query.shape, jnp.float32)
    for index in range(L // QROWS):
        first = index * QROWS
        extent = max(first + QROWS, L // 2)
        query_block = query[first : first + QROWS]
        mem_k = mem_keys[index * groups : (index + 1) * groups]
        mem_v = mem_values[index * groups : (index + 1) * groups]
        local, remote = block_scores(query_block, keys[:extent], mem_k, first, limit)
        lse_block = lse_parts[index][..., None]
        p_local = jnp.exp(local - lse_block)
        p_remote = jnp.exp(remote - lse_block)
        grad_block = grad_context[first : first + QROWS]
        grouped_grad = grad_block.reshape(groups, QBLOCK, heads_here, size)
        dp_local = jnp.einsum(
            "qhd,khd->hqk", grad_block, values[:extent], preferred_element_type=jnp.float32
        )
        dp_remote = jnp.einsum(
            "bqhd,bkhd->hbqk", grouped_grad, mem_v, preferred_element_type=jnp.float32
        )
        dp_remote = dp_remote.reshape(heads_here, QROWS, -1)
        delta = jnp.sum(p_local * dp_local, axis=-1) + jnp.sum(p_remote * dp_remote, axis=-1)
        ds_local = (p_local * (dp_local - delta[..., None])).astype(jnp.bfloat16)
        ds_remote = (p_remote * (dp_remote - delta[..., None])).astype(jnp.bfloat16)
        ds_remote = ds_remote.reshape(heads_here, groups, QBLOCK, -1)
        dq_block = jnp.einsum(
            "hqk,khd->qhd", ds_local, keys[:extent], preferred_element_type=jnp.float32
        )
        dq_extra = jnp.einsum(
            "hbqk,bkhd->bqhd", ds_remote, mem_k, preferred_element_type=jnp.float32
        )
        grad_query_parts.append((dq_block + dq_extra.reshape(dq_block.shape)) * scale)
        dk_part = (
            jnp.einsum("hqk,qhd->khd", ds_local, query_block, preferred_element_type=jnp.float32)
            * scale
        )
        dv_part = jnp.einsum(
            "hqk,qhd->khd",
            p_local.astype(jnp.bfloat16),
            grad_block,
            preferred_element_type=jnp.float32,
        )
        grad_keys = grad_keys.at[:extent].add(dk_part)
        grad_values = grad_values.at[:extent].add(dv_part)
    return (jnp.concatenate(grad_query_parts, axis=0), grad_keys, grad_values)


def tensor_body(
    tokens,
    gain_attn,
    w_query,
    w_key,
    w_value,
    w_out,
    gain_ffn,
    w_gate,
    w_up,
    w_down,
    cache_keys,
    cache_values,
    prefix,
    partner,
    own_blocks,
    partner_blocks,
    grad_out,
):
    micro, shard_len, width = tokens.shape
    cols = w_query.shape[1]
    heads_local = cols // HD
    qblocks = L // QBLOCK
    mem_len = 2 * KR * CBLOCK
    piece_keys = lax.all_gather(cache_keys, "dp", axis=0, tiled=True)
    piece_values = lax.all_gather(cache_values, "dp", axis=0, tiled=True)
    count = piece_keys.shape[0]
    onehot = (partner[:, None] == jnp.arange(count, dtype=jnp.int32)[None, :]).astype(jnp.bfloat16)
    add_keys = jnp.einsum("mn,nkc->mkc", onehot, piece_keys, preferred_element_type=jnp.float32)
    add_values = jnp.einsum("mn,nkc->mkc", onehot, piece_values, preferred_element_type=jnp.float32)
    fetched_keys = add_keys.astype(jnp.bfloat16)
    fetched_values = add_values.astype(jnp.bfloat16)
    totals = (
        jnp.zeros((width, cols), jnp.float32),
        jnp.zeros((width, cols), jnp.float32),
        jnp.zeros((width, cols), jnp.float32),
        jnp.zeros((cols, width), jnp.float32),
        jnp.zeros((width, w_gate.shape[1]), jnp.float32),
        jnp.zeros((width, w_gate.shape[1]), jnp.float32),
        jnp.zeros((w_gate.shape[1], width), jnp.float32),
    )
    shares = tuple(
        (
            jnp.zeros(w.shape, jnp.float32)
            for w in (w_query, w_key, w_value, w_out, w_gate, w_up, w_down)
        )
    )
    gain_total_attn = jnp.zeros((width,), jnp.float32)
    gain_total_ffn = jnp.zeros((width,), jnp.float32)
    out_rows = []
    grad_rows = []
    for step in range(micro):
        fwd = (
            lax.all_gather(gain_attn, "dp", axis=0, tiled=True),
            lax.all_gather(w_query, "dp", axis=0, tiled=True),
            lax.all_gather(w_key, "dp", axis=0, tiled=True),
            lax.all_gather(w_value, "dp", axis=0, tiled=True),
            lax.all_gather(w_out, "dp", axis=1, tiled=True),
            lax.all_gather(gain_ffn, "dp", axis=0, tiled=True),
            lax.all_gather(w_gate, "dp", axis=0, tiled=True),
            lax.all_gather(w_up, "dp", axis=0, tiled=True),
            lax.all_gather(w_down, "dp", axis=1, tiled=True),
        )
        g_attn, wq_full, wk_full, wv_full, wo_full, g_ffn, wg_full, wu_full, wd_full = fwd
        limit = prefix[step]
        own_k = memory_rows(cache_keys[step], own_blocks[step], cols)
        par_k = memory_rows(fetched_keys[step], partner_blocks[step], cols)
        own_v = memory_rows(cache_values[step], own_blocks[step], cols)
        par_v = memory_rows(fetched_values[step], partner_blocks[step], cols)
        mem_keys = jnp.concatenate([own_k, par_k], axis=1).reshape(
            qblocks, mem_len, heads_local, HD
        )
        mem_values = jnp.concatenate([own_v, par_v], axis=1).reshape(
            qblocks, mem_len, heads_local, HD
        )
        token_rows = tokens[step].astype(jnp.float32)
        normed, scale_one = norm_rows(token_rows, g_attn.astype(jnp.float32))
        normed_all = lax.all_gather(normed.astype(jnp.bfloat16), "tensor", axis=0, tiled=True)
        query = (
            jnp.dot(normed_all, wq_full, preferred_element_type=jnp.float32)
            .astype(jnp.bfloat16)
            .reshape(L, heads_local, HD)
        )
        keys = (
            jnp.dot(normed_all, wk_full, preferred_element_type=jnp.float32)
            .astype(jnp.bfloat16)
            .reshape(L, heads_local, HD)
        )
        values = (
            jnp.dot(normed_all, wv_full, preferred_element_type=jnp.float32)
            .astype(jnp.bfloat16)
            .reshape(L, heads_local, HD)
        )
        context_full, lse_parts = attention_forward(
            query, keys, values, mem_keys, mem_values, limit
        )
        context = context_full.reshape(L, cols).astype(jnp.bfloat16)
        mixed = token_rows + lax.psum_scatter(
            jnp.dot(context, wo_full, preferred_element_type=jnp.float32),
            "tensor",
            scatter_dimension=0,
            tiled=True,
        )
        normed_two, scale_two = norm_rows(mixed, g_ffn.astype(jnp.float32))
        normed_two_all = lax.all_gather(
            normed_two.astype(jnp.bfloat16), "tensor", axis=0, tiled=True
        )
        gate = jnp.dot(normed_two_all, wg_full, preferred_element_type=jnp.float32)
        upward = jnp.dot(normed_two_all, wu_full, preferred_element_type=jnp.float32)
        sigma = jax.nn.sigmoid(gate)
        silu_gate = gate * sigma
        hidden = (silu_gate * upward).astype(jnp.bfloat16)
        out_rows.append(
            (
                mixed
                + lax.psum_scatter(
                    jnp.dot(hidden, wd_full, preferred_element_type=jnp.float32).astype(
                        jnp.bfloat16
                    ),
                    "tensor",
                    scatter_dimension=0,
                    tiled=True,
                ).astype(jnp.float32)
            ).astype(jnp.bfloat16)
        )
        bwd = (
            lax.all_gather(gain_attn, "dp", axis=0, tiled=True),
            lax.all_gather(w_query, "dp", axis=0, tiled=True),
            lax.all_gather(w_key, "dp", axis=0, tiled=True),
            lax.all_gather(w_value, "dp", axis=0, tiled=True),
            lax.all_gather(w_out, "dp", axis=1, tiled=True),
            lax.all_gather(gain_ffn, "dp", axis=0, tiled=True),
            lax.all_gather(w_gate, "dp", axis=0, tiled=True),
            lax.all_gather(w_up, "dp", axis=0, tiled=True),
            lax.all_gather(w_down, "dp", axis=1, tiled=True),
        )
        g_attn, wq_full, wk_full, wv_full, wo_full, g_ffn, wg_full, wu_full, wd_full = bwd
        grad_here = grad_out[step]
        grad_all = lax.all_gather(grad_here, "tensor", axis=0, tiled=True)
        d_down = inner_rows(hidden, grad_all)
        grad_hidden = outer_cols(grad_all, wd_full)
        grad_gate = (grad_hidden * upward * sigma * (1.0 + gate * (1.0 - sigma))).astype(
            jnp.bfloat16
        )
        grad_up = (grad_hidden * silu_gate).astype(jnp.bfloat16)
        d_gate = inner_rows(normed_two_all, grad_gate)
        d_up = inner_rows(normed_two_all, grad_up)
        grad_normed_two = lax.psum_scatter(
            outer_cols(grad_gate, wg_full) + outer_cols(grad_up, wu_full),
            "tensor",
            scatter_dimension=0,
            tiled=True,
        )
        grad_mixed_norm, gain_part_ffn = norm_back(
            grad_normed_two, mixed, scale_two, g_ffn.astype(jnp.float32)
        )
        grad_mixed = grad_here.astype(jnp.float32) + grad_mixed_norm
        branch_all = lax.all_gather(grad_mixed.astype(jnp.bfloat16), "tensor", axis=0, tiled=True)
        d_out = inner_rows(context, branch_all)
        grad_context = (
            outer_cols(branch_all, wo_full).astype(jnp.bfloat16).reshape(L, heads_local, HD)
        )
        grad_query, grad_keys, grad_values = attention_backward(
            query, keys, values, mem_keys, mem_values, limit, lse_parts, grad_context
        )
        grad_query = grad_query.reshape(L, cols).astype(jnp.bfloat16)
        grad_keys = grad_keys.reshape(L, cols).astype(jnp.bfloat16)
        grad_values = grad_values.reshape(L, cols).astype(jnp.bfloat16)
        d_query = inner_rows(normed_all, grad_query)
        d_key = inner_rows(normed_all, grad_keys)
        d_value = inner_rows(normed_all, grad_values)
        grad_normed = lax.psum_scatter(
            (
                outer_cols(grad_query, wq_full)
                + outer_cols(grad_keys, wk_full)
                + outer_cols(grad_values, wv_full)
            ).astype(jnp.bfloat16),
            "tensor",
            scatter_dimension=0,
            tiled=True,
        ).astype(jnp.float32)
        grad_token_norm, gain_part_attn = norm_back(
            grad_normed, token_rows, scale_one, g_attn.astype(jnp.float32)
        )
        grad_rows.append(grad_mixed + grad_token_norm)
        gain_total_attn = gain_total_attn + gain_part_attn
        gain_total_ffn = gain_total_ffn + gain_part_ffn
        totals = tuple(
            (
                held + fresh
                for held, fresh in zip(
                    totals, (d_query, d_key, d_value, d_out, d_gate, d_up, d_down)
                )
            )
        )
    shares = (
        lax.psum_scatter(
            totals[0].astype(jnp.bfloat16), "dp", scatter_dimension=0, tiled=True
        ).astype(jnp.float32),
        lax.psum_scatter(
            totals[1].astype(jnp.bfloat16), "dp", scatter_dimension=0, tiled=True
        ).astype(jnp.float32),
        lax.psum_scatter(
            totals[2].astype(jnp.bfloat16), "dp", scatter_dimension=0, tiled=True
        ).astype(jnp.float32),
        lax.psum_scatter(
            totals[3].astype(jnp.bfloat16), "dp", scatter_dimension=1, tiled=True
        ).astype(jnp.float32),
        lax.psum_scatter(
            totals[4].astype(jnp.bfloat16), "dp", scatter_dimension=0, tiled=True
        ).astype(jnp.float32),
        lax.psum_scatter(
            totals[5].astype(jnp.bfloat16), "dp", scatter_dimension=0, tiled=True
        ).astype(jnp.float32),
        lax.psum_scatter(
            totals[6].astype(jnp.bfloat16), "dp", scatter_dimension=1, tiled=True
        ).astype(jnp.float32),
    )
    gain_attn_sum, gain_ffn_sum = lax.psum((gain_total_attn, gain_total_ffn), ("dp", "tensor"))
    return (
        jnp.stack(out_rows, axis=0),
        jnp.stack(grad_rows, axis=0),
        gain_attn_sum,
        shares[0],
        shares[1],
        shares[2],
        shares[3],
        gain_ffn_sum,
        shares[4],
        shares[5],
        shares[6],
    )


TQ = 512
TK = 512
ROWS = 512
HT = 256
SCALE = HD**-0.5
EXP_SCALE = SCALE * 1.4426950408889634
LOG2E = 1.4426950408889634
NT = (((1,), (1,)), ((), ()))
TN = (((0,), (0,)), ((), ()))
F32 = jnp.float32
BF16 = jnp.bfloat16
MIB = 1 << 20


def mm(left, right, dims=(((1,), (0,)), ((), ()))):
    return lax.dot_general(left, right, dims, preferred_element_type=F32)


def fold_max(values):
    best = values[:, :HD]
    for i in range(1, values.shape[1] // HD):
        best = jnp.maximum(best, values[:, i * HD : (i + 1) * HD])
    return best


def fold_sum(values):
    total = values[:, :HD]
    for i in range(1, values.shape[1] // HD):
        total = total + values[:, i * HD : (i + 1) * HD]
    return total


def reach_mask(first, tile, limit):
    rows = first + lax.broadcasted_iota(jnp.int32, (TQ, 1), 0)
    keys = tile * TK + lax.broadcasted_iota(jnp.int32, (1, TK), 1)
    reach = jnp.where(rows < limit, jnp.maximum(rows, limit - 1), rows)
    return keys <= reach


def pick_blocks(meta, block, own, other, buf):
    for i in range(KR):
        c = meta[2 + block * KR + i]
        buf[pl.ds(i * CBLOCK, CBLOCK), :] = own[0, pl.ds(pl.multiple_of(c * CBLOCK, CBLOCK), CBLOCK), :]
        d = meta[2 + (L // QBLOCK) * KR + block * KR + i]
        buf[pl.ds((KR + i) * CBLOCK, CBLOCK), :] = other[d, 0, 0]


def attend_kernel(
    meta, q_ref, k_ref, v_ref, ok_ref, ov_ref, pk_ref, pv_ref, ctx_ref, lse_ref, kbuf, vbuf, sbuf, smem, *, pair
):
    step = pl.program_id(1)
    limit = meta[0]
    first = step * TQ
    free = jnp.where(first < limit, (limit + TK - 1) // TK, 0)
    tiles = jnp.maximum(step + 1, free)
    blocks = TQ // QBLOCK
    for b in range(blocks):
        pick_blocks(meta, step * blocks + b, ok_ref, pk_ref, kbuf.at[b])
        pick_blocks(meta, step * blocks + b, ov_ref, pv_ref, vbuf.at[b])
    state = []
    for h in range(pair):
        cs = pl.ds(h * HD, HD)
        best = []
        for b in range(blocks):
            s = mm(q_ref[pl.ds(b * QBLOCK, QBLOCK), cs], kbuf[b, :, cs], NT)
            smem[h, pl.ds(b * QBLOCK, QBLOCK), :] = s
            best.append(fold_max(s))
        state.append(jnp.concatenate(best, 0))

    def scores(tile, state, masked):
        ks = pl.ds(pl.multiple_of(tile * TK, TK), TK)
        if masked:
            allowed = reach_mask(first, tile, limit)
        new = []
        for h in range(pair):
            cs = pl.ds(h * HD, HD)
            s = mm(q_ref[:, cs], k_ref[ks, cs], NT)
            if masked:
                s = jnp.where(allowed, s, NEGATIVE)
            sbuf[h, tile] = s
            new.append(jnp.maximum(state[h], fold_max(s)))
        return tuple(new)

    state = lax.fori_loop(0, step, lambda tile, s: scores(tile, s, False), tuple(state))
    state = lax.fori_loop(step, tiles, lambda tile, s: scores(tile, s, True), state)
    tops = [jnp.max(s, axis=1, keepdims=True) for s in state]
    state = []
    for h in range(pair):
        cs = pl.ds(h * HD, HD)
        p = jnp.exp2((smem[h] - tops[h]) * EXP_SCALE)
        low = p.astype(BF16)
        parts = [mm(low[b * QBLOCK : (b + 1) * QBLOCK], vbuf[b, :, cs]) for b in range(blocks)]
        state.append((fold_sum(p), jnp.concatenate(parts, 0)))

    def weigh(tile, state):
        ks = pl.ds(pl.multiple_of(tile * TK, TK), TK)
        new = []
        for h in range(pair):
            total, acc = state[h]
            p = jnp.exp2((sbuf[h, tile] - tops[h]) * EXP_SCALE)
            new.append((total + fold_sum(p), acc + mm(p.astype(BF16), v_ref[ks, pl.ds(h * HD, HD)])))
        return tuple(new)

    state = lax.fori_loop(0, tiles, weigh, tuple(state))
    for h in range(pair):
        cs = pl.ds(h * HD, HD)
        total = jnp.sum(state[h][0], axis=1, keepdims=True)
        ctx_ref[:, cs] = (state[h][1] / total).astype(BF16)
        lse_ref[:, cs] = jnp.broadcast_to(tops[h] * SCALE + jnp.log(total), (TQ, HD))


def attend_back_kernel(
    meta, q_ref, k_ref, v_ref, ok_ref, ov_ref, pk_ref, pv_ref, do_ref, ctx_ref, lse_ref,
    dq_ref, dk_ref, dv_ref, kbuf, vbuf, dks, dvs, *, pair
):
    step = pl.program_id(1)
    limit = meta[0]
    first = step * TQ
    free = jnp.where(first < limit, (limit + TK - 1) // TK, 0)
    tiles = jnp.maximum(step + 1, free)
    blocks = TQ // QBLOCK

    @pl.when(step == 0)
    def _():
        dks[...] = jnp.zeros_like(dks)
        dvs[...] = jnp.zeros_like(dvs)

    for b in range(blocks):
        pick_blocks(meta, step * blocks + b, ok_ref, pk_ref, kbuf.at[b])
        pick_blocks(meta, step * blocks + b, ov_ref, pv_ref, vbuf.at[b])
    state = []
    aux = []
    for h in range(pair):
        cs = pl.ds(h * HD, HD)
        delta = jnp.sum(do_ref[:, cs].astype(F32) * ctx_ref[:, cs].astype(F32), axis=1, keepdims=True)
        lse2 = lse_ref[:, cs][:, :1] * LOG2E
        aux.append((lse2, delta))
        parts = []
        for b in range(blocks):
            rs = pl.ds(b * QBLOCK, QBLOCK)
            s = mm(q_ref[rs, cs], kbuf[b, :, cs], NT)
            p = jnp.exp2(s * EXP_SCALE - lse2[b * QBLOCK : (b + 1) * QBLOCK])
            dp = mm(do_ref[rs, cs], vbuf[b, :, cs], NT)
            ds = (p * (dp - delta[b * QBLOCK : (b + 1) * QBLOCK])).astype(BF16)
            parts.append(mm(ds, kbuf[b, :, cs]))
        state.append(jnp.concatenate(parts, 0))

    def grads(tile, state, masked):
        ks = pl.ds(pl.multiple_of(tile * TK, TK), TK)
        if masked:
            allowed = reach_mask(first, tile, limit)
        new = []
        for h in range(pair):
            cs = pl.ds(h * HD, HD)
            lse2, delta = aux[h]
            s = mm(q_ref[:, cs], k_ref[ks, cs], NT)
            p = jnp.exp2(s * EXP_SCALE - lse2)
            if masked:
                p = jnp.where(allowed, p, 0.0)
            dp = mm(do_ref[:, cs], v_ref[ks, cs], NT)
            ds = (p * (dp - delta)).astype(BF16)
            dvs[ks, cs] += mm(p.astype(BF16), do_ref[:, cs], TN)
            dks[ks, cs] += mm(ds, q_ref[:, cs], TN)
            new.append(state[h] + mm(ds, k_ref[ks, cs]))
        return tuple(new)

    state = lax.fori_loop(0, step, lambda tile, s: grads(tile, s, False), tuple(state))
    state = lax.fori_loop(step, tiles, lambda tile, s: grads(tile, s, True), state)
    for h in range(pair):
        dq_ref[:, pl.ds(h * HD, HD)] = (state[h] * SCALE).astype(BF16)

    @pl.when(step == L // TQ - 1)
    def _():
        dk_ref[...] = (dks[...] * SCALE).astype(BF16)
        dv_ref[...] = dvs[...].astype(BF16)


def attention_specs(heads, pair):
    wide = pair * HD
    per = heads // 2 // pair
    groups = heads // pair
    return [
        pl.BlockSpec((TQ, wide), lambda h, i, meta: (i, h)),
        pl.BlockSpec((L, wide), lambda h, i, meta: (0, groups + h)),
        pl.BlockSpec((L, wide), lambda h, i, meta: (0, 2 * groups + h)),
        pl.BlockSpec((1, CACHE_LEN, wide), lambda h, i, meta: ((h // per) ^ meta[1], 0, h % per)),
        pl.BlockSpec((1, CACHE_LEN, wide), lambda h, i, meta: ((h // per) ^ meta[1], 0, h % per)),
        pl.BlockSpec(
            (CACHE_LEN // CBLOCK, 1, 1, CBLOCK, wide),
            lambda h, i, meta: (0, (h // per) ^ meta[1], 0, 0, h % per),
        ),
        pl.BlockSpec(
            (CACHE_LEN // CBLOCK, 1, 1, CBLOCK, wide),
            lambda h, i, meta: (0, (h // per) ^ meta[1], 1, 0, h % per),
        ),
    ]


def attend(meta, qkv, own_k, own_v, fetched, pair=2):
    width = qkv.shape[1] // 3
    heads = width // HD
    wide = pair * HD
    row = pl.BlockSpec((TQ, wide), lambda h, i, meta: (i, h))
    area = L * 1900 * width
    return pl.pallas_call(
        functools.partial(attend_kernel, pair=pair),
        grid_spec=pltpu.PrefetchScalarGridSpec(
            num_scalar_prefetch=1,
            grid=(heads // pair, L // TQ),
            in_specs=attention_specs(heads, pair),
            out_specs=[row, row],
            scratch_shapes=[pltpu.VMEM((TQ // QBLOCK, 2 * KR * CBLOCK, wide), BF16)] * 2
            + [pltpu.VMEM((pair, L // TK, TQ, TK), F32), pltpu.VMEM((pair, TQ, 2 * KR * CBLOCK), F32)],
        ),
        out_shape=[jax.ShapeDtypeStruct((L, width), BF16), jax.ShapeDtypeStruct((L, width), F32)],
        compiler_params=pltpu.CompilerParams(vmem_limit_bytes=40 * MIB),
        cost_estimate=pl.CostEstimate(flops=8 * area, bytes_accessed=30 * MIB, transcendentals=area // HD),
        name="attend",
    )(meta, qkv, qkv, qkv, own_k, own_v, fetched, fetched)


def attend_back(meta, qkv, own_k, own_v, fetched, grad_context, context, lse, pair=2):
    width = context.shape[1]
    heads = width // HD
    wide = pair * HD
    row = pl.BlockSpec((TQ, wide), lambda h, i, meta: (i, h))
    col = pl.BlockSpec((L, wide), lambda h, i, meta: (0, h))
    area = L * 1900 * width
    return pl.pallas_call(
        functools.partial(attend_back_kernel, pair=pair),
        grid_spec=pltpu.PrefetchScalarGridSpec(
            num_scalar_prefetch=1,
            grid=(heads // pair, L // TQ),
            in_specs=attention_specs(heads, pair) + [row, row, row],
            out_specs=[row, col, col],
            scratch_shapes=[pltpu.VMEM((TQ // QBLOCK, 2 * KR * CBLOCK, wide), BF16)] * 2
            + [pltpu.VMEM((L, wide), F32)] * 2,
        ),
        out_shape=[jax.ShapeDtypeStruct((L, width), BF16)] * 3,
        compiler_params=pltpu.CompilerParams(vmem_limit_bytes=48 * MIB),
        cost_estimate=pl.CostEstimate(flops=12 * area, bytes_accessed=40 * MIB, transcendentals=area // HD),
        name="attend_back",
    )(meta, qkv, qkv, qkv, own_k, own_v, fetched, fetched, grad_context, context, lse)


def project_kernel(x_ref, gain_ref, w_ref, normed_ref, qkv_ref):
    rows = x_ref[...].astype(F32)
    scale = lax.rsqrt(jnp.mean(rows * rows, axis=1, keepdims=True) + EPS)
    normed_ref[...] = (rows * scale * gain_ref[...]).astype(BF16)
    left = normed_ref[...]

    def chunk(c, carry):
        cs = pl.ds(pl.multiple_of(c * 512, 512), 512)
        qkv_ref[:, cs] = mm(left, w_ref[:, cs]).astype(BF16)
        return carry

    lax.fori_loop(0, qkv_ref.shape[1] // 512, chunk, 0)


def project(x, gain, weights):
    width = x.shape[1]
    cols = 3 * width
    row = lambda n: pl.BlockSpec((ROWS, n), lambda i: (i, 0))
    whole = lambda n: pl.BlockSpec((width, n), lambda i: (0, 0))
    return pl.pallas_call(
        project_kernel,
        grid=(L // ROWS,),
        in_specs=[row(width), pl.BlockSpec((1, width), lambda i: (0, 0)), whole(cols)],
        out_specs=[row(width), row(cols)],
        out_shape=[jax.ShapeDtypeStruct((L, width), BF16), jax.ShapeDtypeStruct((L, cols), BF16)],
        compiler_params=pltpu.CompilerParams(vmem_limit_bytes=40 * MIB),
        cost_estimate=pl.CostEstimate(flops=2 * L * width * cols, bytes_accessed=26 * MIB, transcendentals=0),
        name="project",
    )(x, gain, weights)


def mix_kernel(x_ref, ctx_ref, gain_ref, w_ref, mixed_ref, normed_ref):
    mixed = x_ref[...].astype(F32) + mm(ctx_ref[...], w_ref[...], NT)
    mixed_ref[...] = mixed
    scale = lax.rsqrt(jnp.mean(mixed * mixed, axis=1, keepdims=True) + EPS)
    normed_ref[...] = (mixed * scale * gain_ref[...]).astype(BF16)


def mix(x, context, gain, weights):
    width = x.shape[1]
    row = pl.BlockSpec((ROWS, width), lambda i: (i, 0))
    return pl.pallas_call(
        mix_kernel,
        grid=(L // ROWS,),
        in_specs=[row, row, pl.BlockSpec((1, width), lambda i: (0, 0)), pl.BlockSpec((width, width), lambda i: (0, 0))],
        out_specs=[row, row],
        out_shape=[jax.ShapeDtypeStruct((L, width), F32), jax.ShapeDtypeStruct((L, width), BF16)],
        compiler_params=pltpu.CompilerParams(vmem_limit_bytes=32 * MIB),
        cost_estimate=pl.CostEstimate(flops=2 * L * width * width, bytes_accessed=22 * MIB, transcendentals=0),
        name="mix",
    )(x, context, gain, weights)


def ffn_kernel(n_ref, g_ref, wg_ref, wu_ref, wd_ref, out_ref, gn_ref, dg_ref, du_ref, dd_ref, acc, ag, au, ad):
    tile = pl.program_id(0)
    last = pl.num_programs(0) - 1

    @pl.when(tile == 0)
    def _():
        acc[...] = jnp.zeros_like(acc)
        gn_ref[...] = jnp.zeros_like(gn_ref)

    ag[...] = jnp.zeros_like(ag)
    au[...] = jnp.zeros_like(au)
    ad[...] = jnp.zeros_like(ad)

    def chunk(r, carry):
        rs = pl.ds(pl.multiple_of(r * ROWS, ROWS), ROWS)
        rows = n_ref[rs, :]
        cotangent = g_ref[rs, :]
        gate = mm(rows, wg_ref[...])
        up = mm(rows, wu_ref[...])
        grad_hidden = mm(cotangent, wd_ref[...])
        sigma = 1.0 / (1.0 + jnp.exp(-gate))
        silu = gate * sigma
        hidden = (silu * up).astype(BF16)
        grad_gate = (grad_hidden * up * (sigma * (1.0 + gate * (1.0 - sigma)))).astype(BF16)
        grad_up = (grad_hidden * silu).astype(BF16)
        acc[rs, :] += mm(hidden, wd_ref[...], NT)
        gn_ref[rs, :] += mm(grad_gate, wg_ref[...], NT) + mm(grad_up, wu_ref[...], NT)
        ag[...] += mm(rows, grad_gate, TN)
        au[...] += mm(rows, grad_up, TN)
        ad[...] += mm(cotangent, hidden, TN)
        return carry

    lax.fori_loop(0, L // ROWS, chunk, 0)
    dg_ref[...] = ag[...].astype(BF16)
    du_ref[...] = au[...].astype(BF16)
    dd_ref[...] = ad[...].astype(BF16)

    @pl.when(tile == last)
    def _():
        out_ref[...] = acc[...].astype(BF16)


def ffn(normed, cotangent, weights, width, hidden):
    once = pl.Buffered(1)
    tiles = hidden // HT
    lead = width // HT
    part = lambda k: pl.BlockSpec((width, HT), lambda j: (0, lead + k * tiles + j))
    whole = pl.BlockSpec((L, width), lambda j: (0, 0), pipeline_mode=once)
    grad = pl.BlockSpec((width, HT), lambda j: (0, j))
    return pl.pallas_call(
        ffn_kernel,
        grid=(tiles,),
        in_specs=[whole, whole, part(0), part(1), part(2)],
        out_specs=[whole, whole, grad, grad, grad],
        out_shape=[jax.ShapeDtypeStruct((L, width), BF16), jax.ShapeDtypeStruct((L, width), F32)]
        + [jax.ShapeDtypeStruct((width, hidden), BF16)] * 3,
        scratch_shapes=[pltpu.VMEM((L, width), F32)] + [pltpu.VMEM((width, HT), F32)] * 3,
        compiler_params=pltpu.CompilerParams(vmem_limit_bytes=56 * MIB),
        cost_estimate=pl.CostEstimate(
            flops=18 * L * width * hidden, bytes_accessed=60 * MIB, transcendentals=L * hidden
        ),
        name="ffn",
    )(normed, cotangent, weights, weights, weights)


def unmix_kernel(mixed_ref, gn_ref, ffn_ref, g_ref, gain_ref, w_ref, out_ref, gm_ref, br_ref, gc_ref, gg_ref):
    mixed = mixed_ref[...]
    grad = gn_ref[...]
    scale = lax.rsqrt(jnp.mean(mixed * mixed, axis=1, keepdims=True) + EPS)
    unit = mixed * scale
    inner = grad * gain_ref[...]
    grad_mixed = g_ref[...].astype(F32) + scale * (inner - unit * jnp.mean(inner * unit, axis=1, keepdims=True))
    out_ref[...] = (mixed + ffn_ref[...].astype(F32)).astype(BF16)
    gm_ref[...] = grad_mixed
    branch = grad_mixed.astype(BF16)
    br_ref[...] = branch
    gc_ref[...] = mm(branch, w_ref[...]).astype(BF16)

    @pl.when(pl.program_id(0) == 0)
    def _():
        gg_ref[...] = jnp.zeros_like(gg_ref)

    gg_ref[...] += jnp.sum(grad * unit, axis=0, keepdims=True)


def unmix(mixed, grad_normed, ffn_out, cotangent, gain, weights):
    width = mixed.shape[1]
    rows = ROWS // 2
    row = pl.BlockSpec((rows, width), lambda i: (i, 0))
    one = pl.BlockSpec((1, width), lambda i: (0, 0))
    return pl.pallas_call(
        unmix_kernel,
        grid=(L // rows,),
        in_specs=[row, row, row, row, one, pl.BlockSpec((width, width), lambda i: (0, 0))],
        out_specs=[row, row, row, row, one],
        out_shape=[
            jax.ShapeDtypeStruct((L, width), BF16),
            jax.ShapeDtypeStruct((L, width), F32),
            jax.ShapeDtypeStruct((L, width), BF16),
            jax.ShapeDtypeStruct((L, width), BF16),
            jax.ShapeDtypeStruct((1, width), F32),
        ],
        compiler_params=pltpu.CompilerParams(vmem_limit_bytes=40 * MIB),
        cost_estimate=pl.CostEstimate(flops=2 * L * width * width, bytes_accessed=46 * MIB, transcendentals=0),
        name="unmix",
    )(mixed, grad_normed, ffn_out, cotangent, gain, weights)


def finish_kernel(x_ref, gm_ref, dq_ref, dk_ref, dv_ref, gain_ref, w_ref, gt_ref, gg_ref):
    width = x_ref.shape[1]
    grad = mm(dq_ref[...], w_ref[:, :width], NT)
    grad += mm(dk_ref[...], w_ref[:, width : 2 * width], NT)
    grad += mm(dv_ref[...], w_ref[:, 2 * width : 3 * width], NT)
    rows = x_ref[...].astype(F32)
    scale = lax.rsqrt(jnp.mean(rows * rows, axis=1, keepdims=True) + EPS)
    unit = rows * scale
    inner = grad * gain_ref[...]
    back = scale * (inner - unit * jnp.mean(inner * unit, axis=1, keepdims=True))
    gt_ref[...] = (gm_ref[...] + back).astype(BF16)

    @pl.when(pl.program_id(0) == 0)
    def _():
        gg_ref[...] = jnp.zeros_like(gg_ref)

    gg_ref[...] += jnp.sum(grad * unit, axis=0, keepdims=True)


def finish(x, grad_mixed, dq, dk, dv, gain, weights):
    width = x.shape[1]
    row = pl.BlockSpec((ROWS, width), lambda i: (i, 0))
    one = pl.BlockSpec((1, width), lambda i: (0, 0))
    return pl.pallas_call(
        finish_kernel,
        grid=(L // ROWS,),
        in_specs=[row, row, row, row, row, one, pl.BlockSpec((width, 3 * width), lambda i: (0, 0))],
        out_specs=[row, one],
        out_shape=[jax.ShapeDtypeStruct((L, width), BF16), jax.ShapeDtypeStruct((1, width), F32)],
        compiler_params=pltpu.CompilerParams(vmem_limit_bytes=48 * MIB),
        cost_estimate=pl.CostEstimate(flops=6 * L * width * width, bytes_accessed=40 * MIB, transcendentals=0),
        name="finish",
    )(x, grad_mixed, dq, dk, dv, gain, weights)


def pick_kernel(table, held_ref, sent_ref, sems):
    def copy(i):
        return pltpu.make_async_copy(held_ref.at[table[i]], sent_ref.at[i], sems.at[i])

    for i in range(sent_ref.shape[0]):
        copy(i).start()
    for i in range(sent_ref.shape[0]):
        copy(i).wait()


def pick_rows(table, held):
    count = held.shape[0]
    return pl.pallas_call(
        pick_kernel,
        grid_spec=pltpu.PrefetchScalarGridSpec(
            num_scalar_prefetch=1,
            grid=(),
            in_specs=[pl.BlockSpec(memory_space=pl.ANY)],
            out_specs=pl.BlockSpec(memory_space=pl.ANY),
            scratch_shapes=[pltpu.SemaphoreType.DMA((count,))],
        ),
        out_shape=jax.ShapeDtypeStruct(held.shape, held.dtype),
        cost_estimate=pl.CostEstimate(flops=0, bytes_accessed=2 * held.size * 2, transcendentals=0),
        name="pick_rows",
    )(table, held)


def swap(values):
    return lax.ppermute(values, "tensor", [(0, 1), (1, 0)])


def sequence_body(
    tokens, gain_attn, w_query, w_key, w_value, w_out, gain_ffn, w_gate, w_up, w_down,
    cache_keys, cache_values, prefix, partner, own_blocks, partner_blocks, grad_out,
):
    micro, shard_len, width = tokens.shape
    devices = lax.axis_size("dp")
    seqs = micro * devices
    rows_held, cols = w_query.shape
    hidden_held = w_gate.shape[1]
    hidden = 2 * hidden_held
    spot = lax.axis_index("tensor")
    exchange = functools.partial(lax.all_to_all, axis_name="tensor", split_axis=0, concat_axis=0, tiled=True)
    chunks = CACHE_LEN // CBLOCK

    small = jnp.concatenate([w_query, w_key, w_value], axis=1)
    small_other = swap(small)
    partner_column = jnp.zeros((rows_held, 1), BF16).at[:micro, 0].set(partner.astype(BF16))
    extra = jnp.concatenate(
        [gain_attn[:, None], gain_ffn[:, None], partner_column, jnp.zeros((rows_held, HD - 3), BF16)], axis=1
    )
    first_rows = jnp.concatenate(
        [
            w_query, small_other[:, :cols], w_key, small_other[:, cols : 2 * cols],
            w_value, small_other[:, 2 * cols :], extra,
        ],
        axis=1,
    )
    first_all = lax.all_gather(first_rows, "dp", axis=0, tiled=True)
    x = exchange(tokens).reshape(L, width)
    cotangent = exchange(grad_out).reshape(L, width)
    own_k = exchange(cache_keys)
    own_v = exchange(cache_values)

    spread = jnp.stack(
        [cache_keys.reshape(micro, chunks, CBLOCK, cols), cache_values.reshape(micro, chunks, CBLOCK, cols)], axis=2
    ).swapaxes(0, 1)
    per = chunks // devices
    held = lax.all_to_all(
        spread.reshape(chunks, micro * 2 * CBLOCK, cols), "dp", split_axis=0, concat_axis=0, tiled=True
    )

    big = jnp.concatenate([w_out.T, w_gate, w_up, w_down.T], axis=1)
    big_other = swap(big)
    a, b, c = cols, cols + hidden_held, cols + 2 * hidden_held
    second_rows = jnp.concatenate(
        [
            big[:, :a], big_other[:, :a], big[:, a:b], big_other[:, a:b],
            big[:, b:c], big_other[:, b:c], big[:, c:], big_other[:, c:],
        ],
        axis=1,
    )
    second_all = lax.all_gather(second_rows, "dp", axis=0, tiled=True)

    tail = first_all[:, 3 * width :]
    gains = tail[:, :2].astype(F32).T
    gain_one, gain_two = gains[:1], gains[1:]
    table = tail[:, 2].reshape(devices, rows_held)[:, :micro].reshape(seqs).astype(jnp.int32)
    sent = pick_rows(table, held.reshape(seqs, 2 * CBLOCK, cols))
    fetched = lax.all_to_all(sent, ("dp", "tensor"), split_axis=0, concat_axis=0, tiled=True)
    fetched = fetched.reshape(chunks, 2, 2, CBLOCK, cols)

    meta = jnp.concatenate(
        [
            prefix[spot][None], spot[None].astype(jnp.int32),
            own_blocks[spot].reshape(-1), partner_blocks[spot].reshape(-1),
        ]
    )
    normed, qkv = project(x, gain_one, first_all)
    context, lse = attend(meta, qkv, own_k, own_v, fetched)
    mixed, normed_two = mix(x, context, gain_two, second_all)
    ffn_out, grad_normed_two, d_gate, d_up, d_down = ffn(normed_two, cotangent, second_all, width, hidden)
    share = functools.partial(lax.psum_scatter, axis_name="dp", scatter_dimension=0, tiled=True)
    ffn_share = share(jnp.concatenate([d_gate, d_up, d_down], axis=1))
    out, grad_mixed, branch, grad_context, gain_part_two = unmix(
        mixed, grad_normed_two, ffn_out, cotangent, gain_two, second_all
    )
    out = exchange(out.reshape(2, shard_len, width))
    d_out = inner_rows(branch, context).astype(BF16)
    dq, dk, dv = attend_back(meta, qkv, own_k, own_v, fetched, grad_context, context, lse)
    d_qkv = [inner_rows(normed, d).astype(BF16) for d in (dq, dk, dv)]
    attn_share = share(jnp.concatenate([d_out] + d_qkv, axis=1))
    grad_tokens, gain_part_one = finish(x, grad_mixed, dq, dk, dv, gain_one, first_all)
    grad_tokens = exchange(grad_tokens.reshape(2, shard_len, width)).astype(F32)

    def halves(values, widths):
        mine, theirs, start = [], [], 0
        for w in widths:
            mine.append(values[:, start : start + w])
            theirs.append(values[:, start + w : start + 2 * w])
            start += 2 * w
        got = swap(jnp.concatenate(theirs, axis=1))
        total = jnp.concatenate(mine, axis=1).astype(F32) + got.astype(F32)
        return jnp.split(total, [sum(widths[: i + 1]) for i in range(len(widths) - 1)], axis=1)

    g_gate, g_up, g_down = halves(ffn_share, [hidden_held] * 3)
    g_out, g_query, g_key, g_value = halves(attn_share, [cols] * 4)
    gain_sums = lax.psum(jnp.concatenate([gain_part_one, gain_part_two], axis=0), ("dp", "tensor"))
    return (
        out, grad_tokens, gain_sums[0], g_query, g_key, g_value, g_out.T, gain_sums[1], g_gate, g_up, g_down.T,
    )


def solution(mesh):
    in_specs = (
        P("dp", "tensor", None),
        P("dp"),
        P("dp", "tensor"),
        P("dp", "tensor"),
        P("dp", "tensor"),
        P("tensor", "dp"),
        P("dp"),
        P("dp", "tensor"),
        P("dp", "tensor"),
        P("tensor", "dp"),
        P("dp", None, "tensor"),
        P("dp", None, "tensor"),
        P("dp"),
        P("dp"),
        P("dp", None, None),
        P("dp", None, None),
        P("dp", "tensor", None),
    )
    out_specs = (
        P("dp", "tensor", None),
        P("dp", "tensor", None),
        P(),
        P("dp", "tensor"),
        P("dp", "tensor"),
        P("dp", "tensor"),
        P("tensor", "dp"),
        P(),
        P("dp", "tensor"),
        P("dp", "tensor"),
        P("tensor", "dp"),
    )
    whole = mesh.shape["tensor"] == 2 and mesh.shape["dp"] == CACHE_LEN // CBLOCK
    body = sequence_body if whole else tensor_body
    return jax.shard_map(body, mesh=mesh, in_specs=in_specs, out_specs=out_specs, check_vma=False)
```

```python
import functools

import jax
import jax.numpy as jnp
from jax import lax
from jax.experimental import pallas as pl
from jax.experimental.pallas import tpu as pltpu
from jax.sharding import PartitionSpec as P

HD = 128
L = 2048
CACHE_LEN = 1024
QBLOCK = 128
CBLOCK = 64
KR = 4
QROWS = 512


EPS = 1e-05
NEGATIVE = -1e30


def norm_rows(values, gain):
    scale_rows = lax.rsqrt(jnp.mean(values * values, axis=-1, keepdims=True) + EPS)
    return (values * scale_rows * gain, scale_rows)


def norm_back(grad_normed, values, scale_rows, gain):
    unit = values * scale_rows
    grad_unit = grad_normed * gain
    grad_values = scale_rows * (
        grad_unit - unit * jnp.mean(grad_unit * unit, axis=-1, keepdims=True)
    )
    return (grad_values, jnp.sum(grad_normed * unit, axis=0))


def inner_rows(left, right):
    return lax.dot_general(
        left, right, (((0,), (0,)), ((), ())), preferred_element_type=jnp.float32
    )


def outer_cols(left, right):
    return lax.dot_general(
        left, right, (((1,), (1,)), ((), ())), preferred_element_type=jnp.float32
    )


def memory_rows(cache_one, chosen, width):
    shaped = cache_one.reshape(CACHE_LEN // CBLOCK, CBLOCK, width)
    return jnp.take(shaped, chosen, axis=0)


def block_scores(query_block, keys_part, mem_part, first_row, limit):
    rows_here, heads_here, size = query_block.shape
    extent = keys_part.shape[0]
    local = jnp.einsum(
        "qhd,khd->hqk", query_block, keys_part, preferred_element_type=jnp.float32
    ) * size ** (-0.5)
    row_ids = first_row + jnp.arange(rows_here, dtype=jnp.int32)[:, None]
    key_ids = jnp.arange(extent, dtype=jnp.int32)[None, :]
    allowed = (key_ids <= row_ids) | (row_ids < limit) & (key_ids < limit)
    local = jnp.where(allowed[None], local, NEGATIVE)
    groups = mem_part.shape[0]
    grouped = query_block.reshape(groups, rows_here // groups, heads_here, size)
    remote = jnp.einsum(
        "bqhd,bkhd->hbqk", grouped, mem_part, preferred_element_type=jnp.float32
    ) * size ** (-0.5)
    return (local, remote.reshape(heads_here, rows_here, -1))


def attention_forward(query, keys, values, mem_keys, mem_values, limit):
    groups = QROWS // QBLOCK
    heads_here = query.shape[1]
    context_parts = []
    lse_parts = []
    for index in range(L // QROWS):
        first = index * QROWS
        extent = max(first + QROWS, L // 2)
        query_block = query[first : first + QROWS]
        mem_k = mem_keys[index * groups : (index + 1) * groups]
        mem_v = mem_values[index * groups : (index + 1) * groups]
        local, remote = block_scores(query_block, keys[:extent], mem_k, first, limit)
        top = jnp.maximum(jnp.max(local, axis=-1), jnp.max(remote, axis=-1))
        e_local = jnp.exp(local - top[..., None])
        e_remote = jnp.exp(remote - top[..., None])
        total = jnp.sum(e_local, axis=-1) + jnp.sum(e_remote, axis=-1)
        p_local = (e_local / total[..., None]).astype(jnp.bfloat16)
        p_remote = (
            (e_remote / total[..., None])
            .astype(jnp.bfloat16)
            .reshape(heads_here, groups, QBLOCK, -1)
        )
        part = jnp.einsum(
            "hqk,khd->qhd", p_local, values[:extent], preferred_element_type=jnp.float32
        )
        extra = jnp.einsum("hbqk,bkhd->bqhd", p_remote, mem_v, preferred_element_type=jnp.float32)
        context_parts.append(part + extra.reshape(part.shape))
        lse_parts.append(top + jnp.log(total))
    return (jnp.concatenate(context_parts, axis=0), lse_parts)


def attention_backward(query, keys, values, mem_keys, mem_values, limit, lse_parts, grad_context):
    groups = QROWS // QBLOCK
    length, heads_here, size = query.shape
    scale = size ** (-0.5)
    grad_query_parts = []
    grad_keys = jnp.zeros(query.shape, jnp.float32)
    grad_values = jnp.zeros(query.shape, jnp.float32)
    for index in range(L // QROWS):
        first = index * QROWS
        extent = max(first + QROWS, L // 2)
        query_block = query[first : first + QROWS]
        mem_k = mem_keys[index * groups : (index + 1) * groups]
        mem_v = mem_values[index * groups : (index + 1) * groups]
        local, remote = block_scores(query_block, keys[:extent], mem_k, first, limit)
        lse_block = lse_parts[index][..., None]
        p_local = jnp.exp(local - lse_block)
        p_remote = jnp.exp(remote - lse_block)
        grad_block = grad_context[first : first + QROWS]
        grouped_grad = grad_block.reshape(groups, QBLOCK, heads_here, size)
        dp_local = jnp.einsum(
            "qhd,khd->hqk", grad_block, values[:extent], preferred_element_type=jnp.float32
        )
        dp_remote = jnp.einsum(
            "bqhd,bkhd->hbqk", grouped_grad, mem_v, preferred_element_type=jnp.float32
        )
        dp_remote = dp_remote.reshape(heads_here, QROWS, -1)
        delta = jnp.sum(p_local * dp_local, axis=-1) + jnp.sum(p_remote * dp_remote, axis=-1)
        ds_local = (p_local * (dp_local - delta[..., None])).astype(jnp.bfloat16)
        ds_remote = (p_remote * (dp_remote - delta[..., None])).astype(jnp.bfloat16)
        ds_remote = ds_remote.reshape(heads_here, groups, QBLOCK, -1)
        dq_block = jnp.einsum(
            "hqk,khd->qhd", ds_local, keys[:extent], preferred_element_type=jnp.float32
        )
        dq_extra = jnp.einsum(
            "hbqk,bkhd->bqhd", ds_remote, mem_k, preferred_element_type=jnp.float32
        )
        grad_query_parts.append((dq_block + dq_extra.reshape(dq_block.shape)) * scale)
        dk_part = (
            jnp.einsum("hqk,qhd->khd", ds_local, query_block, preferred_element_type=jnp.float32)
            * scale
        )
        dv_part = jnp.einsum(
            "hqk,qhd->khd",
            p_local.astype(jnp.bfloat16),
            grad_block,
            preferred_element_type=jnp.float32,
        )
        grad_keys = grad_keys.at[:extent].add(dk_part)
        grad_values = grad_values.at[:extent].add(dv_part)
    return (jnp.concatenate(grad_query_parts, axis=0), grad_keys, grad_values)


def tensor_body(
    tokens,
    gain_attn,
    w_query,
    w_key,
    w_value,
    w_out,
    gain_ffn,
    w_gate,
    w_up,
    w_down,
    cache_keys,
    cache_values,
    prefix,
    partner,
    own_blocks,
    partner_blocks,
    grad_out,
):
    micro, shard_len, width = tokens.shape
    cols = w_query.shape[1]
    heads_local = cols // HD
    qblocks = L // QBLOCK
    mem_len = 2 * KR * CBLOCK
    piece_keys = lax.all_gather(cache_keys, "dp", axis=0, tiled=True)
    piece_values = lax.all_gather(cache_values, "dp", axis=0, tiled=True)
    count = piece_keys.shape[0]
    onehot = (partner[:, None] == jnp.arange(count, dtype=jnp.int32)[None, :]).astype(jnp.bfloat16)
    add_keys = jnp.einsum("mn,nkc->mkc", onehot, piece_keys, preferred_element_type=jnp.float32)
    add_values = jnp.einsum("mn,nkc->mkc", onehot, piece_values, preferred_element_type=jnp.float32)
    fetched_keys = add_keys.astype(jnp.bfloat16)
    fetched_values = add_values.astype(jnp.bfloat16)
    totals = (
        jnp.zeros((width, cols), jnp.float32),
        jnp.zeros((width, cols), jnp.float32),
        jnp.zeros((width, cols), jnp.float32),
        jnp.zeros((cols, width), jnp.float32),
        jnp.zeros((width, w_gate.shape[1]), jnp.float32),
        jnp.zeros((width, w_gate.shape[1]), jnp.float32),
        jnp.zeros((w_gate.shape[1], width), jnp.float32),
    )
    shares = tuple(
        (
            jnp.zeros(w.shape, jnp.float32)
            for w in (w_query, w_key, w_value, w_out, w_gate, w_up, w_down)
        )
    )
    gain_total_attn = jnp.zeros((width,), jnp.float32)
    gain_total_ffn = jnp.zeros((width,), jnp.float32)
    out_rows = []
    grad_rows = []
    for step in range(micro):
        fwd = (
            lax.all_gather(gain_attn, "dp", axis=0, tiled=True),
            lax.all_gather(w_query, "dp", axis=0, tiled=True),
            lax.all_gather(w_key, "dp", axis=0, tiled=True),
            lax.all_gather(w_value, "dp", axis=0, tiled=True),
            lax.all_gather(w_out, "dp", axis=1, tiled=True),
            lax.all_gather(gain_ffn, "dp", axis=0, tiled=True),
            lax.all_gather(w_gate, "dp", axis=0, tiled=True),
            lax.all_gather(w_up, "dp", axis=0, tiled=True),
            lax.all_gather(w_down, "dp", axis=1, tiled=True),
        )
        g_attn, wq_full, wk_full, wv_full, wo_full, g_ffn, wg_full, wu_full, wd_full = fwd
        limit = prefix[step]
        own_k = memory_rows(cache_keys[step], own_blocks[step], cols)
        par_k = memory_rows(fetched_keys[step], partner_blocks[step], cols)
        own_v = memory_rows(cache_values[step], own_blocks[step], cols)
        par_v = memory_rows(fetched_values[step], partner_blocks[step], cols)
        mem_keys = jnp.concatenate([own_k, par_k], axis=1).reshape(
            qblocks, mem_len, heads_local, HD
        )
        mem_values = jnp.concatenate([own_v, par_v], axis=1).reshape(
            qblocks, mem_len, heads_local, HD
        )
        token_rows = tokens[step].astype(jnp.float32)
        normed, scale_one = norm_rows(token_rows, g_attn.astype(jnp.float32))
        normed_all = lax.all_gather(normed.astype(jnp.bfloat16), "tensor", axis=0, tiled=True)
        query = (
            jnp.dot(normed_all, wq_full, preferred_element_type=jnp.float32)
            .astype(jnp.bfloat16)
            .reshape(L, heads_local, HD)
        )
        keys = (
            jnp.dot(normed_all, wk_full, preferred_element_type=jnp.float32)
            .astype(jnp.bfloat16)
            .reshape(L, heads_local, HD)
        )
        values = (
            jnp.dot(normed_all, wv_full, preferred_element_type=jnp.float32)
            .astype(jnp.bfloat16)
            .reshape(L, heads_local, HD)
        )
        context_full, lse_parts = attention_forward(
            query, keys, values, mem_keys, mem_values, limit
        )
        context = context_full.reshape(L, cols).astype(jnp.bfloat16)
        mixed = token_rows + lax.psum_scatter(
            jnp.dot(context, wo_full, preferred_element_type=jnp.float32),
            "tensor",
            scatter_dimension=0,
            tiled=True,
        )
        normed_two, scale_two = norm_rows(mixed, g_ffn.astype(jnp.float32))
        normed_two_all = lax.all_gather(
            normed_two.astype(jnp.bfloat16), "tensor", axis=0, tiled=True
        )
        gate = jnp.dot(normed_two_all, wg_full, preferred_element_type=jnp.float32)
        upward = jnp.dot(normed_two_all, wu_full, preferred_element_type=jnp.float32)
        sigma = jax.nn.sigmoid(gate)
        silu_gate = gate * sigma
        hidden = (silu_gate * upward).astype(jnp.bfloat16)
        out_rows.append(
            (
                mixed
                + lax.psum_scatter(
                    jnp.dot(hidden, wd_full, preferred_element_type=jnp.float32).astype(
                        jnp.bfloat16
                    ),
                    "tensor",
                    scatter_dimension=0,
                    tiled=True,
                ).astype(jnp.float32)
            ).astype(jnp.bfloat16)
        )
        bwd = (
            lax.all_gather(gain_attn, "dp", axis=0, tiled=True),
            lax.all_gather(w_query, "dp", axis=0, tiled=True),
            lax.all_gather(w_key, "dp", axis=0, tiled=True),
            lax.all_gather(w_value, "dp", axis=0, tiled=True),
            lax.all_gather(w_out, "dp", axis=1, tiled=True),
            lax.all_gather(gain_ffn, "dp", axis=0, tiled=True),
            lax.all_gather(w_gate, "dp", axis=0, tiled=True),
            lax.all_gather(w_up, "dp", axis=0, tiled=True),
            lax.all_gather(w_down, "dp", axis=1, tiled=True),
        )
        g_attn, wq_full, wk_full, wv_full, wo_full, g_ffn, wg_full, wu_full, wd_full = bwd
        grad_here = grad_out[step]
        grad_all = lax.all_gather(grad_here, "tensor", axis=0, tiled=True)
        d_down = inner_rows(hidden, grad_all)
        grad_hidden = outer_cols(grad_all, wd_full)
        grad_gate = (grad_hidden * upward * sigma * (1.0 + gate * (1.0 - sigma))).astype(
            jnp.bfloat16
        )
        grad_up = (grad_hidden * silu_gate).astype(jnp.bfloat16)
        d_gate = inner_rows(normed_two_all, grad_gate)
        d_up = inner_rows(normed_two_all, grad_up)
        grad_normed_two = lax.psum_scatter(
            outer_cols(grad_gate, wg_full) + outer_cols(grad_up, wu_full),
            "tensor",
            scatter_dimension=0,
            tiled=True,
        )
        grad_mixed_norm, gain_part_ffn = norm_back(
            grad_normed_two, mixed, scale_two, g_ffn.astype(jnp.float32)
        )
        grad_mixed = grad_here.astype(jnp.float32) + grad_mixed_norm
        branch_all = lax.all_gather(grad_mixed.astype(jnp.bfloat16), "tensor", axis=0, tiled=True)
        d_out = inner_rows(context, branch_all)
        grad_context = (
            outer_cols(branch_all, wo_full).astype(jnp.bfloat16).reshape(L, heads_local, HD)
        )
        grad_query, grad_keys, grad_values = attention_backward(
            query, keys, values, mem_keys, mem_values, limit, lse_parts, grad_context
        )
        grad_query = grad_query.reshape(L, cols).astype(jnp.bfloat16)
        grad_keys = grad_keys.reshape(L, cols).astype(jnp.bfloat16)
        grad_values = grad_values.reshape(L, cols).astype(jnp.bfloat16)
        d_query = inner_rows(normed_all, grad_query)
        d_key = inner_rows(normed_all, grad_keys)
        d_value = inner_rows(normed_all, grad_values)
        grad_normed = lax.psum_scatter(
            (
                outer_cols(grad_query, wq_full)
                + outer_cols(grad_keys, wk_full)
                + outer_cols(grad_values, wv_full)
            ).astype(jnp.bfloat16),
            "tensor",
            scatter_dimension=0,
            tiled=True,
        ).astype(jnp.float32)
        grad_token_norm, gain_part_attn = norm_back(
            grad_normed, token_rows, scale_one, g_attn.astype(jnp.float32)
        )
        grad_rows.append(grad_mixed + grad_token_norm)
        gain_total_attn = gain_total_attn + gain_part_attn
        gain_total_ffn = gain_total_ffn + gain_part_ffn
        totals = tuple(
            (
                held + fresh
                for held, fresh in zip(
                    totals, (d_query, d_key, d_value, d_out, d_gate, d_up, d_down)
                )
            )
        )
    shares = (
        lax.psum_scatter(
            totals[0].astype(jnp.bfloat16), "dp", scatter_dimension=0, tiled=True
        ).astype(jnp.float32),
        lax.psum_scatter(
            totals[1].astype(jnp.bfloat16), "dp", scatter_dimension=0, tiled=True
        ).astype(jnp.float32),
        lax.psum_scatter(
            totals[2].astype(jnp.bfloat16), "dp", scatter_dimension=0, tiled=True
        ).astype(jnp.float32),
        lax.psum_scatter(
            totals[3].astype(jnp.bfloat16), "dp", scatter_dimension=1, tiled=True
        ).astype(jnp.float32),
        lax.psum_scatter(
            totals[4].astype(jnp.bfloat16), "dp", scatter_dimension=0, tiled=True
        ).astype(jnp.float32),
        lax.psum_scatter(
            totals[5].astype(jnp.bfloat16), "dp", scatter_dimension=0, tiled=True
        ).astype(jnp.float32),
        lax.psum_scatter(
            totals[6].astype(jnp.bfloat16), "dp", scatter_dimension=1, tiled=True
        ).astype(jnp.float32),
    )
    gain_attn_sum, gain_ffn_sum = lax.psum((gain_total_attn, gain_total_ffn), ("dp", "tensor"))
    return (
        jnp.stack(out_rows, axis=0),
        jnp.stack(grad_rows, axis=0),
        gain_attn_sum,
        shares[0],
        shares[1],
        shares[2],
        shares[3],
        gain_ffn_sum,
        shares[4],
        shares[5],
        shares[6],
    )


TQ = 512
TK = 512
ROWS = 512
HT = 256
SCALE = HD**-0.5
EXP_SCALE = SCALE * 1.4426950408889634
LOG2E = 1.4426950408889634
NT = (((1,), (1,)), ((), ()))
TN = (((0,), (0,)), ((), ()))
F32 = jnp.float32
BF16 = jnp.bfloat16
MIB = 1 << 20


def mm(left, right, dims=(((1,), (0,)), ((), ()))):
    return lax.dot_general(left, right, dims, preferred_element_type=F32)


def fold_max(values):
    best = values[:, :HD]
    for i in range(1, values.shape[1] // HD):
        best = jnp.maximum(best, values[:, i * HD : (i + 1) * HD])
    return best


def fold_sum(values):
    total = values[:, :HD]
    for i in range(1, values.shape[1] // HD):
        total = total + values[:, i * HD : (i + 1) * HD]
    return total


def reach_mask(first, tile, limit):
    rows = first + lax.broadcasted_iota(jnp.int32, (TQ, 1), 0)
    keys = tile * TK + lax.broadcasted_iota(jnp.int32, (1, TK), 1)
    reach = jnp.where(rows < limit, jnp.maximum(rows, limit - 1), rows)
    return keys <= reach


def pick_blocks(meta, block, own, other, buf):
    for i in range(KR):
        c = meta[2 + block * KR + i]
        buf[pl.ds(i * CBLOCK, CBLOCK), :] = own[0, pl.ds(pl.multiple_of(c * CBLOCK, CBLOCK), CBLOCK), :]
        d = meta[2 + (L // QBLOCK) * KR + block * KR + i]
        buf[pl.ds((KR + i) * CBLOCK, CBLOCK), :] = other[d, 0, 0]


def attend_kernel(
    meta, q_ref, k_ref, v_ref, ok_ref, ov_ref, pk_ref, pv_ref, ctx_ref, lse_ref, kbuf, vbuf, sbuf, smem, *, pair
):
    step = pl.program_id(1)
    limit = meta[0]
    first = step * TQ
    free = jnp.where(first < limit, (limit + TK - 1) // TK, 0)
    tiles = jnp.maximum(step + 1, free)
    blocks = TQ // QBLOCK
    for b in range(blocks):
        pick_blocks(meta, step * blocks + b, ok_ref, pk_ref, kbuf.at[b])
        pick_blocks(meta, step * blocks + b, ov_ref, pv_ref, vbuf.at[b])
    state = []
    for h in range(pair):
        cs = pl.ds(h * HD, HD)
        best = []
        for b in range(blocks):
            s = mm(q_ref[pl.ds(b * QBLOCK, QBLOCK), cs], kbuf[b, :, cs], NT)
            smem[h, pl.ds(b * QBLOCK, QBLOCK), :] = s
            best.append(fold_max(s))
        state.append(jnp.concatenate(best, 0))

    def scores(tile, state, masked):
        ks = pl.ds(pl.multiple_of(tile * TK, TK), TK)
        if masked:
            allowed = reach_mask(first, tile, limit)
        new = []
        for h in range(pair):
            cs = pl.ds(h * HD, HD)
            s = mm(q_ref[:, cs], k_ref[ks, cs], NT)
            if masked:
                s = jnp.where(allowed, s, NEGATIVE)
            sbuf[h, tile] = s
            new.append(jnp.maximum(state[h], fold_max(s)))
        return tuple(new)

    state = lax.fori_loop(0, step, lambda tile, s: scores(tile, s, False), tuple(state))
    state = lax.fori_loop(step, tiles, lambda tile, s: scores(tile, s, True), state)
    tops = [jnp.max(s, axis=1, keepdims=True) for s in state]
    state = []
    for h in range(pair):
        cs = pl.ds(h * HD, HD)
        p = jnp.exp2((smem[h] - tops[h]) * EXP_SCALE)
        low = p.astype(BF16)
        parts = [mm(low[b * QBLOCK : (b + 1) * QBLOCK], vbuf[b, :, cs]) for b in range(blocks)]
        state.append((fold_sum(p), jnp.concatenate(parts, 0)))

    def weigh(tile, state):
        ks = pl.ds(pl.multiple_of(tile * TK, TK), TK)
        new = []
        for h in range(pair):
            total, acc = state[h]
            p = jnp.exp2((sbuf[h, tile] - tops[h]) * EXP_SCALE)
            new.append((total + fold_sum(p), acc + mm(p.astype(BF16), v_ref[ks, pl.ds(h * HD, HD)])))
        return tuple(new)

    state = lax.fori_loop(0, tiles, weigh, tuple(state))
    for h in range(pair):
        cs = pl.ds(h * HD, HD)
        total = jnp.sum(state[h][0], axis=1, keepdims=True)
        ctx_ref[:, cs] = (state[h][1] / total).astype(BF16)
        lse_ref[:, cs] = jnp.broadcast_to(tops[h] * SCALE + jnp.log(total), (TQ, HD))


def attend_back_kernel(
    meta, q_ref, k_ref, v_ref, ok_ref, ov_ref, pk_ref, pv_ref, do_ref, ctx_ref, lse_ref,
    dq_ref, dk_ref, dv_ref, kbuf, vbuf, dks, dvs, *, pair
):
    step = pl.program_id(1)
    limit = meta[0]
    first = step * TQ
    free = jnp.where(first < limit, (limit + TK - 1) // TK, 0)
    tiles = jnp.maximum(step + 1, free)
    blocks = TQ // QBLOCK

    @pl.when(step == 0)
    def _():
        dks[...] = jnp.zeros_like(dks)
        dvs[...] = jnp.zeros_like(dvs)

    for b in range(blocks):
        pick_blocks(meta, step * blocks + b, ok_ref, pk_ref, kbuf.at[b])
        pick_blocks(meta, step * blocks + b, ov_ref, pv_ref, vbuf.at[b])
    state = []
    aux = []
    for h in range(pair):
        cs = pl.ds(h * HD, HD)
        delta = jnp.sum(do_ref[:, cs].astype(F32) * ctx_ref[:, cs].astype(F32), axis=1, keepdims=True)
        lse2 = lse_ref[:, cs][:, :1] * LOG2E
        aux.append((lse2, delta))
        parts = []
        for b in range(blocks):
            rs = pl.ds(b * QBLOCK, QBLOCK)
            s = mm(q_ref[rs, cs], kbuf[b, :, cs], NT)
            p = jnp.exp2(s * EXP_SCALE - lse2[b * QBLOCK : (b + 1) * QBLOCK])
            dp = mm(do_ref[rs, cs], vbuf[b, :, cs], NT)
            ds = (p * (dp - delta[b * QBLOCK : (b + 1) * QBLOCK])).astype(BF16)
            parts.append(mm(ds, kbuf[b, :, cs]))
        state.append(jnp.concatenate(parts, 0))

    def grads(tile, state, masked):
        ks = pl.ds(pl.multiple_of(tile * TK, TK), TK)
        if masked:
            allowed = reach_mask(first, tile, limit)
        new = []
        for h in range(pair):
            cs = pl.ds(h * HD, HD)
            lse2, delta = aux[h]
            s = mm(q_ref[:, cs], k_ref[ks, cs], NT)
            p = jnp.exp2(s * EXP_SCALE - lse2)
            if masked:
                p = jnp.where(allowed, p, 0.0)
            dp = mm(do_ref[:, cs], v_ref[ks, cs], NT)
            ds = (p * (dp - delta)).astype(BF16)
            dvs[ks, cs] += mm(p.astype(BF16), do_ref[:, cs], TN)
            dks[ks, cs] += mm(ds, q_ref[:, cs], TN)
            new.append(state[h] + mm(ds, k_ref[ks, cs]))
        return tuple(new)

    state = lax.fori_loop(0, step, lambda tile, s: grads(tile, s, False), tuple(state))
    state = lax.fori_loop(step, tiles, lambda tile, s: grads(tile, s, True), state)
    for h in range(pair):
        dq_ref[:, pl.ds(h * HD, HD)] = (state[h] * SCALE).astype(BF16)

    @pl.when(step == L // TQ - 1)
    def _():
        dk_ref[...] = (dks[...] * SCALE).astype(BF16)
        dv_ref[...] = dvs[...].astype(BF16)


def attention_specs(heads, pair):
    wide = pair * HD
    per = heads // 2 // pair
    groups = heads // pair
    return [
        pl.BlockSpec((TQ, wide), lambda h, i, meta: (i, h)),
        pl.BlockSpec((L, wide), lambda h, i, meta: (0, groups + h)),
        pl.BlockSpec((L, wide), lambda h, i, meta: (0, 2 * groups + h)),
        pl.BlockSpec((1, CACHE_LEN, wide), lambda h, i, meta: ((h // per) ^ meta[1], 0, h % per)),
        pl.BlockSpec((1, CACHE_LEN, wide), lambda h, i, meta: ((h // per) ^ meta[1], 0, h % per)),
        pl.BlockSpec(
            (CACHE_LEN // CBLOCK, 1, 1, CBLOCK, wide),
            lambda h, i, meta: (0, (h // per) ^ meta[1], 0, 0, h % per),
        ),
        pl.BlockSpec(
            (CACHE_LEN // CBLOCK, 1, 1, CBLOCK, wide),
            lambda h, i, meta: (0, (h // per) ^ meta[1], 1, 0, h % per),
        ),
    ]


def attend(meta, qkv, own_k, own_v, fetched, pair=2):
    width = qkv.shape[1] // 3
    heads = width // HD
    wide = pair * HD
    row = pl.BlockSpec((TQ, wide), lambda h, i, meta: (i, h))
    area = L * 1900 * width
    return pl.pallas_call(
        functools.partial(attend_kernel, pair=pair),
        grid_spec=pltpu.PrefetchScalarGridSpec(
            num_scalar_prefetch=1,
            grid=(heads // pair, L // TQ),
            in_specs=attention_specs(heads, pair),
            out_specs=[row, row],
            scratch_shapes=[pltpu.VMEM((TQ // QBLOCK, 2 * KR * CBLOCK, wide), BF16)] * 2
            + [pltpu.VMEM((pair, L // TK, TQ, TK), F32), pltpu.VMEM((pair, TQ, 2 * KR * CBLOCK), F32)],
        ),
        out_shape=[jax.ShapeDtypeStruct((L, width), BF16), jax.ShapeDtypeStruct((L, width), F32)],
        compiler_params=pltpu.CompilerParams(vmem_limit_bytes=40 * MIB),
        cost_estimate=pl.CostEstimate(flops=8 * area, bytes_accessed=30 * MIB, transcendentals=area // HD),
        name="attend",
    )(meta, qkv, qkv, qkv, own_k, own_v, fetched, fetched)


def attend_back(meta, qkv, own_k, own_v, fetched, grad_context, context, lse, pair=2):
    width = context.shape[1]
    heads = width // HD
    wide = pair * HD
    row = pl.BlockSpec((TQ, wide), lambda h, i, meta: (i, h))
    col = pl.BlockSpec((L, wide), lambda h, i, meta: (0, h))
    area = L * 1900 * width
    return pl.pallas_call(
        functools.partial(attend_back_kernel, pair=pair),
        grid_spec=pltpu.PrefetchScalarGridSpec(
            num_scalar_prefetch=1,
            grid=(heads // pair, L // TQ),
            in_specs=attention_specs(heads, pair) + [row, row, row],
            out_specs=[row, col, col],
            scratch_shapes=[pltpu.VMEM((TQ // QBLOCK, 2 * KR * CBLOCK, wide), BF16)] * 2
            + [pltpu.VMEM((L, wide), F32)] * 2,
        ),
        out_shape=[jax.ShapeDtypeStruct((L, width), BF16)] * 3,
        compiler_params=pltpu.CompilerParams(vmem_limit_bytes=48 * MIB),
        cost_estimate=pl.CostEstimate(flops=12 * area, bytes_accessed=40 * MIB, transcendentals=area // HD),
        name="attend_back",
    )(meta, qkv, qkv, qkv, own_k, own_v, fetched, fetched, grad_context, context, lse)


def project_kernel(x_ref, gain_ref, w_ref, normed_ref, qkv_ref):
    rows = x_ref[...].astype(F32)
    scale = lax.rsqrt(jnp.mean(rows * rows, axis=1, keepdims=True) + EPS)
    normed_ref[...] = (rows * scale * gain_ref[...]).astype(BF16)
    left = normed_ref[...]

    def chunk(c, carry):
        cs = pl.ds(pl.multiple_of(c * 512, 512), 512)
        qkv_ref[:, cs] = mm(left, w_ref[:, cs]).astype(BF16)
        return carry

    lax.fori_loop(0, qkv_ref.shape[1] // 512, chunk, 0)


def project(x, gain, weights):
    width = x.shape[1]
    cols = 3 * width
    row = lambda n: pl.BlockSpec((ROWS, n), lambda i: (i, 0))
    whole = lambda n: pl.BlockSpec((width, n), lambda i: (0, 0))
    return pl.pallas_call(
        project_kernel,
        grid=(L // ROWS,),
        in_specs=[row(width), pl.BlockSpec((1, width), lambda i: (0, 0)), whole(cols)],
        out_specs=[row(width), row(cols)],
        out_shape=[jax.ShapeDtypeStruct((L, width), BF16), jax.ShapeDtypeStruct((L, cols), BF16)],
        compiler_params=pltpu.CompilerParams(vmem_limit_bytes=40 * MIB),
        cost_estimate=pl.CostEstimate(flops=2 * L * width * cols, bytes_accessed=26 * MIB, transcendentals=0),
        name="project",
    )(x, gain, weights)


def mix_kernel(x_ref, ctx_ref, gain_ref, w_ref, mixed_ref, normed_ref):
    mixed = x_ref[...].astype(F32) + mm(ctx_ref[...], w_ref[...], NT)
    mixed_ref[...] = mixed
    scale = lax.rsqrt(jnp.mean(mixed * mixed, axis=1, keepdims=True) + EPS)
    normed_ref[...] = (mixed * scale * gain_ref[...]).astype(BF16)


def mix(x, context, gain, weights):
    width = x.shape[1]
    row = pl.BlockSpec((ROWS, width), lambda i: (i, 0))
    return pl.pallas_call(
        mix_kernel,
        grid=(L // ROWS,),
        in_specs=[row, row, pl.BlockSpec((1, width), lambda i: (0, 0)), pl.BlockSpec((width, width), lambda i: (0, 0))],
        out_specs=[row, row],
        out_shape=[jax.ShapeDtypeStruct((L, width), F32), jax.ShapeDtypeStruct((L, width), BF16)],
        compiler_params=pltpu.CompilerParams(vmem_limit_bytes=32 * MIB),
        cost_estimate=pl.CostEstimate(flops=2 * L * width * width, bytes_accessed=22 * MIB, transcendentals=0),
        name="mix",
    )(x, context, gain, weights)


def ffn_kernel(n_ref, g_ref, wg_ref, wu_ref, wd_ref, out_ref, gn_ref, dg_ref, du_ref, dd_ref, acc, ag, au, ad):
    tile = pl.program_id(0)
    last = pl.num_programs(0) - 1

    @pl.when(tile == 0)
    def _():
        acc[...] = jnp.zeros_like(acc)
        gn_ref[...] = jnp.zeros_like(gn_ref)

    ag[...] = jnp.zeros_like(ag)
    au[...] = jnp.zeros_like(au)
    ad[...] = jnp.zeros_like(ad)

    def chunk(r, carry):
        rs = pl.ds(pl.multiple_of(r * ROWS, ROWS), ROWS)
        rows = n_ref[rs, :]
        cotangent = g_ref[rs, :]
        gate = mm(rows, wg_ref[...])
        up = mm(rows, wu_ref[...])
        grad_hidden = mm(cotangent, wd_ref[...])
        sigma = 1.0 / (1.0 + jnp.exp(-gate))
        silu = gate * sigma
        hidden = (silu * up).astype(BF16)
        grad_gate = (grad_hidden * up * (sigma * (1.0 + gate * (1.0 - sigma)))).astype(BF16)
        grad_up = (grad_hidden * silu).astype(BF16)
        acc[rs, :] += mm(hidden, wd_ref[...], NT)
        gn_ref[rs, :] += mm(grad_gate, wg_ref[...], NT) + mm(grad_up, wu_ref[...], NT)
        ag[...] += mm(rows, grad_gate, TN)
        au[...] += mm(rows, grad_up, TN)
        ad[...] += mm(cotangent, hidden, TN)
        return carry

    lax.fori_loop(0, L // ROWS, chunk, 0)
    dg_ref[...] = ag[...].astype(BF16)
    du_ref[...] = au[...].astype(BF16)
    dd_ref[...] = ad[...].astype(BF16)

    @pl.when(tile == last)
    def _():
        out_ref[...] = acc[...].astype(BF16)


def ffn(normed, cotangent, weights, width, hidden):
    once = pl.Buffered(1)
    tiles = hidden // HT
    lead = width // HT
    part = lambda k: pl.BlockSpec((width, HT), lambda j: (0, lead + k * tiles + j))
    whole = pl.BlockSpec((L, width), lambda j: (0, 0), pipeline_mode=once)
    grad = pl.BlockSpec((width, HT), lambda j: (0, j))
    return pl.pallas_call(
        ffn_kernel,
        grid=(tiles,),
        in_specs=[whole, whole, part(0), part(1), part(2)],
        out_specs=[whole, whole, grad, grad, grad],
        out_shape=[jax.ShapeDtypeStruct((L, width), BF16), jax.ShapeDtypeStruct((L, width), F32)]
        + [jax.ShapeDtypeStruct((width, hidden), BF16)] * 3,
        scratch_shapes=[pltpu.VMEM((L, width), F32)] + [pltpu.VMEM((width, HT), F32)] * 3,
        compiler_params=pltpu.CompilerParams(vmem_limit_bytes=56 * MIB),
        cost_estimate=pl.CostEstimate(
            flops=18 * L * width * hidden, bytes_accessed=60 * MIB, transcendentals=L * hidden
        ),
        name="ffn",
    )(normed, cotangent, weights, weights, weights)


def unmix_kernel(mixed_ref, gn_ref, ffn_ref, g_ref, gain_ref, w_ref, out_ref, gm_ref, br_ref, gc_ref, gg_ref):
    mixed = mixed_ref[...]
    grad = gn_ref[...]
    scale = lax.rsqrt(jnp.mean(mixed * mixed, axis=1, keepdims=True) + EPS)
    unit = mixed * scale
    inner = grad * gain_ref[...]
    grad_mixed = g_ref[...].astype(F32) + scale * (inner - unit * jnp.mean(inner * unit, axis=1, keepdims=True))
    out_ref[...] = (mixed + ffn_ref[...].astype(F32)).astype(BF16)
    gm_ref[...] = grad_mixed
    branch = grad_mixed.astype(BF16)
    br_ref[...] = branch
    gc_ref[...] = mm(branch, w_ref[...]).astype(BF16)

    @pl.when(pl.program_id(0) == 0)
    def _():
        gg_ref[...] = jnp.zeros_like(gg_ref)

    gg_ref[...] += jnp.sum(grad * unit, axis=0, keepdims=True)


def unmix(mixed, grad_normed, ffn_out, cotangent, gain, weights):
    width = mixed.shape[1]
    rows = ROWS // 2
    row = pl.BlockSpec((rows, width), lambda i: (i, 0))
    one = pl.BlockSpec((1, width), lambda i: (0, 0))
    return pl.pallas_call(
        unmix_kernel,
        grid=(L // rows,),
        in_specs=[row, row, row, row, one, pl.BlockSpec((width, width), lambda i: (0, 0))],
        out_specs=[row, row, row, row, one],
        out_shape=[
            jax.ShapeDtypeStruct((L, width), BF16),
            jax.ShapeDtypeStruct((L, width), F32),
            jax.ShapeDtypeStruct((L, width), BF16),
            jax.ShapeDtypeStruct((L, width), BF16),
            jax.ShapeDtypeStruct((1, width), F32),
        ],
        compiler_params=pltpu.CompilerParams(vmem_limit_bytes=40 * MIB),
        cost_estimate=pl.CostEstimate(flops=2 * L * width * width, bytes_accessed=46 * MIB, transcendentals=0),
        name="unmix",
    )(mixed, grad_normed, ffn_out, cotangent, gain, weights)


def finish_kernel(x_ref, gm_ref, dq_ref, dk_ref, dv_ref, gain_ref, w_ref, gt_ref, gg_ref):
    width = x_ref.shape[1]
    grad = mm(dq_ref[...], w_ref[:, :width], NT)
    grad += mm(dk_ref[...], w_ref[:, width : 2 * width], NT)
    grad += mm(dv_ref[...], w_ref[:, 2 * width : 3 * width], NT)
    rows = x_ref[...].astype(F32)
    scale = lax.rsqrt(jnp.mean(rows * rows, axis=1, keepdims=True) + EPS)
    unit = rows * scale
    inner = grad * gain_ref[...]
    back = scale * (inner - unit * jnp.mean(inner * unit, axis=1, keepdims=True))
    gt_ref[...] = (gm_ref[...] + back).astype(BF16)

    @pl.when(pl.program_id(0) == 0)
    def _():
        gg_ref[...] = jnp.zeros_like(gg_ref)

    gg_ref[...] += jnp.sum(grad * unit, axis=0, keepdims=True)


def finish(x, grad_mixed, dq, dk, dv, gain, weights):
    width = x.shape[1]
    row = pl.BlockSpec((ROWS, width), lambda i: (i, 0))
    one = pl.BlockSpec((1, width), lambda i: (0, 0))
    return pl.pallas_call(
        finish_kernel,
        grid=(L // ROWS,),
        in_specs=[row, row, row, row, row, one, pl.BlockSpec((width, 3 * width), lambda i: (0, 0))],
        out_specs=[row, one],
        out_shape=[jax.ShapeDtypeStruct((L, width), BF16), jax.ShapeDtypeStruct((1, width), F32)],
        compiler_params=pltpu.CompilerParams(vmem_limit_bytes=48 * MIB),
        cost_estimate=pl.CostEstimate(flops=6 * L * width * width, bytes_accessed=40 * MIB, transcendentals=0),
        name="finish",
    )(x, grad_mixed, dq, dk, dv, gain, weights)


def pick_kernel(table, held_ref, sent_ref, sems):
    def copy(i):
        return pltpu.make_async_copy(held_ref.at[table[i]], sent_ref.at[i], sems.at[i])

    for i in range(sent_ref.shape[0]):
        copy(i).start()
    for i in range(sent_ref.shape[0]):
        copy(i).wait()


def pick_rows(table, held):
    count = held.shape[0]
    return pl.pallas_call(
        pick_kernel,
        grid_spec=pltpu.PrefetchScalarGridSpec(
            num_scalar_prefetch=1,
            grid=(),
            in_specs=[pl.BlockSpec(memory_space=pl.ANY)],
            out_specs=pl.BlockSpec(memory_space=pltpu.VMEM),
            scratch_shapes=[pltpu.SemaphoreType.DMA((count,))],
        ),
        out_shape=jax.ShapeDtypeStruct(held.shape, held.dtype),
        compiler_params=pltpu.CompilerParams(vmem_limit_bytes=16 * MIB),
        cost_estimate=pl.CostEstimate(flops=0, bytes_accessed=2 * held.size * 2, transcendentals=0),
        name="pick_rows",
    )(table, held)


RING = 8
RIGHT = RING // 2
LEFT = RING - 1 - RIGHT


def spread_kernel(
    tok_ref, ck_ref, cv_ref, small_ref, extra_ref, big_ref,
    x_ref, ok_ref, ov_ref, held_ref, first_ref, second_ref,
    tok_buf, k_buf, v_buf, local_sem, x_send, x_recv, all_send, all_recv, ring_send, ring_recv, pair_send, pair_recv,
):
    me = lax.axis_index("dp")
    spot = lax.axis_index("tensor")
    peer = 1 - spot
    devices = held_ref.shape[0]
    rows, cols = small_ref.shape[0], small_ref.shape[1] // 3
    core = me % 2
    z, y = me // 4, (me // 2) % 2
    place = z + y * (7 - 2 * z)

    def at_place(p):
        yy = p // 4
        return (p + yy * (7 - 2 * p)) * 4 + yy * 2

    def target(dp, tensor):
        return (dp, tensor)

    barrier = pltpu.get_barrier_semaphore()
    for d in range(1, devices):
        pl.semaphore_signal(barrier, inc=1, device_id=target((me + d) % devices, spot), device_id_type=pl.DeviceIdType.MESH)
    pl.semaphore_signal(barrier, inc=1, device_id=target(me, peer), device_id_type=pl.DeviceIdType.MESH)
    pl.semaphore_wait(barrier, devices)

    def remote(src, dst, send, recv, device):
        return pltpu.make_async_remote_copy(
            src_ref=src, dst_ref=dst, send_sem=send, recv_sem=recv,
            device_id=device, device_id_type=pl.DeviceIdType.MESH,
        )

    mine = pl.multiple_of(me * rows, rows)
    across = target(me, peer)
    weight_copies = []
    for i in range(3):
        weight_copies.append(
            remote(
                small_ref.at[:, pl.ds(i * cols, cols)],
                first_ref.at[pl.ds(mine, rows), pl.ds((2 * i + 1) * cols, cols)],
                x_send.at[i], x_recv.at[i], across,
            )
        )
    for copy in weight_copies:
        copy.start()
    for i in range(3):
        first_ref[pl.ds(mine, rows), pl.ds(2 * i * cols, cols)] = small_ref[:, pl.ds(i * cols, cols)]
    first_ref[pl.ds(mine, rows), pl.ds(6 * cols, HD)] = extra_ref[...]

    loads = [
        pltpu.make_async_copy(tok_ref.at[spot], tok_buf, local_sem.at[0]),
        pltpu.make_async_copy(ck_ref.at[spot], k_buf, local_sem.at[1]),
        pltpu.make_async_copy(cv_ref.at[spot], v_buf, local_sem.at[2]),
    ]
    stores = [
        pltpu.make_async_copy(tok_buf, x_ref.at[spot], local_sem.at[3]),
        pltpu.make_async_copy(k_buf, ok_ref.at[spot], local_sem.at[4]),
        pltpu.make_async_copy(v_buf, ov_ref.at[spot], local_sem.at[5]),
    ]
    for copy in loads:
        copy.start()

    x_copies = [remote(tok_ref.at[peer], x_ref.at[spot], x_send.at[3], x_recv.at[3], across)]
    wide = big_ref.shape[1]
    hidden = (wide - cols) // 3
    starts = [(0, cols)] + [(cols + i * hidden, hidden) for i in range(3)]
    own_cols = []
    for i, (start, size) in enumerate(starts):
        base = 2 * start
        own_cols.append(pltpu.make_async_copy(
            big_ref.at[:, pl.ds(start, size)], second_ref.at[:, pl.ds(base, size)], local_sem.at[6 + i]))
        x_copies.append(remote(
            big_ref.at[:, pl.ds(start, size)], second_ref.at[:, pl.ds(base + size, size)],
            x_send.at[4 + i], x_recv.at[4 + i], across))
    x_copies.append(remote(ck_ref.at[peer], ok_ref.at[spot], x_send.at[8], x_recv.at[8], across))
    x_copies.append(remote(cv_ref.at[peer], ov_ref.at[spot], x_send.at[9], x_recv.at[9], across))
    for copy in x_copies + own_cols:
        copy.start()

    def to_device(d, dst_dp):
        chunk = pl.ds(pl.multiple_of(dst_dp * CBLOCK, CBLOCK), CBLOCK)
        dst = target(dst_dp, spot)
        return [
            remote(ck_ref.at[:, chunk, :], held_ref.at[me, :, 0], all_send.at[0, d], all_recv.at[0, d], dst),
            remote(cv_ref.at[:, chunk, :], held_ref.at[me, :, 1], all_send.at[1, d], all_recv.at[1, d], dst),
        ]

    for copy in weight_copies:
        copy.wait_recv()

    def block(p, c):
        return first_ref.at[pl.ds(pl.multiple_of((at_place(p) + c) * rows, rows), rows), :]

    ahead = (place + 1) % RING
    behind = (place + RING - 1) % RING

    def hop(s, direction):
        p = (place + RING - (s - 1)) % RING if direction == 0 else (place + s - 1) % RING
        to = ahead if direction == 0 else behind
        k = (s - 1) * 2 + direction
        return remote(block(p, core), block(p, core), ring_send.at[k], ring_recv.at[k], target(at_place(to) + core, spot))

    def to_pair(i, p):
        return remote(block(p, core), block(p, core), pair_send.at[i], pair_recv.at[i], target(at_place(place) + 1 - core, spot))

    hops = [hop(1, 0), hop(1, 1)]
    for copy in hops:
        copy.start()
    pairs = [to_pair(0, place)]
    pairs[0].start()
    copies = []
    for d in range(1, devices):
        for copy in to_device(d, (me + d) % devices):
            copy.start()
            copies.append(copy)
    chunk = pl.ds(pl.multiple_of(me * CBLOCK, CBLOCK), CBLOCK)
    kept = [
        pltpu.make_async_copy(ck_ref.at[:, chunk, :], held_ref.at[me, :, 0], local_sem.at[10]),
        pltpu.make_async_copy(cv_ref.at[:, chunk, :], held_ref.at[me, :, 1], local_sem.at[11]),
    ]
    for copy in kept:
        copy.start()
    for load, store in zip(loads, stores):
        load.wait()
        store.start()
    for s in range(1, RIGHT + 1):
        for direction in range(2):
            if direction == 1 and s > LEFT:
                continue
            hops[(s - 1) * 2 + direction].wait_recv()
            p = (place + RING - s) % RING if direction == 0 else (place + s) % RING
            if s < (RIGHT if direction == 0 else LEFT):
                nxt = hop(s + 1, direction)
                nxt.start()
                hops.append(nxt)
            pair = to_pair(len(pairs), p)
            pair.start()
            pairs.append(pair)
    for copy in weight_copies + hops:
        copy.wait_send()
    for copy in pairs + x_copies + copies:
        copy.wait()
    for copy in stores + own_cols + kept:
        copy.wait()


def spread(tokens, cache_keys, cache_values, small, extra, big, devices):
    micro, shard_len, width = tokens.shape
    rows, cols = small.shape[0], small.shape[1] // 3
    anywhere = pl.BlockSpec(memory_space=pl.ANY)
    vmem = pl.BlockSpec(memory_space=pltpu.VMEM)
    dma = pltpu.SemaphoreType.DMA
    return pl.pallas_call(
        spread_kernel,
        in_specs=[anywhere, anywhere, anywhere, vmem, vmem, vmem],
        out_specs=[anywhere, anywhere, anywhere, anywhere, vmem, anywhere],
        out_shape=[
            jax.ShapeDtypeStruct((2, shard_len, width), BF16),
            jax.ShapeDtypeStruct((2, CACHE_LEN, cols), BF16),
            jax.ShapeDtypeStruct((2, CACHE_LEN, cols), BF16),
            jax.ShapeDtypeStruct((devices, micro, 2, CBLOCK, cols), BF16),
            jax.ShapeDtypeStruct((rows * devices, 6 * cols + HD), BF16),
            jax.ShapeDtypeStruct((rows, 2 * big.shape[1]), BF16),
        ],
        scratch_shapes=[
            pltpu.VMEM((shard_len, width), BF16),
            pltpu.VMEM((CACHE_LEN, cols), BF16),
            pltpu.VMEM((CACHE_LEN, cols), BF16),
            dma((12,)), dma((10,)), dma((10,)), dma((2, devices)), dma((2, devices)),
            dma((RING - 1,)), dma((RING - 1,)), dma((RING,)), dma((RING,)),
        ],
        compiler_params=pltpu.CompilerParams(collective_id=0, has_side_effects=True, vmem_limit_bytes=32 * MIB),
        cost_estimate=pl.CostEstimate(flops=0, bytes_accessed=300 * MIB, transcendentals=0),
        name="spread",
    )(tokens, cache_keys, cache_values, small, extra, big)


def swap(values):
    return lax.ppermute(values, "tensor", [(0, 1), (1, 0)])


def sequence_body(
    tokens, gain_attn, w_query, w_key, w_value, w_out, gain_ffn, w_gate, w_up, w_down,
    cache_keys, cache_values, prefix, partner, own_blocks, partner_blocks, grad_out,
):
    micro, shard_len, width = tokens.shape
    devices = lax.axis_size("dp")
    seqs = micro * devices
    rows_held, cols = w_query.shape
    hidden_held = w_gate.shape[1]
    hidden = 2 * hidden_held
    spot = lax.axis_index("tensor")
    exchange = functools.partial(lax.all_to_all, axis_name="tensor", split_axis=0, concat_axis=0, tiled=True)
    chunks = CACHE_LEN // CBLOCK

    small = jnp.concatenate([w_query, w_key, w_value], axis=1)
    partner_column = jnp.zeros((rows_held, 1), BF16).at[:micro, 0].set(partner.astype(BF16))
    extra = jnp.concatenate(
        [gain_attn[:, None], gain_ffn[:, None], partner_column, jnp.zeros((rows_held, HD - 3), BF16)], axis=1
    )
    big = jnp.concatenate([w_out.T, w_gate, w_up, w_down.T], axis=1)
    x, own_k, own_v, held, first_all, second_rows = spread(
        tokens, cache_keys, cache_values, small, extra, big, devices
    )
    x = x.reshape(L, width)
    cotangent = exchange(grad_out).reshape(L, width)
    second_all = lax.all_gather(second_rows, "dp", axis=0, tiled=True)

    tail = first_all[:, 3 * width :]
    gains = tail[:, :2].astype(F32).T
    gain_one, gain_two = gains[:1], gains[1:]
    table = tail[:, 2].reshape(devices, rows_held)[:, :micro].reshape(seqs).astype(jnp.int32)
    sent = pick_rows(table, held.reshape(seqs, 2 * CBLOCK, cols))
    fetched = lax.all_to_all(sent, ("dp", "tensor"), split_axis=0, concat_axis=0, tiled=True)
    fetched = fetched.reshape(chunks, 2, 2, CBLOCK, cols)

    meta = jnp.concatenate(
        [
            prefix[spot][None], spot[None].astype(jnp.int32),
            own_blocks[spot].reshape(-1), partner_blocks[spot].reshape(-1),
        ]
    )
    normed, qkv = project(x, gain_one, first_all)
    context, lse = attend(meta, qkv, own_k, own_v, fetched)
    mixed, normed_two = mix(x, context, gain_two, second_all)
    ffn_out, grad_normed_two, d_gate, d_up, d_down = ffn(normed_two, cotangent, second_all, width, hidden)
    share = functools.partial(lax.psum_scatter, axis_name="dp", scatter_dimension=0, tiled=True)
    ffn_share = share(jnp.concatenate([d_gate, d_up, d_down], axis=1))
    out, grad_mixed, branch, grad_context, gain_part_two = unmix(
        mixed, grad_normed_two, ffn_out, cotangent, gain_two, second_all
    )
    out = exchange(out.reshape(2, shard_len, width))
    d_out = inner_rows(branch, context).astype(BF16)
    dq, dk, dv = attend_back(meta, qkv, own_k, own_v, fetched, grad_context, context, lse)
    d_qkv = [inner_rows(normed, d).astype(BF16) for d in (dq, dk, dv)]
    attn_grads, ffn_share, out = lax.optimization_barrier(
        (jnp.concatenate([d_out] + d_qkv, axis=1), ffn_share, out)
    )
    attn_share = share(attn_grads)
    grad_tokens, gain_part_one = finish(x, grad_mixed, dq, dk, dv, gain_one, first_all)
    grad_tokens = exchange(grad_tokens.reshape(2, shard_len, width)).astype(F32)

    def halves(values, widths):
        mine, theirs, start = [], [], 0
        for w in widths:
            mine.append(values[:, start : start + w])
            theirs.append(values[:, start + w : start + 2 * w])
            start += 2 * w
        got = swap(jnp.concatenate(theirs, axis=1))
        total = jnp.concatenate(mine, axis=1).astype(F32) + got.astype(F32)
        return jnp.split(total, [sum(widths[: i + 1]) for i in range(len(widths) - 1)], axis=1)

    g_gate, g_up, g_down = halves(ffn_share, [hidden_held] * 3)
    g_out, g_query, g_key, g_value = halves(attn_share, [cols] * 4)
    gain_sums = lax.psum(jnp.concatenate([gain_part_one, gain_part_two], axis=0), ("dp", "tensor"))
    return (
        out, grad_tokens, gain_sums[0], g_query, g_key, g_value, g_out.T, gain_sums[1], g_gate, g_up, g_down.T,
    )


def solution(mesh):
    in_specs = (
        P("dp", "tensor", None),
        P("dp"),
        P("dp", "tensor"),
        P("dp", "tensor"),
        P("dp", "tensor"),
        P("tensor", "dp"),
        P("dp"),
        P("dp", "tensor"),
        P("dp", "tensor"),
        P("tensor", "dp"),
        P("dp", None, "tensor"),
        P("dp", None, "tensor"),
        P("dp"),
        P("dp"),
        P("dp", None, None),
        P("dp", None, None),
        P("dp", "tensor", None),
    )
    out_specs = (
        P("dp", "tensor", None),
        P("dp", "tensor", None),
        P(),
        P("dp", "tensor"),
        P("dp", "tensor"),
        P("dp", "tensor"),
        P("tensor", "dp"),
        P(),
        P("dp", "tensor"),
        P("dp", "tensor"),
        P("tensor", "dp"),
    )
    whole = mesh.shape["tensor"] == 2 and mesh.shape["dp"] == CACHE_LEN // CBLOCK
    body = sequence_body if whole else tensor_body
    return jax.shard_map(body, mesh=mesh, in_specs=in_specs, out_specs=out_specs, check_vma=False)
```

```python
import functools

import jax
import jax.numpy as jnp
from jax import lax
from jax.experimental import pallas as pl
from jax.experimental.pallas import tpu as pltpu
from jax.sharding import PartitionSpec as P

HD = 128
L = 2048
CACHE_LEN = 1024
QBLOCK = 128
CBLOCK = 64
KR = 4
QROWS = 512


EPS = 1e-05
NEGATIVE = -1e30


def norm_rows(values, gain):
    scale_rows = lax.rsqrt(jnp.mean(values * values, axis=-1, keepdims=True) + EPS)
    return (values * scale_rows * gain, scale_rows)


def norm_back(grad_normed, values, scale_rows, gain):
    unit = values * scale_rows
    grad_unit = grad_normed * gain
    grad_values = scale_rows * (
        grad_unit - unit * jnp.mean(grad_unit * unit, axis=-1, keepdims=True)
    )
    return (grad_values, jnp.sum(grad_normed * unit, axis=0))


def inner_rows(left, right):
    return lax.dot_general(
        left, right, (((0,), (0,)), ((), ())), preferred_element_type=jnp.float32
    )


def outer_cols(left, right):
    return lax.dot_general(
        left, right, (((1,), (1,)), ((), ())), preferred_element_type=jnp.float32
    )


def memory_rows(cache_one, chosen, width):
    shaped = cache_one.reshape(CACHE_LEN // CBLOCK, CBLOCK, width)
    return jnp.take(shaped, chosen, axis=0)


def block_scores(query_block, keys_part, mem_part, first_row, limit):
    rows_here, heads_here, size = query_block.shape
    extent = keys_part.shape[0]
    local = jnp.einsum(
        "qhd,khd->hqk", query_block, keys_part, preferred_element_type=jnp.float32
    ) * size ** (-0.5)
    row_ids = first_row + jnp.arange(rows_here, dtype=jnp.int32)[:, None]
    key_ids = jnp.arange(extent, dtype=jnp.int32)[None, :]
    allowed = (key_ids <= row_ids) | (row_ids < limit) & (key_ids < limit)
    local = jnp.where(allowed[None], local, NEGATIVE)
    groups = mem_part.shape[0]
    grouped = query_block.reshape(groups, rows_here // groups, heads_here, size)
    remote = jnp.einsum(
        "bqhd,bkhd->hbqk", grouped, mem_part, preferred_element_type=jnp.float32
    ) * size ** (-0.5)
    return (local, remote.reshape(heads_here, rows_here, -1))


def attention_forward(query, keys, values, mem_keys, mem_values, limit):
    groups = QROWS // QBLOCK
    heads_here = query.shape[1]
    context_parts = []
    lse_parts = []
    for index in range(L // QROWS):
        first = index * QROWS
        extent = max(first + QROWS, L // 2)
        query_block = query[first : first + QROWS]
        mem_k = mem_keys[index * groups : (index + 1) * groups]
        mem_v = mem_values[index * groups : (index + 1) * groups]
        local, remote = block_scores(query_block, keys[:extent], mem_k, first, limit)
        top = jnp.maximum(jnp.max(local, axis=-1), jnp.max(remote, axis=-1))
        e_local = jnp.exp(local - top[..., None])
        e_remote = jnp.exp(remote - top[..., None])
        total = jnp.sum(e_local, axis=-1) + jnp.sum(e_remote, axis=-1)
        p_local = (e_local / total[..., None]).astype(jnp.bfloat16)
        p_remote = (
            (e_remote / total[..., None])
            .astype(jnp.bfloat16)
            .reshape(heads_here, groups, QBLOCK, -1)
        )
        part = jnp.einsum(
            "hqk,khd->qhd", p_local, values[:extent], preferred_element_type=jnp.float32
        )
        extra = jnp.einsum("hbqk,bkhd->bqhd", p_remote, mem_v, preferred_element_type=jnp.float32)
        context_parts.append(part + extra.reshape(part.shape))
        lse_parts.append(top + jnp.log(total))
    return (jnp.concatenate(context_parts, axis=0), lse_parts)


def attention_backward(query, keys, values, mem_keys, mem_values, limit, lse_parts, grad_context):
    groups = QROWS // QBLOCK
    length, heads_here, size = query.shape
    scale = size ** (-0.5)
    grad_query_parts = []
    grad_keys = jnp.zeros(query.shape, jnp.float32)
    grad_values = jnp.zeros(query.shape, jnp.float32)
    for index in range(L // QROWS):
        first = index * QROWS
        extent = max(first + QROWS, L // 2)
        query_block = query[first : first + QROWS]
        mem_k = mem_keys[index * groups : (index + 1) * groups]
        mem_v = mem_values[index * groups : (index + 1) * groups]
        local, remote = block_scores(query_block, keys[:extent], mem_k, first, limit)
        lse_block = lse_parts[index][..., None]
        p_local = jnp.exp(local - lse_block)
        p_remote = jnp.exp(remote - lse_block)
        grad_block = grad_context[first : first + QROWS]
        grouped_grad = grad_block.reshape(groups, QBLOCK, heads_here, size)
        dp_local = jnp.einsum(
            "qhd,khd->hqk", grad_block, values[:extent], preferred_element_type=jnp.float32
        )
        dp_remote = jnp.einsum(
            "bqhd,bkhd->hbqk", grouped_grad, mem_v, preferred_element_type=jnp.float32
        )
        dp_remote = dp_remote.reshape(heads_here, QROWS, -1)
        delta = jnp.sum(p_local * dp_local, axis=-1) + jnp.sum(p_remote * dp_remote, axis=-1)
        ds_local = (p_local * (dp_local - delta[..., None])).astype(jnp.bfloat16)
        ds_remote = (p_remote * (dp_remote - delta[..., None])).astype(jnp.bfloat16)
        ds_remote = ds_remote.reshape(heads_here, groups, QBLOCK, -1)
        dq_block = jnp.einsum(
            "hqk,khd->qhd", ds_local, keys[:extent], preferred_element_type=jnp.float32
        )
        dq_extra = jnp.einsum(
            "hbqk,bkhd->bqhd", ds_remote, mem_k, preferred_element_type=jnp.float32
        )
        grad_query_parts.append((dq_block + dq_extra.reshape(dq_block.shape)) * scale)
        dk_part = (
            jnp.einsum("hqk,qhd->khd", ds_local, query_block, preferred_element_type=jnp.float32)
            * scale
        )
        dv_part = jnp.einsum(
            "hqk,qhd->khd",
            p_local.astype(jnp.bfloat16),
            grad_block,
            preferred_element_type=jnp.float32,
        )
        grad_keys = grad_keys.at[:extent].add(dk_part)
        grad_values = grad_values.at[:extent].add(dv_part)
    return (jnp.concatenate(grad_query_parts, axis=0), grad_keys, grad_values)


def tensor_body(
    tokens,
    gain_attn,
    w_query,
    w_key,
    w_value,
    w_out,
    gain_ffn,
    w_gate,
    w_up,
    w_down,
    cache_keys,
    cache_values,
    prefix,
    partner,
    own_blocks,
    partner_blocks,
    grad_out,
):
    micro, shard_len, width = tokens.shape
    cols = w_query.shape[1]
    heads_local = cols // HD
    qblocks = L // QBLOCK
    mem_len = 2 * KR * CBLOCK
    piece_keys = lax.all_gather(cache_keys, "dp", axis=0, tiled=True)
    piece_values = lax.all_gather(cache_values, "dp", axis=0, tiled=True)
    count = piece_keys.shape[0]
    onehot = (partner[:, None] == jnp.arange(count, dtype=jnp.int32)[None, :]).astype(jnp.bfloat16)
    add_keys = jnp.einsum("mn,nkc->mkc", onehot, piece_keys, preferred_element_type=jnp.float32)
    add_values = jnp.einsum("mn,nkc->mkc", onehot, piece_values, preferred_element_type=jnp.float32)
    fetched_keys = add_keys.astype(jnp.bfloat16)
    fetched_values = add_values.astype(jnp.bfloat16)
    totals = (
        jnp.zeros((width, cols), jnp.float32),
        jnp.zeros((width, cols), jnp.float32),
        jnp.zeros((width, cols), jnp.float32),
        jnp.zeros((cols, width), jnp.float32),
        jnp.zeros((width, w_gate.shape[1]), jnp.float32),
        jnp.zeros((width, w_gate.shape[1]), jnp.float32),
        jnp.zeros((w_gate.shape[1], width), jnp.float32),
    )
    shares = tuple(
        (
            jnp.zeros(w.shape, jnp.float32)
            for w in (w_query, w_key, w_value, w_out, w_gate, w_up, w_down)
        )
    )
    gain_total_attn = jnp.zeros((width,), jnp.float32)
    gain_total_ffn = jnp.zeros((width,), jnp.float32)
    out_rows = []
    grad_rows = []
    for step in range(micro):
        fwd = (
            lax.all_gather(gain_attn, "dp", axis=0, tiled=True),
            lax.all_gather(w_query, "dp", axis=0, tiled=True),
            lax.all_gather(w_key, "dp", axis=0, tiled=True),
            lax.all_gather(w_value, "dp", axis=0, tiled=True),
            lax.all_gather(w_out, "dp", axis=1, tiled=True),
            lax.all_gather(gain_ffn, "dp", axis=0, tiled=True),
            lax.all_gather(w_gate, "dp", axis=0, tiled=True),
            lax.all_gather(w_up, "dp", axis=0, tiled=True),
            lax.all_gather(w_down, "dp", axis=1, tiled=True),
        )
        g_attn, wq_full, wk_full, wv_full, wo_full, g_ffn, wg_full, wu_full, wd_full = fwd
        limit = prefix[step]
        own_k = memory_rows(cache_keys[step], own_blocks[step], cols)
        par_k = memory_rows(fetched_keys[step], partner_blocks[step], cols)
        own_v = memory_rows(cache_values[step], own_blocks[step], cols)
        par_v = memory_rows(fetched_values[step], partner_blocks[step], cols)
        mem_keys = jnp.concatenate([own_k, par_k], axis=1).reshape(
            qblocks, mem_len, heads_local, HD
        )
        mem_values = jnp.concatenate([own_v, par_v], axis=1).reshape(
            qblocks, mem_len, heads_local, HD
        )
        token_rows = tokens[step].astype(jnp.float32)
        normed, scale_one = norm_rows(token_rows, g_attn.astype(jnp.float32))
        normed_all = lax.all_gather(normed.astype(jnp.bfloat16), "tensor", axis=0, tiled=True)
        query = (
            jnp.dot(normed_all, wq_full, preferred_element_type=jnp.float32)
            .astype(jnp.bfloat16)
            .reshape(L, heads_local, HD)
        )
        keys = (
            jnp.dot(normed_all, wk_full, preferred_element_type=jnp.float32)
            .astype(jnp.bfloat16)
            .reshape(L, heads_local, HD)
        )
        values = (
            jnp.dot(normed_all, wv_full, preferred_element_type=jnp.float32)
            .astype(jnp.bfloat16)
            .reshape(L, heads_local, HD)
        )
        context_full, lse_parts = attention_forward(
            query, keys, values, mem_keys, mem_values, limit
        )
        context = context_full.reshape(L, cols).astype(jnp.bfloat16)
        mixed = token_rows + lax.psum_scatter(
            jnp.dot(context, wo_full, preferred_element_type=jnp.float32),
            "tensor",
            scatter_dimension=0,
            tiled=True,
        )
        normed_two, scale_two = norm_rows(mixed, g_ffn.astype(jnp.float32))
        normed_two_all = lax.all_gather(
            normed_two.astype(jnp.bfloat16), "tensor", axis=0, tiled=True
        )
        gate = jnp.dot(normed_two_all, wg_full, preferred_element_type=jnp.float32)
        upward = jnp.dot(normed_two_all, wu_full, preferred_element_type=jnp.float32)
        sigma = jax.nn.sigmoid(gate)
        silu_gate = gate * sigma
        hidden = (silu_gate * upward).astype(jnp.bfloat16)
        out_rows.append(
            (
                mixed
                + lax.psum_scatter(
                    jnp.dot(hidden, wd_full, preferred_element_type=jnp.float32).astype(
                        jnp.bfloat16
                    ),
                    "tensor",
                    scatter_dimension=0,
                    tiled=True,
                ).astype(jnp.float32)
            ).astype(jnp.bfloat16)
        )
        bwd = (
            lax.all_gather(gain_attn, "dp", axis=0, tiled=True),
            lax.all_gather(w_query, "dp", axis=0, tiled=True),
            lax.all_gather(w_key, "dp", axis=0, tiled=True),
            lax.all_gather(w_value, "dp", axis=0, tiled=True),
            lax.all_gather(w_out, "dp", axis=1, tiled=True),
            lax.all_gather(gain_ffn, "dp", axis=0, tiled=True),
            lax.all_gather(w_gate, "dp", axis=0, tiled=True),
            lax.all_gather(w_up, "dp", axis=0, tiled=True),
            lax.all_gather(w_down, "dp", axis=1, tiled=True),
        )
        g_attn, wq_full, wk_full, wv_full, wo_full, g_ffn, wg_full, wu_full, wd_full = bwd
        grad_here = grad_out[step]
        grad_all = lax.all_gather(grad_here, "tensor", axis=0, tiled=True)
        d_down = inner_rows(hidden, grad_all)
        grad_hidden = outer_cols(grad_all, wd_full)
        grad_gate = (grad_hidden * upward * sigma * (1.0 + gate * (1.0 - sigma))).astype(
            jnp.bfloat16
        )
        grad_up = (grad_hidden * silu_gate).astype(jnp.bfloat16)
        d_gate = inner_rows(normed_two_all, grad_gate)
        d_up = inner_rows(normed_two_all, grad_up)
        grad_normed_two = lax.psum_scatter(
            outer_cols(grad_gate, wg_full) + outer_cols(grad_up, wu_full),
            "tensor",
            scatter_dimension=0,
            tiled=True,
        )
        grad_mixed_norm, gain_part_ffn = norm_back(
            grad_normed_two, mixed, scale_two, g_ffn.astype(jnp.float32)
        )
        grad_mixed = grad_here.astype(jnp.float32) + grad_mixed_norm
        branch_all = lax.all_gather(grad_mixed.astype(jnp.bfloat16), "tensor", axis=0, tiled=True)
        d_out = inner_rows(context, branch_all)
        grad_context = (
            outer_cols(branch_all, wo_full).astype(jnp.bfloat16).reshape(L, heads_local, HD)
        )
        grad_query, grad_keys, grad_values = attention_backward(
            query, keys, values, mem_keys, mem_values, limit, lse_parts, grad_context
        )
        grad_query = grad_query.reshape(L, cols).astype(jnp.bfloat16)
        grad_keys = grad_keys.reshape(L, cols).astype(jnp.bfloat16)
        grad_values = grad_values.reshape(L, cols).astype(jnp.bfloat16)
        d_query = inner_rows(normed_all, grad_query)
        d_key = inner_rows(normed_all, grad_keys)
        d_value = inner_rows(normed_all, grad_values)
        grad_normed = lax.psum_scatter(
            (
                outer_cols(grad_query, wq_full)
                + outer_cols(grad_keys, wk_full)
                + outer_cols(grad_values, wv_full)
            ).astype(jnp.bfloat16),
            "tensor",
            scatter_dimension=0,
            tiled=True,
        ).astype(jnp.float32)
        grad_token_norm, gain_part_attn = norm_back(
            grad_normed, token_rows, scale_one, g_attn.astype(jnp.float32)
        )
        grad_rows.append(grad_mixed + grad_token_norm)
        gain_total_attn = gain_total_attn + gain_part_attn
        gain_total_ffn = gain_total_ffn + gain_part_ffn
        totals = tuple(
            (
                held + fresh
                for held, fresh in zip(
                    totals, (d_query, d_key, d_value, d_out, d_gate, d_up, d_down)
                )
            )
        )
    shares = (
        lax.psum_scatter(
            totals[0].astype(jnp.bfloat16), "dp", scatter_dimension=0, tiled=True
        ).astype(jnp.float32),
        lax.psum_scatter(
            totals[1].astype(jnp.bfloat16), "dp", scatter_dimension=0, tiled=True
        ).astype(jnp.float32),
        lax.psum_scatter(
            totals[2].astype(jnp.bfloat16), "dp", scatter_dimension=0, tiled=True
        ).astype(jnp.float32),
        lax.psum_scatter(
            totals[3].astype(jnp.bfloat16), "dp", scatter_dimension=1, tiled=True
        ).astype(jnp.float32),
        lax.psum_scatter(
            totals[4].astype(jnp.bfloat16), "dp", scatter_dimension=0, tiled=True
        ).astype(jnp.float32),
        lax.psum_scatter(
            totals[5].astype(jnp.bfloat16), "dp", scatter_dimension=0, tiled=True
        ).astype(jnp.float32),
        lax.psum_scatter(
            totals[6].astype(jnp.bfloat16), "dp", scatter_dimension=1, tiled=True
        ).astype(jnp.float32),
    )
    gain_attn_sum, gain_ffn_sum = lax.psum((gain_total_attn, gain_total_ffn), ("dp", "tensor"))
    return (
        jnp.stack(out_rows, axis=0),
        jnp.stack(grad_rows, axis=0),
        gain_attn_sum,
        shares[0],
        shares[1],
        shares[2],
        shares[3],
        gain_ffn_sum,
        shares[4],
        shares[5],
        shares[6],
    )


TQ = 512
TK = 512
ROWS = 512
HT = 256
SCALE = HD**-0.5
EXP_SCALE = SCALE * 1.4426950408889634
LOG2E = 1.4426950408889634
NT = (((1,), (1,)), ((), ()))
TN = (((0,), (0,)), ((), ()))
F32 = jnp.float32
BF16 = jnp.bfloat16
MIB = 1 << 20


def mm(left, right, dims=(((1,), (0,)), ((), ()))):
    return lax.dot_general(left, right, dims, preferred_element_type=F32)


def fold_max(values):
    best = values[:, :HD]
    for i in range(1, values.shape[1] // HD):
        best = jnp.maximum(best, values[:, i * HD : (i + 1) * HD])
    return best


def fold_sum(values):
    total = values[:, :HD]
    for i in range(1, values.shape[1] // HD):
        total = total + values[:, i * HD : (i + 1) * HD]
    return total


def reach_mask(first, tile, limit):
    rows = first + lax.broadcasted_iota(jnp.int32, (TQ, 1), 0)
    keys = tile * TK + lax.broadcasted_iota(jnp.int32, (1, TK), 1)
    reach = jnp.where(rows < limit, jnp.maximum(rows, limit - 1), rows)
    return keys <= reach


def pick_own(meta, block, own, buf):
    for i in range(KR):
        c = meta[2 + block * KR + i]
        buf[pl.ds(i * CBLOCK, CBLOCK), :] = own[0, pl.ds(pl.multiple_of(c * CBLOCK, CBLOCK), CBLOCK), :]


def pick_other(meta, block, other, buf, start=0):
    for i in range(KR):
        d = meta[2 + (L // QBLOCK) * KR + block * KR + i]
        buf[pl.ds(start + i * CBLOCK, CBLOCK), :] = other[d, 0, 0]


def pick_blocks(meta, block, own, other, buf):
    pick_own(meta, block, own, buf)
    pick_other(meta, block, other, buf, KR * CBLOCK)


def attend_kernel(
    meta, q_ref, k_ref, v_ref, ok_ref, ov_ref, ctx_ref, lse_ref, kbuf, vbuf, sbuf, smem, *, pair
):
    step = pl.program_id(1)
    limit = meta[0]
    first = step * TQ
    free = jnp.where(first < limit, (limit + TK - 1) // TK, 0)
    tiles = jnp.maximum(step + 1, free)
    blocks = TQ // QBLOCK
    for b in range(blocks):
        pick_own(meta, step * blocks + b, ok_ref, kbuf.at[b])
        pick_own(meta, step * blocks + b, ov_ref, vbuf.at[b])
    state = []
    for h in range(pair):
        cs = pl.ds(h * HD, HD)
        best = []
        for b in range(blocks):
            s = mm(q_ref[pl.ds(b * QBLOCK, QBLOCK), cs], kbuf[b, :, cs], NT)
            smem[h, pl.ds(b * QBLOCK, QBLOCK), :] = s
            best.append(fold_max(s))
        state.append(jnp.concatenate(best, 0))

    def scores(tile, state, masked):
        ks = pl.ds(pl.multiple_of(tile * TK, TK), TK)
        if masked:
            allowed = reach_mask(first, tile, limit)
        new = []
        for h in range(pair):
            cs = pl.ds(h * HD, HD)
            s = mm(q_ref[:, cs], k_ref[ks, cs], NT)
            if masked:
                s = jnp.where(allowed, s, NEGATIVE)
            sbuf[h, tile] = s
            new.append(jnp.maximum(state[h], fold_max(s)))
        return tuple(new)

    state = lax.fori_loop(0, step, lambda tile, s: scores(tile, s, False), tuple(state))
    state = lax.fori_loop(step, tiles, lambda tile, s: scores(tile, s, True), state)
    tops = [jnp.max(s, axis=1, keepdims=True) for s in state]
    state = []
    for h in range(pair):
        cs = pl.ds(h * HD, HD)
        p = jnp.exp2((smem[h] - tops[h]) * EXP_SCALE)
        low = p.astype(BF16)
        parts = [mm(low[b * QBLOCK : (b + 1) * QBLOCK], vbuf[b, :, cs]) for b in range(blocks)]
        state.append((fold_sum(p), jnp.concatenate(parts, 0)))

    def weigh(tile, state):
        ks = pl.ds(pl.multiple_of(tile * TK, TK), TK)
        new = []
        for h in range(pair):
            total, acc = state[h]
            p = jnp.exp2((sbuf[h, tile] - tops[h]) * EXP_SCALE)
            new.append((total + fold_sum(p), acc + mm(p.astype(BF16), v_ref[ks, pl.ds(h * HD, HD)])))
        return tuple(new)

    state = lax.fori_loop(0, tiles, weigh, tuple(state))
    for h in range(pair):
        cs = pl.ds(h * HD, HD)
        total = jnp.sum(state[h][0], axis=1, keepdims=True)
        ctx_ref[:, cs] = state[h][1] / total
        lse_ref[:, cs] = jnp.broadcast_to(tops[h] * SCALE + jnp.log(total), (TQ, HD))


def attend_other_kernel(meta, q_ref, pk_ref, pv_ref, part_ref, plse_ref, ctx_ref, lse_ref, kbuf, vbuf, *, pair):
    step = pl.program_id(1)
    blocks = TQ // QBLOCK
    for b in range(blocks):
        pick_other(meta, step * blocks + b, pk_ref, kbuf.at[b])
        pick_other(meta, step * blocks + b, pv_ref, vbuf.at[b])
    for h in range(pair):
        cs = pl.ds(h * HD, HD)
        rows = [pl.ds(b * QBLOCK, QBLOCK) for b in range(blocks)]
        s = jnp.concatenate([mm(q_ref[rows[b], cs], kbuf[b, :, cs], NT) for b in range(blocks)], 0)
        before = plse_ref[:, cs]
        top = jnp.maximum(before, jnp.max(fold_max(s), axis=1, keepdims=True) * SCALE)
        keep = jnp.exp(before - top)
        p = jnp.exp2(s * EXP_SCALE - top[:, :1] * LOG2E)
        low = p.astype(BF16)
        more = jnp.concatenate(
            [mm(low[b * QBLOCK : (b + 1) * QBLOCK], vbuf[b, :, cs]) for b in range(blocks)], 0
        )
        total = keep + jnp.sum(fold_sum(p), axis=1, keepdims=True)
        ctx_ref[:, cs] = ((part_ref[:, cs] * keep + more) / total).astype(BF16)
        lse_ref[:, cs] = top + jnp.log(total)


def attend_back_kernel(
    meta, q_ref, k_ref, v_ref, ok_ref, ov_ref, pk_ref, pv_ref, do_ref, ctx_ref, lse_ref,
    dq_ref, dk_ref, dv_ref, kbuf, vbuf, dks, dvs, *, pair
):
    step = pl.program_id(1)
    limit = meta[0]
    first = step * TQ
    free = jnp.where(first < limit, (limit + TK - 1) // TK, 0)
    tiles = jnp.maximum(step + 1, free)
    blocks = TQ // QBLOCK

    @pl.when(step == 0)
    def _():
        dks[...] = jnp.zeros_like(dks)
        dvs[...] = jnp.zeros_like(dvs)

    for b in range(blocks):
        pick_blocks(meta, step * blocks + b, ok_ref, pk_ref, kbuf.at[b])
        pick_blocks(meta, step * blocks + b, ov_ref, pv_ref, vbuf.at[b])
    state = []
    aux = []
    for h in range(pair):
        cs = pl.ds(h * HD, HD)
        delta = jnp.sum(do_ref[:, cs].astype(F32) * ctx_ref[:, cs].astype(F32), axis=1, keepdims=True)
        lse2 = lse_ref[:, cs][:, :1] * LOG2E
        aux.append((lse2, delta))
        parts = []
        for b in range(blocks):
            rs = pl.ds(b * QBLOCK, QBLOCK)
            s = mm(q_ref[rs, cs], kbuf[b, :, cs], NT)
            p = jnp.exp2(s * EXP_SCALE - lse2[b * QBLOCK : (b + 1) * QBLOCK])
            dp = mm(do_ref[rs, cs], vbuf[b, :, cs], NT)
            ds = (p * (dp - delta[b * QBLOCK : (b + 1) * QBLOCK])).astype(BF16)
            parts.append(mm(ds, kbuf[b, :, cs]))
        state.append(jnp.concatenate(parts, 0))

    def grads(tile, state, masked):
        ks = pl.ds(pl.multiple_of(tile * TK, TK), TK)
        if masked:
            allowed = reach_mask(first, tile, limit)
        new = []
        for h in range(pair):
            cs = pl.ds(h * HD, HD)
            lse2, delta = aux[h]
            s = mm(q_ref[:, cs], k_ref[ks, cs], NT)
            p = jnp.exp2(s * EXP_SCALE - lse2)
            if masked:
                p = jnp.where(allowed, p, 0.0)
            dp = mm(do_ref[:, cs], v_ref[ks, cs], NT)
            ds = (p * (dp - delta)).astype(BF16)
            dvs[ks, cs] += mm(p.astype(BF16), do_ref[:, cs], TN)
            dks[ks, cs] += mm(ds, q_ref[:, cs], TN)
            new.append(state[h] + mm(ds, k_ref[ks, cs]))
        return tuple(new)

    state = lax.fori_loop(0, step, lambda tile, s: grads(tile, s, False), tuple(state))
    state = lax.fori_loop(step, tiles, lambda tile, s: grads(tile, s, True), state)
    for h in range(pair):
        dq_ref[:, pl.ds(h * HD, HD)] = (state[h] * SCALE).astype(BF16)

    @pl.when(step == L // TQ - 1)
    def _():
        dk_ref[...] = (dks[...] * SCALE).astype(BF16)
        dv_ref[...] = dvs[...].astype(BF16)


def attention_specs(heads, pair):
    wide = pair * HD
    per = heads // 2 // pair
    groups = heads // pair
    return [
        pl.BlockSpec((TQ, wide), lambda h, i, meta: (i, h)),
        pl.BlockSpec((L, wide), lambda h, i, meta: (0, groups + h)),
        pl.BlockSpec((L, wide), lambda h, i, meta: (0, 2 * groups + h)),
        pl.BlockSpec((1, CACHE_LEN, wide), lambda h, i, meta: ((h // per) ^ meta[1], 0, h % per)),
        pl.BlockSpec((1, CACHE_LEN, wide), lambda h, i, meta: ((h // per) ^ meta[1], 0, h % per)),
        pl.BlockSpec(
            (CACHE_LEN // CBLOCK, 1, 1, CBLOCK, wide),
            lambda h, i, meta: (0, (h // per) ^ meta[1], 0, 0, h % per),
        ),
        pl.BlockSpec(
            (CACHE_LEN // CBLOCK, 1, 1, CBLOCK, wide),
            lambda h, i, meta: (0, (h // per) ^ meta[1], 1, 0, h % per),
        ),
    ]


def attend(meta, qkv, own_k, own_v, pair=2):
    width = qkv.shape[1] // 3
    heads = width // HD
    wide = pair * HD
    row = pl.BlockSpec((TQ, wide), lambda h, i, meta: (i, h))
    area = L * 1600 * width
    return pl.pallas_call(
        functools.partial(attend_kernel, pair=pair),
        grid_spec=pltpu.PrefetchScalarGridSpec(
            num_scalar_prefetch=1,
            grid=(heads // pair, L // TQ),
            in_specs=attention_specs(heads, pair)[:5],
            out_specs=[row, row],
            scratch_shapes=[pltpu.VMEM((TQ // QBLOCK, KR * CBLOCK, wide), BF16)] * 2
            + [pltpu.VMEM((pair, L // TK, TQ, TK), F32), pltpu.VMEM((pair, TQ, KR * CBLOCK), F32)],
        ),
        out_shape=[jax.ShapeDtypeStruct((L, width), F32)] * 2,
        compiler_params=pltpu.CompilerParams(vmem_limit_bytes=40 * MIB),
        cost_estimate=pl.CostEstimate(flops=12 * area, bytes_accessed=30 * MIB, transcendentals=area // HD),
        name="attend",
    )(meta, qkv, qkv, qkv, own_k, own_v)


def attend_other(meta, qkv, fetched, partial, lse, pair=4):
    width = qkv.shape[1] // 3
    heads = width // HD
    wide = pair * HD
    row = pl.BlockSpec((TQ, wide), lambda h, i, meta: (i, h))
    specs = attention_specs(heads, pair)
    return pl.pallas_call(
        functools.partial(attend_other_kernel, pair=pair),
        grid_spec=pltpu.PrefetchScalarGridSpec(
            num_scalar_prefetch=1,
            grid=(heads // pair, L // TQ),
            in_specs=[specs[0], specs[5], specs[6], row, row],
            out_specs=[row, row],
            scratch_shapes=[pltpu.VMEM((TQ // QBLOCK, KR * CBLOCK, wide), BF16)] * 2,
        ),
        out_shape=[jax.ShapeDtypeStruct((L, width), BF16), jax.ShapeDtypeStruct((L, width), F32)],
        compiler_params=pltpu.CompilerParams(vmem_limit_bytes=40 * MIB),
        cost_estimate=pl.CostEstimate(
            flops=4 * L * 256 * width, bytes_accessed=30 * MIB, transcendentals=L * 256 * heads
        ),
        name="attend_other",
    )(meta, qkv, fetched, fetched, partial, lse)


def attend_back(meta, qkv, own_k, own_v, fetched, grad_context, context, lse, pair=2):
    width = context.shape[1]
    heads = width // HD
    wide = pair * HD
    row = pl.BlockSpec((TQ, wide), lambda h, i, meta: (i, h))
    col = pl.BlockSpec((L, wide), lambda h, i, meta: (0, h))
    area = L * 1900 * width
    return pl.pallas_call(
        functools.partial(attend_back_kernel, pair=pair),
        grid_spec=pltpu.PrefetchScalarGridSpec(
            num_scalar_prefetch=1,
            grid=(heads // pair, L // TQ),
            in_specs=attention_specs(heads, pair) + [row, row, row],
            out_specs=[row, col, col],
            scratch_shapes=[pltpu.VMEM((TQ // QBLOCK, 2 * KR * CBLOCK, wide), BF16)] * 2
            + [pltpu.VMEM((L, wide), F32)] * 2,
        ),
        out_shape=[jax.ShapeDtypeStruct((L, width), BF16)] * 3,
        compiler_params=pltpu.CompilerParams(vmem_limit_bytes=48 * MIB),
        cost_estimate=pl.CostEstimate(flops=12 * area, bytes_accessed=40 * MIB, transcendentals=area // HD),
        name="attend_back",
    )(meta, qkv, qkv, qkv, own_k, own_v, fetched, fetched, grad_context, context, lse)


def project_kernel(x_ref, gain_ref, w_ref, normed_ref, qkv_ref):
    rows = x_ref[...].astype(F32)
    scale = lax.rsqrt(jnp.mean(rows * rows, axis=1, keepdims=True) + EPS)
    normed_ref[...] = (rows * scale * gain_ref[...]).astype(BF16)
    left = normed_ref[...]

    def chunk(c, carry):
        cs = pl.ds(pl.multiple_of(c * 512, 512), 512)
        qkv_ref[:, cs] = mm(left, w_ref[:, cs]).astype(BF16)
        return carry

    lax.fori_loop(0, qkv_ref.shape[1] // 512, chunk, 0)


def project(x, gain, weights):
    width = x.shape[1]
    cols = 3 * width
    row = lambda n: pl.BlockSpec((ROWS, n), lambda i: (i, 0))
    whole = lambda n: pl.BlockSpec((width, n), lambda i: (0, 0))
    return pl.pallas_call(
        project_kernel,
        grid=(L // ROWS,),
        in_specs=[row(width), pl.BlockSpec((1, width), lambda i: (0, 0)), whole(cols)],
        out_specs=[row(width), row(cols)],
        out_shape=[jax.ShapeDtypeStruct((L, width), BF16), jax.ShapeDtypeStruct((L, cols), BF16)],
        compiler_params=pltpu.CompilerParams(vmem_limit_bytes=40 * MIB),
        cost_estimate=pl.CostEstimate(flops=2 * L * width * cols, bytes_accessed=26 * MIB, transcendentals=0),
        name="project",
    )(x, gain, weights)


def mix_kernel(x_ref, ctx_ref, gain_ref, w_ref, mixed_ref, normed_ref):
    mixed = x_ref[...].astype(F32) + mm(ctx_ref[...], w_ref[...], NT)
    mixed_ref[...] = mixed
    scale = lax.rsqrt(jnp.mean(mixed * mixed, axis=1, keepdims=True) + EPS)
    normed_ref[...] = (mixed * scale * gain_ref[...]).astype(BF16)


def mix(x, context, gain, weights):
    width = x.shape[1]
    row = pl.BlockSpec((ROWS, width), lambda i: (i, 0))
    return pl.pallas_call(
        mix_kernel,
        grid=(L // ROWS,),
        in_specs=[row, row, pl.BlockSpec((1, width), lambda i: (0, 0)), pl.BlockSpec((width, width), lambda i: (0, 0))],
        out_specs=[row, row],
        out_shape=[jax.ShapeDtypeStruct((L, width), F32), jax.ShapeDtypeStruct((L, width), BF16)],
        compiler_params=pltpu.CompilerParams(vmem_limit_bytes=32 * MIB),
        cost_estimate=pl.CostEstimate(flops=2 * L * width * width, bytes_accessed=22 * MIB, transcendentals=0),
        name="mix",
    )(x, context, gain, weights)


def ffn_kernel(n_ref, g_ref, wg_ref, wu_ref, wd_ref, out_ref, gn_ref, grads_ref, acc, ag, au, ad):
    tile = pl.program_id(0)
    last = pl.num_programs(0) - 1

    @pl.when(tile == 0)
    def _():
        acc[...] = jnp.zeros_like(acc)
        gn_ref[...] = jnp.zeros_like(gn_ref)

    ag[...] = jnp.zeros_like(ag)
    au[...] = jnp.zeros_like(au)
    ad[...] = jnp.zeros_like(ad)

    def chunk(r, carry):
        rs = pl.ds(pl.multiple_of(r * ROWS, ROWS), ROWS)
        rows = n_ref[rs, :]
        cotangent = g_ref[rs, :]
        gate = mm(rows, wg_ref[...])
        up = mm(rows, wu_ref[...])
        grad_hidden = mm(cotangent, wd_ref[...])
        sigma = 1.0 / (1.0 + jnp.exp(-gate))
        silu = gate * sigma
        hidden = (silu * up).astype(BF16)
        grad_gate = (grad_hidden * up * (sigma * (1.0 + gate * (1.0 - sigma)))).astype(BF16)
        grad_up = (grad_hidden * silu).astype(BF16)
        acc[rs, :] += mm(hidden, wd_ref[...], NT)
        gn_ref[rs, :] += mm(grad_gate, wg_ref[...], NT) + mm(grad_up, wu_ref[...], NT)
        ag[...] += mm(rows, grad_gate, TN)
        au[...] += mm(rows, grad_up, TN)
        ad[...] += mm(cotangent, hidden, TN)
        return carry

    lax.fori_loop(0, L // ROWS, chunk, 0)
    grads_ref[:, :HT] = ag[...].astype(BF16)
    grads_ref[:, HT : 2 * HT] = au[...].astype(BF16)
    grads_ref[:, 2 * HT :] = ad[...].astype(BF16)

    @pl.when(tile == last)
    def _():
        out_ref[...] = acc[...].astype(BF16)


def ffn(normed, cotangent, weights, width, hidden):
    once = pl.Buffered(1)
    tiles = hidden // HT
    lead = width // HT
    part = lambda k: pl.BlockSpec((width, HT), lambda j: (0, lead + k * tiles + j))
    whole = pl.BlockSpec((L, width), lambda j: (0, 0), pipeline_mode=once)
    grad = pl.BlockSpec((width, 3 * HT), lambda j: (0, j))
    return pl.pallas_call(
        ffn_kernel,
        grid=(tiles,),
        in_specs=[whole, whole, part(0), part(1), part(2)],
        out_specs=[whole, whole, grad],
        out_shape=[jax.ShapeDtypeStruct((L, width), BF16), jax.ShapeDtypeStruct((L, width), F32)]
        + [jax.ShapeDtypeStruct((width, 3 * hidden), BF16)],
        scratch_shapes=[pltpu.VMEM((L, width), F32)] + [pltpu.VMEM((width, HT), F32)] * 3,
        compiler_params=pltpu.CompilerParams(vmem_limit_bytes=56 * MIB),
        cost_estimate=pl.CostEstimate(
            flops=18 * L * width * hidden, bytes_accessed=60 * MIB, transcendentals=L * hidden
        ),
        name="ffn",
    )(normed, cotangent, weights, weights, weights)


def unmix_kernel(mixed_ref, gn_ref, ffn_ref, g_ref, gain_ref, w_ref, out_ref, gm_ref, br_ref, gc_ref, gg_ref):
    mixed = mixed_ref[...]
    grad = gn_ref[...]
    scale = lax.rsqrt(jnp.mean(mixed * mixed, axis=1, keepdims=True) + EPS)
    unit = mixed * scale
    inner = grad * gain_ref[...]
    grad_mixed = g_ref[...].astype(F32) + scale * (inner - unit * jnp.mean(inner * unit, axis=1, keepdims=True))
    out_ref[...] = (mixed + ffn_ref[...].astype(F32)).astype(BF16)
    gm_ref[...] = grad_mixed
    branch = grad_mixed.astype(BF16)
    br_ref[...] = branch
    gc_ref[...] = mm(branch, w_ref[...]).astype(BF16)

    @pl.when(pl.program_id(0) == 0)
    def _():
        gg_ref[...] = jnp.zeros_like(gg_ref)

    gg_ref[...] += jnp.sum(grad * unit, axis=0, keepdims=True)


def unmix(mixed, grad_normed, ffn_out, cotangent, gain, weights):
    width = mixed.shape[1]
    rows = ROWS // 2
    row = pl.BlockSpec((rows, width), lambda i: (i, 0))
    one = pl.BlockSpec((1, width), lambda i: (0, 0))
    return pl.pallas_call(
        unmix_kernel,
        grid=(L // rows,),
        in_specs=[row, row, row, row, one, pl.BlockSpec((width, width), lambda i: (0, 0))],
        out_specs=[row, row, row, row, one],
        out_shape=[
            jax.ShapeDtypeStruct((L, width), BF16),
            jax.ShapeDtypeStruct((L, width), F32),
            jax.ShapeDtypeStruct((L, width), BF16),
            jax.ShapeDtypeStruct((L, width), BF16),
            jax.ShapeDtypeStruct((1, width), F32),
        ],
        compiler_params=pltpu.CompilerParams(vmem_limit_bytes=40 * MIB),
        cost_estimate=pl.CostEstimate(flops=2 * L * width * width, bytes_accessed=46 * MIB, transcendentals=0),
        name="unmix",
    )(mixed, grad_normed, ffn_out, cotangent, gain, weights)


RING = 8
RIGHT = RING // 2
LEFT = RING - 1 - RIGHT


def ring_place(p):
    y = p // 4
    return (p + y * (7 - 2 * p)) * 2 + y


def meet(devices, me, spot):
    barrier = pltpu.get_barrier_semaphore()
    for d in range(1, devices):
        pl.semaphore_signal(
            barrier, inc=1, device_id=((me + d) % devices, spot), device_id_type=pl.DeviceIdType.MESH
        )
    pl.semaphore_signal(barrier, inc=1, device_id=(me, 1 - spot), device_id_type=pl.DeviceIdType.MESH)
    pl.semaphore_wait(barrier, devices)


def remote(src, dst, send, recv, device):
    return pltpu.make_async_remote_copy(
        src_ref=src, dst_ref=dst, send_sem=send, recv_sem=recv, device_id=device, device_id_type=pl.DeviceIdType.MESH
    )


FT = 256


def finish_kernel(
    x_ref, gm_ref, n_ref, ctx_ref, br_ref, dq_ref, dk_ref, dv_ref, w_ref, gain_ref, gain_two_ref,
    gt_ref, sums_ref, share_ref,
    n_buf, ctx_buf, br_buf, dq_buf, dk_buf, dv_buf, w_buf, x_buf, gm_buf, gt_buf,
    part, got, land, across, gains, gain_land,
    load_sem, x_sem, gm_sem, gt_sem, pair_send, pair_recv, ring_send, ring_recv, x_send, x_recv, g_send, g_recv,
    *, devices,
):
    me = lax.axis_index("dp")
    spot = lax.axis_index("tensor")
    core = me % 2
    z, y = me // 4, (me // 2) % 2
    place = z + y * (7 - 2 * z)
    width = n_buf.shape[1]
    half = width // 2
    rows = part.shape[2]
    loads = [
        pltpu.make_async_copy(src, dst, load_sem.at[i])
        for i, (src, dst) in enumerate(
            [
                (ctx_ref, ctx_buf), (br_ref, br_buf), (n_ref, n_buf), (dv_ref, dv_buf),
                (dk_ref, dk_buf), (dq_ref, dq_buf), (w_ref.at[:, pl.ds(0, 3 * width)], w_buf),
            ]
        )
    ]
    for copy in loads:
        copy.start()
    meet(devices, me, spot)

    def tile_in(t, slot):
        rs = pl.ds(pl.multiple_of(t * FT, FT), FT)
        return [
            pltpu.make_async_copy(x_ref.at[rs, :], x_buf.at[slot], x_sem.at[slot]),
            pltpu.make_async_copy(gm_ref.at[rs, :], gm_buf.at[slot], gm_sem.at[slot]),
        ]

    def tile_out(t, slot):
        rs = pl.ds(pl.multiple_of(t * FT, FT), FT)
        return pltpu.make_async_copy(gt_buf.at[slot], gt_ref.at[rs, :], gt_sem.at[slot])

    for copy in tile_in(0, 0):
        copy.start()

    pair = (me + 1 - 2 * core, spot)

    def to_pair(m):
        cs = pl.ds(m * width, width)
        return remote(part.at[:, 1 - core, :, cs], got.at[:, :, cs], pair_send.at[m], pair_recv.at[m], pair)

    def product(m, left, right):
        def chunk(c, carry):
            cs = pl.ds(pl.multiple_of(c * half, half), half)
            value = mm(left[...], right[:, cs], TN).astype(BF16)
            part[:, :, :, pl.ds(pl.multiple_of(m * width + c * half, half), half)] = value.reshape(
                part.shape[0], 2, rows, half
            )
            return carry

        lax.fori_loop(0, 2, chunk, 0)
        to_pair(m).start()

    def join(m):
        to_pair(m).wait_recv()
        cs = pl.ds(m * width, width)

        def one(b, carry):
            got[b, :, cs] = (got[b, :, cs].astype(F32) + part[b, core, :, cs].astype(F32)).astype(BF16)
            return carry

        lax.fori_loop(0, part.shape[0], one, 0)

    span = 2 * width
    neighbours = [(place + 1) % RING, (place + RING - 1) % RING]

    def held_block(direction, s):
        p = (place + 2 * RING - 1 - s) % RING if direction == 0 else (place + 1 + s) % RING
        return got.at[ring_place(p), :, pl.ds(direction * span, span)]

    def hop(direction, s):
        to = ring_place(neighbours[direction]) * 2 + core
        return remote(
            held_block(direction, s), land.at[direction, s],
            ring_send.at[direction, s], ring_recv.at[direction, s], (to, spot),
        )

    def advance(direction, s, more=True):
        hop(direction, s).wait_recv()
        block = held_block(direction, s + 1)
        block[...] = (block[...].astype(F32) + land[direction, s].astype(F32)).astype(BF16)
        if more:
            hop(direction, s + 1).start()

    def finish_rows(t, slot):
        for copy in tile_in(t, slot):
            copy.wait()
        rs = pl.ds(pl.multiple_of(t * FT, FT), FT)
        grad = mm(dq_buf[rs, :], w_buf[:, :width], NT)
        grad += mm(dk_buf[rs, :], w_buf[:, width : 2 * width], NT)
        grad += mm(dv_buf[rs, :], w_buf[:, 2 * width :], NT)
        values = x_buf[slot].astype(F32)
        scale = lax.rsqrt(jnp.mean(values * values, axis=1, keepdims=True) + EPS)
        unit = values * scale
        inner = grad * gain_ref[...]
        back = scale * (inner - unit * jnp.mean(inner * unit, axis=1, keepdims=True))
        gt_buf[slot] = (gm_buf[slot] + back).astype(BF16)
        gains[:1, :] += jnp.sum(grad * unit, axis=0, keepdims=True)

    for i in (0, 1):
        loads[i].wait()
    product(0, br_buf, ctx_buf)
    for i in (2, 3):
        loads[i].wait()
    product(1, n_buf, dv_buf)
    join(0)
    join(1)
    hop(0, 0).start()
    loads[4].wait()
    product(2, n_buf, dk_buf)
    advance(0, 0)
    loads[5].wait()
    product(3, n_buf, dq_buf)
    advance(0, 1)
    join(2)
    join(3)
    hop(1, 0).start()
    loads[6].wait()
    gains[:1, :] = jnp.zeros((1, width), F32)
    gains[1:, :] = gain_two_ref[...]

    def sweep(i, carry):
        for slot in (0, 1):
            t = 2 * i + slot
            if slot == 0:
                for copy in tile_in(t + 1, 1):
                    copy.start()
            else:

                @pl.when(i < 3)
                def _():
                    for copy in tile_in(t + 1, 0):
                        copy.start()

            @pl.when(i > 0)
            def _():
                tile_out(t - 2, slot).wait()

            finish_rows(t, slot)
            tile_out(t, slot).start()
        advance(0, i + 2)
        advance(1, i)
        return carry

    lax.fori_loop(0, L // FT // 2, sweep, 0)

    partners = [
        (me + 1 - 2 * core, spot),
        (me + 2 - 4 * y, spot),
        (me + 4 - 8 * (z % 2), spot),
        (me + 8 - 16 * (z // 2), spot),
        (me, 1 - spot),
    ]

    def add_gains(r):
        return remote(gains, gain_land.at[r], g_send.at[r], g_recv.at[r], partners[r])

    def gain_round(r):
        add_gains(r).wait()
        gains[...] = gains[...] + gain_land[r]
        if r < 4:
            add_gains(r + 1).start()

    own = ring_place(place)
    peer = (me, 1 - spot)

    def over(m):
        return remote(
            got.at[own, :, pl.ds(m * width + half, half)], across.at[:, pl.ds(m * half, half)],
            x_send.at[m], x_recv.at[m], peer,
        )

    add_gains(0).start()
    advance(0, 6, False)
    over(0).start()
    over(1).start()
    gain_round(0)
    advance(1, 4)
    gain_round(1)
    gain_round(2)
    advance(1, 5)
    gain_round(3)
    gain_round(4)
    advance(1, 6, False)
    over(2).start()
    over(3).start()
    sums_ref[...] = gains[...]
    for m in range(4):
        over(m).wait_recv()
        cs = pl.ds(m * half, half)
        share_ref[:, cs] = got[own, :, pl.ds(m * width, half)].astype(F32) + across[:, cs].astype(F32)
    for m in range(4):
        over(m).wait_send()
        to_pair(m).wait_send()
    for s in range(RING - 1):
        hop(0, s).wait_send()
        hop(1, s).wait_send()
    tile_out(L // FT - 2, 0).wait()
    tile_out(L // FT - 1, 1).wait()


def finish(x, grad_mixed, normed, context, branch, dq, dk, dv, weights, gain, gain_two_part, devices):
    width = x.shape[1]
    rows = width // devices
    anywhere = pl.BlockSpec(memory_space=pltpu.HBM)
    vmem = pl.BlockSpec(memory_space=pltpu.VMEM)
    dma = pltpu.SemaphoreType.DMA
    whole = pltpu.VMEM((L, width), BF16)
    return pl.pallas_call(
        functools.partial(finish_kernel, devices=devices),
        in_specs=[anywhere] * 9 + [vmem] * 2,
        out_specs=[anywhere, vmem, vmem],
        out_shape=[
            jax.ShapeDtypeStruct((L, width), BF16),
            jax.ShapeDtypeStruct((2, width), F32),
            jax.ShapeDtypeStruct((rows, 2 * width), F32),
        ],
        scratch_shapes=[
            whole, whole, whole, whole, whole, whole, pltpu.VMEM((width, 3 * width), BF16),
            pltpu.VMEM((2, FT, width), BF16), pltpu.VMEM((2, FT, width), F32), pltpu.VMEM((2, FT, width), BF16),
            pltpu.VMEM((RING, 2, rows, 4 * width), BF16),
            pltpu.VMEM((RING, rows, 4 * width), BF16),
            pltpu.VMEM((2, RING - 1, rows, 2 * width), BF16),
            pltpu.VMEM((rows, 2 * width), BF16),
            pltpu.VMEM((2, width), F32), pltpu.VMEM((5, 2, width), F32),
            dma((7,)), dma((2,)), dma((2,)), dma((2,)), dma((4,)), dma((4,)),
            dma((2, RING - 1)), dma((2, RING - 1)), dma((4,)), dma((4,)), dma((5,)), dma((5,)),
        ],
        compiler_params=pltpu.CompilerParams(collective_id=1, has_side_effects=True, vmem_limit_bytes=60 * MIB),
        cost_estimate=pl.CostEstimate(flops=14 * L * width * width, bytes_accessed=80 * MIB, transcendentals=0),
        name="finish",
    )(x, grad_mixed, normed, context, branch, dq, dk, dv, weights, gain, gain_two_part)


def pick_kernel(table, held_ref, sent_ref, sems):
    def copy(i):
        return pltpu.make_async_copy(held_ref.at[table[i]], sent_ref.at[i], sems.at[i])

    for i in range(sent_ref.shape[0]):
        copy(i).start()
    for i in range(sent_ref.shape[0]):
        copy(i).wait()


def pick_rows(table, held):
    count = held.shape[0]
    return pl.pallas_call(
        pick_kernel,
        grid_spec=pltpu.PrefetchScalarGridSpec(
            num_scalar_prefetch=1,
            grid=(),
            in_specs=[pl.BlockSpec(memory_space=pl.ANY)],
            out_specs=pl.BlockSpec(memory_space=pltpu.VMEM),
            scratch_shapes=[pltpu.SemaphoreType.DMA((count,))],
        ),
        out_shape=jax.ShapeDtypeStruct(held.shape, held.dtype),
        compiler_params=pltpu.CompilerParams(vmem_limit_bytes=16 * MIB),
        cost_estimate=pl.CostEstimate(flops=0, bytes_accessed=2 * held.size * 2, transcendentals=0),
        name="pick_rows",
    )(table, held)


def spread_kernel(
    tok_ref, ck_ref, cv_ref, small_ref, extra_ref, big_ref,
    x_ref, ok_ref, ov_ref, held_ref, first_ref, second_ref,
    tok_buf, k_buf, v_buf, local_sem, x_send, x_recv, all_send, all_recv, ring_send, ring_recv, pair_send, pair_recv,
):
    me = lax.axis_index("dp")
    spot = lax.axis_index("tensor")
    peer = 1 - spot
    devices = held_ref.shape[0]
    rows, cols = small_ref.shape[0], small_ref.shape[1] // 3
    core = me % 2
    z, y = me // 4, (me // 2) % 2
    place = z + y * (7 - 2 * z)

    def at_place(p):
        yy = p // 4
        return (p + yy * (7 - 2 * p)) * 4 + yy * 2

    def target(dp, tensor):
        return (dp, tensor)

    barrier = pltpu.get_barrier_semaphore()
    for d in range(1, devices):
        pl.semaphore_signal(barrier, inc=1, device_id=target((me + d) % devices, spot), device_id_type=pl.DeviceIdType.MESH)
    pl.semaphore_signal(barrier, inc=1, device_id=target(me, peer), device_id_type=pl.DeviceIdType.MESH)
    pl.semaphore_wait(barrier, devices)

    def remote(src, dst, send, recv, device):
        return pltpu.make_async_remote_copy(
            src_ref=src, dst_ref=dst, send_sem=send, recv_sem=recv,
            device_id=device, device_id_type=pl.DeviceIdType.MESH,
        )

    mine = pl.multiple_of(me * rows, rows)
    across = target(me, peer)
    weight_copies = []
    for i in range(3):
        weight_copies.append(
            remote(
                small_ref.at[:, pl.ds(i * cols, cols)],
                first_ref.at[pl.ds(mine, rows), pl.ds((2 * i + 1) * cols, cols)],
                x_send.at[i], x_recv.at[i], across,
            )
        )
    for copy in weight_copies:
        copy.start()
    for i in range(3):
        first_ref[pl.ds(mine, rows), pl.ds(2 * i * cols, cols)] = small_ref[:, pl.ds(i * cols, cols)]
    first_ref[pl.ds(mine, rows), pl.ds(6 * cols, HD)] = extra_ref[...]

    loads = [
        pltpu.make_async_copy(tok_ref.at[spot], tok_buf, local_sem.at[0]),
        pltpu.make_async_copy(ck_ref.at[spot], k_buf, local_sem.at[1]),
        pltpu.make_async_copy(cv_ref.at[spot], v_buf, local_sem.at[2]),
    ]
    stores = [
        pltpu.make_async_copy(tok_buf, x_ref.at[spot], local_sem.at[3]),
        pltpu.make_async_copy(k_buf, ok_ref.at[spot], local_sem.at[4]),
        pltpu.make_async_copy(v_buf, ov_ref.at[spot], local_sem.at[5]),
    ]
    for copy in loads:
        copy.start()

    x_copies = [remote(tok_ref.at[peer], x_ref.at[spot], x_send.at[3], x_recv.at[3], across)]
    wide = big_ref.shape[1]
    hidden = (wide - cols) // 3
    starts = [(0, cols)] + [(cols + i * hidden, hidden) for i in range(3)]
    own_cols = []
    for i, (start, size) in enumerate(starts):
        base = 2 * start
        own_cols.append(pltpu.make_async_copy(
            big_ref.at[:, pl.ds(start, size)], second_ref.at[:, pl.ds(base, size)], local_sem.at[6 + i]))
        x_copies.append(remote(
            big_ref.at[:, pl.ds(start, size)], second_ref.at[:, pl.ds(base + size, size)],
            x_send.at[4 + i], x_recv.at[4 + i], across))
    x_copies.append(remote(ck_ref.at[peer], ok_ref.at[spot], x_send.at[8], x_recv.at[8], across))
    x_copies.append(remote(cv_ref.at[peer], ov_ref.at[spot], x_send.at[9], x_recv.at[9], across))
    for copy in x_copies + own_cols:
        copy.start()

    def to_device(d, dst_dp):
        chunk = pl.ds(pl.multiple_of(dst_dp * CBLOCK, CBLOCK), CBLOCK)
        dst = target(dst_dp, spot)
        return [
            remote(ck_ref.at[:, chunk, :], held_ref.at[me, :, 0], all_send.at[0, d], all_recv.at[0, d], dst),
            remote(cv_ref.at[:, chunk, :], held_ref.at[me, :, 1], all_send.at[1, d], all_recv.at[1, d], dst),
        ]

    for copy in weight_copies:
        copy.wait_recv()

    def block(p, c):
        return first_ref.at[pl.ds(pl.multiple_of((at_place(p) + c) * rows, rows), rows), :]

    ahead = (place + 1) % RING
    behind = (place + RING - 1) % RING

    def hop(s, direction):
        p = (place + RING - (s - 1)) % RING if direction == 0 else (place + s - 1) % RING
        to = ahead if direction == 0 else behind
        k = (s - 1) * 2 + direction
        return remote(block(p, core), block(p, core), ring_send.at[k], ring_recv.at[k], target(at_place(to) + core, spot))

    def to_pair(i, p):
        return remote(block(p, core), block(p, core), pair_send.at[i], pair_recv.at[i], target(at_place(place) + 1 - core, spot))

    hops = [hop(1, 0), hop(1, 1)]
    for copy in hops:
        copy.start()
    pairs = [to_pair(0, place)]
    pairs[0].start()
    copies = []
    for d in range(1, devices):
        for copy in to_device(d, (me + d) % devices):
            copy.start()
            copies.append(copy)
    chunk = pl.ds(pl.multiple_of(me * CBLOCK, CBLOCK), CBLOCK)
    kept = [
        pltpu.make_async_copy(ck_ref.at[:, chunk, :], held_ref.at[me, :, 0], local_sem.at[10]),
        pltpu.make_async_copy(cv_ref.at[:, chunk, :], held_ref.at[me, :, 1], local_sem.at[11]),
    ]
    for copy in kept:
        copy.start()
    for load, store in zip(loads, stores):
        load.wait()
        store.start()
    for s in range(1, RIGHT + 1):
        for direction in range(2):
            if direction == 1 and s > LEFT:
                continue
            hops[(s - 1) * 2 + direction].wait_recv()
            p = (place + RING - s) % RING if direction == 0 else (place + s) % RING
            if s < (RIGHT if direction == 0 else LEFT):
                nxt = hop(s + 1, direction)
                nxt.start()
                hops.append(nxt)
            pair = to_pair(len(pairs), p)
            pair.start()
            pairs.append(pair)
    for copy in weight_copies + hops:
        copy.wait_send()
    for copy in pairs + x_copies + copies:
        copy.wait()
    for copy in stores + own_cols + kept:
        copy.wait()


def spread(tokens, cache_keys, cache_values, small, extra, big, devices):
    micro, shard_len, width = tokens.shape
    rows, cols = small.shape[0], small.shape[1] // 3
    anywhere = pl.BlockSpec(memory_space=pltpu.HBM)
    vmem = pl.BlockSpec(memory_space=pltpu.VMEM)
    dma = pltpu.SemaphoreType.DMA
    return pl.pallas_call(
        spread_kernel,
        in_specs=[anywhere, anywhere, anywhere, vmem, vmem, vmem],
        out_specs=[anywhere, anywhere, anywhere, anywhere, vmem, anywhere],
        out_shape=[
            jax.ShapeDtypeStruct((2, shard_len, width), BF16),
            jax.ShapeDtypeStruct((2, CACHE_LEN, cols), BF16),
            jax.ShapeDtypeStruct((2, CACHE_LEN, cols), BF16),
            jax.ShapeDtypeStruct((devices, micro, 2, CBLOCK, cols), BF16),
            jax.ShapeDtypeStruct((rows * devices, 6 * cols + HD), BF16),
            jax.ShapeDtypeStruct((rows, 2 * big.shape[1]), BF16),
        ],
        scratch_shapes=[
            pltpu.VMEM((shard_len, width), BF16),
            pltpu.VMEM((CACHE_LEN, cols), BF16),
            pltpu.VMEM((CACHE_LEN, cols), BF16),
            dma((12,)), dma((10,)), dma((10,)), dma((2, devices)), dma((2, devices)),
            dma((RING - 1,)), dma((RING - 1,)), dma((RING,)), dma((RING,)),
        ],
        compiler_params=pltpu.CompilerParams(collective_id=0, has_side_effects=True, vmem_limit_bytes=32 * MIB),
        cost_estimate=pl.CostEstimate(flops=0, bytes_accessed=300 * MIB, transcendentals=0),
        name="spread",
    )(tokens, cache_keys, cache_values, small, extra, big)


def swap(values):
    return lax.ppermute(values, "tensor", [(0, 1), (1, 0)])


def sequence_body(
    tokens, gain_attn, w_query, w_key, w_value, w_out, gain_ffn, w_gate, w_up, w_down,
    cache_keys, cache_values, prefix, partner, own_blocks, partner_blocks, grad_out,
):
    micro, shard_len, width = tokens.shape
    devices = lax.axis_size("dp")
    seqs = micro * devices
    rows_held, cols = w_query.shape
    hidden_held = w_gate.shape[1]
    hidden = 2 * hidden_held
    spot = lax.axis_index("tensor")
    exchange = functools.partial(lax.all_to_all, axis_name="tensor", split_axis=0, concat_axis=0, tiled=True)
    chunks = CACHE_LEN // CBLOCK

    small = jnp.concatenate([w_query, w_key, w_value], axis=1)
    partner_column = jnp.zeros((rows_held, 1), BF16).at[:micro, 0].set(partner.astype(BF16))
    extra = jnp.concatenate(
        [gain_attn[:, None], gain_ffn[:, None], partner_column, jnp.zeros((rows_held, HD - 3), BF16)], axis=1
    )
    big = jnp.concatenate([w_out.T, w_gate, w_up, w_down.T], axis=1)
    x, own_k, own_v, held, first_all, second_rows = spread(
        tokens, cache_keys, cache_values, small, extra, big, devices
    )
    x = x.reshape(L, width)
    cotangent = exchange(grad_out).reshape(L, width)
    second_all = lax.all_gather(second_rows, "dp", axis=0, tiled=True)

    tail = lax.optimization_barrier(first_all[:, 3 * width :])
    gains = mm((jnp.arange(2)[:, None] == jnp.arange(HD)[None, :]).astype(BF16), tail, NT)
    gain_one, gain_two = gains[:1], gains[1:]
    table = tail[:, 2].reshape(devices, rows_held)[:, :micro].reshape(seqs).astype(jnp.int32)
    sent = pick_rows(table, held.reshape(seqs, 2 * CBLOCK, cols))
    fetched = lax.all_to_all(sent, ("dp", "tensor"), split_axis=0, concat_axis=0, tiled=True)
    fetched = fetched.reshape(chunks, 2, 2, CBLOCK, cols)

    meta = jnp.concatenate(
        [
            prefix[spot][None], spot[None].astype(jnp.int32),
            own_blocks[spot].reshape(-1), partner_blocks[spot].reshape(-1),
        ]
    )
    normed, qkv = project(x, gain_one, first_all)
    partial, partial_lse = attend(meta, qkv, own_k, own_v)
    context, lse = attend_other(meta, qkv, fetched, partial, partial_lse)
    mixed, normed_two = mix(x, context, gain_two, second_all)
    ffn_out, grad_normed_two, ffn_grads = ffn(normed_two, cotangent, second_all, width, hidden)
    share = functools.partial(lax.psum_scatter, axis_name="dp", scatter_dimension=0, tiled=True)
    ffn_share = share(ffn_grads)
    out, grad_mixed, branch, grad_context, gain_part_two = unmix(
        mixed, grad_normed_two, ffn_out, cotangent, gain_two, second_all
    )
    out = exchange(out.reshape(2, shard_len, width))
    dq, dk, dv = attend_back(meta, qkv, own_k, own_v, fetched, grad_context, context, lse)
    dq, out, ffn_share = lax.optimization_barrier((dq, out, ffn_share))
    grad_tokens, gain_sums, attn_share = finish(
        x, grad_mixed, normed, context, branch, dq, dk, dv, first_all, gain_one, gain_part_two, devices
    )
    grad_tokens = exchange(grad_tokens.reshape(2, shard_len, width)).astype(F32)
    g_out, g_value, g_key, g_query = jnp.split(attn_share, 4, axis=1)
    pieces = ffn_share.reshape(rows_held, hidden // HT, 3, HT).swapaxes(1, 2).reshape(rows_held, 3, hidden)
    got = swap(pieces[:, :, hidden_held:])
    total = pieces[:, :, :hidden_held].astype(F32) + got.astype(F32)
    g_gate, g_up, g_down = total[:, 0], total[:, 1], total[:, 2]
    return (
        out, grad_tokens, gain_sums[0], g_query, g_key, g_value, g_out.T, gain_sums[1], g_gate, g_up, g_down.T,
    )


def solution(mesh):
    in_specs = (
        P("dp", "tensor", None),
        P("dp"),
        P("dp", "tensor"),
        P("dp", "tensor"),
        P("dp", "tensor"),
        P("tensor", "dp"),
        P("dp"),
        P("dp", "tensor"),
        P("dp", "tensor"),
        P("tensor", "dp"),
        P("dp", None, "tensor"),
        P("dp", None, "tensor"),
        P("dp"),
        P("dp"),
        P("dp", None, None),
        P("dp", None, None),
        P("dp", "tensor", None),
    )
    out_specs = (
        P("dp", "tensor", None),
        P("dp", "tensor", None),
        P(),
        P("dp", "tensor"),
        P("dp", "tensor"),
        P("dp", "tensor"),
        P("tensor", "dp"),
        P(),
        P("dp", "tensor"),
        P("dp", "tensor"),
        P("tensor", "dp"),
    )
    whole = mesh.shape["tensor"] == 2 and mesh.shape["dp"] == CACHE_LEN // CBLOCK
    body = sequence_body if whole else tensor_body
    return jax.shard_map(body, mesh=mesh, in_specs=in_specs, out_specs=out_specs, check_vma=False)
```

```python
import functools

import jax
import jax.numpy as jnp
from jax import lax
from jax.experimental import pallas as pl
from jax.experimental.pallas import tpu as pltpu
from jax.sharding import PartitionSpec as P

HD = 128
L = 2048
CACHE_LEN = 1024
QBLOCK = 128
CBLOCK = 64
KR = 4
QROWS = 512


EPS = 1e-05
NEGATIVE = -1e30


def norm_rows(values, gain):
    scale_rows = lax.rsqrt(jnp.mean(values * values, axis=-1, keepdims=True) + EPS)
    return (values * scale_rows * gain, scale_rows)


def norm_back(grad_normed, values, scale_rows, gain):
    unit = values * scale_rows
    grad_unit = grad_normed * gain
    grad_values = scale_rows * (
        grad_unit - unit * jnp.mean(grad_unit * unit, axis=-1, keepdims=True)
    )
    return (grad_values, jnp.sum(grad_normed * unit, axis=0))


def inner_rows(left, right):
    return lax.dot_general(
        left, right, (((0,), (0,)), ((), ())), preferred_element_type=jnp.float32
    )


def outer_cols(left, right):
    return lax.dot_general(
        left, right, (((1,), (1,)), ((), ())), preferred_element_type=jnp.float32
    )


def memory_rows(cache_one, chosen, width):
    shaped = cache_one.reshape(CACHE_LEN // CBLOCK, CBLOCK, width)
    return jnp.take(shaped, chosen, axis=0)


def block_scores(query_block, keys_part, mem_part, first_row, limit):
    rows_here, heads_here, size = query_block.shape
    extent = keys_part.shape[0]
    local = jnp.einsum(
        "qhd,khd->hqk", query_block, keys_part, preferred_element_type=jnp.float32
    ) * size ** (-0.5)
    row_ids = first_row + jnp.arange(rows_here, dtype=jnp.int32)[:, None]
    key_ids = jnp.arange(extent, dtype=jnp.int32)[None, :]
    allowed = (key_ids <= row_ids) | (row_ids < limit) & (key_ids < limit)
    local = jnp.where(allowed[None], local, NEGATIVE)
    groups = mem_part.shape[0]
    grouped = query_block.reshape(groups, rows_here // groups, heads_here, size)
    remote = jnp.einsum(
        "bqhd,bkhd->hbqk", grouped, mem_part, preferred_element_type=jnp.float32
    ) * size ** (-0.5)
    return (local, remote.reshape(heads_here, rows_here, -1))


def attention_forward(query, keys, values, mem_keys, mem_values, limit):
    groups = QROWS // QBLOCK
    heads_here = query.shape[1]
    context_parts = []
    lse_parts = []
    for index in range(L // QROWS):
        first = index * QROWS
        extent = max(first + QROWS, L // 2)
        query_block = query[first : first + QROWS]
        mem_k = mem_keys[index * groups : (index + 1) * groups]
        mem_v = mem_values[index * groups : (index + 1) * groups]
        local, remote = block_scores(query_block, keys[:extent], mem_k, first, limit)
        top = jnp.maximum(jnp.max(local, axis=-1), jnp.max(remote, axis=-1))
        e_local = jnp.exp(local - top[..., None])
        e_remote = jnp.exp(remote - top[..., None])
        total = jnp.sum(e_local, axis=-1) + jnp.sum(e_remote, axis=-1)
        p_local = (e_local / total[..., None]).astype(jnp.bfloat16)
        p_remote = (
            (e_remote / total[..., None])
            .astype(jnp.bfloat16)
            .reshape(heads_here, groups, QBLOCK, -1)
        )
        part = jnp.einsum(
            "hqk,khd->qhd", p_local, values[:extent], preferred_element_type=jnp.float32
        )
        extra = jnp.einsum("hbqk,bkhd->bqhd", p_remote, mem_v, preferred_element_type=jnp.float32)
        context_parts.append(part + extra.reshape(part.shape))
        lse_parts.append(top + jnp.log(total))
    return (jnp.concatenate(context_parts, axis=0), lse_parts)


def attention_backward(query, keys, values, mem_keys, mem_values, limit, lse_parts, grad_context):
    groups = QROWS // QBLOCK
    length, heads_here, size = query.shape
    scale = size ** (-0.5)
    grad_query_parts = []
    grad_keys = jnp.zeros(query.shape, jnp.float32)
    grad_values = jnp.zeros(query.shape, jnp.float32)
    for index in range(L // QROWS):
        first = index * QROWS
        extent = max(first + QROWS, L // 2)
        query_block = query[first : first + QROWS]
        mem_k = mem_keys[index * groups : (index + 1) * groups]
        mem_v = mem_values[index * groups : (index + 1) * groups]
        local, remote = block_scores(query_block, keys[:extent], mem_k, first, limit)
        lse_block = lse_parts[index][..., None]
        p_local = jnp.exp(local - lse_block)
        p_remote = jnp.exp(remote - lse_block)
        grad_block = grad_context[first : first + QROWS]
        grouped_grad = grad_block.reshape(groups, QBLOCK, heads_here, size)
        dp_local = jnp.einsum(
            "qhd,khd->hqk", grad_block, values[:extent], preferred_element_type=jnp.float32
        )
        dp_remote = jnp.einsum(
            "bqhd,bkhd->hbqk", grouped_grad, mem_v, preferred_element_type=jnp.float32
        )
        dp_remote = dp_remote.reshape(heads_here, QROWS, -1)
        delta = jnp.sum(p_local * dp_local, axis=-1) + jnp.sum(p_remote * dp_remote, axis=-1)
        ds_local = (p_local * (dp_local - delta[..., None])).astype(jnp.bfloat16)
        ds_remote = (p_remote * (dp_remote - delta[..., None])).astype(jnp.bfloat16)
        ds_remote = ds_remote.reshape(heads_here, groups, QBLOCK, -1)
        dq_block = jnp.einsum(
            "hqk,khd->qhd", ds_local, keys[:extent], preferred_element_type=jnp.float32
        )
        dq_extra = jnp.einsum(
            "hbqk,bkhd->bqhd", ds_remote, mem_k, preferred_element_type=jnp.float32
        )
        grad_query_parts.append((dq_block + dq_extra.reshape(dq_block.shape)) * scale)
        dk_part = (
            jnp.einsum("hqk,qhd->khd", ds_local, query_block, preferred_element_type=jnp.float32)
            * scale
        )
        dv_part = jnp.einsum(
            "hqk,qhd->khd",
            p_local.astype(jnp.bfloat16),
            grad_block,
            preferred_element_type=jnp.float32,
        )
        grad_keys = grad_keys.at[:extent].add(dk_part)
        grad_values = grad_values.at[:extent].add(dv_part)
    return (jnp.concatenate(grad_query_parts, axis=0), grad_keys, grad_values)


def tensor_body(
    tokens,
    gain_attn,
    w_query,
    w_key,
    w_value,
    w_out,
    gain_ffn,
    w_gate,
    w_up,
    w_down,
    cache_keys,
    cache_values,
    prefix,
    partner,
    own_blocks,
    partner_blocks,
    grad_out,
):
    micro, shard_len, width = tokens.shape
    cols = w_query.shape[1]
    heads_local = cols // HD
    qblocks = L // QBLOCK
    mem_len = 2 * KR * CBLOCK
    piece_keys = lax.all_gather(cache_keys, "dp", axis=0, tiled=True)
    piece_values = lax.all_gather(cache_values, "dp", axis=0, tiled=True)
    count = piece_keys.shape[0]
    onehot = (partner[:, None] == jnp.arange(count, dtype=jnp.int32)[None, :]).astype(jnp.bfloat16)
    add_keys = jnp.einsum("mn,nkc->mkc", onehot, piece_keys, preferred_element_type=jnp.float32)
    add_values = jnp.einsum("mn,nkc->mkc", onehot, piece_values, preferred_element_type=jnp.float32)
    fetched_keys = add_keys.astype(jnp.bfloat16)
    fetched_values = add_values.astype(jnp.bfloat16)
    totals = (
        jnp.zeros((width, cols), jnp.float32),
        jnp.zeros((width, cols), jnp.float32),
        jnp.zeros((width, cols), jnp.float32),
        jnp.zeros((cols, width), jnp.float32),
        jnp.zeros((width, w_gate.shape[1]), jnp.float32),
        jnp.zeros((width, w_gate.shape[1]), jnp.float32),
        jnp.zeros((w_gate.shape[1], width), jnp.float32),
    )
    shares = tuple(
        (
            jnp.zeros(w.shape, jnp.float32)
            for w in (w_query, w_key, w_value, w_out, w_gate, w_up, w_down)
        )
    )
    gain_total_attn = jnp.zeros((width,), jnp.float32)
    gain_total_ffn = jnp.zeros((width,), jnp.float32)
    out_rows = []
    grad_rows = []
    for step in range(micro):
        fwd = (
            lax.all_gather(gain_attn, "dp", axis=0, tiled=True),
            lax.all_gather(w_query, "dp", axis=0, tiled=True),
            lax.all_gather(w_key, "dp", axis=0, tiled=True),
            lax.all_gather(w_value, "dp", axis=0, tiled=True),
            lax.all_gather(w_out, "dp", axis=1, tiled=True),
            lax.all_gather(gain_ffn, "dp", axis=0, tiled=True),
            lax.all_gather(w_gate, "dp", axis=0, tiled=True),
            lax.all_gather(w_up, "dp", axis=0, tiled=True),
            lax.all_gather(w_down, "dp", axis=1, tiled=True),
        )
        g_attn, wq_full, wk_full, wv_full, wo_full, g_ffn, wg_full, wu_full, wd_full = fwd
        limit = prefix[step]
        own_k = memory_rows(cache_keys[step], own_blocks[step], cols)
        par_k = memory_rows(fetched_keys[step], partner_blocks[step], cols)
        own_v = memory_rows(cache_values[step], own_blocks[step], cols)
        par_v = memory_rows(fetched_values[step], partner_blocks[step], cols)
        mem_keys = jnp.concatenate([own_k, par_k], axis=1).reshape(
            qblocks, mem_len, heads_local, HD
        )
        mem_values = jnp.concatenate([own_v, par_v], axis=1).reshape(
            qblocks, mem_len, heads_local, HD
        )
        token_rows = tokens[step].astype(jnp.float32)
        normed, scale_one = norm_rows(token_rows, g_attn.astype(jnp.float32))
        normed_all = lax.all_gather(normed.astype(jnp.bfloat16), "tensor", axis=0, tiled=True)
        query = (
            jnp.dot(normed_all, wq_full, preferred_element_type=jnp.float32)
            .astype(jnp.bfloat16)
            .reshape(L, heads_local, HD)
        )
        keys = (
            jnp.dot(normed_all, wk_full, preferred_element_type=jnp.float32)
            .astype(jnp.bfloat16)
            .reshape(L, heads_local, HD)
        )
        values = (
            jnp.dot(normed_all, wv_full, preferred_element_type=jnp.float32)
            .astype(jnp.bfloat16)
            .reshape(L, heads_local, HD)
        )
        context_full, lse_parts = attention_forward(
            query, keys, values, mem_keys, mem_values, limit
        )
        context = context_full.reshape(L, cols).astype(jnp.bfloat16)
        mixed = token_rows + lax.psum_scatter(
            jnp.dot(context, wo_full, preferred_element_type=jnp.float32),
            "tensor",
            scatter_dimension=0,
            tiled=True,
        )
        normed_two, scale_two = norm_rows(mixed, g_ffn.astype(jnp.float32))
        normed_two_all = lax.all_gather(
            normed_two.astype(jnp.bfloat16), "tensor", axis=0, tiled=True
        )
        gate = jnp.dot(normed_two_all, wg_full, preferred_element_type=jnp.float32)
        upward = jnp.dot(normed_two_all, wu_full, preferred_element_type=jnp.float32)
        sigma = jax.nn.sigmoid(gate)
        silu_gate = gate * sigma
        hidden = (silu_gate * upward).astype(jnp.bfloat16)
        out_rows.append(
            (
                mixed
                + lax.psum_scatter(
                    jnp.dot(hidden, wd_full, preferred_element_type=jnp.float32).astype(
                        jnp.bfloat16
                    ),
                    "tensor",
                    scatter_dimension=0,
                    tiled=True,
                ).astype(jnp.float32)
            ).astype(jnp.bfloat16)
        )
        bwd = (
            lax.all_gather(gain_attn, "dp", axis=0, tiled=True),
            lax.all_gather(w_query, "dp", axis=0, tiled=True),
            lax.all_gather(w_key, "dp", axis=0, tiled=True),
            lax.all_gather(w_value, "dp", axis=0, tiled=True),
            lax.all_gather(w_out, "dp", axis=1, tiled=True),
            lax.all_gather(gain_ffn, "dp", axis=0, tiled=True),
            lax.all_gather(w_gate, "dp", axis=0, tiled=True),
            lax.all_gather(w_up, "dp", axis=0, tiled=True),
            lax.all_gather(w_down, "dp", axis=1, tiled=True),
        )
        g_attn, wq_full, wk_full, wv_full, wo_full, g_ffn, wg_full, wu_full, wd_full = bwd
        grad_here = grad_out[step]
        grad_all = lax.all_gather(grad_here, "tensor", axis=0, tiled=True)
        d_down = inner_rows(hidden, grad_all)
        grad_hidden = outer_cols(grad_all, wd_full)
        grad_gate = (grad_hidden * upward * sigma * (1.0 + gate * (1.0 - sigma))).astype(
            jnp.bfloat16
        )
        grad_up = (grad_hidden * silu_gate).astype(jnp.bfloat16)
        d_gate = inner_rows(normed_two_all, grad_gate)
        d_up = inner_rows(normed_two_all, grad_up)
        grad_normed_two = lax.psum_scatter(
            outer_cols(grad_gate, wg_full) + outer_cols(grad_up, wu_full),
            "tensor",
            scatter_dimension=0,
            tiled=True,
        )
        grad_mixed_norm, gain_part_ffn = norm_back(
            grad_normed_two, mixed, scale_two, g_ffn.astype(jnp.float32)
        )
        grad_mixed = grad_here.astype(jnp.float32) + grad_mixed_norm
        branch_all = lax.all_gather(grad_mixed.astype(jnp.bfloat16), "tensor", axis=0, tiled=True)
        d_out = inner_rows(context, branch_all)
        grad_context = (
            outer_cols(branch_all, wo_full).astype(jnp.bfloat16).reshape(L, heads_local, HD)
        )
        grad_query, grad_keys, grad_values = attention_backward(
            query, keys, values, mem_keys, mem_values, limit, lse_parts, grad_context
        )
        grad_query = grad_query.reshape(L, cols).astype(jnp.bfloat16)
        grad_keys = grad_keys.reshape(L, cols).astype(jnp.bfloat16)
        grad_values = grad_values.reshape(L, cols).astype(jnp.bfloat16)
        d_query = inner_rows(normed_all, grad_query)
        d_key = inner_rows(normed_all, grad_keys)
        d_value = inner_rows(normed_all, grad_values)
        grad_normed = lax.psum_scatter(
            (
                outer_cols(grad_query, wq_full)
                + outer_cols(grad_keys, wk_full)
                + outer_cols(grad_values, wv_full)
            ).astype(jnp.bfloat16),
            "tensor",
            scatter_dimension=0,
            tiled=True,
        ).astype(jnp.float32)
        grad_token_norm, gain_part_attn = norm_back(
            grad_normed, token_rows, scale_one, g_attn.astype(jnp.float32)
        )
        grad_rows.append(grad_mixed + grad_token_norm)
        gain_total_attn = gain_total_attn + gain_part_attn
        gain_total_ffn = gain_total_ffn + gain_part_ffn
        totals = tuple(
            (
                held + fresh
                for held, fresh in zip(
                    totals, (d_query, d_key, d_value, d_out, d_gate, d_up, d_down)
                )
            )
        )
    shares = (
        lax.psum_scatter(
            totals[0].astype(jnp.bfloat16), "dp", scatter_dimension=0, tiled=True
        ).astype(jnp.float32),
        lax.psum_scatter(
            totals[1].astype(jnp.bfloat16), "dp", scatter_dimension=0, tiled=True
        ).astype(jnp.float32),
        lax.psum_scatter(
            totals[2].astype(jnp.bfloat16), "dp", scatter_dimension=0, tiled=True
        ).astype(jnp.float32),
        lax.psum_scatter(
            totals[3].astype(jnp.bfloat16), "dp", scatter_dimension=1, tiled=True
        ).astype(jnp.float32),
        lax.psum_scatter(
            totals[4].astype(jnp.bfloat16), "dp", scatter_dimension=0, tiled=True
        ).astype(jnp.float32),
        lax.psum_scatter(
            totals[5].astype(jnp.bfloat16), "dp", scatter_dimension=0, tiled=True
        ).astype(jnp.float32),
        lax.psum_scatter(
            totals[6].astype(jnp.bfloat16), "dp", scatter_dimension=1, tiled=True
        ).astype(jnp.float32),
    )
    gain_attn_sum, gain_ffn_sum = lax.psum((gain_total_attn, gain_total_ffn), ("dp", "tensor"))
    return (
        jnp.stack(out_rows, axis=0),
        jnp.stack(grad_rows, axis=0),
        gain_attn_sum,
        shares[0],
        shares[1],
        shares[2],
        shares[3],
        gain_ffn_sum,
        shares[4],
        shares[5],
        shares[6],
    )


TQ = 512
TK = 512
ROWS = 512
HT = 256
SCALE = HD**-0.5
EXP_SCALE = SCALE * 1.4426950408889634
LOG2E = 1.4426950408889634
NT = (((1,), (1,)), ((), ()))
TN = (((0,), (0,)), ((), ()))
F32 = jnp.float32
BF16 = jnp.bfloat16
MIB = 1 << 20


def mm(left, right, dims=(((1,), (0,)), ((), ()))):
    return lax.dot_general(left, right, dims, preferred_element_type=F32)


def fold_max(values):
    best = values[:, :HD]
    for i in range(1, values.shape[1] // HD):
        best = jnp.maximum(best, values[:, i * HD : (i + 1) * HD])
    return best


def fold_sum(values):
    total = values[:, :HD]
    for i in range(1, values.shape[1] // HD):
        total = total + values[:, i * HD : (i + 1) * HD]
    return total


def reach_mask(first, tile, limit):
    rows = first + lax.broadcasted_iota(jnp.int32, (TQ, 1), 0)
    keys = tile * TK + lax.broadcasted_iota(jnp.int32, (1, TK), 1)
    reach = jnp.where(rows < limit, jnp.maximum(rows, limit - 1), rows)
    return keys <= reach


def pick_own(meta, block, own, buf):
    for i in range(KR):
        c = meta[2 + block * KR + i]
        buf[pl.ds(i * CBLOCK, CBLOCK), :] = own[0, pl.ds(pl.multiple_of(c * CBLOCK, CBLOCK), CBLOCK), :]


def pick_other(meta, block, other, buf, start=0):
    for i in range(KR):
        d = meta[2 + (L // QBLOCK) * KR + block * KR + i]
        buf[pl.ds(start + i * CBLOCK, CBLOCK), :] = other[d, 0, 0]


def pick_blocks(meta, block, own, other, buf):
    pick_own(meta, block, own, buf)
    pick_other(meta, block, other, buf, KR * CBLOCK)


def attend_kernel(
    meta, q_ref, k_ref, v_ref, ok_ref, ov_ref, ctx_ref, lse_ref, kbuf, vbuf, sbuf, smem, *, pair
):
    step = pl.program_id(1)
    limit = meta[0]
    first = step * TQ
    free = jnp.where(first < limit, (limit + TK - 1) // TK, 0)
    tiles = jnp.maximum(step + 1, free)
    blocks = TQ // QBLOCK
    for b in range(blocks):
        pick_own(meta, step * blocks + b, ok_ref, kbuf.at[b])
        pick_own(meta, step * blocks + b, ov_ref, vbuf.at[b])
    state = []
    for h in range(pair):
        cs = pl.ds(h * HD, HD)
        best = []
        for b in range(blocks):
            s = mm(q_ref[pl.ds(b * QBLOCK, QBLOCK), cs], kbuf[b, :, cs], NT)
            smem[h, pl.ds(b * QBLOCK, QBLOCK), :] = s
            best.append(fold_max(s))
        state.append(jnp.concatenate(best, 0))

    def scores(tile, state, masked):
        ks = pl.ds(pl.multiple_of(tile * TK, TK), TK)
        if masked:
            allowed = reach_mask(first, tile, limit)
        new = []
        for h in range(pair):
            cs = pl.ds(h * HD, HD)
            s = mm(q_ref[:, cs], k_ref[ks, cs], NT)
            if masked:
                s = jnp.where(allowed, s, NEGATIVE)
            sbuf[h, tile] = s
            new.append(jnp.maximum(state[h], fold_max(s)))
        return tuple(new)

    state = lax.fori_loop(0, step, lambda tile, s: scores(tile, s, False), tuple(state))
    state = lax.fori_loop(step, tiles, lambda tile, s: scores(tile, s, True), state)
    tops = [jnp.max(s, axis=1, keepdims=True) for s in state]
    state = []
    for h in range(pair):
        cs = pl.ds(h * HD, HD)
        p = jnp.exp2((smem[h] - tops[h]) * EXP_SCALE)
        low = p.astype(BF16)
        parts = [mm(low[b * QBLOCK : (b + 1) * QBLOCK], vbuf[b, :, cs]) for b in range(blocks)]
        state.append((fold_sum(p), jnp.concatenate(parts, 0)))

    def weigh(tile, state):
        ks = pl.ds(pl.multiple_of(tile * TK, TK), TK)
        new = []
        for h in range(pair):
            total, acc = state[h]
            p = jnp.exp2((sbuf[h, tile] - tops[h]) * EXP_SCALE)
            new.append((total + fold_sum(p), acc + mm(p.astype(BF16), v_ref[ks, pl.ds(h * HD, HD)])))
        return tuple(new)

    state = lax.fori_loop(0, tiles, weigh, tuple(state))
    for h in range(pair):
        cs = pl.ds(h * HD, HD)
        total = jnp.sum(state[h][0], axis=1, keepdims=True)
        ctx_ref[:, cs] = state[h][1] / total
        lse_ref[:, cs] = jnp.broadcast_to(tops[h] * SCALE + jnp.log(total), (TQ, HD))


def attend_other_kernel(meta, q_ref, pk_ref, pv_ref, part_ref, plse_ref, ctx_ref, lse_ref, kbuf, vbuf, *, pair):
    step = pl.program_id(1)
    blocks = TQ // QBLOCK
    for b in range(blocks):
        pick_other(meta, step * blocks + b, pk_ref, kbuf.at[b])
        pick_other(meta, step * blocks + b, pv_ref, vbuf.at[b])
    for h in range(pair):
        cs = pl.ds(h * HD, HD)
        rows = [pl.ds(b * QBLOCK, QBLOCK) for b in range(blocks)]
        s = jnp.concatenate([mm(q_ref[rows[b], cs], kbuf[b, :, cs], NT) for b in range(blocks)], 0)
        before = plse_ref[:, cs]
        top = jnp.maximum(before, jnp.max(fold_max(s), axis=1, keepdims=True) * SCALE)
        keep = jnp.exp(before - top)
        p = jnp.exp2(s * EXP_SCALE - top[:, :1] * LOG2E)
        low = p.astype(BF16)
        more = jnp.concatenate(
            [mm(low[b * QBLOCK : (b + 1) * QBLOCK], vbuf[b, :, cs]) for b in range(blocks)], 0
        )
        total = keep + jnp.sum(fold_sum(p), axis=1, keepdims=True)
        ctx_ref[:, cs] = ((part_ref[:, cs] * keep + more) / total).astype(BF16)
        lse_ref[:, cs] = top + jnp.log(total)


def attend_back_kernel(
    meta, q_ref, k_ref, v_ref, ok_ref, ov_ref, pk_ref, pv_ref, do_ref, ctx_ref, lse_ref,
    dq_ref, dk_ref, dv_ref, kbuf, vbuf, dks, dvs, *, pair
):
    step = pl.program_id(1)
    limit = meta[0]
    first = step * TQ
    free = jnp.where(first < limit, (limit + TK - 1) // TK, 0)
    tiles = jnp.maximum(step + 1, free)
    blocks = TQ // QBLOCK

    @pl.when(step == 0)
    def _():
        dks[...] = jnp.zeros_like(dks)
        dvs[...] = jnp.zeros_like(dvs)

    for b in range(blocks):
        pick_blocks(meta, step * blocks + b, ok_ref, pk_ref, kbuf.at[b])
        pick_blocks(meta, step * blocks + b, ov_ref, pv_ref, vbuf.at[b])
    state = []
    aux = []
    for h in range(pair):
        cs = pl.ds(h * HD, HD)
        delta = jnp.sum(do_ref[:, cs].astype(F32) * ctx_ref[:, cs].astype(F32), axis=1, keepdims=True)
        lse2 = lse_ref[:, cs][:, :1] * LOG2E
        aux.append((lse2, delta))
        parts = []
        for b in range(blocks):
            rs = pl.ds(b * QBLOCK, QBLOCK)
            s = mm(q_ref[rs, cs], kbuf[b, :, cs], NT)
            p = jnp.exp2(s * EXP_SCALE - lse2[b * QBLOCK : (b + 1) * QBLOCK])
            dp = mm(do_ref[rs, cs], vbuf[b, :, cs], NT)
            ds = (p * (dp - delta[b * QBLOCK : (b + 1) * QBLOCK])).astype(BF16)
            parts.append(mm(ds, kbuf[b, :, cs]))
        state.append(jnp.concatenate(parts, 0))

    def grads(tile, state, masked):
        ks = pl.ds(pl.multiple_of(tile * TK, TK), TK)
        if masked:
            allowed = reach_mask(first, tile, limit)
        new = []
        for h in range(pair):
            cs = pl.ds(h * HD, HD)
            lse2, delta = aux[h]
            s = mm(q_ref[:, cs], k_ref[ks, cs], NT)
            p = jnp.exp2(s * EXP_SCALE - lse2)
            if masked:
                p = jnp.where(allowed, p, 0.0)
            dp = mm(do_ref[:, cs], v_ref[ks, cs], NT)
            ds = (p * (dp - delta)).astype(BF16)
            dvs[ks, cs] += mm(p.astype(BF16), do_ref[:, cs], TN)
            dks[ks, cs] += mm(ds, q_ref[:, cs], TN)
            new.append(state[h] + mm(ds, k_ref[ks, cs]))
        return tuple(new)

    state = lax.fori_loop(0, step, lambda tile, s: grads(tile, s, False), tuple(state))
    state = lax.fori_loop(step, tiles, lambda tile, s: grads(tile, s, True), state)
    for h in range(pair):
        dq_ref[:, pl.ds(h * HD, HD)] = (state[h] * SCALE).astype(BF16)

    @pl.when(step == L // TQ - 1)
    def _():
        dk_ref[...] = (dks[...] * SCALE).astype(BF16)
        dv_ref[...] = dvs[...].astype(BF16)


def attention_specs(heads, pair):
    wide = pair * HD
    per = heads // 2 // pair
    groups = heads // pair
    return [
        pl.BlockSpec((TQ, wide), lambda h, i, meta: (i, h)),
        pl.BlockSpec((L, wide), lambda h, i, meta: (0, groups + h)),
        pl.BlockSpec((L, wide), lambda h, i, meta: (0, 2 * groups + h)),
        pl.BlockSpec((1, CACHE_LEN, wide), lambda h, i, meta: ((h // per) ^ meta[1], 0, h % per)),
        pl.BlockSpec((1, CACHE_LEN, wide), lambda h, i, meta: ((h // per) ^ meta[1], 0, h % per)),
        pl.BlockSpec(
            (CACHE_LEN // CBLOCK, 1, 1, CBLOCK, wide),
            lambda h, i, meta: (0, (h // per) ^ meta[1], 0, 0, h % per),
        ),
        pl.BlockSpec(
            (CACHE_LEN // CBLOCK, 1, 1, CBLOCK, wide),
            lambda h, i, meta: (0, (h // per) ^ meta[1], 1, 0, h % per),
        ),
    ]


def attend(meta, qkv, own_k, own_v, pair=2):
    width = qkv.shape[1] // 3
    heads = width // HD
    wide = pair * HD
    row = pl.BlockSpec((TQ, wide), lambda h, i, meta: (i, h))
    area = L * 1600 * width
    return pl.pallas_call(
        functools.partial(attend_kernel, pair=pair),
        grid_spec=pltpu.PrefetchScalarGridSpec(
            num_scalar_prefetch=1,
            grid=(heads // pair, L // TQ),
            in_specs=attention_specs(heads, pair)[:5],
            out_specs=[row, row],
            scratch_shapes=[pltpu.VMEM((TQ // QBLOCK, KR * CBLOCK, wide), BF16)] * 2
            + [pltpu.VMEM((pair, L // TK, TQ, TK), F32), pltpu.VMEM((pair, TQ, KR * CBLOCK), F32)],
        ),
        out_shape=[jax.ShapeDtypeStruct((L, width), F32)] * 2,
        compiler_params=pltpu.CompilerParams(vmem_limit_bytes=40 * MIB),
        cost_estimate=pl.CostEstimate(flops=12 * area, bytes_accessed=30 * MIB, transcendentals=area // HD),
        name="attend",
    )(meta, qkv, qkv, qkv, own_k, own_v)


def attend_other(meta, qkv, fetched, partial, lse, pair=4):
    width = qkv.shape[1] // 3
    heads = width // HD
    wide = pair * HD
    row = pl.BlockSpec((TQ, wide), lambda h, i, meta: (i, h))
    specs = attention_specs(heads, pair)
    return pl.pallas_call(
        functools.partial(attend_other_kernel, pair=pair),
        grid_spec=pltpu.PrefetchScalarGridSpec(
            num_scalar_prefetch=1,
            grid=(heads // pair, L // TQ),
            in_specs=[specs[0], specs[5], specs[6], row, row],
            out_specs=[row, row],
            scratch_shapes=[pltpu.VMEM((TQ // QBLOCK, KR * CBLOCK, wide), BF16)] * 2,
        ),
        out_shape=[jax.ShapeDtypeStruct((L, width), BF16), jax.ShapeDtypeStruct((L, width), F32)],
        compiler_params=pltpu.CompilerParams(vmem_limit_bytes=40 * MIB),
        cost_estimate=pl.CostEstimate(
            flops=4 * L * 256 * width, bytes_accessed=30 * MIB, transcendentals=L * 256 * heads
        ),
        name="attend_other",
    )(meta, qkv, fetched, fetched, partial, lse)


def attend_back(meta, qkv, own_k, own_v, fetched, grad_context, context, lse, pair=2):
    width = context.shape[1]
    heads = width // HD
    wide = pair * HD
    row = pl.BlockSpec((TQ, wide), lambda h, i, meta: (i, h))
    col = pl.BlockSpec((L, wide), lambda h, i, meta: (0, h))
    area = L * 1900 * width
    return pl.pallas_call(
        functools.partial(attend_back_kernel, pair=pair),
        grid_spec=pltpu.PrefetchScalarGridSpec(
            num_scalar_prefetch=1,
            grid=(heads // pair, L // TQ),
            in_specs=attention_specs(heads, pair) + [row, row, row],
            out_specs=[row, col, col],
            scratch_shapes=[pltpu.VMEM((TQ // QBLOCK, 2 * KR * CBLOCK, wide), BF16)] * 2
            + [pltpu.VMEM((L, wide), F32)] * 2,
        ),
        out_shape=[jax.ShapeDtypeStruct((L, width), BF16)] * 3,
        compiler_params=pltpu.CompilerParams(vmem_limit_bytes=48 * MIB),
        cost_estimate=pl.CostEstimate(flops=12 * area, bytes_accessed=40 * MIB, transcendentals=area // HD),
        name="attend_back",
    )(meta, qkv, qkv, qkv, own_k, own_v, fetched, fetched, grad_context, context, lse)


def project_kernel(x_ref, gain_ref, w_ref, normed_ref, qkv_ref):
    rows = x_ref[...].astype(F32)
    scale = lax.rsqrt(jnp.mean(rows * rows, axis=1, keepdims=True) + EPS)
    normed_ref[...] = (rows * scale * gain_ref[...]).astype(BF16)
    left = normed_ref[...]

    def chunk(c, carry):
        cs = pl.ds(pl.multiple_of(c * 512, 512), 512)
        qkv_ref[:, cs] = mm(left, w_ref[:, cs]).astype(BF16)
        return carry

    lax.fori_loop(0, qkv_ref.shape[1] // 512, chunk, 0)


def project(x, gain, weights):
    width = x.shape[1]
    cols = 3 * width
    row = lambda n: pl.BlockSpec((ROWS, n), lambda i: (i, 0))
    whole = lambda n: pl.BlockSpec((width, n), lambda i: (0, 0))
    return pl.pallas_call(
        project_kernel,
        grid=(L // ROWS,),
        in_specs=[row(width), pl.BlockSpec((1, width), lambda i: (0, 0)), whole(cols)],
        out_specs=[row(width), row(cols)],
        out_shape=[jax.ShapeDtypeStruct((L, width), BF16), jax.ShapeDtypeStruct((L, cols), BF16)],
        compiler_params=pltpu.CompilerParams(vmem_limit_bytes=40 * MIB),
        cost_estimate=pl.CostEstimate(flops=2 * L * width * cols, bytes_accessed=26 * MIB, transcendentals=0),
        name="project",
    )(x, gain, weights)


def mix_kernel(x_ref, ctx_ref, gain_ref, w_ref, mixed_ref, normed_ref):
    mixed = x_ref[...].astype(F32) + mm(ctx_ref[...], w_ref[...], NT)
    mixed_ref[...] = mixed
    scale = lax.rsqrt(jnp.mean(mixed * mixed, axis=1, keepdims=True) + EPS)
    normed_ref[...] = (mixed * scale * gain_ref[...]).astype(BF16)


def mix(x, context, gain, weights):
    width = x.shape[1]
    row = pl.BlockSpec((ROWS, width), lambda i: (i, 0))
    return pl.pallas_call(
        mix_kernel,
        grid=(L // ROWS,),
        in_specs=[row, row, pl.BlockSpec((1, width), lambda i: (0, 0)), pl.BlockSpec((width, width), lambda i: (0, 0))],
        out_specs=[row, row],
        out_shape=[jax.ShapeDtypeStruct((L, width), F32), jax.ShapeDtypeStruct((L, width), BF16)],
        compiler_params=pltpu.CompilerParams(vmem_limit_bytes=32 * MIB),
        cost_estimate=pl.CostEstimate(flops=2 * L * width * width, bytes_accessed=22 * MIB, transcendentals=0),
        name="mix",
    )(x, context, gain, weights)


RING = 8
RIGHT = RING // 2
LEFT = RING - 1 - RIGHT


def ring_place(p):
    y = p // 4
    return (p + y * (7 - 2 * p)) * 2 + y


def meet(devices, me, spot):
    barrier = pltpu.get_barrier_semaphore()
    for d in range(1, devices):
        pl.semaphore_signal(
            barrier, inc=1, device_id=((me + d) % devices, spot), device_id_type=pl.DeviceIdType.MESH
        )
    pl.semaphore_signal(barrier, inc=1, device_id=(me, 1 - spot), device_id_type=pl.DeviceIdType.MESH)
    pl.semaphore_wait(barrier, devices)


def remote(src, dst, send, recv, device):
    return pltpu.make_async_remote_copy(
        src_ref=src, dst_ref=dst, send_sem=send, recv_sem=recv, device_id=device, device_id_type=pl.DeviceIdType.MESH
    )


def ffn_kernel(
    n_ref, g_ref, wg0, wg1, wu0, wu1, wd0, wd1, out_ref, gn_ref, share_ref,
    acc, ag, au, ad, part, got, passed, land, pair_send, pair_recv, x_send, x_recv, *, devices,
):
    tile = pl.program_id(0)
    tiles = pl.num_programs(0)
    me = lax.axis_index("dp")
    spot = lax.axis_index("tensor")
    core = me % 2
    pair = (me + 1 - 2 * core, spot)
    peer = (me, 1 - spot)
    side = HT // 2

    @pl.when(tile == 0)
    def _():
        barrier = pltpu.get_barrier_semaphore()
        for device in (pair, peer):
            pl.semaphore_signal(barrier, inc=1, device_id=device, device_id_type=pl.DeviceIdType.MESH)
        pl.semaphore_wait(barrier, 2)
        acc[...] = jnp.zeros_like(acc)
        gn_ref[...] = jnp.zeros_like(gn_ref)

    def to_pair(k):
        return remote(part.at[k % 2, :, 1 - core], got.at[k], pair_send.at[k], pair_recv.at[k], pair)

    def to_peer(k):
        return remote(passed.at[k % 2], land.at[k], x_send.at[k], x_recv.at[k], peer)

    def join(k):
        to_pair(k).wait()

        @pl.when(k >= 2)
        def _():
            to_peer(k - 2).wait_send()

        def one(b, carry):
            total = got[k, b].astype(F32) + part[k % 2, b, core].astype(F32)
            low = total.astype(BF16)
            for m in range(3):
                passed[k % 2, b, :, m * side : (m + 1) * side] = low[:, m * HT + side : (m + 1) * HT]
                got[k, b, :, m * side : (m + 1) * side] = low[:, m * HT : m * HT + side]
            return carry

        lax.fori_loop(0, part.shape[1], one, 0)
        to_peer(k).start()

    def settle(k):
        to_peer(k).wait_recv()

        def one(b, carry):
            total = got[k, b, :, : 3 * side].astype(F32) + land[k, b].astype(F32)
            rs = pl.ds(pl.multiple_of(b * part.shape[3], part.shape[3]), part.shape[3])
            share_ref[rs, pl.ds(pl.multiple_of(k * 3 * side, 3 * side), 3 * side)] = total.astype(BF16)
            return carry

        lax.fori_loop(0, part.shape[1], one, 0)

    ag[...] = jnp.zeros_like(ag)
    au[...] = jnp.zeros_like(au)
    ad[...] = jnp.zeros_like(ad)
    wg = jnp.concatenate([wg0[...], wg1[...]], axis=1)
    wu = jnp.concatenate([wu0[...], wu1[...]], axis=1)
    wd = jnp.concatenate([wd0[...], wd1[...]], axis=1)

    def chunk(r, carry):
        rs = pl.ds(pl.multiple_of(r * ROWS, ROWS), ROWS)
        rows = n_ref[rs, :]
        cotangent = g_ref[rs, :]
        gate = mm(rows, wg)
        up = mm(rows, wu)
        grad_hidden = mm(cotangent, wd)
        sigma = 1.0 / (1.0 + jnp.exp(-gate))
        silu = gate * sigma
        hidden = (silu * up).astype(BF16)
        grad_gate = (grad_hidden * up * (sigma * (1.0 + gate * (1.0 - sigma)))).astype(BF16)
        grad_up = (grad_hidden * silu).astype(BF16)
        acc[rs, :] += mm(hidden, wd, NT)
        gn_ref[rs, :] += mm(grad_gate, wg, NT) + mm(grad_up, wu, NT)
        ag[...] += mm(rows, grad_gate, TN)
        au[...] += mm(rows, grad_up, TN)
        ad[...] += mm(cotangent, hidden, TN)
        return carry

    lax.fori_loop(0, L // ROWS, chunk, 0)
    for m, held in enumerate((ag, au, ad)):
        part[tile % 2, :, :, :, m * HT : (m + 1) * HT] = held[...].astype(BF16).reshape(part.shape[1:4] + (HT,))
    to_pair(tile).start()

    @pl.when(tile > 0)
    def _():
        join(tile - 1)

    @pl.when(tile > 1)
    def _():
        settle(tile - 2)

    @pl.when(tile == tiles - 1)
    def _():
        join(tile)
        settle(tile - 1)
        out_ref[...] = acc[...].astype(BF16)
        settle(tile)
        to_peer(tile - 1).wait_send()
        to_peer(tile).wait_send()


def ffn(normed, cotangent, weights, width, hidden, devices):
    once = pl.Buffered(1)
    tiles = hidden // HT
    side = HT // 2
    rows = width // devices
    chips = devices // 2
    lead = width // side
    part = lambda k: pl.BlockSpec((width, side), lambda j: (0, lead + k * tiles + j))
    whole = pl.BlockSpec((L, width), lambda j: (0, 0), pipeline_mode=once)
    dma = pltpu.SemaphoreType.DMA
    return pl.pallas_call(
        functools.partial(ffn_kernel, devices=devices),
        grid=(tiles,),
        in_specs=[whole, whole] + [part(k) for k in range(6)],
        out_specs=[
            whole, whole, pl.BlockSpec((width // 2, 3 * hidden // 2), lambda j: (0, 0), pipeline_mode=once)
        ],
        out_shape=[
            jax.ShapeDtypeStruct((L, width), BF16),
            jax.ShapeDtypeStruct((L, width), F32),
            jax.ShapeDtypeStruct((width // 2, 3 * hidden // 2), BF16),
        ],
        scratch_shapes=[pltpu.VMEM((L, width), F32)]
        + [pltpu.VMEM((width, HT), F32)] * 3
        + [
            pltpu.VMEM((2, chips, 2, rows, 3 * HT), BF16),
            pltpu.VMEM((tiles, chips, rows, 3 * HT), BF16),
            pltpu.VMEM((2, chips, rows, 3 * side), BF16),
            pltpu.VMEM((tiles, chips, rows, 3 * side), BF16),
            dma((tiles,)), dma((tiles,)), dma((tiles,)), dma((tiles,)),
        ],
        compiler_params=pltpu.CompilerParams(collective_id=2, has_side_effects=True, vmem_limit_bytes=61 * MIB),
        cost_estimate=pl.CostEstimate(
            flops=18 * L * width * hidden, bytes_accessed=60 * MIB, transcendentals=L * hidden
        ),
        name="ffn",
    )(normed, cotangent, *([weights] * 6))


def unmix_kernel(mixed_ref, gn_ref, ffn_ref, g_ref, gain_ref, w_ref, out_ref, gm_ref, br_ref, gc_ref, gg_ref):
    mixed = mixed_ref[...]
    grad = gn_ref[...]
    scale = lax.rsqrt(jnp.mean(mixed * mixed, axis=1, keepdims=True) + EPS)
    unit = mixed * scale
    inner = grad * gain_ref[...]
    grad_mixed = g_ref[...].astype(F32) + scale * (inner - unit * jnp.mean(inner * unit, axis=1, keepdims=True))
    out_ref[...] = (mixed + ffn_ref[...].astype(F32)).astype(BF16)
    gm_ref[...] = grad_mixed
    branch = grad_mixed.astype(BF16)
    br_ref[...] = branch
    gc_ref[...] = mm(branch, w_ref[...]).astype(BF16)

    @pl.when(pl.program_id(0) == 0)
    def _():
        gg_ref[...] = jnp.zeros_like(gg_ref)

    gg_ref[...] += jnp.sum(grad * unit, axis=0, keepdims=True)


def unmix(mixed, grad_normed, ffn_out, cotangent, gain, weights):
    width = mixed.shape[1]
    rows = ROWS // 2
    row = pl.BlockSpec((rows, width), lambda i: (i, 0))
    one = pl.BlockSpec((1, width), lambda i: (0, 0))
    return pl.pallas_call(
        unmix_kernel,
        grid=(L // rows,),
        in_specs=[row, row, row, row, one, pl.BlockSpec((width, width), lambda i: (0, 0))],
        out_specs=[row, row, row, row, one],
        out_shape=[
            jax.ShapeDtypeStruct((L, width), BF16),
            jax.ShapeDtypeStruct((L, width), F32),
            jax.ShapeDtypeStruct((L, width), BF16),
            jax.ShapeDtypeStruct((L, width), BF16),
            jax.ShapeDtypeStruct((1, width), F32),
        ],
        compiler_params=pltpu.CompilerParams(vmem_limit_bytes=40 * MIB),
        cost_estimate=pl.CostEstimate(flops=2 * L * width * width, bytes_accessed=46 * MIB, transcendentals=0),
        name="unmix",
    )(mixed, grad_normed, ffn_out, cotangent, gain, weights)


FT = 256


def finish_kernel(
    x_ref, gm_ref, n_ref, ctx_ref, br_ref, dq_ref, dk_ref, dv_ref, w_ref, gain_ref, gain_two_ref,
    gt_ref, sums_ref, share_ref,
    n_buf, ctx_buf, br_buf, dq_buf, dk_buf, dv_buf, w_buf, x_buf, gm_buf, gt_buf,
    part, got, land, across, gains, gain_land,
    load_sem, x_sem, gm_sem, gt_sem, gt_recv, pair_send, pair_recv, ring_send, ring_recv, x_send, x_recv, g_send, g_recv,
    *, devices,
):
    me = lax.axis_index("dp")
    spot = lax.axis_index("tensor")
    core = me % 2
    z, y = me // 4, (me // 2) % 2
    place = z + y * (7 - 2 * z)
    width = n_buf.shape[1]
    half = width // 2
    rows = part.shape[2]
    loads = [
        pltpu.make_async_copy(src, dst, load_sem.at[i])
        for i, (src, dst) in enumerate(
            [
                (ctx_ref, ctx_buf), (br_ref, br_buf), (n_ref, n_buf), (dv_ref, dv_buf),
                (dk_ref, dk_buf), (dq_ref, dq_buf), (w_ref.at[:, pl.ds(0, 3 * width)], w_buf),
            ]
        )
    ]
    for copy in loads:
        copy.start()
    meet(devices, me, spot)

    def tile_in(t, slot):
        rs = pl.ds(pl.multiple_of(t * FT, FT), FT)
        return [
            pltpu.make_async_copy(x_ref.at[rs, :], x_buf.at[slot], x_sem.at[slot]),
            pltpu.make_async_copy(gm_ref.at[rs, :], gm_buf.at[slot], gm_sem.at[slot]),
        ]

    held = L // FT // 2

    def give(k, slot):
        rs = pl.ds(pl.multiple_of(k * FT, FT), FT)
        return remote(
            gt_buf.at[slot], gt_ref.at[spot, rs, :], gt_sem.at[slot], gt_recv.at[k], (me, 1 - spot)
        )

    def keep(k, slot):
        rs = pl.ds(pl.multiple_of(k * FT, FT), FT)
        return pltpu.make_async_copy(gt_buf.at[slot], gt_ref.at[spot, rs, :], gt_sem.at[slot])

    def tile_of(k):
        return (k + held * (1 - spot)) % (2 * held)

    for copy in tile_in(tile_of(0), 0):
        copy.start()

    pair = (me + 1 - 2 * core, spot)

    def to_pair(m):
        cs = pl.ds(m * width, width)
        return remote(part.at[:, 1 - core, :, cs], got.at[:, :, cs], pair_send.at[m], pair_recv.at[m], pair)

    def product(m, left, right):
        def chunk(c, carry):
            cs = pl.ds(pl.multiple_of(c * half, half), half)
            value = mm(left[...], right[:, cs], TN).astype(BF16)
            part[:, :, :, pl.ds(pl.multiple_of(m * width + c * half, half), half)] = value.reshape(
                part.shape[0], 2, rows, half
            )
            return carry

        lax.fori_loop(0, 2, chunk, 0)
        to_pair(m).start()

    def join(m):
        to_pair(m).wait_recv()
        cs = pl.ds(m * width, width)

        def one(b, carry):
            got[b, :, cs] = (got[b, :, cs].astype(F32) + part[b, core, :, cs].astype(F32)).astype(BF16)
            return carry

        lax.fori_loop(0, part.shape[0], one, 0)

    span = 2 * width
    neighbours = [(place + 1) % RING, (place + RING - 1) % RING]

    def held_block(direction, s):
        p = (place + 2 * RING - 1 - s) % RING if direction == 0 else (place + 1 + s) % RING
        return got.at[ring_place(p), :, pl.ds(direction * span, span)]

    def hop(direction, s):
        to = ring_place(neighbours[direction]) * 2 + core
        return remote(
            held_block(direction, s), land.at[direction, s],
            ring_send.at[direction, s], ring_recv.at[direction, s], (to, spot),
        )

    def advance(direction, s, more=True):
        hop(direction, s).wait_recv()
        block = held_block(direction, s + 1)
        block[...] = (block[...].astype(F32) + land[direction, s].astype(F32)).astype(BF16)
        if more:
            hop(direction, s + 1).start()

    def finish_rows(t, slot, k):
        for copy in tile_in(t, slot):
            copy.wait()
        rs = pl.ds(pl.multiple_of(t * FT, FT), FT)
        grad = mm(dq_buf[rs, :], w_buf[:, :width], NT)
        grad += mm(dk_buf[rs, :], w_buf[:, width : 2 * width], NT)
        grad += mm(dv_buf[rs, :], w_buf[:, 2 * width :], NT)
        values = x_buf[slot].astype(F32)
        scale = lax.rsqrt(jnp.mean(values * values, axis=1, keepdims=True) + EPS)
        unit = values * scale
        inner = grad * gain_ref[...]
        back = scale * (inner - unit * jnp.mean(inner * unit, axis=1, keepdims=True))
        gt_buf[k] = (gm_buf[slot] + back).astype(BF16)
        gains[:1, :] += jnp.sum(grad * unit, axis=0, keepdims=True)

    for i in (0, 1):
        loads[i].wait()
    product(0, br_buf, ctx_buf)
    for i in (2, 3):
        loads[i].wait()
    product(1, n_buf, dv_buf)
    join(0)
    join(1)
    hop(0, 0).start()
    loads[4].wait()
    product(2, n_buf, dk_buf)
    advance(0, 0)
    loads[5].wait()
    product(3, n_buf, dq_buf)
    advance(0, 1)
    join(2)
    join(3)
    hop(1, 0).start()
    loads[6].wait()
    gains[:1, :] = jnp.zeros((1, width), F32)
    gains[1:, :] = gain_two_ref[...]

    def sweep(i, carry):
        for slot in (0, 1):
            k = 2 * i + slot
            if slot == 0:
                for copy in tile_in(tile_of(k + 1), 1):
                    copy.start()
            else:

                @pl.when(i < 3)
                def _():
                    for copy in tile_in(tile_of(k + 1), 0):
                        copy.start()

            finish_rows(tile_of(k), slot, k)

            @pl.when(i < 2)
            def _():
                give(k, k).start()

            @pl.when(i >= 2)
            def _():
                keep(k - held, k).start()

        advance(0, i + 2)
        advance(1, i)
        return carry

    lax.fori_loop(0, held, sweep, 0)

    partners = [
        (me + 1 - 2 * core, spot),
        (me + 2 - 4 * y, spot),
        (me + 4 - 8 * (z % 2), spot),
        (me + 8 - 16 * (z // 2), spot),
        (me, 1 - spot),
    ]

    def add_gains(r):
        return remote(gains, gain_land.at[r], g_send.at[r], g_recv.at[r], partners[r])

    def gain_round(r):
        add_gains(r).wait()
        gains[...] = gains[...] + gain_land[r]
        if r < 4:
            add_gains(r + 1).start()

    own = ring_place(place)
    peer = (me, 1 - spot)

    def over(m):
        return remote(
            got.at[own, :, pl.ds(m * width + half, half)], across.at[:, pl.ds(m * half, half)],
            x_send.at[m], x_recv.at[m], peer,
        )

    add_gains(0).start()
    advance(0, 6, False)
    over(0).start()
    over(1).start()
    gain_round(0)
    advance(1, 4)
    gain_round(1)
    gain_round(2)
    advance(1, 5)
    gain_round(3)
    gain_round(4)
    advance(1, 6, False)
    over(2).start()
    over(3).start()
    sums_ref[...] = gains[...]
    for m in range(4):
        over(m).wait_recv()
        cs = pl.ds(m * half, half)
        share_ref[:, cs] = got[own, :, pl.ds(m * width, half)].astype(F32) + across[:, cs].astype(F32)
    for m in range(4):
        over(m).wait_send()
        to_pair(m).wait_send()
    for s in range(RING - 1):
        hop(0, s).wait_send()
        hop(1, s).wait_send()
    for k in range(held):
        give(k, k).wait()
        keep(k, k + held).wait()


def finish(x, grad_mixed, normed, context, branch, dq, dk, dv, weights, gain, gain_two_part, devices):
    width = x.shape[1]
    rows = width // devices
    anywhere = pl.BlockSpec(memory_space=pltpu.HBM)
    vmem = pl.BlockSpec(memory_space=pltpu.VMEM)
    dma = pltpu.SemaphoreType.DMA
    whole = pltpu.VMEM((L, width), BF16)
    return pl.pallas_call(
        functools.partial(finish_kernel, devices=devices),
        in_specs=[anywhere] * 9 + [vmem] * 2,
        out_specs=[anywhere, vmem, vmem],
        out_shape=[
            jax.ShapeDtypeStruct((2, L // 2, width), BF16),
            jax.ShapeDtypeStruct((2, width), F32),
            jax.ShapeDtypeStruct((rows, 2 * width), F32),
        ],
        scratch_shapes=[
            whole, whole, whole, whole, whole, whole, pltpu.VMEM((width, 3 * width), BF16),
            pltpu.VMEM((2, FT, width), BF16), pltpu.VMEM((2, FT, width), F32), pltpu.VMEM((L // FT, FT, width), BF16),
            pltpu.VMEM((RING, 2, rows, 4 * width), BF16),
            pltpu.VMEM((RING, rows, 4 * width), BF16),
            pltpu.VMEM((2, RING - 1, rows, 2 * width), BF16),
            pltpu.VMEM((rows, 2 * width), BF16),
            pltpu.VMEM((2, width), F32), pltpu.VMEM((5, 2, width), F32),
            dma((7,)), dma((2,)), dma((2,)), dma((2 * (L // FT // 2),)), dma((L // FT // 2,)), dma((4,)), dma((4,)),
            dma((2, RING - 1)), dma((2, RING - 1)), dma((4,)), dma((4,)), dma((5,)), dma((5,)),
        ],
        compiler_params=pltpu.CompilerParams(collective_id=1, has_side_effects=True, vmem_limit_bytes=60 * MIB),
        cost_estimate=pl.CostEstimate(flops=14 * L * width * width, bytes_accessed=80 * MIB, transcendentals=0),
        name="finish",
    )(x, grad_mixed, normed, context, branch, dq, dk, dv, weights, gain, gain_two_part)


def pick_kernel(table, held_ref, sent_ref, sems):
    def copy(i):
        return pltpu.make_async_copy(held_ref.at[table[i]], sent_ref.at[i], sems.at[i])

    for i in range(sent_ref.shape[0]):
        copy(i).start()
    for i in range(sent_ref.shape[0]):
        copy(i).wait()


def pick_rows(table, held):
    count = held.shape[0]
    return pl.pallas_call(
        pick_kernel,
        grid_spec=pltpu.PrefetchScalarGridSpec(
            num_scalar_prefetch=1,
            grid=(),
            in_specs=[pl.BlockSpec(memory_space=pl.ANY)],
            out_specs=pl.BlockSpec(memory_space=pltpu.VMEM),
            scratch_shapes=[pltpu.SemaphoreType.DMA((count,))],
        ),
        out_shape=jax.ShapeDtypeStruct(held.shape, held.dtype),
        compiler_params=pltpu.CompilerParams(vmem_limit_bytes=16 * MIB),
        cost_estimate=pl.CostEstimate(flops=0, bytes_accessed=2 * held.size * 2, transcendentals=0),
        name="pick_rows",
    )(table, held)


def spread_kernel(
    tok_ref, ck_ref, cv_ref, small_ref, extra_ref, big_ref,
    x_ref, ok_ref, ov_ref, held_ref, first_ref, second_ref,
    tok_buf, k_buf, v_buf, local_sem, x_send, x_recv, all_send, all_recv, ring_send, ring_recv, pair_send, pair_recv,
):
    me = lax.axis_index("dp")
    spot = lax.axis_index("tensor")
    peer = 1 - spot
    devices = held_ref.shape[0]
    rows, cols = small_ref.shape[0], small_ref.shape[1] // 3
    core = me % 2
    z, y = me // 4, (me // 2) % 2
    place = z + y * (7 - 2 * z)

    def at_place(p):
        yy = p // 4
        return (p + yy * (7 - 2 * p)) * 4 + yy * 2

    def target(dp, tensor):
        return (dp, tensor)

    barrier = pltpu.get_barrier_semaphore()
    for d in range(1, devices):
        pl.semaphore_signal(barrier, inc=1, device_id=target((me + d) % devices, spot), device_id_type=pl.DeviceIdType.MESH)
    pl.semaphore_signal(barrier, inc=1, device_id=target(me, peer), device_id_type=pl.DeviceIdType.MESH)
    pl.semaphore_wait(barrier, devices)

    def remote(src, dst, send, recv, device):
        return pltpu.make_async_remote_copy(
            src_ref=src, dst_ref=dst, send_sem=send, recv_sem=recv,
            device_id=device, device_id_type=pl.DeviceIdType.MESH,
        )

    mine = pl.multiple_of(me * rows, rows)
    across = target(me, peer)
    weight_copies = []
    for i in range(3):
        weight_copies.append(
            remote(
                small_ref.at[:, pl.ds(i * cols, cols)],
                first_ref.at[pl.ds(mine, rows), pl.ds((2 * i + 1) * cols, cols)],
                x_send.at[i], x_recv.at[i], across,
            )
        )
    for copy in weight_copies:
        copy.start()
    for i in range(3):
        first_ref[pl.ds(mine, rows), pl.ds(2 * i * cols, cols)] = small_ref[:, pl.ds(i * cols, cols)]
    first_ref[pl.ds(mine, rows), pl.ds(6 * cols, HD)] = extra_ref[...]

    loads = [
        pltpu.make_async_copy(tok_ref.at[spot], tok_buf, local_sem.at[0]),
        pltpu.make_async_copy(ck_ref.at[spot], k_buf, local_sem.at[1]),
        pltpu.make_async_copy(cv_ref.at[spot], v_buf, local_sem.at[2]),
    ]
    stores = [
        pltpu.make_async_copy(tok_buf, x_ref.at[spot], local_sem.at[3]),
        pltpu.make_async_copy(k_buf, ok_ref.at[spot], local_sem.at[4]),
        pltpu.make_async_copy(v_buf, ov_ref.at[spot], local_sem.at[5]),
    ]
    for copy in loads:
        copy.start()

    x_copies = [remote(tok_ref.at[peer], x_ref.at[spot], x_send.at[3], x_recv.at[3], across)]
    wide = big_ref.shape[1]
    hidden = (wide - cols) // 3
    starts = [(0, cols)] + [(cols + i * hidden, hidden) for i in range(3)]
    own_cols = []
    for i, (start, size) in enumerate(starts):
        base = 2 * start
        own_cols.append(pltpu.make_async_copy(
            big_ref.at[:, pl.ds(start, size)], second_ref.at[:, pl.ds(base, size)], local_sem.at[6 + i]))
        x_copies.append(remote(
            big_ref.at[:, pl.ds(start, size)], second_ref.at[:, pl.ds(base + size, size)],
            x_send.at[4 + i], x_recv.at[4 + i], across))
    x_copies.append(remote(ck_ref.at[peer], ok_ref.at[spot], x_send.at[8], x_recv.at[8], across))
    x_copies.append(remote(cv_ref.at[peer], ov_ref.at[spot], x_send.at[9], x_recv.at[9], across))
    for copy in x_copies + own_cols:
        copy.start()

    def to_device(d, dst_dp):
        chunk = pl.ds(pl.multiple_of(dst_dp * CBLOCK, CBLOCK), CBLOCK)
        dst = target(dst_dp, spot)
        return [
            remote(ck_ref.at[:, chunk, :], held_ref.at[me, :, 0], all_send.at[0, d], all_recv.at[0, d], dst),
            remote(cv_ref.at[:, chunk, :], held_ref.at[me, :, 1], all_send.at[1, d], all_recv.at[1, d], dst),
        ]

    for copy in weight_copies:
        copy.wait_recv()

    def block(p, c):
        return first_ref.at[pl.ds(pl.multiple_of((at_place(p) + c) * rows, rows), rows), :]

    ahead = (place + 1) % RING
    behind = (place + RING - 1) % RING

    def hop(s, direction):
        p = (place + RING - (s - 1)) % RING if direction == 0 else (place + s - 1) % RING
        to = ahead if direction == 0 else behind
        k = (s - 1) * 2 + direction
        return remote(block(p, core), block(p, core), ring_send.at[k], ring_recv.at[k], target(at_place(to) + core, spot))

    def to_pair(i, p):
        return remote(block(p, core), block(p, core), pair_send.at[i], pair_recv.at[i], target(at_place(place) + 1 - core, spot))

    hops = [hop(1, 0), hop(1, 1)]
    for copy in hops:
        copy.start()
    pairs = [to_pair(0, place)]
    pairs[0].start()
    copies = []
    for d in range(1, devices):
        for copy in to_device(d, (me + d) % devices):
            copy.start()
            copies.append(copy)
    chunk = pl.ds(pl.multiple_of(me * CBLOCK, CBLOCK), CBLOCK)
    kept = [
        pltpu.make_async_copy(ck_ref.at[:, chunk, :], held_ref.at[me, :, 0], local_sem.at[10]),
        pltpu.make_async_copy(cv_ref.at[:, chunk, :], held_ref.at[me, :, 1], local_sem.at[11]),
    ]
    for copy in kept:
        copy.start()
    for load, store in zip(loads, stores):
        load.wait()
        store.start()
    for s in range(1, RIGHT + 1):
        for direction in range(2):
            if direction == 1 and s > LEFT:
                continue
            hops[(s - 1) * 2 + direction].wait_recv()
            p = (place + RING - s) % RING if direction == 0 else (place + s) % RING
            if s < (RIGHT if direction == 0 else LEFT):
                nxt = hop(s + 1, direction)
                nxt.start()
                hops.append(nxt)
            pair = to_pair(len(pairs), p)
            pair.start()
            pairs.append(pair)
    for copy in weight_copies + hops:
        copy.wait_send()
    for copy in pairs + x_copies + copies:
        copy.wait()
    for copy in stores + own_cols + kept:
        copy.wait()


def spread(tokens, cache_keys, cache_values, small, extra, big, devices):
    micro, shard_len, width = tokens.shape
    rows, cols = small.shape[0], small.shape[1] // 3
    anywhere = pl.BlockSpec(memory_space=pltpu.HBM)
    vmem = pl.BlockSpec(memory_space=pltpu.VMEM)
    dma = pltpu.SemaphoreType.DMA
    return pl.pallas_call(
        spread_kernel,
        in_specs=[anywhere, anywhere, anywhere, vmem, vmem, vmem],
        out_specs=[anywhere, anywhere, anywhere, anywhere, vmem, anywhere],
        out_shape=[
            jax.ShapeDtypeStruct((2, shard_len, width), BF16),
            jax.ShapeDtypeStruct((2, CACHE_LEN, cols), BF16),
            jax.ShapeDtypeStruct((2, CACHE_LEN, cols), BF16),
            jax.ShapeDtypeStruct((devices, micro, 2, CBLOCK, cols), BF16),
            jax.ShapeDtypeStruct((rows * devices, 6 * cols + HD), BF16),
            jax.ShapeDtypeStruct((rows, 2 * big.shape[1]), BF16),
        ],
        scratch_shapes=[
            pltpu.VMEM((shard_len, width), BF16),
            pltpu.VMEM((CACHE_LEN, cols), BF16),
            pltpu.VMEM((CACHE_LEN, cols), BF16),
            dma((12,)), dma((10,)), dma((10,)), dma((2, devices)), dma((2, devices)),
            dma((RING - 1,)), dma((RING - 1,)), dma((RING,)), dma((RING,)),
        ],
        compiler_params=pltpu.CompilerParams(collective_id=0, has_side_effects=True, vmem_limit_bytes=32 * MIB),
        cost_estimate=pl.CostEstimate(flops=0, bytes_accessed=300 * MIB, transcendentals=0),
        name="spread",
    )(tokens, cache_keys, cache_values, small, extra, big)


def swap(values):
    return lax.ppermute(values, "tensor", [(0, 1), (1, 0)])


def sequence_body(
    tokens, gain_attn, w_query, w_key, w_value, w_out, gain_ffn, w_gate, w_up, w_down,
    cache_keys, cache_values, prefix, partner, own_blocks, partner_blocks, grad_out,
):
    micro, shard_len, width = tokens.shape
    devices = lax.axis_size("dp")
    seqs = micro * devices
    rows_held, cols = w_query.shape
    hidden_held = w_gate.shape[1]
    hidden = 2 * hidden_held
    spot = lax.axis_index("tensor")
    exchange = functools.partial(lax.all_to_all, axis_name="tensor", split_axis=0, concat_axis=0, tiled=True)
    chunks = CACHE_LEN // CBLOCK

    small = jnp.concatenate([w_query, w_key, w_value], axis=1)
    partner_column = jnp.zeros((rows_held, 1), BF16).at[:micro, 0].set(partner.astype(BF16))
    extra = jnp.concatenate(
        [gain_attn[:, None], gain_ffn[:, None], partner_column, jnp.zeros((rows_held, HD - 3), BF16)], axis=1
    )
    big = jnp.concatenate([w_out.T, w_gate, w_up, w_down.T], axis=1)
    x, own_k, own_v, held, first_all, second_rows = spread(
        tokens, cache_keys, cache_values, small, extra, big, devices
    )
    x = x.reshape(L, width)
    theirs = swap(lax.dynamic_index_in_dim(grad_out, 1 - spot, 0, keepdims=False))
    mine = lax.dynamic_index_in_dim(grad_out, spot, 0, keepdims=False)
    cotangent = jnp.where(spot == 0, jnp.concatenate([mine, theirs], 0), jnp.concatenate([theirs, mine], 0))
    second_all = lax.all_gather(second_rows, "dp", axis=0, tiled=True)

    tail = lax.optimization_barrier(first_all[:, 3 * width :])
    gains = mm((jnp.arange(2)[:, None] == jnp.arange(HD)[None, :]).astype(BF16), tail, NT)
    gain_one, gain_two = gains[:1], gains[1:]
    table = tail[:, 2].reshape(devices, rows_held)[:, :micro].reshape(seqs).astype(jnp.int32)
    sent = pick_rows(table, held.reshape(seqs, 2 * CBLOCK, cols))
    fetched = lax.all_to_all(sent, ("dp", "tensor"), split_axis=0, concat_axis=0, tiled=True)
    fetched = fetched.reshape(chunks, 2, 2, CBLOCK, cols)

    meta = jnp.concatenate(
        [
            prefix[spot][None], spot[None].astype(jnp.int32),
            own_blocks[spot].reshape(-1), partner_blocks[spot].reshape(-1),
        ]
    )
    normed, qkv = project(x, gain_one, first_all)
    partial, partial_lse = attend(meta, qkv, own_k, own_v)
    context, lse = attend_other(meta, qkv, fetched, partial, partial_lse)
    mixed, normed_two = mix(x, context, gain_two, second_all)
    ffn_out, grad_normed_two, ffn_grads = ffn(normed_two, cotangent, second_all, width, hidden, devices)
    ffn_share = lax.psum_scatter(
        ffn_grads, "dp", scatter_dimension=0, tiled=True,
        axis_index_groups=[list(range(c, devices, 2)) for c in range(2)],
    )
    out, grad_mixed, branch, grad_context, gain_part_two = unmix(
        mixed, grad_normed_two, ffn_out, cotangent, gain_two, second_all
    )
    out = exchange(out.reshape(2, shard_len, width))
    dq, dk, dv = attend_back(meta, qkv, own_k, own_v, fetched, grad_context, context, lse)
    dq, out = lax.optimization_barrier((dq, out))
    grad_tokens, gain_sums, attn_share = finish(
        x, grad_mixed, normed, context, branch, dq, dk, dv, first_all, gain_one, gain_part_two, devices
    )
    grad_tokens = grad_tokens.astype(F32)
    g_out, g_value, g_key, g_query = jnp.split(attn_share, 4, axis=1)
    pieces = ffn_share.reshape(rows_held, hidden // HT, 3, HT // 2).swapaxes(1, 2)
    pieces = pieces.reshape(rows_held, 3, hidden_held).astype(F32)
    g_gate, g_up, g_down = pieces[:, 0], pieces[:, 1], pieces[:, 2]
    return (
        out, grad_tokens, gain_sums[0], g_query, g_key, g_value, g_out.T, gain_sums[1], g_gate, g_up, g_down.T,
    )


def solution(mesh):
    in_specs = (
        P("dp", "tensor", None),
        P("dp"),
        P("dp", "tensor"),
        P("dp", "tensor"),
        P("dp", "tensor"),
        P("tensor", "dp"),
        P("dp"),
        P("dp", "tensor"),
        P("dp", "tensor"),
        P("tensor", "dp"),
        P("dp", None, "tensor"),
        P("dp", None, "tensor"),
        P("dp"),
        P("dp"),
        P("dp", None, None),
        P("dp", None, None),
        P("dp", "tensor", None),
    )
    out_specs = (
        P("dp", "tensor", None),
        P("dp", "tensor", None),
        P(),
        P("dp", "tensor"),
        P("dp", "tensor"),
        P("dp", "tensor"),
        P("tensor", "dp"),
        P(),
        P("dp", "tensor"),
        P("dp", "tensor"),
        P("tensor", "dp"),
    )
    whole = mesh.shape["tensor"] == 2 and mesh.shape["dp"] == CACHE_LEN // CBLOCK
    body = sequence_body if whole else tensor_body
    return jax.shard_map(body, mesh=mesh, in_specs=in_specs, out_specs=out_specs, check_vma=False)
```

```python
import functools

import jax
import jax.numpy as jnp
from jax import lax
from jax.experimental import pallas as pl
from jax.experimental.pallas import tpu as pltpu
from jax.sharding import PartitionSpec as P

HD = 128
L = 2048
CACHE_LEN = 1024
QBLOCK = 128
CBLOCK = 64
KR = 4
QROWS = 512


EPS = 1e-05
NEGATIVE = -1e30


def norm_rows(values, gain):
    scale_rows = lax.rsqrt(jnp.mean(values * values, axis=-1, keepdims=True) + EPS)
    return (values * scale_rows * gain, scale_rows)


def norm_back(grad_normed, values, scale_rows, gain):
    unit = values * scale_rows
    grad_unit = grad_normed * gain
    grad_values = scale_rows * (
        grad_unit - unit * jnp.mean(grad_unit * unit, axis=-1, keepdims=True)
    )
    return (grad_values, jnp.sum(grad_normed * unit, axis=0))


def inner_rows(left, right):
    return lax.dot_general(
        left, right, (((0,), (0,)), ((), ())), preferred_element_type=jnp.float32
    )


def outer_cols(left, right):
    return lax.dot_general(
        left, right, (((1,), (1,)), ((), ())), preferred_element_type=jnp.float32
    )


def memory_rows(cache_one, chosen, width):
    shaped = cache_one.reshape(CACHE_LEN // CBLOCK, CBLOCK, width)
    return jnp.take(shaped, chosen, axis=0)


def block_scores(query_block, keys_part, mem_part, first_row, limit):
    rows_here, heads_here, size = query_block.shape
    extent = keys_part.shape[0]
    local = jnp.einsum(
        "qhd,khd->hqk", query_block, keys_part, preferred_element_type=jnp.float32
    ) * size ** (-0.5)
    row_ids = first_row + jnp.arange(rows_here, dtype=jnp.int32)[:, None]
    key_ids = jnp.arange(extent, dtype=jnp.int32)[None, :]
    allowed = (key_ids <= row_ids) | (row_ids < limit) & (key_ids < limit)
    local = jnp.where(allowed[None], local, NEGATIVE)
    groups = mem_part.shape[0]
    grouped = query_block.reshape(groups, rows_here // groups, heads_here, size)
    remote = jnp.einsum(
        "bqhd,bkhd->hbqk", grouped, mem_part, preferred_element_type=jnp.float32
    ) * size ** (-0.5)
    return (local, remote.reshape(heads_here, rows_here, -1))


def attention_forward(query, keys, values, mem_keys, mem_values, limit):
    groups = QROWS // QBLOCK
    heads_here = query.shape[1]
    context_parts = []
    lse_parts = []
    for index in range(L // QROWS):
        first = index * QROWS
        extent = max(first + QROWS, L // 2)
        query_block = query[first : first + QROWS]
        mem_k = mem_keys[index * groups : (index + 1) * groups]
        mem_v = mem_values[index * groups : (index + 1) * groups]
        local, remote = block_scores(query_block, keys[:extent], mem_k, first, limit)
        top = jnp.maximum(jnp.max(local, axis=-1), jnp.max(remote, axis=-1))
        e_local = jnp.exp(local - top[..., None])
        e_remote = jnp.exp(remote - top[..., None])
        total = jnp.sum(e_local, axis=-1) + jnp.sum(e_remote, axis=-1)
        p_local = (e_local / total[..., None]).astype(jnp.bfloat16)
        p_remote = (
            (e_remote / total[..., None])
            .astype(jnp.bfloat16)
            .reshape(heads_here, groups, QBLOCK, -1)
        )
        part = jnp.einsum(
            "hqk,khd->qhd", p_local, values[:extent], preferred_element_type=jnp.float32
        )
        extra = jnp.einsum("hbqk,bkhd->bqhd", p_remote, mem_v, preferred_element_type=jnp.float32)
        context_parts.append(part + extra.reshape(part.shape))
        lse_parts.append(top + jnp.log(total))
    return (jnp.concatenate(context_parts, axis=0), lse_parts)


def attention_backward(query, keys, values, mem_keys, mem_values, limit, lse_parts, grad_context):
    groups = QROWS // QBLOCK
    length, heads_here, size = query.shape
    scale = size ** (-0.5)
    grad_query_parts = []
    grad_keys = jnp.zeros(query.shape, jnp.float32)
    grad_values = jnp.zeros(query.shape, jnp.float32)
    for index in range(L // QROWS):
        first = index * QROWS
        extent = max(first + QROWS, L // 2)
        query_block = query[first : first + QROWS]
        mem_k = mem_keys[index * groups : (index + 1) * groups]
        mem_v = mem_values[index * groups : (index + 1) * groups]
        local, remote = block_scores(query_block, keys[:extent], mem_k, first, limit)
        lse_block = lse_parts[index][..., None]
        p_local = jnp.exp(local - lse_block)
        p_remote = jnp.exp(remote - lse_block)
        grad_block = grad_context[first : first + QROWS]
        grouped_grad = grad_block.reshape(groups, QBLOCK, heads_here, size)
        dp_local = jnp.einsum(
            "qhd,khd->hqk", grad_block, values[:extent], preferred_element_type=jnp.float32
        )
        dp_remote = jnp.einsum(
            "bqhd,bkhd->hbqk", grouped_grad, mem_v, preferred_element_type=jnp.float32
        )
        dp_remote = dp_remote.reshape(heads_here, QROWS, -1)
        delta = jnp.sum(p_local * dp_local, axis=-1) + jnp.sum(p_remote * dp_remote, axis=-1)
        ds_local = (p_local * (dp_local - delta[..., None])).astype(jnp.bfloat16)
        ds_remote = (p_remote * (dp_remote - delta[..., None])).astype(jnp.bfloat16)
        ds_remote = ds_remote.reshape(heads_here, groups, QBLOCK, -1)
        dq_block = jnp.einsum(
            "hqk,khd->qhd", ds_local, keys[:extent], preferred_element_type=jnp.float32
        )
        dq_extra = jnp.einsum(
            "hbqk,bkhd->bqhd", ds_remote, mem_k, preferred_element_type=jnp.float32
        )
        grad_query_parts.append((dq_block + dq_extra.reshape(dq_block.shape)) * scale)
        dk_part = (
            jnp.einsum("hqk,qhd->khd", ds_local, query_block, preferred_element_type=jnp.float32)
            * scale
        )
        dv_part = jnp.einsum(
            "hqk,qhd->khd",
            p_local.astype(jnp.bfloat16),
            grad_block,
            preferred_element_type=jnp.float32,
        )
        grad_keys = grad_keys.at[:extent].add(dk_part)
        grad_values = grad_values.at[:extent].add(dv_part)
    return (jnp.concatenate(grad_query_parts, axis=0), grad_keys, grad_values)


def tensor_body(
    tokens,
    gain_attn,
    w_query,
    w_key,
    w_value,
    w_out,
    gain_ffn,
    w_gate,
    w_up,
    w_down,
    cache_keys,
    cache_values,
    prefix,
    partner,
    own_blocks,
    partner_blocks,
    grad_out,
):
    micro, shard_len, width = tokens.shape
    cols = w_query.shape[1]
    heads_local = cols // HD
    qblocks = L // QBLOCK
    mem_len = 2 * KR * CBLOCK
    piece_keys = lax.all_gather(cache_keys, "dp", axis=0, tiled=True)
    piece_values = lax.all_gather(cache_values, "dp", axis=0, tiled=True)
    count = piece_keys.shape[0]
    onehot = (partner[:, None] == jnp.arange(count, dtype=jnp.int32)[None, :]).astype(jnp.bfloat16)
    add_keys = jnp.einsum("mn,nkc->mkc", onehot, piece_keys, preferred_element_type=jnp.float32)
    add_values = jnp.einsum("mn,nkc->mkc", onehot, piece_values, preferred_element_type=jnp.float32)
    fetched_keys = add_keys.astype(jnp.bfloat16)
    fetched_values = add_values.astype(jnp.bfloat16)
    totals = (
        jnp.zeros((width, cols), jnp.float32),
        jnp.zeros((width, cols), jnp.float32),
        jnp.zeros((width, cols), jnp.float32),
        jnp.zeros((cols, width), jnp.float32),
        jnp.zeros((width, w_gate.shape[1]), jnp.float32),
        jnp.zeros((width, w_gate.shape[1]), jnp.float32),
        jnp.zeros((w_gate.shape[1], width), jnp.float32),
    )
    shares = tuple(
        (
            jnp.zeros(w.shape, jnp.float32)
            for w in (w_query, w_key, w_value, w_out, w_gate, w_up, w_down)
        )
    )
    gain_total_attn = jnp.zeros((width,), jnp.float32)
    gain_total_ffn = jnp.zeros((width,), jnp.float32)
    out_rows = []
    grad_rows = []
    for step in range(micro):
        fwd = (
            lax.all_gather(gain_attn, "dp", axis=0, tiled=True),
            lax.all_gather(w_query, "dp", axis=0, tiled=True),
            lax.all_gather(w_key, "dp", axis=0, tiled=True),
            lax.all_gather(w_value, "dp", axis=0, tiled=True),
            lax.all_gather(w_out, "dp", axis=1, tiled=True),
            lax.all_gather(gain_ffn, "dp", axis=0, tiled=True),
            lax.all_gather(w_gate, "dp", axis=0, tiled=True),
            lax.all_gather(w_up, "dp", axis=0, tiled=True),
            lax.all_gather(w_down, "dp", axis=1, tiled=True),
        )
        g_attn, wq_full, wk_full, wv_full, wo_full, g_ffn, wg_full, wu_full, wd_full = fwd
        limit = prefix[step]
        own_k = memory_rows(cache_keys[step], own_blocks[step], cols)
        par_k = memory_rows(fetched_keys[step], partner_blocks[step], cols)
        own_v = memory_rows(cache_values[step], own_blocks[step], cols)
        par_v = memory_rows(fetched_values[step], partner_blocks[step], cols)
        mem_keys = jnp.concatenate([own_k, par_k], axis=1).reshape(
            qblocks, mem_len, heads_local, HD
        )
        mem_values = jnp.concatenate([own_v, par_v], axis=1).reshape(
            qblocks, mem_len, heads_local, HD
        )
        token_rows = tokens[step].astype(jnp.float32)
        normed, scale_one = norm_rows(token_rows, g_attn.astype(jnp.float32))
        normed_all = lax.all_gather(normed.astype(jnp.bfloat16), "tensor", axis=0, tiled=True)
        query = (
            jnp.dot(normed_all, wq_full, preferred_element_type=jnp.float32)
            .astype(jnp.bfloat16)
            .reshape(L, heads_local, HD)
        )
        keys = (
            jnp.dot(normed_all, wk_full, preferred_element_type=jnp.float32)
            .astype(jnp.bfloat16)
            .reshape(L, heads_local, HD)
        )
        values = (
            jnp.dot(normed_all, wv_full, preferred_element_type=jnp.float32)
            .astype(jnp.bfloat16)
            .reshape(L, heads_local, HD)
        )
        context_full, lse_parts = attention_forward(
            query, keys, values, mem_keys, mem_values, limit
        )
        context = context_full.reshape(L, cols).astype(jnp.bfloat16)
        mixed = token_rows + lax.psum_scatter(
            jnp.dot(context, wo_full, preferred_element_type=jnp.float32),
            "tensor",
            scatter_dimension=0,
            tiled=True,
        )
        normed_two, scale_two = norm_rows(mixed, g_ffn.astype(jnp.float32))
        normed_two_all = lax.all_gather(
            normed_two.astype(jnp.bfloat16), "tensor", axis=0, tiled=True
        )
        gate = jnp.dot(normed_two_all, wg_full, preferred_element_type=jnp.float32)
        upward = jnp.dot(normed_two_all, wu_full, preferred_element_type=jnp.float32)
        sigma = jax.nn.sigmoid(gate)
        silu_gate = gate * sigma
        hidden = (silu_gate * upward).astype(jnp.bfloat16)
        out_rows.append(
            (
                mixed
                + lax.psum_scatter(
                    jnp.dot(hidden, wd_full, preferred_element_type=jnp.float32).astype(
                        jnp.bfloat16
                    ),
                    "tensor",
                    scatter_dimension=0,
                    tiled=True,
                ).astype(jnp.float32)
            ).astype(jnp.bfloat16)
        )
        bwd = (
            lax.all_gather(gain_attn, "dp", axis=0, tiled=True),
            lax.all_gather(w_query, "dp", axis=0, tiled=True),
            lax.all_gather(w_key, "dp", axis=0, tiled=True),
            lax.all_gather(w_value, "dp", axis=0, tiled=True),
            lax.all_gather(w_out, "dp", axis=1, tiled=True),
            lax.all_gather(gain_ffn, "dp", axis=0, tiled=True),
            lax.all_gather(w_gate, "dp", axis=0, tiled=True),
            lax.all_gather(w_up, "dp", axis=0, tiled=True),
            lax.all_gather(w_down, "dp", axis=1, tiled=True),
        )
        g_attn, wq_full, wk_full, wv_full, wo_full, g_ffn, wg_full, wu_full, wd_full = bwd
        grad_here = grad_out[step]
        grad_all = lax.all_gather(grad_here, "tensor", axis=0, tiled=True)
        d_down = inner_rows(hidden, grad_all)
        grad_hidden = outer_cols(grad_all, wd_full)
        grad_gate = (grad_hidden * upward * sigma * (1.0 + gate * (1.0 - sigma))).astype(
            jnp.bfloat16
        )
        grad_up = (grad_hidden * silu_gate).astype(jnp.bfloat16)
        d_gate = inner_rows(normed_two_all, grad_gate)
        d_up = inner_rows(normed_two_all, grad_up)
        grad_normed_two = lax.psum_scatter(
            outer_cols(grad_gate, wg_full) + outer_cols(grad_up, wu_full),
            "tensor",
            scatter_dimension=0,
            tiled=True,
        )
        grad_mixed_norm, gain_part_ffn = norm_back(
            grad_normed_two, mixed, scale_two, g_ffn.astype(jnp.float32)
        )
        grad_mixed = grad_here.astype(jnp.float32) + grad_mixed_norm
        branch_all = lax.all_gather(grad_mixed.astype(jnp.bfloat16), "tensor", axis=0, tiled=True)
        d_out = inner_rows(context, branch_all)
        grad_context = (
            outer_cols(branch_all, wo_full).astype(jnp.bfloat16).reshape(L, heads_local, HD)
        )
        grad_query, grad_keys, grad_values = attention_backward(
            query, keys, values, mem_keys, mem_values, limit, lse_parts, grad_context
        )
        grad_query = grad_query.reshape(L, cols).astype(jnp.bfloat16)
        grad_keys = grad_keys.reshape(L, cols).astype(jnp.bfloat16)
        grad_values = grad_values.reshape(L, cols).astype(jnp.bfloat16)
        d_query = inner_rows(normed_all, grad_query)
        d_key = inner_rows(normed_all, grad_keys)
        d_value = inner_rows(normed_all, grad_values)
        grad_normed = lax.psum_scatter(
            (
                outer_cols(grad_query, wq_full)
                + outer_cols(grad_keys, wk_full)
                + outer_cols(grad_values, wv_full)
            ).astype(jnp.bfloat16),
            "tensor",
            scatter_dimension=0,
            tiled=True,
        ).astype(jnp.float32)
        grad_token_norm, gain_part_attn = norm_back(
            grad_normed, token_rows, scale_one, g_attn.astype(jnp.float32)
        )
        grad_rows.append(grad_mixed + grad_token_norm)
        gain_total_attn = gain_total_attn + gain_part_attn
        gain_total_ffn = gain_total_ffn + gain_part_ffn
        totals = tuple(
            (
                held + fresh
                for held, fresh in zip(
                    totals, (d_query, d_key, d_value, d_out, d_gate, d_up, d_down)
                )
            )
        )
    shares = (
        lax.psum_scatter(
            totals[0].astype(jnp.bfloat16), "dp", scatter_dimension=0, tiled=True
        ).astype(jnp.float32),
        lax.psum_scatter(
            totals[1].astype(jnp.bfloat16), "dp", scatter_dimension=0, tiled=True
        ).astype(jnp.float32),
        lax.psum_scatter(
            totals[2].astype(jnp.bfloat16), "dp", scatter_dimension=0, tiled=True
        ).astype(jnp.float32),
        lax.psum_scatter(
            totals[3].astype(jnp.bfloat16), "dp", scatter_dimension=1, tiled=True
        ).astype(jnp.float32),
        lax.psum_scatter(
            totals[4].astype(jnp.bfloat16), "dp", scatter_dimension=0, tiled=True
        ).astype(jnp.float32),
        lax.psum_scatter(
            totals[5].astype(jnp.bfloat16), "dp", scatter_dimension=0, tiled=True
        ).astype(jnp.float32),
        lax.psum_scatter(
            totals[6].astype(jnp.bfloat16), "dp", scatter_dimension=1, tiled=True
        ).astype(jnp.float32),
    )
    gain_attn_sum, gain_ffn_sum = lax.psum((gain_total_attn, gain_total_ffn), ("dp", "tensor"))
    return (
        jnp.stack(out_rows, axis=0),
        jnp.stack(grad_rows, axis=0),
        gain_attn_sum,
        shares[0],
        shares[1],
        shares[2],
        shares[3],
        gain_ffn_sum,
        shares[4],
        shares[5],
        shares[6],
    )


TQ = 512
TK = 512
ROWS = 512
HT = 256
SCALE = HD**-0.5
EXP_SCALE = SCALE * 1.4426950408889634
LOG2E = 1.4426950408889634
NT = (((1,), (1,)), ((), ()))
TN = (((0,), (0,)), ((), ()))
F32 = jnp.float32
BF16 = jnp.bfloat16
MIB = 1 << 20


def mm(left, right, dims=(((1,), (0,)), ((), ()))):
    return lax.dot_general(left, right, dims, preferred_element_type=F32)


def fold_max(values):
    best = values[:, :HD]
    for i in range(1, values.shape[1] // HD):
        best = jnp.maximum(best, values[:, i * HD : (i + 1) * HD])
    return best


def fold_sum(values):
    total = values[:, :HD]
    for i in range(1, values.shape[1] // HD):
        total = total + values[:, i * HD : (i + 1) * HD]
    return total


def reach_mask(first, tile, limit):
    rows = first + lax.broadcasted_iota(jnp.int32, (TQ, 1), 0)
    keys = tile * TK + lax.broadcasted_iota(jnp.int32, (1, TK), 1)
    reach = jnp.where(rows < limit, jnp.maximum(rows, limit - 1), rows)
    return keys <= reach


def pick_own(meta, block, own, buf):
    for i in range(KR):
        c = meta[2 + block * KR + i]
        buf[pl.ds(i * CBLOCK, CBLOCK), :] = own[0, pl.ds(pl.multiple_of(c * CBLOCK, CBLOCK), CBLOCK), :]


def pick_other(meta, block, other, buf, start=0):
    for i in range(KR):
        d = meta[2 + (L // QBLOCK) * KR + block * KR + i]
        buf[pl.ds(start + i * CBLOCK, CBLOCK), :] = other[d, 0, 0]


def pick_blocks(meta, block, own, other, buf):
    pick_own(meta, block, own, buf)
    pick_other(meta, block, other, buf, KR * CBLOCK)


def attend_kernel(
    meta, q_ref, k_ref, v_ref, ok_ref, ov_ref, ctx_ref, lse_ref, kbuf, vbuf, sbuf, smem, *, pair
):
    step = pl.program_id(1)
    limit = meta[0]
    first = step * TQ
    free = jnp.where(first < limit, (limit + TK - 1) // TK, 0)
    tiles = jnp.maximum(step + 1, free)
    blocks = TQ // QBLOCK
    for b in range(blocks):
        pick_own(meta, step * blocks + b, ok_ref, kbuf.at[b])
        pick_own(meta, step * blocks + b, ov_ref, vbuf.at[b])
    state = []
    for h in range(pair):
        cs = pl.ds(h * HD, HD)
        best = []
        for b in range(blocks):
            s = mm(q_ref[pl.ds(b * QBLOCK, QBLOCK), cs], kbuf[b, :, cs], NT)
            smem[h, pl.ds(b * QBLOCK, QBLOCK), :] = s
            best.append(fold_max(s))
        state.append(jnp.concatenate(best, 0))

    def scores(tile, state, masked):
        ks = pl.ds(pl.multiple_of(tile * TK, TK), TK)
        if masked:
            allowed = reach_mask(first, tile, limit)
        new = []
        for h in range(pair):
            cs = pl.ds(h * HD, HD)
            s = mm(q_ref[:, cs], k_ref[ks, cs], NT)
            if masked:
                s = jnp.where(allowed, s, NEGATIVE)
            sbuf[h, tile] = s
            new.append(jnp.maximum(state[h], fold_max(s)))
        return tuple(new)

    state = lax.fori_loop(0, step, lambda tile, s: scores(tile, s, False), tuple(state))
    state = lax.fori_loop(step, tiles, lambda tile, s: scores(tile, s, True), state)
    tops = [jnp.max(s, axis=1, keepdims=True) for s in state]
    state = []
    for h in range(pair):
        cs = pl.ds(h * HD, HD)
        p = jnp.exp2((smem[h] - tops[h]) * EXP_SCALE)
        low = p.astype(BF16)
        parts = [mm(low[b * QBLOCK : (b + 1) * QBLOCK], vbuf[b, :, cs]) for b in range(blocks)]
        state.append((fold_sum(p), jnp.concatenate(parts, 0)))

    def weigh(tile, state):
        ks = pl.ds(pl.multiple_of(tile * TK, TK), TK)
        new = []
        for h in range(pair):
            total, acc = state[h]
            p = jnp.exp2((sbuf[h, tile] - tops[h]) * EXP_SCALE)
            new.append((total + fold_sum(p), acc + mm(p.astype(BF16), v_ref[ks, pl.ds(h * HD, HD)])))
        return tuple(new)

    state = lax.fori_loop(0, tiles, weigh, tuple(state))
    for h in range(pair):
        cs = pl.ds(h * HD, HD)
        total = jnp.sum(state[h][0], axis=1, keepdims=True)
        ctx_ref[:, cs] = state[h][1] / total
        lse_ref[:, cs] = jnp.broadcast_to(tops[h] * SCALE + jnp.log(total), (TQ, HD))


def attend_other_kernel(meta, q_ref, pk_ref, pv_ref, part_ref, plse_ref, ctx_ref, lse_ref, kbuf, vbuf, *, pair):
    step = pl.program_id(1)
    blocks = TQ // QBLOCK
    for b in range(blocks):
        pick_other(meta, step * blocks + b, pk_ref, kbuf.at[b])
        pick_other(meta, step * blocks + b, pv_ref, vbuf.at[b])
    for h in range(pair):
        cs = pl.ds(h * HD, HD)
        rows = [pl.ds(b * QBLOCK, QBLOCK) for b in range(blocks)]
        s = jnp.concatenate([mm(q_ref[rows[b], cs], kbuf[b, :, cs], NT) for b in range(blocks)], 0)
        before = plse_ref[:, cs]
        top = jnp.maximum(before, jnp.max(fold_max(s), axis=1, keepdims=True) * SCALE)
        keep = jnp.exp(before - top)
        p = jnp.exp2(s * EXP_SCALE - top[:, :1] * LOG2E)
        low = p.astype(BF16)
        more = jnp.concatenate(
            [mm(low[b * QBLOCK : (b + 1) * QBLOCK], vbuf[b, :, cs]) for b in range(blocks)], 0
        )
        total = keep + jnp.sum(fold_sum(p), axis=1, keepdims=True)
        ctx_ref[:, cs] = ((part_ref[:, cs] * keep + more) / total).astype(BF16)
        lse_ref[:, cs] = top + jnp.log(total)


def attend_back_kernel(
    meta, q_ref, k_ref, v_ref, ok_ref, ov_ref, pk_ref, pv_ref, do_ref, ctx_ref, lse_ref,
    dq_ref, dk_ref, dv_ref, kbuf, vbuf, dks, dvs, *, pair
):
    step = pl.program_id(1)
    limit = meta[0]
    first = step * TQ
    free = jnp.where(first < limit, (limit + TK - 1) // TK, 0)
    tiles = jnp.maximum(step + 1, free)
    blocks = TQ // QBLOCK

    @pl.when(step == 0)
    def _():
        dks[...] = jnp.zeros_like(dks)
        dvs[...] = jnp.zeros_like(dvs)

    for b in range(blocks):
        pick_blocks(meta, step * blocks + b, ok_ref, pk_ref, kbuf.at[b])
        pick_blocks(meta, step * blocks + b, ov_ref, pv_ref, vbuf.at[b])
    state = []
    aux = []
    for h in range(pair):
        cs = pl.ds(h * HD, HD)
        delta = jnp.sum(do_ref[:, cs].astype(F32) * ctx_ref[:, cs].astype(F32), axis=1, keepdims=True)
        lse2 = lse_ref[:, cs][:, :1] * LOG2E
        aux.append((lse2, delta))
        parts = []
        for b in range(blocks):
            rs = pl.ds(b * QBLOCK, QBLOCK)
            s = mm(q_ref[rs, cs], kbuf[b, :, cs], NT)
            p = jnp.exp2(s * EXP_SCALE - lse2[b * QBLOCK : (b + 1) * QBLOCK])
            dp = mm(do_ref[rs, cs], vbuf[b, :, cs], NT)
            ds = (p * (dp - delta[b * QBLOCK : (b + 1) * QBLOCK])).astype(BF16)
            parts.append(mm(ds, kbuf[b, :, cs]))
        state.append(jnp.concatenate(parts, 0))

    def grads(tile, state, masked):
        ks = pl.ds(pl.multiple_of(tile * TK, TK), TK)
        if masked:
            allowed = reach_mask(first, tile, limit)
        new = []
        for h in range(pair):
            cs = pl.ds(h * HD, HD)
            lse2, delta = aux[h]
            s = mm(q_ref[:, cs], k_ref[ks, cs], NT)
            p = jnp.exp2(s * EXP_SCALE - lse2)
            if masked:
                p = jnp.where(allowed, p, 0.0)
            dp = mm(do_ref[:, cs], v_ref[ks, cs], NT)
            ds = (p * (dp - delta)).astype(BF16)
            dvs[ks, cs] += mm(p.astype(BF16), do_ref[:, cs], TN)
            dks[ks, cs] += mm(ds, q_ref[:, cs], TN)
            new.append(state[h] + mm(ds, k_ref[ks, cs]))
        return tuple(new)

    state = lax.fori_loop(0, step, lambda tile, s: grads(tile, s, False), tuple(state))
    state = lax.fori_loop(step, tiles, lambda tile, s: grads(tile, s, True), state)
    for h in range(pair):
        dq_ref[:, pl.ds(h * HD, HD)] = (state[h] * SCALE).astype(BF16)

    @pl.when(step == L // TQ - 1)
    def _():
        dk_ref[...] = (dks[...] * SCALE).astype(BF16)
        dv_ref[...] = dvs[...].astype(BF16)


def attention_specs(heads, pair):
    wide = pair * HD
    per = heads // 2 // pair
    groups = heads // pair
    return [
        pl.BlockSpec((TQ, wide), lambda h, i, meta: (i, h)),
        pl.BlockSpec((L, wide), lambda h, i, meta: (0, groups + h)),
        pl.BlockSpec((L, wide), lambda h, i, meta: (0, 2 * groups + h)),
        pl.BlockSpec((1, CACHE_LEN, wide), lambda h, i, meta: ((h // per) ^ meta[1], 0, h % per)),
        pl.BlockSpec((1, CACHE_LEN, wide), lambda h, i, meta: ((h // per) ^ meta[1], 0, h % per)),
        pl.BlockSpec(
            (CACHE_LEN // CBLOCK, 1, 1, CBLOCK, wide),
            lambda h, i, meta: (0, (h // per) ^ meta[1], 0, 0, h % per),
        ),
        pl.BlockSpec(
            (CACHE_LEN // CBLOCK, 1, 1, CBLOCK, wide),
            lambda h, i, meta: (0, (h // per) ^ meta[1], 1, 0, h % per),
        ),
    ]


def attend(meta, qkv, own_k, own_v, pair=2):
    width = qkv.shape[1] // 3
    heads = width // HD
    wide = pair * HD
    row = pl.BlockSpec((TQ, wide), lambda h, i, meta: (i, h))
    area = L * 1600 * width
    return pl.pallas_call(
        functools.partial(attend_kernel, pair=pair),
        grid_spec=pltpu.PrefetchScalarGridSpec(
            num_scalar_prefetch=1,
            grid=(heads // pair, L // TQ),
            in_specs=attention_specs(heads, pair)[:5],
            out_specs=[row, row],
            scratch_shapes=[pltpu.VMEM((TQ // QBLOCK, KR * CBLOCK, wide), BF16)] * 2
            + [pltpu.VMEM((pair, L // TK, TQ, TK), F32), pltpu.VMEM((pair, TQ, KR * CBLOCK), F32)],
        ),
        out_shape=[jax.ShapeDtypeStruct((L, width), F32)] * 2,
        compiler_params=pltpu.CompilerParams(vmem_limit_bytes=60 * MIB),
        cost_estimate=pl.CostEstimate(flops=12 * area, bytes_accessed=30 * MIB, transcendentals=area // HD),
        name="attend",
    )(meta, qkv, qkv, qkv, own_k, own_v)


def attend_other(meta, qkv, fetched, partial, lse, pair=4):
    width = qkv.shape[1] // 3
    heads = width // HD
    wide = pair * HD
    row = pl.BlockSpec((TQ, wide), lambda h, i, meta: (i, h))
    specs = attention_specs(heads, pair)
    return pl.pallas_call(
        functools.partial(attend_other_kernel, pair=pair),
        grid_spec=pltpu.PrefetchScalarGridSpec(
            num_scalar_prefetch=1,
            grid=(heads // pair, L // TQ),
            in_specs=[specs[0], specs[5], specs[6], row, row],
            out_specs=[row, row],
            scratch_shapes=[pltpu.VMEM((TQ // QBLOCK, KR * CBLOCK, wide), BF16)] * 2,
        ),
        out_shape=[jax.ShapeDtypeStruct((L, width), BF16), jax.ShapeDtypeStruct((L, width), F32)],
        compiler_params=pltpu.CompilerParams(vmem_limit_bytes=60 * MIB),
        cost_estimate=pl.CostEstimate(
            flops=4 * L * 256 * width, bytes_accessed=30 * MIB, transcendentals=L * 256 * heads
        ),
        name="attend_other",
    )(meta, qkv, fetched, fetched, partial, lse)


def attend_back(meta, qkv, own_k, own_v, fetched, grad_context, context, lse, pair=2):
    width = context.shape[1]
    heads = width // HD
    wide = pair * HD
    row = pl.BlockSpec((TQ, wide), lambda h, i, meta: (i, h))
    col = pl.BlockSpec((L, wide), lambda h, i, meta: (0, h))
    area = L * 1900 * width
    return pl.pallas_call(
        functools.partial(attend_back_kernel, pair=pair),
        grid_spec=pltpu.PrefetchScalarGridSpec(
            num_scalar_prefetch=1,
            grid=(heads // pair, L // TQ),
            in_specs=attention_specs(heads, pair) + [row, row, row],
            out_specs=[row, col, col],
            scratch_shapes=[pltpu.VMEM((TQ // QBLOCK, 2 * KR * CBLOCK, wide), BF16)] * 2
            + [pltpu.VMEM((L, wide), F32)] * 2,
        ),
        out_shape=[jax.ShapeDtypeStruct((L, width), BF16)] * 3,
        compiler_params=pltpu.CompilerParams(vmem_limit_bytes=60 * MIB),
        cost_estimate=pl.CostEstimate(flops=12 * area, bytes_accessed=40 * MIB, transcendentals=area // HD),
        name="attend_back",
    )(meta, qkv, qkv, qkv, own_k, own_v, fetched, fetched, grad_context, context, lse)


def project_kernel(x_ref, gain_ref, w_ref, normed_ref, qkv_ref):
    rows = x_ref[...].astype(F32)
    scale = lax.rsqrt(jnp.mean(rows * rows, axis=1, keepdims=True) + EPS)
    normed_ref[...] = (rows * scale * gain_ref[...]).astype(BF16)
    left = normed_ref[...]

    def chunk(c, carry):
        cs = pl.ds(pl.multiple_of(c * 512, 512), 512)
        qkv_ref[:, cs] = mm(left, w_ref[:, cs]).astype(BF16)
        return carry

    lax.fori_loop(0, qkv_ref.shape[1] // 512, chunk, 0)


def project(x, gain, weights):
    width = x.shape[1]
    cols = 3 * width
    row = lambda n: pl.BlockSpec((ROWS, n), lambda i: (i, 0))
    whole = lambda n: pl.BlockSpec((width, n), lambda i: (0, 0))
    return pl.pallas_call(
        project_kernel,
        grid=(L // ROWS,),
        in_specs=[row(width), pl.BlockSpec((1, width), lambda i: (0, 0)), whole(cols)],
        out_specs=[row(width), row(cols)],
        out_shape=[jax.ShapeDtypeStruct((L, width), BF16), jax.ShapeDtypeStruct((L, cols), BF16)],
        compiler_params=pltpu.CompilerParams(vmem_limit_bytes=60 * MIB),
        cost_estimate=pl.CostEstimate(flops=2 * L * width * cols, bytes_accessed=26 * MIB, transcendentals=0),
        name="project",
    )(x, gain, weights)


def mix_kernel(x_ref, ctx_ref, gain_ref, w_ref, mixed_ref, normed_ref):
    mixed = x_ref[...].astype(F32) + mm(ctx_ref[...], w_ref[...], NT)
    mixed_ref[...] = mixed
    scale = lax.rsqrt(jnp.mean(mixed * mixed, axis=1, keepdims=True) + EPS)
    normed_ref[...] = (mixed * scale * gain_ref[...]).astype(BF16)


def mix(x, context, gain, weights):
    width = x.shape[1]
    row = pl.BlockSpec((ROWS, width), lambda i: (i, 0))
    return pl.pallas_call(
        mix_kernel,
        grid=(L // ROWS,),
        in_specs=[row, row, pl.BlockSpec((1, width), lambda i: (0, 0)), pl.BlockSpec((width, width), lambda i: (0, 0))],
        out_specs=[row, row],
        out_shape=[jax.ShapeDtypeStruct((L, width), F32), jax.ShapeDtypeStruct((L, width), BF16)],
        compiler_params=pltpu.CompilerParams(vmem_limit_bytes=60 * MIB),
        cost_estimate=pl.CostEstimate(flops=2 * L * width * width, bytes_accessed=22 * MIB, transcendentals=0),
        name="mix",
    )(x, context, gain, weights)


RING = 8
RIGHT = RING // 2
LEFT = RING - 1 - RIGHT


def ring_place(p):
    y = p // 4
    return (p + y * (7 - 2 * p)) * 2 + y


def meet(devices, me, spot):
    barrier = pltpu.get_barrier_semaphore()
    for d in range(1, devices):
        pl.semaphore_signal(
            barrier, inc=1, device_id=((me + d) % devices, spot), device_id_type=pl.DeviceIdType.MESH
        )
    pl.semaphore_signal(barrier, inc=1, device_id=(me, 1 - spot), device_id_type=pl.DeviceIdType.MESH)
    pl.semaphore_wait(barrier, devices)


def remote(src, dst, send, recv, device):
    return pltpu.make_async_remote_copy(
        src_ref=src, dst_ref=dst, send_sem=send, recv_sem=recv, device_id=device, device_id_type=pl.DeviceIdType.MESH
    )


UT = 256


def ffn_kernel(
    n_ref, g_ref, wg0, wg1, wu0, wu1, wd0, wd1, gain_ref, mixed_ref, wo_ref,
    share_ref, gg_ref, out_ref, gm_ref, br_ref, gc_ref,
    acc, gn, hid, duo, part, got, passed, keep, land,
    wo_buf, mixed_buf, out_buf, br_buf, gc_buf,
    pair_send, pair_recv, x_send, x_recv, wo_sem, mixed_sem, done_sem, *, devices,
):
    tile = pl.program_id(0)
    tiles = pl.num_programs(0)
    me = lax.axis_index("dp")
    spot = lax.axis_index("tensor")
    core = me % 2
    pair = (me + 1 - 2 * core, spot)
    peer = (me, 1 - spot)
    side = HT // 2
    width = n_ref.shape[1]
    wo_copy = pltpu.make_async_copy(wo_ref.at[:, pl.ds(0, width)], wo_buf, wo_sem)

    @pl.when(tile == 0)
    def _():
        barrier = pltpu.get_barrier_semaphore()
        for device in (pair, peer):
            pl.semaphore_signal(barrier, inc=1, device_id=device, device_id_type=pl.DeviceIdType.MESH)
        pl.semaphore_wait(barrier, 2)
        acc[...] = jnp.zeros_like(acc)
        gn[...] = jnp.zeros_like(gn)

    def to_pair(k):
        return remote(part.at[k % 2, :, 1 - core], got.at[k % 2], pair_send.at[k % 2], pair_recv.at[k % 2], pair)

    def to_peer(k):
        return remote(passed.at[k % 2], land.at[k % 4], x_send.at[k % 2], x_recv.at[k % 4], peer)

    def join(k):
        slot = (k + 2) % 2
        total = (got[slot].astype(F32) + part[slot, :, core].astype(F32)).astype(BF16)
        for m in range(3):
            passed[slot, :, :, m * side : (m + 1) * side] = total[:, :, m * HT + side : (m + 1) * HT]
            keep[(k + 4) % 4, :, :, m * side : (m + 1) * side] = total[:, :, m * HT : m * HT + side]

    def settle(k):
        slot = (jnp.maximum(k, -1) + 4) % 4
        total = (keep[slot].astype(F32) + land[slot].astype(F32)).astype(BF16)
        place = pl.multiple_of(jnp.maximum(k, 0) * 3 * side, 3 * side)
        share_ref[:, pl.ds(place, 3 * side)] = total.reshape(share_ref.shape[0], 3 * side)

    wgu = jnp.concatenate([wg0[...], wg1[...], wu0[...], wu1[...]], axis=1)
    wd = jnp.concatenate([wd0[...], wd1[...]], axis=1)

    def chunk(r):
        rs = pl.ds(r * ROWS, ROWS)
        both = mm(n_ref[rs, :], wgu)
        grad_hidden = mm(g_ref[rs, :], wd)
        gate, up = both[:, :HT], both[:, HT:]
        sigma = 1.0 / (1.0 + jnp.exp(-gate))
        silu = gate * sigma
        hidden = (silu * up).astype(BF16)
        grad_gate = grad_hidden * up * (sigma * (1.0 + gate * (1.0 - sigma)))
        grads = jnp.concatenate([grad_gate.astype(BF16), (grad_hidden * silu).astype(BF16)], axis=1)
        acc[rs, :] += mm(hidden, wd, NT)
        gn[rs, :] += mm(grads, wgu, NT)
        hid[rs, :] = hidden
        duo[rs, :] = grads

    @pl.when(tile > 2)
    def _():
        to_peer(tile - 3).wait()

    settle(tile - 3)
    for r in range(L // ROWS):
        chunk(r)

    @pl.when(tile > 0)
    def _():
        to_pair(tile - 1).wait()

    join(tile - 1)
    slot = tile % 2
    shape = part.shape[1:4]
    part[slot, :, :, :, : 2 * HT] = mm(n_ref[...], duo[...], TN).astype(BF16).reshape(shape + (2 * HT,))
    part[slot, :, :, :, 2 * HT :] = mm(g_ref[...], hid[...], TN).astype(BF16).reshape(shape + (HT,))
    to_pair(tile).start()

    @pl.when(tile > 0)
    def _():
        to_peer(tile - 1).start()

    def rows_of(t):
        return pl.ds(pl.multiple_of(t * UT, UT), UT)

    def fetch(t):
        return pltpu.make_async_copy(mixed_ref.at[rows_of(t), :], mixed_buf.at[t % 2], mixed_sem.at[t % 2])

    def write(t):
        sources = [out_buf.at[t % 2], gn.at[rows_of(t), :], br_buf.at[t % 2], gc_buf.at[t % 2]]
        return [
            pltpu.make_async_copy(source, ref.at[rows_of(t), :], done_sem.at[i, t % 2])
            for i, (source, ref) in enumerate(zip(sources, [out_ref, gm_ref, br_ref, gc_ref]))
        ]

    def unmix(t, carry):
        @pl.when(t < L // UT - 1)
        def _():
            fetch(t + 1).start()

        fetch(t).wait()

        @pl.when(t > 1)
        def _():
            for copy in write(t - 2):
                copy.wait()

        rs = rows_of(t)
        now = t % 2
        mixed = mixed_buf[now]
        grad = gn[rs, :]
        scale = lax.rsqrt(jnp.mean(mixed * mixed, axis=1, keepdims=True) + EPS)
        unit = mixed * scale
        inner = grad * gain_ref[...]
        back = scale * (inner - unit * jnp.mean(inner * unit, axis=1, keepdims=True))
        grad_mixed = g_ref[rs, :].astype(F32) + back
        out_buf[now] = (mixed + acc[rs, :]).astype(BF16)
        gn[rs, :] = grad_mixed
        branch = grad_mixed.astype(BF16)
        br_buf[now] = branch
        gc_buf[now] = mm(branch, wo_buf[...]).astype(BF16)
        gg_ref[...] += jnp.sum(grad * unit, axis=0, keepdims=True)
        for copy in write(t):
            copy.start()
        return carry

    @pl.when(tile == tiles - 1)
    def _():
        wo_copy.start()
        fetch(0).start()
        gg_ref[...] = jnp.zeros_like(gg_ref)
        to_peer(tile - 2).wait()
        settle(tile - 2)
        wo_copy.wait()
        lax.fori_loop(0, 4, unmix, 0)
        to_pair(tile).wait()
        join(tile)
        to_peer(tile).start()
        lax.fori_loop(4, L // UT, unmix, 0)
        to_peer(tile - 1).wait()
        settle(tile - 1)
        to_peer(tile).wait()
        settle(tile)
        for t in (L // UT - 2, L // UT - 1):
            for copy in write(t):
                copy.wait()


def ffn(normed, cotangent, weights, gain, mixed, width, hidden, devices):
    once = pl.Buffered(1)
    tiles = hidden // HT
    side = HT // 2
    rows = width // devices
    chips = devices // 2
    lead = width // side
    part = lambda k: pl.BlockSpec((width, side), lambda j: (0, lead + k * tiles + j))
    whole = pl.BlockSpec((L, width), lambda j: (0, 0), pipeline_mode=once)
    fixed = lambda shape: pl.BlockSpec(shape, lambda j: (0, 0), pipeline_mode=once)
    hbm = pl.BlockSpec(memory_space=pltpu.HBM)
    dma = pltpu.SemaphoreType.DMA
    tile = lambda kind: pltpu.VMEM((2, UT, width), kind)
    return pl.pallas_call(
        functools.partial(ffn_kernel, devices=devices),
        grid=(tiles,),
        in_specs=[whole, whole] + [part(k) for k in range(6)] + [fixed((1, width)), hbm, hbm],
        out_specs=[fixed((width // 2, 3 * hidden // 2)), fixed((1, width)), hbm, hbm, hbm, hbm],
        out_shape=[
            jax.ShapeDtypeStruct((width // 2, 3 * hidden // 2), BF16),
            jax.ShapeDtypeStruct((1, width), F32),
            jax.ShapeDtypeStruct((L, width), BF16),
            jax.ShapeDtypeStruct((L, width), F32),
            jax.ShapeDtypeStruct((L, width), BF16),
            jax.ShapeDtypeStruct((L, width), BF16),
        ],
        scratch_shapes=[
            pltpu.VMEM((L, width), F32), pltpu.VMEM((L, width), F32),
            pltpu.VMEM((L, HT), BF16), pltpu.VMEM((L, 2 * HT), BF16),
            pltpu.VMEM((2, chips, 2, rows, 3 * HT), BF16),
            pltpu.VMEM((2, chips, rows, 3 * HT), BF16),
            pltpu.VMEM((2, chips, rows, 3 * side), BF16),
            pltpu.VMEM((4, chips, rows, 3 * side), BF16),
            pltpu.VMEM((4, chips, rows, 3 * side), BF16),
            pltpu.VMEM((width, width), BF16), tile(F32), tile(BF16), tile(BF16), tile(BF16),
            dma((2,)), dma((2,)), dma((2,)), dma((4,)), dma, dma((2,)), dma((4, 2)),
        ],
        compiler_params=pltpu.CompilerParams(collective_id=2, has_side_effects=True, vmem_limit_bytes=61 * MIB),
        cost_estimate=pl.CostEstimate(
            flops=18 * L * width * hidden, bytes_accessed=60 * MIB, transcendentals=L * hidden
        ),
        name="ffn",
    )(normed, cotangent, *([weights] * 6), gain, mixed, weights)


FT = 256


def finish_kernel(
    x_ref, gm_ref, n_ref, ctx_ref, br_ref, dq_ref, dk_ref, dv_ref, w_ref, gain_ref, gain_two_ref,
    gt_ref, sums_ref, share_ref,
    n_buf, ctx_buf, br_buf, dq_buf, dk_buf, dv_buf, w_buf, x_buf, gm_buf, gt_buf,
    part, got, land, across, gains, gain_land,
    load_sem, x_sem, gm_sem, gt_sem, gt_recv, pair_send, pair_recv, ring_send, ring_recv, x_send, x_recv, g_send, g_recv,
    *, devices,
):
    me = lax.axis_index("dp")
    spot = lax.axis_index("tensor")
    core = me % 2
    z, y = me // 4, (me // 2) % 2
    place = z + y * (7 - 2 * z)
    width = n_buf.shape[1]
    half = width // 2
    rows = part.shape[2]
    loads = [
        pltpu.make_async_copy(src, dst, load_sem.at[i])
        for i, (src, dst) in enumerate(
            [
                (ctx_ref, ctx_buf), (br_ref, br_buf), (n_ref, n_buf), (dv_ref, dv_buf),
                (dk_ref, dk_buf), (dq_ref, dq_buf), (w_ref.at[:, pl.ds(0, 3 * width)], w_buf),
            ]
        )
    ]
    for copy in loads:
        copy.start()
    meet(devices, me, spot)

    def tile_in(t, slot):
        rs = pl.ds(pl.multiple_of(t * FT, FT), FT)
        return [
            pltpu.make_async_copy(x_ref.at[rs, :], x_buf.at[slot], x_sem.at[slot]),
            pltpu.make_async_copy(gm_ref.at[rs, :], gm_buf.at[slot], gm_sem.at[slot]),
        ]

    held = L // FT // 2

    def give(k, slot):
        rs = pl.ds(pl.multiple_of(k * FT, FT), FT)
        return remote(
            gt_buf.at[slot], gt_ref.at[spot, rs, :], gt_sem.at[slot], gt_recv.at[k], (me, 1 - spot)
        )

    def keep(k, slot):
        rs = pl.ds(pl.multiple_of(k * FT, FT), FT)
        return pltpu.make_async_copy(gt_buf.at[slot], gt_ref.at[spot, rs, :], gt_sem.at[slot])

    def tile_of(k):
        return (k + held * (1 - spot)) % (2 * held)

    for copy in tile_in(tile_of(0), 0):
        copy.start()

    pair = (me + 1 - 2 * core, spot)

    def to_pair(m):
        cs = pl.ds(m * width, width)
        return remote(part.at[:, 1 - core, :, cs], got.at[:, :, cs], pair_send.at[m], pair_recv.at[m], pair)

    def product(m, left, right):
        def chunk(c, carry):
            cs = pl.ds(pl.multiple_of(c * half, half), half)
            value = mm(left[...], right[:, cs], TN).astype(BF16)
            part[:, :, :, pl.ds(pl.multiple_of(m * width + c * half, half), half)] = value.reshape(
                part.shape[0], 2, rows, half
            )
            return carry

        lax.fori_loop(0, 2, chunk, 0)
        to_pair(m).start()

    def join(m):
        to_pair(m).wait_recv()
        cs = pl.ds(m * width, width)

        def one(b, carry):
            got[b, :, cs] = (got[b, :, cs].astype(F32) + part[b, core, :, cs].astype(F32)).astype(BF16)
            return carry

        lax.fori_loop(0, part.shape[0], one, 0)

    span = 2 * width
    neighbours = [(place + 1) % RING, (place + RING - 1) % RING]

    def held_block(direction, s):
        p = (place + 2 * RING - 1 - s) % RING if direction == 0 else (place + 1 + s) % RING
        return got.at[ring_place(p), :, pl.ds(direction * span, span)]

    def hop(direction, s):
        to = ring_place(neighbours[direction]) * 2 + core
        return remote(
            held_block(direction, s), land.at[direction, s],
            ring_send.at[direction, s], ring_recv.at[direction, s], (to, spot),
        )

    def advance(direction, s, more=True):
        hop(direction, s).wait_recv()
        block = held_block(direction, s + 1)
        block[...] = (block[...].astype(F32) + land[direction, s].astype(F32)).astype(BF16)
        if more:
            hop(direction, s + 1).start()

    def finish_rows(t, slot, k):
        for copy in tile_in(t, slot):
            copy.wait()
        rs = pl.ds(pl.multiple_of(t * FT, FT), FT)
        grad = mm(dq_buf[rs, :], w_buf[:, :width], NT)
        grad += mm(dk_buf[rs, :], w_buf[:, width : 2 * width], NT)
        grad += mm(dv_buf[rs, :], w_buf[:, 2 * width :], NT)
        values = x_buf[slot].astype(F32)
        scale = lax.rsqrt(jnp.mean(values * values, axis=1, keepdims=True) + EPS)
        unit = values * scale
        inner = grad * gain_ref[...]
        back = scale * (inner - unit * jnp.mean(inner * unit, axis=1, keepdims=True))
        gt_buf[k] = (gm_buf[slot] + back).astype(BF16)
        gains[:1, :] += jnp.sum(grad * unit, axis=0, keepdims=True)

    for i in (0, 1):
        loads[i].wait()
    product(0, br_buf, ctx_buf)
    for i in (2, 3):
        loads[i].wait()
    product(1, n_buf, dv_buf)
    join(0)
    join(1)
    hop(0, 0).start()
    loads[4].wait()
    product(2, n_buf, dk_buf)
    advance(0, 0)
    loads[5].wait()
    product(3, n_buf, dq_buf)
    advance(0, 1)
    join(2)
    join(3)
    hop(1, 0).start()
    loads[6].wait()
    gains[:1, :] = jnp.zeros((1, width), F32)
    gains[1:, :] = gain_two_ref[...]

    def sweep(i, carry):
        for slot in (0, 1):
            k = 2 * i + slot
            if slot == 0:
                for copy in tile_in(tile_of(k + 1), 1):
                    copy.start()
            else:

                @pl.when(i < 3)
                def _():
                    for copy in tile_in(tile_of(k + 1), 0):
                        copy.start()

            finish_rows(tile_of(k), slot, k)

            @pl.when(i < 2)
            def _():
                give(k, k).start()

            @pl.when(i >= 2)
            def _():
                keep(k - held, k).start()

        advance(0, i + 2)
        advance(1, i)
        return carry

    lax.fori_loop(0, held, sweep, 0)

    partners = [
        (me + 1 - 2 * core, spot),
        (me + 2 - 4 * y, spot),
        (me + 4 - 8 * (z % 2), spot),
        (me + 8 - 16 * (z // 2), spot),
        (me, 1 - spot),
    ]

    def add_gains(r):
        return remote(gains, gain_land.at[r], g_send.at[r], g_recv.at[r], partners[r])

    def gain_round(r):
        add_gains(r).wait()
        gains[...] = gains[...] + gain_land[r]
        if r < 4:
            add_gains(r + 1).start()

    own = ring_place(place)
    peer = (me, 1 - spot)

    def over(m):
        return remote(
            got.at[own, :, pl.ds(m * width + half, half)], across.at[:, pl.ds(m * half, half)],
            x_send.at[m], x_recv.at[m], peer,
        )

    add_gains(0).start()
    advance(0, 6, False)
    over(0).start()
    over(1).start()
    gain_round(0)
    advance(1, 4)
    gain_round(1)
    gain_round(2)
    advance(1, 5)
    gain_round(3)
    gain_round(4)
    advance(1, 6, False)
    over(2).start()
    over(3).start()
    sums_ref[...] = gains[...]
    for m in range(4):
        over(m).wait_recv()
        cs = pl.ds(m * half, half)
        share_ref[:, cs] = got[own, :, pl.ds(m * width, half)].astype(F32) + across[:, cs].astype(F32)
    for m in range(4):
        over(m).wait_send()
        to_pair(m).wait_send()
    for s in range(RING - 1):
        hop(0, s).wait_send()
        hop(1, s).wait_send()
    for k in range(held):
        give(k, k).wait()
        keep(k, k + held).wait()


def finish(x, grad_mixed, normed, context, branch, dq, dk, dv, weights, gain, gain_two_part, devices):
    width = x.shape[1]
    rows = width // devices
    anywhere = pl.BlockSpec(memory_space=pltpu.HBM)
    vmem = pl.BlockSpec(memory_space=pltpu.VMEM)
    dma = pltpu.SemaphoreType.DMA
    whole = pltpu.VMEM((L, width), BF16)
    return pl.pallas_call(
        functools.partial(finish_kernel, devices=devices),
        in_specs=[anywhere] * 9 + [vmem] * 2,
        out_specs=[anywhere, vmem, vmem],
        out_shape=[
            jax.ShapeDtypeStruct((2, L // 2, width), BF16),
            jax.ShapeDtypeStruct((2, width), F32),
            jax.ShapeDtypeStruct((rows, 2 * width), F32),
        ],
        scratch_shapes=[
            whole, whole, whole, whole, whole, whole, pltpu.VMEM((width, 3 * width), BF16),
            pltpu.VMEM((2, FT, width), BF16), pltpu.VMEM((2, FT, width), F32), pltpu.VMEM((L // FT, FT, width), BF16),
            pltpu.VMEM((RING, 2, rows, 4 * width), BF16),
            pltpu.VMEM((RING, rows, 4 * width), BF16),
            pltpu.VMEM((2, RING - 1, rows, 2 * width), BF16),
            pltpu.VMEM((rows, 2 * width), BF16),
            pltpu.VMEM((2, width), F32), pltpu.VMEM((5, 2, width), F32),
            dma((7,)), dma((2,)), dma((2,)), dma((2 * (L // FT // 2),)), dma((L // FT // 2,)), dma((4,)), dma((4,)),
            dma((2, RING - 1)), dma((2, RING - 1)), dma((4,)), dma((4,)), dma((5,)), dma((5,)),
        ],
        compiler_params=pltpu.CompilerParams(collective_id=1, has_side_effects=True, vmem_limit_bytes=60 * MIB),
        cost_estimate=pl.CostEstimate(flops=14 * L * width * width, bytes_accessed=80 * MIB, transcendentals=0),
        name="finish",
    )(x, grad_mixed, normed, context, branch, dq, dk, dv, weights, gain, gain_two_part)


def pick_kernel(table, held_ref, sent_ref, sems):
    def copy(i):
        return pltpu.make_async_copy(held_ref.at[table[i]], sent_ref.at[i], sems.at[i])

    for i in range(sent_ref.shape[0]):
        copy(i).start()
    for i in range(sent_ref.shape[0]):
        copy(i).wait()


def pick_rows(table, held):
    count = held.shape[0]
    return pl.pallas_call(
        pick_kernel,
        grid_spec=pltpu.PrefetchScalarGridSpec(
            num_scalar_prefetch=1,
            grid=(),
            in_specs=[pl.BlockSpec(memory_space=pl.ANY)],
            out_specs=pl.BlockSpec(memory_space=pltpu.VMEM),
            scratch_shapes=[pltpu.SemaphoreType.DMA((count,))],
        ),
        out_shape=jax.ShapeDtypeStruct(held.shape, held.dtype),
        compiler_params=pltpu.CompilerParams(vmem_limit_bytes=60 * MIB),
        cost_estimate=pl.CostEstimate(flops=0, bytes_accessed=2 * held.size * 2, transcendentals=0),
        name="pick_rows",
    )(table, held)


def spread_kernel(
    tok_ref, ck_ref, cv_ref, small_ref, extra_ref, big_ref,
    x_ref, ok_ref, ov_ref, held_ref, first_ref, second_ref,
    tok_buf, k_buf, v_buf, local_sem, x_send, x_recv, all_send, all_recv, ring_send, ring_recv, pair_send, pair_recv,
):
    me = lax.axis_index("dp")
    spot = lax.axis_index("tensor")
    peer = 1 - spot
    devices = held_ref.shape[0]
    rows, cols = small_ref.shape[0], small_ref.shape[1] // 3
    core = me % 2
    z, y = me // 4, (me // 2) % 2
    place = z + y * (7 - 2 * z)

    def at_place(p):
        yy = p // 4
        return (p + yy * (7 - 2 * p)) * 4 + yy * 2

    def target(dp, tensor):
        return (dp, tensor)

    barrier = pltpu.get_barrier_semaphore()
    for d in range(1, devices):
        pl.semaphore_signal(barrier, inc=1, device_id=target((me + d) % devices, spot), device_id_type=pl.DeviceIdType.MESH)
    pl.semaphore_signal(barrier, inc=1, device_id=target(me, peer), device_id_type=pl.DeviceIdType.MESH)
    pl.semaphore_wait(barrier, devices)

    def remote(src, dst, send, recv, device):
        return pltpu.make_async_remote_copy(
            src_ref=src, dst_ref=dst, send_sem=send, recv_sem=recv,
            device_id=device, device_id_type=pl.DeviceIdType.MESH,
        )

    mine = pl.multiple_of(me * rows, rows)
    across = target(me, peer)
    weight_copies = []
    for i in range(3):
        weight_copies.append(
            remote(
                small_ref.at[:, pl.ds(i * cols, cols)],
                first_ref.at[pl.ds(mine, rows), pl.ds((2 * i + 1) * cols, cols)],
                x_send.at[i], x_recv.at[i], across,
            )
        )
    for copy in weight_copies:
        copy.start()
    for i in range(3):
        first_ref[pl.ds(mine, rows), pl.ds(2 * i * cols, cols)] = small_ref[:, pl.ds(i * cols, cols)]
    first_ref[pl.ds(mine, rows), pl.ds(6 * cols, HD)] = extra_ref[...]

    loads = [
        pltpu.make_async_copy(tok_ref.at[spot], tok_buf, local_sem.at[0]),
        pltpu.make_async_copy(ck_ref.at[spot], k_buf, local_sem.at[1]),
        pltpu.make_async_copy(cv_ref.at[spot], v_buf, local_sem.at[2]),
    ]
    stores = [
        pltpu.make_async_copy(tok_buf, x_ref.at[spot], local_sem.at[3]),
        pltpu.make_async_copy(k_buf, ok_ref.at[spot], local_sem.at[4]),
        pltpu.make_async_copy(v_buf, ov_ref.at[spot], local_sem.at[5]),
    ]
    for copy in loads:
        copy.start()

    x_copies = [remote(tok_ref.at[peer], x_ref.at[spot], x_send.at[3], x_recv.at[3], across)]
    wide = big_ref.shape[1]
    hidden = (wide - cols) // 3
    starts = [(0, cols)] + [(cols + i * hidden, hidden) for i in range(3)]
    own_cols = []
    for i, (start, size) in enumerate(starts):
        base = 2 * start
        own_cols.append(pltpu.make_async_copy(
            big_ref.at[:, pl.ds(start, size)], second_ref.at[:, pl.ds(base, size)], local_sem.at[6 + i]))
        x_copies.append(remote(
            big_ref.at[:, pl.ds(start, size)], second_ref.at[:, pl.ds(base + size, size)],
            x_send.at[4 + i], x_recv.at[4 + i], across))
    x_copies.append(remote(ck_ref.at[peer], ok_ref.at[spot], x_send.at[8], x_recv.at[8], across))
    x_copies.append(remote(cv_ref.at[peer], ov_ref.at[spot], x_send.at[9], x_recv.at[9], across))
    for copy in x_copies + own_cols:
        copy.start()

    def to_device(d, dst_dp):
        chunk = pl.ds(pl.multiple_of(dst_dp * CBLOCK, CBLOCK), CBLOCK)
        dst = target(dst_dp, spot)
        return [
            remote(ck_ref.at[:, chunk, :], held_ref.at[me, :, 0], all_send.at[0, d], all_recv.at[0, d], dst),
            remote(cv_ref.at[:, chunk, :], held_ref.at[me, :, 1], all_send.at[1, d], all_recv.at[1, d], dst),
        ]

    for copy in weight_copies:
        copy.wait_recv()

    def block(p, c):
        return first_ref.at[pl.ds(pl.multiple_of((at_place(p) + c) * rows, rows), rows), :]

    ahead = (place + 1) % RING
    behind = (place + RING - 1) % RING

    def hop(s, direction):
        p = (place + RING - (s - 1)) % RING if direction == 0 else (place + s - 1) % RING
        to = ahead if direction == 0 else behind
        k = (s - 1) * 2 + direction
        return remote(block(p, core), block(p, core), ring_send.at[k], ring_recv.at[k], target(at_place(to) + core, spot))

    def to_pair(i, p):
        return remote(block(p, core), block(p, core), pair_send.at[i], pair_recv.at[i], target(at_place(place) + 1 - core, spot))

    hops = [hop(1, 0), hop(1, 1)]
    for copy in hops:
        copy.start()
    pairs = [to_pair(0, place)]
    pairs[0].start()
    copies = []
    for d in range(1, devices):
        for copy in to_device(d, (me + d) % devices):
            copy.start()
            copies.append(copy)
    chunk = pl.ds(pl.multiple_of(me * CBLOCK, CBLOCK), CBLOCK)
    kept = [
        pltpu.make_async_copy(ck_ref.at[:, chunk, :], held_ref.at[me, :, 0], local_sem.at[10]),
        pltpu.make_async_copy(cv_ref.at[:, chunk, :], held_ref.at[me, :, 1], local_sem.at[11]),
    ]
    for copy in kept:
        copy.start()
    for load, store in zip(loads, stores):
        load.wait()
        store.start()
    for s in range(1, RIGHT + 1):
        for direction in range(2):
            if direction == 1 and s > LEFT:
                continue
            hops[(s - 1) * 2 + direction].wait_recv()
            p = (place + RING - s) % RING if direction == 0 else (place + s) % RING
            if s < (RIGHT if direction == 0 else LEFT):
                nxt = hop(s + 1, direction)
                nxt.start()
                hops.append(nxt)
            pair = to_pair(len(pairs), p)
            pair.start()
            pairs.append(pair)
    for copy in weight_copies + hops:
        copy.wait_send()
    for copy in pairs + x_copies + copies:
        copy.wait()
    for copy in stores + own_cols + kept:
        copy.wait()


def spread(tokens, cache_keys, cache_values, small, extra, big, devices):
    micro, shard_len, width = tokens.shape
    rows, cols = small.shape[0], small.shape[1] // 3
    anywhere = pl.BlockSpec(memory_space=pltpu.HBM)
    vmem = pl.BlockSpec(memory_space=pltpu.VMEM)
    dma = pltpu.SemaphoreType.DMA
    return pl.pallas_call(
        spread_kernel,
        in_specs=[anywhere, anywhere, anywhere, vmem, vmem, vmem],
        out_specs=[anywhere, anywhere, anywhere, anywhere, vmem, anywhere],
        out_shape=[
            jax.ShapeDtypeStruct((2, shard_len, width), BF16),
            jax.ShapeDtypeStruct((2, CACHE_LEN, cols), BF16),
            jax.ShapeDtypeStruct((2, CACHE_LEN, cols), BF16),
            jax.ShapeDtypeStruct((devices, micro, 2, CBLOCK, cols), BF16),
            jax.ShapeDtypeStruct((rows * devices, 6 * cols + HD), BF16),
            jax.ShapeDtypeStruct((rows, 2 * big.shape[1]), BF16),
        ],
        scratch_shapes=[
            pltpu.VMEM((shard_len, width), BF16),
            pltpu.VMEM((CACHE_LEN, cols), BF16),
            pltpu.VMEM((CACHE_LEN, cols), BF16),
            dma((12,)), dma((10,)), dma((10,)), dma((2, devices)), dma((2, devices)),
            dma((RING - 1,)), dma((RING - 1,)), dma((RING,)), dma((RING,)),
        ],
        compiler_params=pltpu.CompilerParams(collective_id=0, has_side_effects=True, vmem_limit_bytes=60 * MIB),
        cost_estimate=pl.CostEstimate(flops=0, bytes_accessed=300 * MIB, transcendentals=0),
        name="spread",
    )(tokens, cache_keys, cache_values, small, extra, big)


def swap(values):
    return lax.ppermute(values, "tensor", [(0, 1), (1, 0)])


def sequence_body(
    tokens, gain_attn, w_query, w_key, w_value, w_out, gain_ffn, w_gate, w_up, w_down,
    cache_keys, cache_values, prefix, partner, own_blocks, partner_blocks, grad_out,
):
    micro, shard_len, width = tokens.shape
    devices = lax.axis_size("dp")
    seqs = micro * devices
    rows_held, cols = w_query.shape
    hidden_held = w_gate.shape[1]
    hidden = 2 * hidden_held
    spot = lax.axis_index("tensor")
    exchange = functools.partial(lax.all_to_all, axis_name="tensor", split_axis=0, concat_axis=0, tiled=True)
    chunks = CACHE_LEN // CBLOCK

    small = jnp.concatenate([w_query, w_key, w_value], axis=1)
    partner_column = jnp.zeros((rows_held, 1), BF16).at[:micro, 0].set(partner.astype(BF16))
    extra = jnp.concatenate(
        [gain_attn[:, None], gain_ffn[:, None], partner_column, jnp.zeros((rows_held, HD - 3), BF16)], axis=1
    )
    big = jnp.concatenate([w_out.T, w_gate, w_up, w_down.T], axis=1)
    x, own_k, own_v, held, first_all, second_rows = spread(
        tokens, cache_keys, cache_values, small, extra, big, devices
    )
    x = x.reshape(L, width)
    theirs = swap(lax.dynamic_index_in_dim(grad_out, 1 - spot, 0, keepdims=False))
    mine = lax.dynamic_index_in_dim(grad_out, spot, 0, keepdims=False)
    cotangent = jnp.where(spot == 0, jnp.concatenate([mine, theirs], 0), jnp.concatenate([theirs, mine], 0))
    second_all = lax.all_gather(second_rows, "dp", axis=0, tiled=True)

    tail = lax.optimization_barrier(first_all[:, 3 * width :])
    gains = mm((jnp.arange(2)[:, None] == jnp.arange(HD)[None, :]).astype(BF16), tail, NT)
    gain_one, gain_two = gains[:1], gains[1:]
    table = tail[:, 2].reshape(devices, rows_held)[:, :micro].reshape(seqs).astype(jnp.int32)
    sent = pick_rows(table, held.reshape(seqs, 2 * CBLOCK, cols))
    fetched = lax.all_to_all(sent, ("dp", "tensor"), split_axis=0, concat_axis=0, tiled=True)
    fetched = fetched.reshape(chunks, 2, 2, CBLOCK, cols)

    meta = jnp.concatenate(
        [
            prefix[spot][None], spot[None].astype(jnp.int32),
            own_blocks[spot].reshape(-1), partner_blocks[spot].reshape(-1),
        ]
    )
    normed, qkv = project(x, gain_one, first_all)
    partial, partial_lse = attend(meta, qkv, own_k, own_v)
    context, lse = attend_other(meta, qkv, fetched, partial, partial_lse)
    mixed, normed_two = mix(x, context, gain_two, second_all)
    ffn_grads, gain_part_two, out, grad_mixed, branch, grad_context = ffn(
        normed_two, cotangent, second_all, gain_two, mixed, width, hidden, devices
    )
    ffn_share = lax.psum_scatter(
        ffn_grads, "dp", scatter_dimension=0, tiled=True,
        axis_index_groups=[list(range(c, devices, 2)) for c in range(2)],
    )
    out = exchange(out.reshape(2, shard_len, width))
    dq, dk, dv = attend_back(meta, qkv, own_k, own_v, fetched, grad_context, context, lse)
    dq, out = lax.optimization_barrier((dq, out))
    grad_tokens, gain_sums, attn_share = finish(
        x, grad_mixed, normed, context, branch, dq, dk, dv, first_all, gain_one, gain_part_two, devices
    )
    grad_tokens = grad_tokens.astype(F32)
    g_out, g_value, g_key, g_query = jnp.split(attn_share, 4, axis=1)
    pieces = ffn_share.reshape(rows_held, hidden // HT, 3, HT // 2).swapaxes(1, 2)
    pieces = pieces.reshape(rows_held, 3, hidden_held).astype(F32)
    g_gate, g_up, g_down = pieces[:, 0], pieces[:, 1], pieces[:, 2]
    return (
        out, grad_tokens, gain_sums[0], g_query, g_key, g_value, g_out.T, gain_sums[1], g_gate, g_up, g_down.T,
    )


def solution(mesh):
    in_specs = (
        P("dp", "tensor", None),
        P("dp"),
        P("dp", "tensor"),
        P("dp", "tensor"),
        P("dp", "tensor"),
        P("tensor", "dp"),
        P("dp"),
        P("dp", "tensor"),
        P("dp", "tensor"),
        P("tensor", "dp"),
        P("dp", None, "tensor"),
        P("dp", None, "tensor"),
        P("dp"),
        P("dp"),
        P("dp", None, None),
        P("dp", None, None),
        P("dp", "tensor", None),
    )
    out_specs = (
        P("dp", "tensor", None),
        P("dp", "tensor", None),
        P(),
        P("dp", "tensor"),
        P("dp", "tensor"),
        P("dp", "tensor"),
        P("tensor", "dp"),
        P(),
        P("dp", "tensor"),
        P("dp", "tensor"),
        P("tensor", "dp"),
    )
    whole = mesh.shape["tensor"] == 2 and mesh.shape["dp"] == CACHE_LEN // CBLOCK
    body = sequence_body if whole else tensor_body
    return jax.shard_map(body, mesh=mesh, in_specs=in_specs, out_specs=out_specs, check_vma=False)
```

```python
import functools

import jax
import jax.numpy as jnp
from jax import lax
from jax.experimental import pallas as pl
from jax.experimental.pallas import tpu as pltpu
from jax.sharding import PartitionSpec as P

HD = 128
L = 2048
CACHE_LEN = 1024
QBLOCK = 128
CBLOCK = 64
KR = 4
QROWS = 512


EPS = 1e-05
NEGATIVE = -1e30


def norm_rows(values, gain):
    scale_rows = lax.rsqrt(jnp.mean(values * values, axis=-1, keepdims=True) + EPS)
    return (values * scale_rows * gain, scale_rows)


def norm_back(grad_normed, values, scale_rows, gain):
    unit = values * scale_rows
    grad_unit = grad_normed * gain
    grad_values = scale_rows * (
        grad_unit - unit * jnp.mean(grad_unit * unit, axis=-1, keepdims=True)
    )
    return (grad_values, jnp.sum(grad_normed * unit, axis=0))


def inner_rows(left, right):
    return lax.dot_general(
        left, right, (((0,), (0,)), ((), ())), preferred_element_type=jnp.float32
    )


def outer_cols(left, right):
    return lax.dot_general(
        left, right, (((1,), (1,)), ((), ())), preferred_element_type=jnp.float32
    )


def memory_rows(cache_one, chosen, width):
    shaped = cache_one.reshape(CACHE_LEN // CBLOCK, CBLOCK, width)
    return jnp.take(shaped, chosen, axis=0)


def block_scores(query_block, keys_part, mem_part, first_row, limit):
    rows_here, heads_here, size = query_block.shape
    extent = keys_part.shape[0]
    local = jnp.einsum(
        "qhd,khd->hqk", query_block, keys_part, preferred_element_type=jnp.float32
    ) * size ** (-0.5)
    row_ids = first_row + jnp.arange(rows_here, dtype=jnp.int32)[:, None]
    key_ids = jnp.arange(extent, dtype=jnp.int32)[None, :]
    allowed = (key_ids <= row_ids) | (row_ids < limit) & (key_ids < limit)
    local = jnp.where(allowed[None], local, NEGATIVE)
    groups = mem_part.shape[0]
    grouped = query_block.reshape(groups, rows_here // groups, heads_here, size)
    remote = jnp.einsum(
        "bqhd,bkhd->hbqk", grouped, mem_part, preferred_element_type=jnp.float32
    ) * size ** (-0.5)
    return (local, remote.reshape(heads_here, rows_here, -1))


def attention_forward(query, keys, values, mem_keys, mem_values, limit):
    groups = QROWS // QBLOCK
    heads_here = query.shape[1]
    context_parts = []
    lse_parts = []
    for index in range(L // QROWS):
        first = index * QROWS
        extent = max(first + QROWS, L // 2)
        query_block = query[first : first + QROWS]
        mem_k = mem_keys[index * groups : (index + 1) * groups]
        mem_v = mem_values[index * groups : (index + 1) * groups]
        local, remote = block_scores(query_block, keys[:extent], mem_k, first, limit)
        top = jnp.maximum(jnp.max(local, axis=-1), jnp.max(remote, axis=-1))
        e_local = jnp.exp(local - top[..., None])
        e_remote = jnp.exp(remote - top[..., None])
        total = jnp.sum(e_local, axis=-1) + jnp.sum(e_remote, axis=-1)
        p_local = (e_local / total[..., None]).astype(jnp.bfloat16)
        p_remote = (
            (e_remote / total[..., None])
            .astype(jnp.bfloat16)
            .reshape(heads_here, groups, QBLOCK, -1)
        )
        part = jnp.einsum(
            "hqk,khd->qhd", p_local, values[:extent], preferred_element_type=jnp.float32
        )
        extra = jnp.einsum("hbqk,bkhd->bqhd", p_remote, mem_v, preferred_element_type=jnp.float32)
        context_parts.append(part + extra.reshape(part.shape))
        lse_parts.append(top + jnp.log(total))
    return (jnp.concatenate(context_parts, axis=0), lse_parts)


def attention_backward(query, keys, values, mem_keys, mem_values, limit, lse_parts, grad_context):
    groups = QROWS // QBLOCK
    length, heads_here, size = query.shape
    scale = size ** (-0.5)
    grad_query_parts = []
    grad_keys = jnp.zeros(query.shape, jnp.float32)
    grad_values = jnp.zeros(query.shape, jnp.float32)
    for index in range(L // QROWS):
        first = index * QROWS
        extent = max(first + QROWS, L // 2)
        query_block = query[first : first + QROWS]
        mem_k = mem_keys[index * groups : (index + 1) * groups]
        mem_v = mem_values[index * groups : (index + 1) * groups]
        local, remote = block_scores(query_block, keys[:extent], mem_k, first, limit)
        lse_block = lse_parts[index][..., None]
        p_local = jnp.exp(local - lse_block)
        p_remote = jnp.exp(remote - lse_block)
        grad_block = grad_context[first : first + QROWS]
        grouped_grad = grad_block.reshape(groups, QBLOCK, heads_here, size)
        dp_local = jnp.einsum(
            "qhd,khd->hqk", grad_block, values[:extent], preferred_element_type=jnp.float32
        )
        dp_remote = jnp.einsum(
            "bqhd,bkhd->hbqk", grouped_grad, mem_v, preferred_element_type=jnp.float32
        )
        dp_remote = dp_remote.reshape(heads_here, QROWS, -1)
        delta = jnp.sum(p_local * dp_local, axis=-1) + jnp.sum(p_remote * dp_remote, axis=-1)
        ds_local = (p_local * (dp_local - delta[..., None])).astype(jnp.bfloat16)
        ds_remote = (p_remote * (dp_remote - delta[..., None])).astype(jnp.bfloat16)
        ds_remote = ds_remote.reshape(heads_here, groups, QBLOCK, -1)
        dq_block = jnp.einsum(
            "hqk,khd->qhd", ds_local, keys[:extent], preferred_element_type=jnp.float32
        )
        dq_extra = jnp.einsum(
            "hbqk,bkhd->bqhd", ds_remote, mem_k, preferred_element_type=jnp.float32
        )
        grad_query_parts.append((dq_block + dq_extra.reshape(dq_block.shape)) * scale)
        dk_part = (
            jnp.einsum("hqk,qhd->khd", ds_local, query_block, preferred_element_type=jnp.float32)
            * scale
        )
        dv_part = jnp.einsum(
            "hqk,qhd->khd",
            p_local.astype(jnp.bfloat16),
            grad_block,
            preferred_element_type=jnp.float32,
        )
        grad_keys = grad_keys.at[:extent].add(dk_part)
        grad_values = grad_values.at[:extent].add(dv_part)
    return (jnp.concatenate(grad_query_parts, axis=0), grad_keys, grad_values)


def tensor_body(
    tokens,
    gain_attn,
    w_query,
    w_key,
    w_value,
    w_out,
    gain_ffn,
    w_gate,
    w_up,
    w_down,
    cache_keys,
    cache_values,
    prefix,
    partner,
    own_blocks,
    partner_blocks,
    grad_out,
):
    micro, shard_len, width = tokens.shape
    cols = w_query.shape[1]
    heads_local = cols // HD
    qblocks = L // QBLOCK
    mem_len = 2 * KR * CBLOCK
    piece_keys = lax.all_gather(cache_keys, "dp", axis=0, tiled=True)
    piece_values = lax.all_gather(cache_values, "dp", axis=0, tiled=True)
    count = piece_keys.shape[0]
    onehot = (partner[:, None] == jnp.arange(count, dtype=jnp.int32)[None, :]).astype(jnp.bfloat16)
    add_keys = jnp.einsum("mn,nkc->mkc", onehot, piece_keys, preferred_element_type=jnp.float32)
    add_values = jnp.einsum("mn,nkc->mkc", onehot, piece_values, preferred_element_type=jnp.float32)
    fetched_keys = add_keys.astype(jnp.bfloat16)
    fetched_values = add_values.astype(jnp.bfloat16)
    totals = (
        jnp.zeros((width, cols), jnp.float32),
        jnp.zeros((width, cols), jnp.float32),
        jnp.zeros((width, cols), jnp.float32),
        jnp.zeros((cols, width), jnp.float32),
        jnp.zeros((width, w_gate.shape[1]), jnp.float32),
        jnp.zeros((width, w_gate.shape[1]), jnp.float32),
        jnp.zeros((w_gate.shape[1], width), jnp.float32),
    )
    shares = tuple(
        (
            jnp.zeros(w.shape, jnp.float32)
            for w in (w_query, w_key, w_value, w_out, w_gate, w_up, w_down)
        )
    )
    gain_total_attn = jnp.zeros((width,), jnp.float32)
    gain_total_ffn = jnp.zeros((width,), jnp.float32)
    out_rows = []
    grad_rows = []
    for step in range(micro):
        fwd = (
            lax.all_gather(gain_attn, "dp", axis=0, tiled=True),
            lax.all_gather(w_query, "dp", axis=0, tiled=True),
            lax.all_gather(w_key, "dp", axis=0, tiled=True),
            lax.all_gather(w_value, "dp", axis=0, tiled=True),
            lax.all_gather(w_out, "dp", axis=1, tiled=True),
            lax.all_gather(gain_ffn, "dp", axis=0, tiled=True),
            lax.all_gather(w_gate, "dp", axis=0, tiled=True),
            lax.all_gather(w_up, "dp", axis=0, tiled=True),
            lax.all_gather(w_down, "dp", axis=1, tiled=True),
        )
        g_attn, wq_full, wk_full, wv_full, wo_full, g_ffn, wg_full, wu_full, wd_full = fwd
        limit = prefix[step]
        own_k = memory_rows(cache_keys[step], own_blocks[step], cols)
        par_k = memory_rows(fetched_keys[step], partner_blocks[step], cols)
        own_v = memory_rows(cache_values[step], own_blocks[step], cols)
        par_v = memory_rows(fetched_values[step], partner_blocks[step], cols)
        mem_keys = jnp.concatenate([own_k, par_k], axis=1).reshape(
            qblocks, mem_len, heads_local, HD
        )
        mem_values = jnp.concatenate([own_v, par_v], axis=1).reshape(
            qblocks, mem_len, heads_local, HD
        )
        token_rows = tokens[step].astype(jnp.float32)
        normed, scale_one = norm_rows(token_rows, g_attn.astype(jnp.float32))
        normed_all = lax.all_gather(normed.astype(jnp.bfloat16), "tensor", axis=0, tiled=True)
        query = (
            jnp.dot(normed_all, wq_full, preferred_element_type=jnp.float32)
            .astype(jnp.bfloat16)
            .reshape(L, heads_local, HD)
        )
        keys = (
            jnp.dot(normed_all, wk_full, preferred_element_type=jnp.float32)
            .astype(jnp.bfloat16)
            .reshape(L, heads_local, HD)
        )
        values = (
            jnp.dot(normed_all, wv_full, preferred_element_type=jnp.float32)
            .astype(jnp.bfloat16)
            .reshape(L, heads_local, HD)
        )
        context_full, lse_parts = attention_forward(
            query, keys, values, mem_keys, mem_values, limit
        )
        context = context_full.reshape(L, cols).astype(jnp.bfloat16)
        mixed = token_rows + lax.psum_scatter(
            jnp.dot(context, wo_full, preferred_element_type=jnp.float32),
            "tensor",
            scatter_dimension=0,
            tiled=True,
        )
        normed_two, scale_two = norm_rows(mixed, g_ffn.astype(jnp.float32))
        normed_two_all = lax.all_gather(
            normed_two.astype(jnp.bfloat16), "tensor", axis=0, tiled=True
        )
        gate = jnp.dot(normed_two_all, wg_full, preferred_element_type=jnp.float32)
        upward = jnp.dot(normed_two_all, wu_full, preferred_element_type=jnp.float32)
        sigma = jax.nn.sigmoid(gate)
        silu_gate = gate * sigma
        hidden = (silu_gate * upward).astype(jnp.bfloat16)
        out_rows.append(
            (
                mixed
                + lax.psum_scatter(
                    jnp.dot(hidden, wd_full, preferred_element_type=jnp.float32).astype(
                        jnp.bfloat16
                    ),
                    "tensor",
                    scatter_dimension=0,
                    tiled=True,
                ).astype(jnp.float32)
            ).astype(jnp.bfloat16)
        )
        bwd = (
            lax.all_gather(gain_attn, "dp", axis=0, tiled=True),
            lax.all_gather(w_query, "dp", axis=0, tiled=True),
            lax.all_gather(w_key, "dp", axis=0, tiled=True),
            lax.all_gather(w_value, "dp", axis=0, tiled=True),
            lax.all_gather(w_out, "dp", axis=1, tiled=True),
            lax.all_gather(gain_ffn, "dp", axis=0, tiled=True),
            lax.all_gather(w_gate, "dp", axis=0, tiled=True),
            lax.all_gather(w_up, "dp", axis=0, tiled=True),
            lax.all_gather(w_down, "dp", axis=1, tiled=True),
        )
        g_attn, wq_full, wk_full, wv_full, wo_full, g_ffn, wg_full, wu_full, wd_full = bwd
        grad_here = grad_out[step]
        grad_all = lax.all_gather(grad_here, "tensor", axis=0, tiled=True)
        d_down = inner_rows(hidden, grad_all)
        grad_hidden = outer_cols(grad_all, wd_full)
        grad_gate = (grad_hidden * upward * sigma * (1.0 + gate * (1.0 - sigma))).astype(
            jnp.bfloat16
        )
        grad_up = (grad_hidden * silu_gate).astype(jnp.bfloat16)
        d_gate = inner_rows(normed_two_all, grad_gate)
        d_up = inner_rows(normed_two_all, grad_up)
        grad_normed_two = lax.psum_scatter(
            outer_cols(grad_gate, wg_full) + outer_cols(grad_up, wu_full),
            "tensor",
            scatter_dimension=0,
            tiled=True,
        )
        grad_mixed_norm, gain_part_ffn = norm_back(
            grad_normed_two, mixed, scale_two, g_ffn.astype(jnp.float32)
        )
        grad_mixed = grad_here.astype(jnp.float32) + grad_mixed_norm
        branch_all = lax.all_gather(grad_mixed.astype(jnp.bfloat16), "tensor", axis=0, tiled=True)
        d_out = inner_rows(context, branch_all)
        grad_context = (
            outer_cols(branch_all, wo_full).astype(jnp.bfloat16).reshape(L, heads_local, HD)
        )
        grad_query, grad_keys, grad_values = attention_backward(
            query, keys, values, mem_keys, mem_values, limit, lse_parts, grad_context
        )
        grad_query = grad_query.reshape(L, cols).astype(jnp.bfloat16)
        grad_keys = grad_keys.reshape(L, cols).astype(jnp.bfloat16)
        grad_values = grad_values.reshape(L, cols).astype(jnp.bfloat16)
        d_query = inner_rows(normed_all, grad_query)
        d_key = inner_rows(normed_all, grad_keys)
        d_value = inner_rows(normed_all, grad_values)
        grad_normed = lax.psum_scatter(
            (
                outer_cols(grad_query, wq_full)
                + outer_cols(grad_keys, wk_full)
                + outer_cols(grad_values, wv_full)
            ).astype(jnp.bfloat16),
            "tensor",
            scatter_dimension=0,
            tiled=True,
        ).astype(jnp.float32)
        grad_token_norm, gain_part_attn = norm_back(
            grad_normed, token_rows, scale_one, g_attn.astype(jnp.float32)
        )
        grad_rows.append(grad_mixed + grad_token_norm)
        gain_total_attn = gain_total_attn + gain_part_attn
        gain_total_ffn = gain_total_ffn + gain_part_ffn
        totals = tuple(
            (
                held + fresh
                for held, fresh in zip(
                    totals, (d_query, d_key, d_value, d_out, d_gate, d_up, d_down)
                )
            )
        )
    shares = (
        lax.psum_scatter(
            totals[0].astype(jnp.bfloat16), "dp", scatter_dimension=0, tiled=True
        ).astype(jnp.float32),
        lax.psum_scatter(
            totals[1].astype(jnp.bfloat16), "dp", scatter_dimension=0, tiled=True
        ).astype(jnp.float32),
        lax.psum_scatter(
            totals[2].astype(jnp.bfloat16), "dp", scatter_dimension=0, tiled=True
        ).astype(jnp.float32),
        lax.psum_scatter(
            totals[3].astype(jnp.bfloat16), "dp", scatter_dimension=1, tiled=True
        ).astype(jnp.float32),
        lax.psum_scatter(
            totals[4].astype(jnp.bfloat16), "dp", scatter_dimension=0, tiled=True
        ).astype(jnp.float32),
        lax.psum_scatter(
            totals[5].astype(jnp.bfloat16), "dp", scatter_dimension=0, tiled=True
        ).astype(jnp.float32),
        lax.psum_scatter(
            totals[6].astype(jnp.bfloat16), "dp", scatter_dimension=1, tiled=True
        ).astype(jnp.float32),
    )
    gain_attn_sum, gain_ffn_sum = lax.psum((gain_total_attn, gain_total_ffn), ("dp", "tensor"))
    return (
        jnp.stack(out_rows, axis=0),
        jnp.stack(grad_rows, axis=0),
        gain_attn_sum,
        shares[0],
        shares[1],
        shares[2],
        shares[3],
        gain_ffn_sum,
        shares[4],
        shares[5],
        shares[6],
    )


TQ = 512
TK = 512
ROWS = 512
HT = 256
SCALE = HD**-0.5
EXP_SCALE = SCALE * 1.4426950408889634
LOG2E = 1.4426950408889634
NT = (((1,), (1,)), ((), ()))
TN = (((0,), (0,)), ((), ()))
F32 = jnp.float32
BF16 = jnp.bfloat16
MIB = 1 << 20


def mm(left, right, dims=(((1,), (0,)), ((), ()))):
    return lax.dot_general(left, right, dims, preferred_element_type=F32)


def fold_max(values):
    best = values[:, :HD]
    for i in range(1, values.shape[1] // HD):
        best = jnp.maximum(best, values[:, i * HD : (i + 1) * HD])
    return best


def fold_sum(values):
    total = values[:, :HD]
    for i in range(1, values.shape[1] // HD):
        total = total + values[:, i * HD : (i + 1) * HD]
    return total


def reach_mask(first, tile, limit):
    rows = first + lax.broadcasted_iota(jnp.int32, (TQ, 1), 0)
    keys = tile * TK + lax.broadcasted_iota(jnp.int32, (1, TK), 1)
    reach = jnp.where(rows < limit, jnp.maximum(rows, limit - 1), rows)
    return keys <= reach


def pick_own(meta, block, own, buf):
    for i in range(KR):
        c = meta[2 + block * KR + i]
        buf[pl.ds(i * CBLOCK, CBLOCK), :] = own[0, pl.ds(pl.multiple_of(c * CBLOCK, CBLOCK), CBLOCK), :]


def pick_other(meta, block, other, buf, start=0):
    for i in range(KR):
        d = meta[2 + (L // QBLOCK) * KR + block * KR + i]
        buf[pl.ds(start + i * CBLOCK, CBLOCK), :] = other[d, 0, 0]


def pick_blocks(meta, block, own, other, buf):
    pick_own(meta, block, own, buf)
    pick_other(meta, block, other, buf, KR * CBLOCK)


def attend_kernel(
    meta, q_ref, k_ref, v_ref, ok_ref, ov_ref, ctx_ref, lse_ref, kbuf, vbuf, sbuf, smem, *, pair
):
    step = pl.program_id(1)
    limit = meta[0]
    first = step * TQ
    free = jnp.where(first < limit, (limit + TK - 1) // TK, 0)
    tiles = jnp.maximum(step + 1, free)
    blocks = TQ // QBLOCK
    for b in range(blocks):
        pick_own(meta, step * blocks + b, ok_ref, kbuf.at[b])
        pick_own(meta, step * blocks + b, ov_ref, vbuf.at[b])
    state = []
    for h in range(pair):
        cs = pl.ds(h * HD, HD)
        best = []
        for b in range(blocks):
            s = mm(q_ref[pl.ds(b * QBLOCK, QBLOCK), cs], kbuf[b, :, cs], NT)
            smem[h, pl.ds(b * QBLOCK, QBLOCK), :] = s
            best.append(fold_max(s))
        state.append(jnp.concatenate(best, 0))

    def scores(tile, state, masked):
        ks = pl.ds(pl.multiple_of(tile * TK, TK), TK)
        if masked:
            allowed = reach_mask(first, tile, limit)
        new = []
        for h in range(pair):
            cs = pl.ds(h * HD, HD)
            s = mm(q_ref[:, cs], k_ref[ks, cs], NT)
            if masked:
                s = jnp.where(allowed, s, NEGATIVE)
            sbuf[h, tile] = s
            new.append(jnp.maximum(state[h], fold_max(s)))
        return tuple(new)

    state = lax.fori_loop(0, step, lambda tile, s: scores(tile, s, False), tuple(state))
    state = lax.fori_loop(step, tiles, lambda tile, s: scores(tile, s, True), state)
    tops = [jnp.max(s, axis=1, keepdims=True) for s in state]
    state = []
    for h in range(pair):
        cs = pl.ds(h * HD, HD)
        p = jnp.exp2((smem[h] - tops[h]) * EXP_SCALE)
        low = p.astype(BF16)
        parts = [mm(low[b * QBLOCK : (b + 1) * QBLOCK], vbuf[b, :, cs]) for b in range(blocks)]
        state.append((fold_sum(p), jnp.concatenate(parts, 0)))

    def weigh(tile, state):
        ks = pl.ds(pl.multiple_of(tile * TK, TK), TK)
        new = []
        for h in range(pair):
            total, acc = state[h]
            p = jnp.exp2((sbuf[h, tile] - tops[h]) * EXP_SCALE)
            new.append((total + fold_sum(p), acc + mm(p.astype(BF16), v_ref[ks, pl.ds(h * HD, HD)])))
        return tuple(new)

    state = lax.fori_loop(0, tiles, weigh, tuple(state))
    for h in range(pair):
        cs = pl.ds(h * HD, HD)
        total = jnp.sum(state[h][0], axis=1, keepdims=True)
        ctx_ref[:, cs] = state[h][1] / total
        lse_ref[:, cs] = jnp.broadcast_to(tops[h] * SCALE + jnp.log(total), (TQ, HD))


def attend_other_kernel(meta, q_ref, pk_ref, pv_ref, part_ref, plse_ref, ctx_ref, lse_ref, kbuf, vbuf, *, pair):
    step = pl.program_id(1)
    blocks = TQ // QBLOCK
    for b in range(blocks):
        pick_other(meta, step * blocks + b, pk_ref, kbuf.at[b])
        pick_other(meta, step * blocks + b, pv_ref, vbuf.at[b])
    for h in range(pair):
        cs = pl.ds(h * HD, HD)
        rows = [pl.ds(b * QBLOCK, QBLOCK) for b in range(blocks)]
        s = jnp.concatenate([mm(q_ref[rows[b], cs], kbuf[b, :, cs], NT) for b in range(blocks)], 0)
        before = plse_ref[:, cs]
        top = jnp.maximum(before, jnp.max(fold_max(s), axis=1, keepdims=True) * SCALE)
        keep = jnp.exp(before - top)
        p = jnp.exp2(s * EXP_SCALE - top[:, :1] * LOG2E)
        low = p.astype(BF16)
        more = jnp.concatenate(
            [mm(low[b * QBLOCK : (b + 1) * QBLOCK], vbuf[b, :, cs]) for b in range(blocks)], 0
        )
        total = keep + jnp.sum(fold_sum(p), axis=1, keepdims=True)
        ctx_ref[:, cs] = ((part_ref[:, cs] * keep + more) / total).astype(BF16)
        lse_ref[:, cs] = top + jnp.log(total)


def attend_back_kernel(
    meta, q_ref, k_ref, v_ref, ok_ref, ov_ref, pk_ref, pv_ref, do_ref, ctx_ref, lse_ref,
    dq_ref, dk_ref, dv_ref, kbuf, vbuf, dks, dvs, *, pair
):
    step = pl.program_id(1)
    limit = meta[0]
    first = step * TQ
    free = jnp.where(first < limit, (limit + TK - 1) // TK, 0)
    tiles = jnp.maximum(step + 1, free)
    blocks = TQ // QBLOCK

    @pl.when(step == 0)
    def _():
        dks[...] = jnp.zeros_like(dks)
        dvs[...] = jnp.zeros_like(dvs)

    for b in range(blocks):
        pick_blocks(meta, step * blocks + b, ok_ref, pk_ref, kbuf.at[b])
        pick_blocks(meta, step * blocks + b, ov_ref, pv_ref, vbuf.at[b])
    state = []
    aux = []
    for h in range(pair):
        cs = pl.ds(h * HD, HD)
        delta = jnp.sum(do_ref[:, cs].astype(F32) * ctx_ref[:, cs].astype(F32), axis=1, keepdims=True)
        lse2 = lse_ref[:, cs][:, :1] * LOG2E
        aux.append((lse2, delta))
        parts = []
        for b in range(blocks):
            rs = pl.ds(b * QBLOCK, QBLOCK)
            s = mm(q_ref[rs, cs], kbuf[b, :, cs], NT)
            p = jnp.exp2(s * EXP_SCALE - lse2[b * QBLOCK : (b + 1) * QBLOCK])
            dp = mm(do_ref[rs, cs], vbuf[b, :, cs], NT)
            ds = (p * (dp - delta[b * QBLOCK : (b + 1) * QBLOCK])).astype(BF16)
            parts.append(mm(ds, kbuf[b, :, cs]))
        state.append(jnp.concatenate(parts, 0))

    def grads(tile, state, masked):
        ks = pl.ds(pl.multiple_of(tile * TK, TK), TK)
        if masked:
            allowed = reach_mask(first, tile, limit)
        new = []
        for h in range(pair):
            cs = pl.ds(h * HD, HD)
            lse2, delta = aux[h]
            s = mm(q_ref[:, cs], k_ref[ks, cs], NT)
            p = jnp.exp2(s * EXP_SCALE - lse2)
            if masked:
                p = jnp.where(allowed, p, 0.0)
            dp = mm(do_ref[:, cs], v_ref[ks, cs], NT)
            ds = (p * (dp - delta)).astype(BF16)
            dvs[ks, cs] += mm(p.astype(BF16), do_ref[:, cs], TN)
            dks[ks, cs] += mm(ds, q_ref[:, cs], TN)
            new.append(state[h] + mm(ds, k_ref[ks, cs]))
        return tuple(new)

    state = lax.fori_loop(0, step, lambda tile, s: grads(tile, s, False), tuple(state))
    state = lax.fori_loop(step, tiles, lambda tile, s: grads(tile, s, True), state)
    for h in range(pair):
        dq_ref[:, pl.ds(h * HD, HD)] = (state[h] * SCALE).astype(BF16)

    @pl.when(step == L // TQ - 1)
    def _():
        dk_ref[...] = (dks[...] * SCALE).astype(BF16)
        dv_ref[...] = dvs[...].astype(BF16)


def attention_specs(heads, pair):
    wide = pair * HD
    per = heads // 2 // pair
    groups = heads // pair
    return [
        pl.BlockSpec((TQ, wide), lambda h, i, meta: (i, h)),
        pl.BlockSpec((L, wide), lambda h, i, meta: (0, groups + h)),
        pl.BlockSpec((L, wide), lambda h, i, meta: (0, 2 * groups + h)),
        pl.BlockSpec((1, CACHE_LEN, wide), lambda h, i, meta: ((h // per) ^ meta[1], 0, h % per)),
        pl.BlockSpec((1, CACHE_LEN, wide), lambda h, i, meta: ((h // per) ^ meta[1], 0, h % per)),
        pl.BlockSpec(
            (CACHE_LEN // CBLOCK, 1, 1, CBLOCK, wide),
            lambda h, i, meta: (0, (h // per) ^ meta[1], 0, 0, h % per),
        ),
        pl.BlockSpec(
            (CACHE_LEN // CBLOCK, 1, 1, CBLOCK, wide),
            lambda h, i, meta: (0, (h // per) ^ meta[1], 1, 0, h % per),
        ),
    ]


def attend(meta, qkv, own_k, own_v, pair=4):
    width = qkv.shape[1] // 3
    heads = width // HD
    wide = pair * HD
    row = pl.BlockSpec((TQ, wide), lambda h, i, meta: (i, h))
    area = L * 1600 * width
    return pl.pallas_call(
        functools.partial(attend_kernel, pair=pair),
        grid_spec=pltpu.PrefetchScalarGridSpec(
            num_scalar_prefetch=1,
            grid=(heads // pair, L // TQ),
            in_specs=attention_specs(heads, pair)[:5],
            out_specs=[row, row],
            scratch_shapes=[pltpu.VMEM((TQ // QBLOCK, KR * CBLOCK, wide), BF16)] * 2
            + [pltpu.VMEM((pair, L // TK, TQ, TK), F32), pltpu.VMEM((pair, TQ, KR * CBLOCK), F32)],
        ),
        out_shape=[jax.ShapeDtypeStruct((L, width), F32)] * 2,
        compiler_params=pltpu.CompilerParams(vmem_limit_bytes=60 * MIB),
        cost_estimate=pl.CostEstimate(flops=12 * area, bytes_accessed=30 * MIB, transcendentals=area // HD),
        name="attend",
    )(meta, qkv, qkv, qkv, own_k, own_v)


def attend_other(meta, qkv, fetched, partial, lse, pair=4):
    width = qkv.shape[1] // 3
    heads = width // HD
    wide = pair * HD
    row = pl.BlockSpec((TQ, wide), lambda h, i, meta: (i, h))
    specs = attention_specs(heads, pair)
    return pl.pallas_call(
        functools.partial(attend_other_kernel, pair=pair),
        grid_spec=pltpu.PrefetchScalarGridSpec(
            num_scalar_prefetch=1,
            grid=(heads // pair, L // TQ),
            in_specs=[specs[0], specs[5], specs[6], row, row],
            out_specs=[row, row],
            scratch_shapes=[pltpu.VMEM((TQ // QBLOCK, KR * CBLOCK, wide), BF16)] * 2,
        ),
        out_shape=[jax.ShapeDtypeStruct((L, width), BF16), jax.ShapeDtypeStruct((L, width), F32)],
        compiler_params=pltpu.CompilerParams(vmem_limit_bytes=60 * MIB),
        cost_estimate=pl.CostEstimate(
            flops=4 * L * 256 * width, bytes_accessed=30 * MIB, transcendentals=L * 256 * heads
        ),
        name="attend_other",
    )(meta, qkv, fetched, fetched, partial, lse)


def attend_back(meta, qkv, own_k, own_v, fetched, grad_context, context, lse, pair=4):
    width = context.shape[1]
    heads = width // HD
    wide = pair * HD
    row = pl.BlockSpec((TQ, wide), lambda h, i, meta: (i, h))
    col = pl.BlockSpec((L, wide), lambda h, i, meta: (0, h))
    area = L * 1900 * width
    return pl.pallas_call(
        functools.partial(attend_back_kernel, pair=pair),
        grid_spec=pltpu.PrefetchScalarGridSpec(
            num_scalar_prefetch=1,
            grid=(heads // pair, L // TQ),
            in_specs=attention_specs(heads, pair) + [row, row, row],
            out_specs=[row, col, col],
            scratch_shapes=[pltpu.VMEM((TQ // QBLOCK, 2 * KR * CBLOCK, wide), BF16)] * 2
            + [pltpu.VMEM((L, wide), F32)] * 2,
        ),
        out_shape=[jax.ShapeDtypeStruct((L, width), BF16)] * 3,
        compiler_params=pltpu.CompilerParams(vmem_limit_bytes=60 * MIB),
        cost_estimate=pl.CostEstimate(flops=12 * area, bytes_accessed=40 * MIB, transcendentals=area // HD),
        name="attend_back",
    )(meta, qkv, qkv, qkv, own_k, own_v, fetched, fetched, grad_context, context, lse)


def project_kernel(x_ref, gain_ref, w_ref, normed_ref, qkv_ref):
    rows = x_ref[...].astype(F32)
    scale = lax.rsqrt(jnp.mean(rows * rows, axis=1, keepdims=True) + EPS)
    normed_ref[...] = (rows * scale * gain_ref[...]).astype(BF16)
    left = normed_ref[...]

    def chunk(c, carry):
        cs = pl.ds(pl.multiple_of(c * 512, 512), 512)
        qkv_ref[:, cs] = mm(left, w_ref[:, cs]).astype(BF16)
        return carry

    lax.fori_loop(0, qkv_ref.shape[1] // 512, chunk, 0)


def project(x, gain, weights):
    width = x.shape[1]
    cols = 3 * width
    row = lambda n: pl.BlockSpec((ROWS, n), lambda i: (i, 0))
    whole = lambda n: pl.BlockSpec((width, n), lambda i: (0, 0))
    return pl.pallas_call(
        project_kernel,
        grid=(L // ROWS,),
        in_specs=[row(width), pl.BlockSpec((1, width), lambda i: (0, 0)), whole(cols)],
        out_specs=[row(width), row(cols)],
        out_shape=[jax.ShapeDtypeStruct((L, width), BF16), jax.ShapeDtypeStruct((L, cols), BF16)],
        compiler_params=pltpu.CompilerParams(vmem_limit_bytes=60 * MIB),
        cost_estimate=pl.CostEstimate(flops=2 * L * width * cols, bytes_accessed=26 * MIB, transcendentals=0),
        name="project",
    )(x, gain, weights)


def mix_kernel(x_ref, ctx_ref, gain_ref, w_ref, mixed_ref, normed_ref):
    mixed = x_ref[...].astype(F32) + mm(ctx_ref[...], w_ref[...], NT)
    mixed_ref[...] = mixed
    scale = lax.rsqrt(jnp.mean(mixed * mixed, axis=1, keepdims=True) + EPS)
    normed_ref[...] = (mixed * scale * gain_ref[...]).astype(BF16)


def mix(x, context, gain, weights):
    width = x.shape[1]
    row = pl.BlockSpec((ROWS, width), lambda i: (i, 0))
    return pl.pallas_call(
        mix_kernel,
        grid=(L // ROWS,),
        in_specs=[row, row, pl.BlockSpec((1, width), lambda i: (0, 0)), pl.BlockSpec((width, width), lambda i: (0, 0))],
        out_specs=[row, row],
        out_shape=[jax.ShapeDtypeStruct((L, width), F32), jax.ShapeDtypeStruct((L, width), BF16)],
        compiler_params=pltpu.CompilerParams(vmem_limit_bytes=60 * MIB),
        cost_estimate=pl.CostEstimate(flops=2 * L * width * width, bytes_accessed=22 * MIB, transcendentals=0),
        name="mix",
    )(x, context, gain, weights)


RING = 8
RIGHT = RING // 2
LEFT = RING - 1 - RIGHT


def ring_place(p):
    y = p // 4
    return (p + y * (7 - 2 * p)) * 2 + y


def meet(devices, me, spot):
    barrier = pltpu.get_barrier_semaphore()
    for d in range(1, devices):
        pl.semaphore_signal(
            barrier, inc=1, device_id=((me + d) % devices, spot), device_id_type=pl.DeviceIdType.MESH
        )
    pl.semaphore_signal(barrier, inc=1, device_id=(me, 1 - spot), device_id_type=pl.DeviceIdType.MESH)
    pl.semaphore_wait(barrier, devices)


def remote(src, dst, send, recv, device):
    return pltpu.make_async_remote_copy(
        src_ref=src, dst_ref=dst, send_sem=send, recv_sem=recv, device_id=device, device_id_type=pl.DeviceIdType.MESH
    )


UT = 256


def ffn_kernel(
    n_ref, g_ref, wg0, wg1, wu0, wu1, wd0, wd1, gain_ref, mixed_ref, wo_ref,
    share_ref, gg_ref, out_ref, gm_ref, br_ref, gc_ref,
    acc, gn, hid, duo, part, got, passed, keep, land,
    wo_buf, mixed_buf, out_buf, br_buf, gc_buf,
    pair_send, pair_recv, x_send, x_recv, wo_sem, mixed_sem, done_sem, *, devices,
):
    tile = pl.program_id(0)
    tiles = pl.num_programs(0)
    me = lax.axis_index("dp")
    spot = lax.axis_index("tensor")
    core = me % 2
    pair = (me + 1 - 2 * core, spot)
    peer = (me, 1 - spot)
    side = HT // 2
    width = n_ref.shape[1]
    wo_copy = pltpu.make_async_copy(wo_ref.at[:, pl.ds(0, width)], wo_buf, wo_sem)

    @pl.when(tile == 0)
    def _():
        barrier = pltpu.get_barrier_semaphore()
        for device in (pair, peer):
            pl.semaphore_signal(barrier, inc=1, device_id=device, device_id_type=pl.DeviceIdType.MESH)
        pl.semaphore_wait(barrier, 2)
        acc[...] = jnp.zeros_like(acc)
        gn[...] = jnp.zeros_like(gn)

    def to_pair(k):
        return remote(part.at[k % 2, :, 1 - core], got.at[k % 2], pair_send.at[k % 2], pair_recv.at[k % 2], pair)

    def to_peer(k):
        return remote(passed.at[k % 2], land.at[k % 4], x_send.at[k % 2], x_recv.at[k % 4], peer)

    def join(k):
        slot = (k + 2) % 2
        total = (got[slot].astype(F32) + part[slot, :, core].astype(F32)).astype(BF16)
        for m in range(3):
            passed[slot, :, :, m * side : (m + 1) * side] = total[:, :, m * HT + side : (m + 1) * HT]
            keep[(k + 4) % 4, :, :, m * side : (m + 1) * side] = total[:, :, m * HT : m * HT + side]

    def settle(k):
        slot = (jnp.maximum(k, -1) + 4) % 4
        total = (keep[slot].astype(F32) + land[slot].astype(F32)).astype(BF16)
        total = total.reshape(share_ref.shape[0], 3 * side)
        for m in range(3):
            place = pl.multiple_of((m * tiles + jnp.maximum(k, 0)) * side, side)
            share_ref[:, pl.ds(place, side)] = total[:, m * side : (m + 1) * side]

    wgu = jnp.concatenate([wg0[...], wg1[...], wu0[...], wu1[...]], axis=1)
    wd = jnp.concatenate([wd0[...], wd1[...]], axis=1)

    def chunk(r):
        rs = pl.ds(r * ROWS, ROWS)
        both = mm(n_ref[rs, :], wgu)
        grad_hidden = mm(g_ref[rs, :], wd)
        gate, up = both[:, :HT], both[:, HT:]
        sigma = 1.0 / (1.0 + jnp.exp(-gate))
        silu = gate * sigma
        hidden = (silu * up).astype(BF16)
        grad_gate = grad_hidden * up * (sigma * (1.0 + gate * (1.0 - sigma)))
        grads = jnp.concatenate([grad_gate.astype(BF16), (grad_hidden * silu).astype(BF16)], axis=1)
        acc[rs, :] += mm(hidden, wd, NT)
        gn[rs, :] += mm(grads, wgu, NT)
        hid[rs, :] = hidden
        duo[rs, :] = grads

    @pl.when(tile > 2)
    def _():
        to_peer(tile - 3).wait()

    settle(tile - 3)
    for r in range(L // ROWS):
        chunk(r)

    @pl.when(tile > 0)
    def _():
        to_pair(tile - 1).wait()

    join(tile - 1)
    slot = tile % 2
    shape = part.shape[1:4]
    part[slot, :, :, :, : 2 * HT] = mm(n_ref[...], duo[...], TN).astype(BF16).reshape(shape + (2 * HT,))
    part[slot, :, :, :, 2 * HT :] = mm(g_ref[...], hid[...], TN).astype(BF16).reshape(shape + (HT,))
    to_pair(tile).start()

    @pl.when(tile > 0)
    def _():
        to_peer(tile - 1).start()

    def rows_of(t):
        return pl.ds(pl.multiple_of(t * UT, UT), UT)

    def fetch(t):
        return pltpu.make_async_copy(mixed_ref.at[rows_of(t), :], mixed_buf.at[t % 2], mixed_sem.at[t % 2])

    def write(t):
        sources = [out_buf.at[t % 2], gn.at[rows_of(t), :], br_buf.at[t % 2], gc_buf.at[t % 2]]
        return [
            pltpu.make_async_copy(source, ref.at[rows_of(t), :], done_sem.at[i, t % 2])
            for i, (source, ref) in enumerate(zip(sources, [out_ref, gm_ref, br_ref, gc_ref]))
        ]

    def unmix(t, carry):
        @pl.when(t < L // UT - 1)
        def _():
            fetch(t + 1).start()

        fetch(t).wait()

        @pl.when(t > 1)
        def _():
            for copy in write(t - 2):
                copy.wait()

        rs = rows_of(t)
        now = t % 2
        mixed = mixed_buf[now]
        grad = gn[rs, :]
        scale = lax.rsqrt(jnp.mean(mixed * mixed, axis=1, keepdims=True) + EPS)
        unit = mixed * scale
        inner = grad * gain_ref[...]
        back = scale * (inner - unit * jnp.mean(inner * unit, axis=1, keepdims=True))
        grad_mixed = g_ref[rs, :].astype(F32) + back
        out_buf[now] = (mixed + acc[rs, :]).astype(BF16)
        gn[rs, :] = grad_mixed
        branch = grad_mixed.astype(BF16)
        br_buf[now] = branch
        gc_buf[now] = mm(branch, wo_buf[...]).astype(BF16)
        gg_ref[...] += jnp.sum(grad * unit, axis=0, keepdims=True)
        for copy in write(t):
            copy.start()
        return carry

    @pl.when(tile == tiles - 1)
    def _():
        wo_copy.start()
        fetch(0).start()
        gg_ref[...] = jnp.zeros_like(gg_ref)
        to_peer(tile - 2).wait()
        settle(tile - 2)
        wo_copy.wait()
        lax.fori_loop(0, 4, unmix, 0)
        to_pair(tile).wait()
        join(tile)
        to_peer(tile).start()
        lax.fori_loop(4, L // UT, unmix, 0)
        to_peer(tile - 1).wait()
        settle(tile - 1)
        to_peer(tile).wait()
        settle(tile)
        for t in (L // UT - 2, L // UT - 1):
            for copy in write(t):
                copy.wait()


def ffn(normed, cotangent, weights, gain, mixed, width, hidden, devices):
    once = pl.Buffered(1)
    tiles = hidden // HT
    side = HT // 2
    rows = width // devices
    chips = devices // 2
    lead = width // side
    part = lambda k: pl.BlockSpec((width, side), lambda j: (0, lead + k * tiles + j))
    whole = pl.BlockSpec((L, width), lambda j: (0, 0), pipeline_mode=once)
    fixed = lambda shape: pl.BlockSpec(shape, lambda j: (0, 0), pipeline_mode=once)
    hbm = pl.BlockSpec(memory_space=pltpu.HBM)
    dma = pltpu.SemaphoreType.DMA
    tile = lambda kind: pltpu.VMEM((2, UT, width), kind)
    return pl.pallas_call(
        functools.partial(ffn_kernel, devices=devices),
        grid=(tiles,),
        in_specs=[whole, whole] + [part(k) for k in range(6)] + [fixed((1, width)), hbm, hbm],
        out_specs=[fixed((width // 2, 3 * hidden // 2)), fixed((1, width)), hbm, hbm, hbm, hbm],
        out_shape=[
            jax.ShapeDtypeStruct((width // 2, 3 * hidden // 2), BF16),
            jax.ShapeDtypeStruct((1, width), F32),
            jax.ShapeDtypeStruct((L, width), BF16),
            jax.ShapeDtypeStruct((L, width), F32),
            jax.ShapeDtypeStruct((L, width), BF16),
            jax.ShapeDtypeStruct((L, width), BF16),
        ],
        scratch_shapes=[
            pltpu.VMEM((L, width), F32), pltpu.VMEM((L, width), F32),
            pltpu.VMEM((L, HT), BF16), pltpu.VMEM((L, 2 * HT), BF16),
            pltpu.VMEM((2, chips, 2, rows, 3 * HT), BF16),
            pltpu.VMEM((2, chips, rows, 3 * HT), BF16),
            pltpu.VMEM((2, chips, rows, 3 * side), BF16),
            pltpu.VMEM((4, chips, rows, 3 * side), BF16),
            pltpu.VMEM((4, chips, rows, 3 * side), BF16),
            pltpu.VMEM((width, width), BF16), tile(F32), tile(BF16), tile(BF16), tile(BF16),
            dma((2,)), dma((2,)), dma((2,)), dma((4,)), dma, dma((2,)), dma((4, 2)),
        ],
        compiler_params=pltpu.CompilerParams(collective_id=2, has_side_effects=True, vmem_limit_bytes=61 * MIB),
        cost_estimate=pl.CostEstimate(
            flops=18 * L * width * hidden, bytes_accessed=60 * MIB, transcendentals=L * hidden
        ),
        name="ffn",
    )(normed, cotangent, *([weights] * 6), gain, mixed, weights)


FT = 256


def finish_kernel(
    x_ref, gm_ref, n_ref, ctx_ref, br_ref, dq_ref, dk_ref, dv_ref, w_ref, gain_ref, gain_two_ref,
    gt_ref, sums_ref, share_ref,
    n_buf, ctx_buf, br_buf, dq_buf, dk_buf, dv_buf, w_buf, x_buf, gm_buf, gt_buf,
    part, got, land, across, gains, gain_land,
    load_sem, x_sem, gm_sem, gt_sem, gt_recv, pair_send, pair_recv, ring_send, ring_recv, x_send, x_recv, g_send, g_recv,
    *, devices,
):
    me = lax.axis_index("dp")
    spot = lax.axis_index("tensor")
    core = me % 2
    z, y = me // 4, (me // 2) % 2
    place = z + y * (7 - 2 * z)
    width = n_buf.shape[1]
    half = width // 2
    rows = part.shape[2]
    loads = [
        pltpu.make_async_copy(src, dst, load_sem.at[i])
        for i, (src, dst) in enumerate(
            [
                (ctx_ref, ctx_buf), (br_ref, br_buf), (n_ref, n_buf), (dv_ref, dv_buf),
                (dk_ref, dk_buf), (dq_ref, dq_buf), (w_ref.at[:, pl.ds(0, 3 * width)], w_buf),
            ]
        )
    ]
    for copy in loads:
        copy.start()
    meet(devices, me, spot)

    def tile_in(t, slot):
        rs = pl.ds(pl.multiple_of(t * FT, FT), FT)
        return [
            pltpu.make_async_copy(x_ref.at[rs, :], x_buf.at[slot], x_sem.at[slot]),
            pltpu.make_async_copy(gm_ref.at[rs, :], gm_buf.at[slot], gm_sem.at[slot]),
        ]

    held = L // FT // 2

    def give(k, slot):
        rs = pl.ds(pl.multiple_of(k * FT, FT), FT)
        return remote(
            gt_buf.at[slot], gt_ref.at[spot, rs, :], gt_sem.at[slot], gt_recv.at[k], (me, 1 - spot)
        )

    def keep(k, slot):
        rs = pl.ds(pl.multiple_of(k * FT, FT), FT)
        return pltpu.make_async_copy(gt_buf.at[slot], gt_ref.at[spot, rs, :], gt_sem.at[slot])

    def tile_of(k):
        return (k + held * (1 - spot)) % (2 * held)

    for copy in tile_in(tile_of(0), 0):
        copy.start()

    pair = (me + 1 - 2 * core, spot)

    def column(m, h):
        return (m // 2) * 2 * width + h * width + (m % 2) * half

    def to_pair(m, h):
        cs = pl.ds(column(m, h), half)
        return remote(
            part.at[:, 1 - core, :, cs], got.at[:, :, cs], pair_send.at[m, h], pair_recv.at[m, h], pair
        )

    def product(m, left, right):
        for h in range(2):
            value = mm(left[...], right[:, h * half : (h + 1) * half], TN).astype(BF16)
            part[:, :, :, column(m, h) : column(m, h) + half] = value.reshape(part.shape[0], 2, rows, half)
            to_pair(m, h).start()

    def join(m, h):
        to_pair(m, h).wait_recv()
        cs = pl.ds(column(m, h), half)
        got[:, :, cs] = (got[:, :, cs].astype(F32) + part[:, core, :, cs].astype(F32)).astype(BF16)

    neighbours = [(place + 1) % RING, (place + RING - 1) % RING]

    def held_block(g, direction, s):
        p = (place + 2 * RING - 1 - s) % RING if direction == 0 else (place + 1 + s) % RING
        return got.at[ring_place(p), :, pl.ds((2 * g + direction) * width, width)]

    def hop(g, direction, s):
        to = ring_place(neighbours[direction]) * 2 + core
        return remote(
            held_block(g, direction, s), land.at[g, direction, s],
            ring_send.at[g, direction, s], ring_recv.at[g, direction, s], (to, spot),
        )

    def advance(g, s, more=True):
        for direction in range(2):
            hop(g, direction, s).wait_recv()
            block = held_block(g, direction, s + 1)
            block[...] = (block[...].astype(F32) + land[g, direction, s].astype(F32)).astype(BF16)
            if more:
                hop(g, direction, s + 1).start()

    def launch(g):
        for h in range(2):
            join(2 * g, h)
            join(2 * g + 1, h)
            hop(g, h, 0).start()

    def finish_rows(t, slot, k):
        for copy in tile_in(t, slot):
            copy.wait()
        rs = pl.ds(pl.multiple_of(t * FT, FT), FT)
        grad = mm(dq_buf[rs, :], w_buf[:, :width], NT)
        grad += mm(dk_buf[rs, :], w_buf[:, width : 2 * width], NT)
        grad += mm(dv_buf[rs, :], w_buf[:, 2 * width :], NT)
        values = x_buf[slot].astype(F32)
        scale = lax.rsqrt(jnp.mean(values * values, axis=1, keepdims=True) + EPS)
        unit = values * scale
        inner = grad * gain_ref[...]
        back = scale * (inner - unit * jnp.mean(inner * unit, axis=1, keepdims=True))
        gt_buf[k] = (gm_buf[slot] + back).astype(BF16)
        gains[:1, :] += jnp.sum(grad * unit, axis=0, keepdims=True)

    def two_tiles(j, advances, give_away):
        for slot in (0, 1):
            k = 2 * j + slot
            if slot == 0 or give_away:
                for copy in tile_in(tile_of(k + 1), 1 - slot):
                    copy.start()
            else:

                @pl.when(j < held - 1)
                def _():
                    for copy in tile_in(tile_of(k + 1), 0):
                        copy.start()

            finish_rows(tile_of(k), slot, k)
            if give_away:
                give(k, k).start()
            else:
                keep(k - held, k).start()
        for g, s in advances:
            advance(g, s)

    gains[:1, :] = jnp.zeros((1, width), F32)
    gains[1:, :] = gain_two_ref[...]
    for i in (0, 1):
        loads[i].wait()
    product(0, br_buf, ctx_buf)
    for i in (2, 3):
        loads[i].wait()
    product(1, n_buf, dv_buf)
    launch(0)
    for i in (4, 5, 6):
        loads[i].wait()

    def theirs(j, carry):
        two_tiles(j, [(0, j)], True)
        return carry

    def ours(j, carry):
        two_tiles(j, [(0, j + 2), (1, j - 2)], False)
        return carry

    lax.fori_loop(0, held // 2, theirs, 0)
    product(2, n_buf, dk_buf)
    advance(0, 2)
    product(3, n_buf, dq_buf)
    advance(0, 3)
    launch(1)
    lax.fori_loop(held // 2, held, ours, 0)

    partners = [
        (me + 1 - 2 * core, spot),
        (me + 2 - 4 * y, spot),
        (me + 4 - 8 * (z % 2), spot),
        (me + 8 - 16 * (z // 2), spot),
        (me, 1 - spot),
    ]

    def add_gains(r):
        return remote(gains, gain_land.at[r], g_send.at[r], g_recv.at[r], partners[r])

    def gain_round(r):
        add_gains(r).wait()
        gains[...] = gains[...] + gain_land[r]
        if r < 4:
            add_gains(r + 1).start()

    own = ring_place(place)
    peer = (me, 1 - spot)

    def over(g):
        return remote(
            got.at[own, :, pl.ds((2 * g + 1) * width, width)], across.at[:, pl.ds(g * width, width)],
            x_send.at[g], x_recv.at[g], peer,
        )

    add_gains(0).start()
    advance(0, 6, False)
    over(0).start()
    advance(1, 2)
    gain_round(0)
    advance(1, 3)
    gain_round(1)
    advance(1, 4)
    gain_round(2)
    advance(1, 5)
    gain_round(3)
    advance(1, 6, False)
    over(1).start()
    gain_round(4)
    sums_ref[...] = gains[...]
    for g in range(2):
        over(g).wait_recv()
        cs = pl.ds(g * width, width)
        share_ref[:, cs] = got[own, :, pl.ds(2 * g * width, width)].astype(F32) + across[:, cs].astype(F32)
    for g in range(2):
        over(g).wait_send()
        for direction in range(2):
            for s in range(RING - 1):
                hop(g, direction, s).wait_send()
    for m in range(4):
        for h in range(2):
            to_pair(m, h).wait_send()
    for k in range(held):
        give(k, k).wait()
        keep(k, k + held).wait()


def finish(x, grad_mixed, normed, context, branch, dq, dk, dv, weights, gain, gain_two_part, devices):
    width = x.shape[1]
    rows = width // devices
    anywhere = pl.BlockSpec(memory_space=pltpu.HBM)
    vmem = pl.BlockSpec(memory_space=pltpu.VMEM)
    dma = pltpu.SemaphoreType.DMA
    whole = pltpu.VMEM((L, width), BF16)
    return pl.pallas_call(
        functools.partial(finish_kernel, devices=devices),
        in_specs=[anywhere] * 9 + [vmem] * 2,
        out_specs=[anywhere, vmem, vmem],
        out_shape=[
            jax.ShapeDtypeStruct((2, L // 2, width), BF16),
            jax.ShapeDtypeStruct((2, width), F32),
            jax.ShapeDtypeStruct((rows, 2 * width), F32),
        ],
        scratch_shapes=[
            whole, whole, whole, whole, whole, whole, pltpu.VMEM((width, 3 * width), BF16),
            pltpu.VMEM((2, FT, width), BF16), pltpu.VMEM((2, FT, width), F32), pltpu.VMEM((L // FT, FT, width), BF16),
            pltpu.VMEM((RING, 2, rows, 4 * width), BF16),
            pltpu.VMEM((RING, rows, 4 * width), BF16),
            pltpu.VMEM((2, 2, RING - 1, rows, width), BF16),
            pltpu.VMEM((rows, 2 * width), BF16),
            pltpu.VMEM((2, width), F32), pltpu.VMEM((5, 2, width), F32),
            dma((7,)), dma((2,)), dma((2,)), dma((2 * (L // FT // 2),)), dma((L // FT // 2,)), dma((4, 2)), dma((4, 2)),
            dma((2, 2, RING - 1)), dma((2, 2, RING - 1)), dma((2,)), dma((2,)), dma((5,)), dma((5,)),
        ],
        compiler_params=pltpu.CompilerParams(collective_id=1, has_side_effects=True, vmem_limit_bytes=60 * MIB),
        cost_estimate=pl.CostEstimate(flops=14 * L * width * width, bytes_accessed=80 * MIB, transcendentals=0),
        name="finish",
    )(x, grad_mixed, normed, context, branch, dq, dk, dv, weights, gain, gain_two_part)


def pick_kernel(table, held_ref, sent_ref, sems):
    def copy(i):
        return pltpu.make_async_copy(held_ref.at[table[i]], sent_ref.at[i], sems.at[i])

    for i in range(sent_ref.shape[0]):
        copy(i).start()
    for i in range(sent_ref.shape[0]):
        copy(i).wait()


def pick_rows(table, held):
    count = held.shape[0]
    return pl.pallas_call(
        pick_kernel,
        grid_spec=pltpu.PrefetchScalarGridSpec(
            num_scalar_prefetch=1,
            grid=(),
            in_specs=[pl.BlockSpec(memory_space=pl.ANY)],
            out_specs=pl.BlockSpec(memory_space=pltpu.VMEM),
            scratch_shapes=[pltpu.SemaphoreType.DMA((count,))],
        ),
        out_shape=jax.ShapeDtypeStruct(held.shape, held.dtype),
        compiler_params=pltpu.CompilerParams(vmem_limit_bytes=60 * MIB),
        cost_estimate=pl.CostEstimate(flops=0, bytes_accessed=2 * held.size * 2, transcendentals=0),
        name="pick_rows",
    )(table, held)


def spread_kernel(
    tok_ref, ck_ref, cv_ref, small_ref, extra_ref, big_ref,
    x_ref, ok_ref, ov_ref, held_ref, first_ref, second_ref,
    tok_buf, k_buf, v_buf, local_sem, x_send, x_recv, all_send, all_recv, ring_send, ring_recv, pair_send, pair_recv,
):
    me = lax.axis_index("dp")
    spot = lax.axis_index("tensor")
    peer = 1 - spot
    devices = held_ref.shape[0]
    rows, cols = small_ref.shape[0], small_ref.shape[1] // 3
    core = me % 2
    z, y = me // 4, (me // 2) % 2
    place = z + y * (7 - 2 * z)

    def at_place(p):
        yy = p // 4
        return (p + yy * (7 - 2 * p)) * 4 + yy * 2

    def target(dp, tensor):
        return (dp, tensor)

    barrier = pltpu.get_barrier_semaphore()
    for d in range(1, devices):
        pl.semaphore_signal(barrier, inc=1, device_id=target((me + d) % devices, spot), device_id_type=pl.DeviceIdType.MESH)
    pl.semaphore_signal(barrier, inc=1, device_id=target(me, peer), device_id_type=pl.DeviceIdType.MESH)
    pl.semaphore_wait(barrier, devices)

    def remote(src, dst, send, recv, device):
        return pltpu.make_async_remote_copy(
            src_ref=src, dst_ref=dst, send_sem=send, recv_sem=recv,
            device_id=device, device_id_type=pl.DeviceIdType.MESH,
        )

    mine = pl.multiple_of(me * rows, rows)
    across = target(me, peer)
    weight_copies = []
    for i in range(3):
        weight_copies.append(
            remote(
                small_ref.at[:, pl.ds(i * cols, cols)],
                first_ref.at[pl.ds(mine, rows), pl.ds((2 * i + 1) * cols, cols)],
                x_send.at[i], x_recv.at[i], across,
            )
        )
    for copy in weight_copies:
        copy.start()
    for i in range(3):
        first_ref[pl.ds(mine, rows), pl.ds(2 * i * cols, cols)] = small_ref[:, pl.ds(i * cols, cols)]
    first_ref[pl.ds(mine, rows), pl.ds(6 * cols, HD)] = extra_ref[...]

    loads = [
        pltpu.make_async_copy(tok_ref.at[spot], tok_buf, local_sem.at[0]),
        pltpu.make_async_copy(ck_ref.at[spot], k_buf, local_sem.at[1]),
        pltpu.make_async_copy(cv_ref.at[spot], v_buf, local_sem.at[2]),
    ]
    stores = [
        pltpu.make_async_copy(tok_buf, x_ref.at[spot], local_sem.at[3]),
        pltpu.make_async_copy(k_buf, ok_ref.at[spot], local_sem.at[4]),
        pltpu.make_async_copy(v_buf, ov_ref.at[spot], local_sem.at[5]),
    ]
    for copy in loads:
        copy.start()

    x_copies = [remote(tok_ref.at[peer], x_ref.at[spot], x_send.at[3], x_recv.at[3], across)]
    wide = big_ref.shape[1]
    hidden = (wide - cols) // 3
    starts = [(0, cols)] + [(cols + i * hidden, hidden) for i in range(3)]
    own_cols = []
    for i, (start, size) in enumerate(starts):
        base = 2 * start
        own_cols.append(pltpu.make_async_copy(
            big_ref.at[:, pl.ds(start, size)], second_ref.at[:, pl.ds(base, size)], local_sem.at[6 + i]))
        x_copies.append(remote(
            big_ref.at[:, pl.ds(start, size)], second_ref.at[:, pl.ds(base + size, size)],
            x_send.at[4 + i], x_recv.at[4 + i], across))
    x_copies.append(remote(ck_ref.at[peer], ok_ref.at[spot], x_send.at[8], x_recv.at[8], across))
    x_copies.append(remote(cv_ref.at[peer], ov_ref.at[spot], x_send.at[9], x_recv.at[9], across))
    for copy in x_copies + own_cols:
        copy.start()

    def to_device(d, dst_dp):
        chunk = pl.ds(pl.multiple_of(dst_dp * CBLOCK, CBLOCK), CBLOCK)
        dst = target(dst_dp, spot)
        return [
            remote(ck_ref.at[:, chunk, :], held_ref.at[me, :, 0], all_send.at[0, d], all_recv.at[0, d], dst),
            remote(cv_ref.at[:, chunk, :], held_ref.at[me, :, 1], all_send.at[1, d], all_recv.at[1, d], dst),
        ]

    for copy in weight_copies:
        copy.wait_recv()

    def block(p, c):
        return first_ref.at[pl.ds(pl.multiple_of((at_place(p) + c) * rows, rows), rows), :]

    ahead = (place + 1) % RING
    behind = (place + RING - 1) % RING

    def hop(s, direction):
        p = (place + RING - (s - 1)) % RING if direction == 0 else (place + s - 1) % RING
        to = ahead if direction == 0 else behind
        k = (s - 1) * 2 + direction
        return remote(block(p, core), block(p, core), ring_send.at[k], ring_recv.at[k], target(at_place(to) + core, spot))

    def to_pair(i, p):
        return remote(block(p, core), block(p, core), pair_send.at[i], pair_recv.at[i], target(at_place(place) + 1 - core, spot))

    hops = [hop(1, 0), hop(1, 1)]
    for copy in hops:
        copy.start()
    pairs = [to_pair(0, place)]
    pairs[0].start()
    copies = []
    for d in range(1, devices):
        for copy in to_device(d, (me + d) % devices):
            copy.start()
            copies.append(copy)
    chunk = pl.ds(pl.multiple_of(me * CBLOCK, CBLOCK), CBLOCK)
    kept = [
        pltpu.make_async_copy(ck_ref.at[:, chunk, :], held_ref.at[me, :, 0], local_sem.at[10]),
        pltpu.make_async_copy(cv_ref.at[:, chunk, :], held_ref.at[me, :, 1], local_sem.at[11]),
    ]
    for copy in kept:
        copy.start()
    for load, store in zip(loads, stores):
        load.wait()
        store.start()
    for s in range(1, RIGHT + 1):
        for direction in range(2):
            if direction == 1 and s > LEFT:
                continue
            hops[(s - 1) * 2 + direction].wait_recv()
            p = (place + RING - s) % RING if direction == 0 else (place + s) % RING
            if s < (RIGHT if direction == 0 else LEFT):
                nxt = hop(s + 1, direction)
                nxt.start()
                hops.append(nxt)
            pair = to_pair(len(pairs), p)
            pair.start()
            pairs.append(pair)
    for copy in weight_copies + hops:
        copy.wait_send()
    for copy in pairs + x_copies + copies:
        copy.wait()
    for copy in stores + own_cols + kept:
        copy.wait()


def spread(tokens, cache_keys, cache_values, small, extra, big, devices):
    micro, shard_len, width = tokens.shape
    rows, cols = small.shape[0], small.shape[1] // 3
    anywhere = pl.BlockSpec(memory_space=pltpu.HBM)
    vmem = pl.BlockSpec(memory_space=pltpu.VMEM)
    dma = pltpu.SemaphoreType.DMA
    return pl.pallas_call(
        spread_kernel,
        in_specs=[anywhere, anywhere, anywhere, vmem, vmem, vmem],
        out_specs=[anywhere, anywhere, anywhere, anywhere, vmem, anywhere],
        out_shape=[
            jax.ShapeDtypeStruct((2, shard_len, width), BF16),
            jax.ShapeDtypeStruct((2, CACHE_LEN, cols), BF16),
            jax.ShapeDtypeStruct((2, CACHE_LEN, cols), BF16),
            jax.ShapeDtypeStruct((devices, micro, 2, CBLOCK, cols), BF16),
            jax.ShapeDtypeStruct((rows * devices, 6 * cols + HD), BF16),
            jax.ShapeDtypeStruct((rows, 2 * big.shape[1]), BF16),
        ],
        scratch_shapes=[
            pltpu.VMEM((shard_len, width), BF16),
            pltpu.VMEM((CACHE_LEN, cols), BF16),
            pltpu.VMEM((CACHE_LEN, cols), BF16),
            dma((12,)), dma((10,)), dma((10,)), dma((2, devices)), dma((2, devices)),
            dma((RING - 1,)), dma((RING - 1,)), dma((RING,)), dma((RING,)),
        ],
        compiler_params=pltpu.CompilerParams(collective_id=0, has_side_effects=True, vmem_limit_bytes=60 * MIB),
        cost_estimate=pl.CostEstimate(flops=0, bytes_accessed=300 * MIB, transcendentals=0),
        name="spread",
    )(tokens, cache_keys, cache_values, small, extra, big)


def swap(values):
    return lax.ppermute(values, "tensor", [(0, 1), (1, 0)])


def sequence_body(
    tokens, gain_attn, w_query, w_key, w_value, w_out, gain_ffn, w_gate, w_up, w_down,
    cache_keys, cache_values, prefix, partner, own_blocks, partner_blocks, grad_out,
):
    micro, shard_len, width = tokens.shape
    devices = lax.axis_size("dp")
    seqs = micro * devices
    rows_held, cols = w_query.shape
    hidden_held = w_gate.shape[1]
    hidden = 2 * hidden_held
    spot = lax.axis_index("tensor")
    exchange = functools.partial(lax.all_to_all, axis_name="tensor", split_axis=0, concat_axis=0, tiled=True)
    chunks = CACHE_LEN // CBLOCK

    small = jnp.concatenate([w_query, w_key, w_value], axis=1)
    partner_column = jnp.zeros((rows_held, 1), BF16).at[:micro, 0].set(partner.astype(BF16))
    extra = jnp.concatenate(
        [gain_attn[:, None], gain_ffn[:, None], partner_column, jnp.zeros((rows_held, HD - 3), BF16)], axis=1
    )
    big = jnp.concatenate([w_out.T, w_gate, w_up, w_down.T], axis=1)
    x, own_k, own_v, held, first_all, second_rows = spread(
        tokens, cache_keys, cache_values, small, extra, big, devices
    )
    x = x.reshape(L, width)
    theirs = swap(lax.dynamic_index_in_dim(grad_out, 1 - spot, 0, keepdims=False))
    mine = lax.dynamic_index_in_dim(grad_out, spot, 0, keepdims=False)
    cotangent = jnp.where(spot == 0, jnp.concatenate([mine, theirs], 0), jnp.concatenate([theirs, mine], 0))
    second_all = lax.all_gather(second_rows, "dp", axis=0, tiled=True)

    tail = lax.optimization_barrier(first_all[:, 3 * width :])
    gains = mm((jnp.arange(2)[:, None] == jnp.arange(HD)[None, :]).astype(BF16), tail, NT)
    gain_one, gain_two = gains[:1], gains[1:]
    table = tail[:, 2].reshape(devices, rows_held)[:, :micro].reshape(seqs).astype(jnp.int32)
    sent = pick_rows(table, held.reshape(seqs, 2 * CBLOCK, cols))
    fetched = lax.all_to_all(sent, ("dp", "tensor"), split_axis=0, concat_axis=0, tiled=True)
    fetched = fetched.reshape(chunks, 2, 2, CBLOCK, cols)

    meta = jnp.concatenate(
        [
            prefix[spot][None], spot[None].astype(jnp.int32),
            own_blocks[spot].reshape(-1), partner_blocks[spot].reshape(-1),
        ]
    )
    normed, qkv = project(x, gain_one, first_all)
    partial, partial_lse = attend(meta, qkv, own_k, own_v)
    context, lse = attend_other(meta, qkv, fetched, partial, partial_lse)
    mixed, normed_two = mix(x, context, gain_two, second_all)
    ffn_grads, gain_part_two, out, grad_mixed, branch, grad_context = ffn(
        normed_two, cotangent, second_all, gain_two, mixed, width, hidden, devices
    )
    ffn_share = lax.psum_scatter(
        ffn_grads, "dp", scatter_dimension=0, tiled=True,
        axis_index_groups=[list(range(c, devices, 2)) for c in range(2)],
    )
    out = exchange(out.reshape(2, shard_len, width))
    dq, dk, dv = attend_back(meta, qkv, own_k, own_v, fetched, grad_context, context, lse)
    dq, out = lax.optimization_barrier((dq, out))
    grad_tokens, gain_sums, attn_share = finish(
        x, grad_mixed, normed, context, branch, dq, dk, dv, first_all, gain_one, gain_part_two, devices
    )
    grad_tokens = grad_tokens.astype(F32)
    g_out, g_value, g_key, g_query = jnp.split(attn_share, 4, axis=1)
    g_gate, g_up, g_down = [
        ffn_share[:, i * hidden_held : (i + 1) * hidden_held].astype(F32) for i in range(3)
    ]
    return (
        out, grad_tokens, gain_sums[0], g_query, g_key, g_value, g_out.T, gain_sums[1], g_gate, g_up, g_down.T,
    )


def solution(mesh):
    in_specs = (
        P("dp", "tensor", None),
        P("dp"),
        P("dp", "tensor"),
        P("dp", "tensor"),
        P("dp", "tensor"),
        P("tensor", "dp"),
        P("dp"),
        P("dp", "tensor"),
        P("dp", "tensor"),
        P("tensor", "dp"),
        P("dp", None, "tensor"),
        P("dp", None, "tensor"),
        P("dp"),
        P("dp"),
        P("dp", None, None),
        P("dp", None, None),
        P("dp", "tensor", None),
    )
    out_specs = (
        P("dp", "tensor", None),
        P("dp", "tensor", None),
        P(),
        P("dp", "tensor"),
        P("dp", "tensor"),
        P("dp", "tensor"),
        P("tensor", "dp"),
        P(),
        P("dp", "tensor"),
        P("dp", "tensor"),
        P("tensor", "dp"),
    )
    whole = mesh.shape["tensor"] == 2 and mesh.shape["dp"] == CACHE_LEN // CBLOCK
    body = sequence_body if whole else tensor_body
    return jax.shard_map(body, mesh=mesh, in_specs=in_specs, out_specs=out_specs, check_vma=False)
```

```python
import functools

import jax
import jax.numpy as jnp
from jax import lax
from jax.experimental import pallas as pl
from jax.experimental.pallas import tpu as pltpu
from jax.sharding import PartitionSpec as P

HD = 128
L = 2048
CACHE_LEN = 1024
QBLOCK = 128
CBLOCK = 64
KR = 4
QROWS = 512


EPS = 1e-05
NEGATIVE = -1e30


def norm_rows(values, gain):
    scale_rows = lax.rsqrt(jnp.mean(values * values, axis=-1, keepdims=True) + EPS)
    return (values * scale_rows * gain, scale_rows)


def norm_back(grad_normed, values, scale_rows, gain):
    unit = values * scale_rows
    grad_unit = grad_normed * gain
    grad_values = scale_rows * (
        grad_unit - unit * jnp.mean(grad_unit * unit, axis=-1, keepdims=True)
    )
    return (grad_values, jnp.sum(grad_normed * unit, axis=0))


def inner_rows(left, right):
    return lax.dot_general(
        left, right, (((0,), (0,)), ((), ())), preferred_element_type=jnp.float32
    )


def outer_cols(left, right):
    return lax.dot_general(
        left, right, (((1,), (1,)), ((), ())), preferred_element_type=jnp.float32
    )


def memory_rows(cache_one, chosen, width):
    shaped = cache_one.reshape(CACHE_LEN // CBLOCK, CBLOCK, width)
    return jnp.take(shaped, chosen, axis=0)


def block_scores(query_block, keys_part, mem_part, first_row, limit):
    rows_here, heads_here, size = query_block.shape
    extent = keys_part.shape[0]
    local = jnp.einsum(
        "qhd,khd->hqk", query_block, keys_part, preferred_element_type=jnp.float32
    ) * size ** (-0.5)
    row_ids = first_row + jnp.arange(rows_here, dtype=jnp.int32)[:, None]
    key_ids = jnp.arange(extent, dtype=jnp.int32)[None, :]
    allowed = (key_ids <= row_ids) | (row_ids < limit) & (key_ids < limit)
    local = jnp.where(allowed[None], local, NEGATIVE)
    groups = mem_part.shape[0]
    grouped = query_block.reshape(groups, rows_here // groups, heads_here, size)
    remote = jnp.einsum(
        "bqhd,bkhd->hbqk", grouped, mem_part, preferred_element_type=jnp.float32
    ) * size ** (-0.5)
    return (local, remote.reshape(heads_here, rows_here, -1))


def attention_forward(query, keys, values, mem_keys, mem_values, limit):
    groups = QROWS // QBLOCK
    heads_here = query.shape[1]
    context_parts = []
    lse_parts = []
    for index in range(L // QROWS):
        first = index * QROWS
        extent = max(first + QROWS, L // 2)
        query_block = query[first : first + QROWS]
        mem_k = mem_keys[index * groups : (index + 1) * groups]
        mem_v = mem_values[index * groups : (index + 1) * groups]
        local, remote = block_scores(query_block, keys[:extent], mem_k, first, limit)
        top = jnp.maximum(jnp.max(local, axis=-1), jnp.max(remote, axis=-1))
        e_local = jnp.exp(local - top[..., None])
        e_remote = jnp.exp(remote - top[..., None])
        total = jnp.sum(e_local, axis=-1) + jnp.sum(e_remote, axis=-1)
        p_local = (e_local / total[..., None]).astype(jnp.bfloat16)
        p_remote = (
            (e_remote / total[..., None])
            .astype(jnp.bfloat16)
            .reshape(heads_here, groups, QBLOCK, -1)
        )
        part = jnp.einsum(
            "hqk,khd->qhd", p_local, values[:extent], preferred_element_type=jnp.float32
        )
        extra = jnp.einsum("hbqk,bkhd->bqhd", p_remote, mem_v, preferred_element_type=jnp.float32)
        context_parts.append(part + extra.reshape(part.shape))
        lse_parts.append(top + jnp.log(total))
    return (jnp.concatenate(context_parts, axis=0), lse_parts)


def attention_backward(query, keys, values, mem_keys, mem_values, limit, lse_parts, grad_context):
    groups = QROWS // QBLOCK
    length, heads_here, size = query.shape
    scale = size ** (-0.5)
    grad_query_parts = []
    grad_keys = jnp.zeros(query.shape, jnp.float32)
    grad_values = jnp.zeros(query.shape, jnp.float32)
    for index in range(L // QROWS):
        first = index * QROWS
        extent = max(first + QROWS, L // 2)
        query_block = query[first : first + QROWS]
        mem_k = mem_keys[index * groups : (index + 1) * groups]
        mem_v = mem_values[index * groups : (index + 1) * groups]
        local, remote = block_scores(query_block, keys[:extent], mem_k, first, limit)
        lse_block = lse_parts[index][..., None]
        p_local = jnp.exp(local - lse_block)
        p_remote = jnp.exp(remote - lse_block)
        grad_block = grad_context[first : first + QROWS]
        grouped_grad = grad_block.reshape(groups, QBLOCK, heads_here, size)
        dp_local = jnp.einsum(
            "qhd,khd->hqk", grad_block, values[:extent], preferred_element_type=jnp.float32
        )
        dp_remote = jnp.einsum(
            "bqhd,bkhd->hbqk", grouped_grad, mem_v, preferred_element_type=jnp.float32
        )
        dp_remote = dp_remote.reshape(heads_here, QROWS, -1)
        delta = jnp.sum(p_local * dp_local, axis=-1) + jnp.sum(p_remote * dp_remote, axis=-1)
        ds_local = (p_local * (dp_local - delta[..., None])).astype(jnp.bfloat16)
        ds_remote = (p_remote * (dp_remote - delta[..., None])).astype(jnp.bfloat16)
        ds_remote = ds_remote.reshape(heads_here, groups, QBLOCK, -1)
        dq_block = jnp.einsum(
            "hqk,khd->qhd", ds_local, keys[:extent], preferred_element_type=jnp.float32
        )
        dq_extra = jnp.einsum(
            "hbqk,bkhd->bqhd", ds_remote, mem_k, preferred_element_type=jnp.float32
        )
        grad_query_parts.append((dq_block + dq_extra.reshape(dq_block.shape)) * scale)
        dk_part = (
            jnp.einsum("hqk,qhd->khd", ds_local, query_block, preferred_element_type=jnp.float32)
            * scale
        )
        dv_part = jnp.einsum(
            "hqk,qhd->khd",
            p_local.astype(jnp.bfloat16),
            grad_block,
            preferred_element_type=jnp.float32,
        )
        grad_keys = grad_keys.at[:extent].add(dk_part)
        grad_values = grad_values.at[:extent].add(dv_part)
    return (jnp.concatenate(grad_query_parts, axis=0), grad_keys, grad_values)


def tensor_body(
    tokens,
    gain_attn,
    w_query,
    w_key,
    w_value,
    w_out,
    gain_ffn,
    w_gate,
    w_up,
    w_down,
    cache_keys,
    cache_values,
    prefix,
    partner,
    own_blocks,
    partner_blocks,
    grad_out,
):
    micro, shard_len, width = tokens.shape
    cols = w_query.shape[1]
    heads_local = cols // HD
    qblocks = L // QBLOCK
    mem_len = 2 * KR * CBLOCK
    piece_keys = lax.all_gather(cache_keys, "dp", axis=0, tiled=True)
    piece_values = lax.all_gather(cache_values, "dp", axis=0, tiled=True)
    count = piece_keys.shape[0]
    onehot = (partner[:, None] == jnp.arange(count, dtype=jnp.int32)[None, :]).astype(jnp.bfloat16)
    add_keys = jnp.einsum("mn,nkc->mkc", onehot, piece_keys, preferred_element_type=jnp.float32)
    add_values = jnp.einsum("mn,nkc->mkc", onehot, piece_values, preferred_element_type=jnp.float32)
    fetched_keys = add_keys.astype(jnp.bfloat16)
    fetched_values = add_values.astype(jnp.bfloat16)
    totals = (
        jnp.zeros((width, cols), jnp.float32),
        jnp.zeros((width, cols), jnp.float32),
        jnp.zeros((width, cols), jnp.float32),
        jnp.zeros((cols, width), jnp.float32),
        jnp.zeros((width, w_gate.shape[1]), jnp.float32),
        jnp.zeros((width, w_gate.shape[1]), jnp.float32),
        jnp.zeros((w_gate.shape[1], width), jnp.float32),
    )
    shares = tuple(
        (
            jnp.zeros(w.shape, jnp.float32)
            for w in (w_query, w_key, w_value, w_out, w_gate, w_up, w_down)
        )
    )
    gain_total_attn = jnp.zeros((width,), jnp.float32)
    gain_total_ffn = jnp.zeros((width,), jnp.float32)
    out_rows = []
    grad_rows = []
    for step in range(micro):
        fwd = (
            lax.all_gather(gain_attn, "dp", axis=0, tiled=True),
            lax.all_gather(w_query, "dp", axis=0, tiled=True),
            lax.all_gather(w_key, "dp", axis=0, tiled=True),
            lax.all_gather(w_value, "dp", axis=0, tiled=True),
            lax.all_gather(w_out, "dp", axis=1, tiled=True),
            lax.all_gather(gain_ffn, "dp", axis=0, tiled=True),
            lax.all_gather(w_gate, "dp", axis=0, tiled=True),
            lax.all_gather(w_up, "dp", axis=0, tiled=True),
            lax.all_gather(w_down, "dp", axis=1, tiled=True),
        )
        g_attn, wq_full, wk_full, wv_full, wo_full, g_ffn, wg_full, wu_full, wd_full = fwd
        limit = prefix[step]
        own_k = memory_rows(cache_keys[step], own_blocks[step], cols)
        par_k = memory_rows(fetched_keys[step], partner_blocks[step], cols)
        own_v = memory_rows(cache_values[step], own_blocks[step], cols)
        par_v = memory_rows(fetched_values[step], partner_blocks[step], cols)
        mem_keys = jnp.concatenate([own_k, par_k], axis=1).reshape(
            qblocks, mem_len, heads_local, HD
        )
        mem_values = jnp.concatenate([own_v, par_v], axis=1).reshape(
            qblocks, mem_len, heads_local, HD
        )
        token_rows = tokens[step].astype(jnp.float32)
        normed, scale_one = norm_rows(token_rows, g_attn.astype(jnp.float32))
        normed_all = lax.all_gather(normed.astype(jnp.bfloat16), "tensor", axis=0, tiled=True)
        query = (
            jnp.dot(normed_all, wq_full, preferred_element_type=jnp.float32)
            .astype(jnp.bfloat16)
            .reshape(L, heads_local, HD)
        )
        keys = (
            jnp.dot(normed_all, wk_full, preferred_element_type=jnp.float32)
            .astype(jnp.bfloat16)
            .reshape(L, heads_local, HD)
        )
        values = (
            jnp.dot(normed_all, wv_full, preferred_element_type=jnp.float32)
            .astype(jnp.bfloat16)
            .reshape(L, heads_local, HD)
        )
        context_full, lse_parts = attention_forward(
            query, keys, values, mem_keys, mem_values, limit
        )
        context = context_full.reshape(L, cols).astype(jnp.bfloat16)
        mixed = token_rows + lax.psum_scatter(
            jnp.dot(context, wo_full, preferred_element_type=jnp.float32),
            "tensor",
            scatter_dimension=0,
            tiled=True,
        )
        normed_two, scale_two = norm_rows(mixed, g_ffn.astype(jnp.float32))
        normed_two_all = lax.all_gather(
            normed_two.astype(jnp.bfloat16), "tensor", axis=0, tiled=True
        )
        gate = jnp.dot(normed_two_all, wg_full, preferred_element_type=jnp.float32)
        upward = jnp.dot(normed_two_all, wu_full, preferred_element_type=jnp.float32)
        sigma = jax.nn.sigmoid(gate)
        silu_gate = gate * sigma
        hidden = (silu_gate * upward).astype(jnp.bfloat16)
        out_rows.append(
            (
                mixed
                + lax.psum_scatter(
                    jnp.dot(hidden, wd_full, preferred_element_type=jnp.float32).astype(
                        jnp.bfloat16
                    ),
                    "tensor",
                    scatter_dimension=0,
                    tiled=True,
                ).astype(jnp.float32)
            ).astype(jnp.bfloat16)
        )
        bwd = (
            lax.all_gather(gain_attn, "dp", axis=0, tiled=True),
            lax.all_gather(w_query, "dp", axis=0, tiled=True),
            lax.all_gather(w_key, "dp", axis=0, tiled=True),
            lax.all_gather(w_value, "dp", axis=0, tiled=True),
            lax.all_gather(w_out, "dp", axis=1, tiled=True),
            lax.all_gather(gain_ffn, "dp", axis=0, tiled=True),
            lax.all_gather(w_gate, "dp", axis=0, tiled=True),
            lax.all_gather(w_up, "dp", axis=0, tiled=True),
            lax.all_gather(w_down, "dp", axis=1, tiled=True),
        )
        g_attn, wq_full, wk_full, wv_full, wo_full, g_ffn, wg_full, wu_full, wd_full = bwd
        grad_here = grad_out[step]
        grad_all = lax.all_gather(grad_here, "tensor", axis=0, tiled=True)
        d_down = inner_rows(hidden, grad_all)
        grad_hidden = outer_cols(grad_all, wd_full)
        grad_gate = (grad_hidden * upward * sigma * (1.0 + gate * (1.0 - sigma))).astype(
            jnp.bfloat16
        )
        grad_up = (grad_hidden * silu_gate).astype(jnp.bfloat16)
        d_gate = inner_rows(normed_two_all, grad_gate)
        d_up = inner_rows(normed_two_all, grad_up)
        grad_normed_two = lax.psum_scatter(
            outer_cols(grad_gate, wg_full) + outer_cols(grad_up, wu_full),
            "tensor",
            scatter_dimension=0,
            tiled=True,
        )
        grad_mixed_norm, gain_part_ffn = norm_back(
            grad_normed_two, mixed, scale_two, g_ffn.astype(jnp.float32)
        )
        grad_mixed = grad_here.astype(jnp.float32) + grad_mixed_norm
        branch_all = lax.all_gather(grad_mixed.astype(jnp.bfloat16), "tensor", axis=0, tiled=True)
        d_out = inner_rows(context, branch_all)
        grad_context = (
            outer_cols(branch_all, wo_full).astype(jnp.bfloat16).reshape(L, heads_local, HD)
        )
        grad_query, grad_keys, grad_values = attention_backward(
            query, keys, values, mem_keys, mem_values, limit, lse_parts, grad_context
        )
        grad_query = grad_query.reshape(L, cols).astype(jnp.bfloat16)
        grad_keys = grad_keys.reshape(L, cols).astype(jnp.bfloat16)
        grad_values = grad_values.reshape(L, cols).astype(jnp.bfloat16)
        d_query = inner_rows(normed_all, grad_query)
        d_key = inner_rows(normed_all, grad_keys)
        d_value = inner_rows(normed_all, grad_values)
        grad_normed = lax.psum_scatter(
            (
                outer_cols(grad_query, wq_full)
                + outer_cols(grad_keys, wk_full)
                + outer_cols(grad_values, wv_full)
            ).astype(jnp.bfloat16),
            "tensor",
            scatter_dimension=0,
            tiled=True,
        ).astype(jnp.float32)
        grad_token_norm, gain_part_attn = norm_back(
            grad_normed, token_rows, scale_one, g_attn.astype(jnp.float32)
        )
        grad_rows.append(grad_mixed + grad_token_norm)
        gain_total_attn = gain_total_attn + gain_part_attn
        gain_total_ffn = gain_total_ffn + gain_part_ffn
        totals = tuple(
            (
                held + fresh
                for held, fresh in zip(
                    totals, (d_query, d_key, d_value, d_out, d_gate, d_up, d_down)
                )
            )
        )
    shares = (
        lax.psum_scatter(
            totals[0].astype(jnp.bfloat16), "dp", scatter_dimension=0, tiled=True
        ).astype(jnp.float32),
        lax.psum_scatter(
            totals[1].astype(jnp.bfloat16), "dp", scatter_dimension=0, tiled=True
        ).astype(jnp.float32),
        lax.psum_scatter(
            totals[2].astype(jnp.bfloat16), "dp", scatter_dimension=0, tiled=True
        ).astype(jnp.float32),
        lax.psum_scatter(
            totals[3].astype(jnp.bfloat16), "dp", scatter_dimension=1, tiled=True
        ).astype(jnp.float32),
        lax.psum_scatter(
            totals[4].astype(jnp.bfloat16), "dp", scatter_dimension=0, tiled=True
        ).astype(jnp.float32),
        lax.psum_scatter(
            totals[5].astype(jnp.bfloat16), "dp", scatter_dimension=0, tiled=True
        ).astype(jnp.float32),
        lax.psum_scatter(
            totals[6].astype(jnp.bfloat16), "dp", scatter_dimension=1, tiled=True
        ).astype(jnp.float32),
    )
    gain_attn_sum, gain_ffn_sum = lax.psum((gain_total_attn, gain_total_ffn), ("dp", "tensor"))
    return (
        jnp.stack(out_rows, axis=0),
        jnp.stack(grad_rows, axis=0),
        gain_attn_sum,
        shares[0],
        shares[1],
        shares[2],
        shares[3],
        gain_ffn_sum,
        shares[4],
        shares[5],
        shares[6],
    )


TQ = 512
TK = 512
ROWS = 512
HT = 256
SCALE = HD**-0.5
EXP_SCALE = SCALE * 1.4426950408889634
LOG2E = 1.4426950408889634
NT = (((1,), (1,)), ((), ()))
TN = (((0,), (0,)), ((), ()))
F32 = jnp.float32
BF16 = jnp.bfloat16
MIB = 1 << 20


def mm(left, right, dims=(((1,), (0,)), ((), ()))):
    return lax.dot_general(left, right, dims, preferred_element_type=F32)


def fold_max(values):
    best = values[:, :HD]
    for i in range(1, values.shape[1] // HD):
        best = jnp.maximum(best, values[:, i * HD : (i + 1) * HD])
    return best


def fold_sum(values):
    total = values[:, :HD]
    for i in range(1, values.shape[1] // HD):
        total = total + values[:, i * HD : (i + 1) * HD]
    return total


def reach_mask(first, tile, limit):
    rows = first + lax.broadcasted_iota(jnp.int32, (TQ, 1), 0)
    keys = tile * TK + lax.broadcasted_iota(jnp.int32, (1, TK), 1)
    reach = jnp.where(rows < limit, jnp.maximum(rows, limit - 1), rows)
    return keys <= reach


def pick_own(meta, block, own, buf):
    for i in range(KR):
        c = meta[2 + block * KR + i]
        buf[pl.ds(i * CBLOCK, CBLOCK), :] = own[0, pl.ds(pl.multiple_of(c * CBLOCK, CBLOCK), CBLOCK), :]


def pick_other(meta, block, other, buf, start=0):
    for i in range(KR):
        d = meta[2 + (L // QBLOCK) * KR + block * KR + i]
        buf[pl.ds(start + i * CBLOCK, CBLOCK), :] = other[d, 0, 0]


def pick_blocks(meta, block, own, other, buf):
    pick_own(meta, block, own, buf)
    pick_other(meta, block, other, buf, KR * CBLOCK)


def attend_kernel(
    meta, q_ref, k_ref, v_ref, ok_ref, ov_ref, ctx_ref, lse_ref, kbuf, vbuf, sbuf, smem, *, pair
):
    step = pl.program_id(1)
    limit = meta[0]
    first = step * TQ
    free = jnp.where(first < limit, (limit + TK - 1) // TK, 0)
    tiles = jnp.maximum(step + 1, free)
    blocks = TQ // QBLOCK
    for b in range(blocks):
        pick_own(meta, step * blocks + b, ok_ref, kbuf.at[b])
        pick_own(meta, step * blocks + b, ov_ref, vbuf.at[b])
    state = []
    for h in range(pair):
        cs = pl.ds(h * HD, HD)
        best = []
        for b in range(blocks):
            s = mm(q_ref[pl.ds(b * QBLOCK, QBLOCK), cs], kbuf[b, :, cs], NT)
            smem[h, pl.ds(b * QBLOCK, QBLOCK), :] = s
            best.append(fold_max(s))
        state.append(jnp.concatenate(best, 0))

    def scores(tile, state, masked):
        ks = pl.ds(pl.multiple_of(tile * TK, TK), TK)
        if masked:
            allowed = reach_mask(first, tile, limit)
        new = []
        for h in range(pair):
            cs = pl.ds(h * HD, HD)
            s = mm(q_ref[:, cs], k_ref[ks, cs], NT)
            if masked:
                s = jnp.where(allowed, s, NEGATIVE)
            sbuf[h, tile] = s
            new.append(jnp.maximum(state[h], fold_max(s)))
        return tuple(new)

    state = lax.fori_loop(0, step, lambda tile, s: scores(tile, s, False), tuple(state))
    state = lax.fori_loop(step, tiles, lambda tile, s: scores(tile, s, True), state)
    tops = [jnp.max(s, axis=1, keepdims=True) for s in state]
    state = []
    for h in range(pair):
        cs = pl.ds(h * HD, HD)
        p = jnp.exp2((smem[h] - tops[h]) * EXP_SCALE)
        low = p.astype(BF16)
        parts = [mm(low[b * QBLOCK : (b + 1) * QBLOCK], vbuf[b, :, cs]) for b in range(blocks)]
        state.append((fold_sum(p), jnp.concatenate(parts, 0)))

    def weigh(tile, state):
        ks = pl.ds(pl.multiple_of(tile * TK, TK), TK)
        new = []
        for h in range(pair):
            total, acc = state[h]
            p = jnp.exp2((sbuf[h, tile] - tops[h]) * EXP_SCALE)
            new.append((total + fold_sum(p), acc + mm(p.astype(BF16), v_ref[ks, pl.ds(h * HD, HD)])))
        return tuple(new)

    state = lax.fori_loop(0, tiles, weigh, tuple(state))
    for h in range(pair):
        cs = pl.ds(h * HD, HD)
        total = jnp.sum(state[h][0], axis=1, keepdims=True)
        ctx_ref[:, cs] = state[h][1] / total
        lse_ref[:, cs] = jnp.broadcast_to(tops[h] * SCALE + jnp.log(total), (TQ, HD))


def attend_other_kernel(meta, q_ref, pk_ref, pv_ref, part_ref, plse_ref, ctx_ref, lse_ref, kbuf, vbuf, *, pair):
    step = pl.program_id(1)
    blocks = TQ // QBLOCK
    for b in range(blocks):
        pick_other(meta, step * blocks + b, pk_ref, kbuf.at[b])
        pick_other(meta, step * blocks + b, pv_ref, vbuf.at[b])
    for h in range(pair):
        cs = pl.ds(h * HD, HD)
        rows = [pl.ds(b * QBLOCK, QBLOCK) for b in range(blocks)]
        s = jnp.concatenate([mm(q_ref[rows[b], cs], kbuf[b, :, cs], NT) for b in range(blocks)], 0)
        before = plse_ref[:, cs]
        top = jnp.maximum(before, jnp.max(fold_max(s), axis=1, keepdims=True) * SCALE)
        keep = jnp.exp(before - top)
        p = jnp.exp2(s * EXP_SCALE - top[:, :1] * LOG2E)
        low = p.astype(BF16)
        more = jnp.concatenate(
            [mm(low[b * QBLOCK : (b + 1) * QBLOCK], vbuf[b, :, cs]) for b in range(blocks)], 0
        )
        total = keep + jnp.sum(fold_sum(p), axis=1, keepdims=True)
        ctx_ref[:, cs] = ((part_ref[:, cs] * keep + more) / total).astype(BF16)
        lse_ref[:, cs] = top + jnp.log(total)


def attend_back_kernel(
    meta, q_ref, k_ref, v_ref, ok_ref, ov_ref, pk_ref, pv_ref, do_ref, ctx_ref, lse_ref,
    dq_ref, dk_ref, dv_ref, kbuf, vbuf, dks, dvs, *, pair
):
    step = pl.program_id(1)
    limit = meta[0]
    first = step * TQ
    free = jnp.where(first < limit, (limit + TK - 1) // TK, 0)
    tiles = jnp.maximum(step + 1, free)
    blocks = TQ // QBLOCK

    @pl.when(step == 0)
    def _():
        dks[...] = jnp.zeros_like(dks)
        dvs[...] = jnp.zeros_like(dvs)

    for b in range(blocks):
        pick_blocks(meta, step * blocks + b, ok_ref, pk_ref, kbuf.at[b])
        pick_blocks(meta, step * blocks + b, ov_ref, pv_ref, vbuf.at[b])
    state = []
    aux = []
    for h in range(pair):
        cs = pl.ds(h * HD, HD)
        delta = jnp.sum(do_ref[:, cs].astype(F32) * ctx_ref[:, cs].astype(F32), axis=1, keepdims=True)
        lse2 = lse_ref[:, cs][:, :1] * LOG2E
        aux.append((lse2, delta))
        parts = []
        for b in range(blocks):
            rs = pl.ds(b * QBLOCK, QBLOCK)
            s = mm(q_ref[rs, cs], kbuf[b, :, cs], NT)
            p = jnp.exp2(s * EXP_SCALE - lse2[b * QBLOCK : (b + 1) * QBLOCK])
            dp = mm(do_ref[rs, cs], vbuf[b, :, cs], NT)
            ds = (p * (dp - delta[b * QBLOCK : (b + 1) * QBLOCK])).astype(BF16)
            parts.append(mm(ds, kbuf[b, :, cs]))
        state.append(jnp.concatenate(parts, 0))

    def grads(tile, state, masked):
        ks = pl.ds(pl.multiple_of(tile * TK, TK), TK)
        if masked:
            allowed = reach_mask(first, tile, limit)
        new = []
        for h in range(pair):
            cs = pl.ds(h * HD, HD)
            lse2, delta = aux[h]
            s = mm(q_ref[:, cs], k_ref[ks, cs], NT)
            p = jnp.exp2(s * EXP_SCALE - lse2)
            if masked:
                p = jnp.where(allowed, p, 0.0)
            dp = mm(do_ref[:, cs], v_ref[ks, cs], NT)
            ds = (p * (dp - delta)).astype(BF16)
            dvs[ks, cs] += mm(p.astype(BF16), do_ref[:, cs], TN)
            dks[ks, cs] += mm(ds, q_ref[:, cs], TN)
            new.append(state[h] + mm(ds, k_ref[ks, cs]))
        return tuple(new)

    state = lax.fori_loop(0, step, lambda tile, s: grads(tile, s, False), tuple(state))
    state = lax.fori_loop(step, tiles, lambda tile, s: grads(tile, s, True), state)
    for h in range(pair):
        dq_ref[:, pl.ds(h * HD, HD)] = (state[h] * SCALE).astype(BF16)

    @pl.when(step == L // TQ - 1)
    def _():
        dk_ref[...] = (dks[...] * SCALE).astype(BF16)
        dv_ref[...] = dvs[...].astype(BF16)


def attention_specs(heads, pair):
    wide = pair * HD
    per = heads // 2 // pair
    groups = heads // pair
    return [
        pl.BlockSpec((TQ, wide), lambda h, i, meta: (i, h)),
        pl.BlockSpec((L, wide), lambda h, i, meta: (0, groups + h)),
        pl.BlockSpec((L, wide), lambda h, i, meta: (0, 2 * groups + h)),
        pl.BlockSpec((1, CACHE_LEN, wide), lambda h, i, meta: ((h // per) ^ meta[1], 0, h % per)),
        pl.BlockSpec((1, CACHE_LEN, wide), lambda h, i, meta: ((h // per) ^ meta[1], 0, h % per)),
        pl.BlockSpec(
            (CACHE_LEN // CBLOCK, 1, 1, CBLOCK, wide),
            lambda h, i, meta: (0, (h // per) ^ meta[1], 0, 0, h % per),
        ),
        pl.BlockSpec(
            (CACHE_LEN // CBLOCK, 1, 1, CBLOCK, wide),
            lambda h, i, meta: (0, (h // per) ^ meta[1], 1, 0, h % per),
        ),
    ]


def attend(meta, qkv, own_k, own_v, pair=4):
    width = qkv.shape[1] // 3
    heads = width // HD
    wide = pair * HD
    row = pl.BlockSpec((TQ, wide), lambda h, i, meta: (i, h))
    area = L * 1600 * width
    return pl.pallas_call(
        functools.partial(attend_kernel, pair=pair),
        grid_spec=pltpu.PrefetchScalarGridSpec(
            num_scalar_prefetch=1,
            grid=(heads // pair, L // TQ),
            in_specs=attention_specs(heads, pair)[:5],
            out_specs=[row, row],
            scratch_shapes=[pltpu.VMEM((TQ // QBLOCK, KR * CBLOCK, wide), BF16)] * 2
            + [pltpu.VMEM((pair, L // TK, TQ, TK), F32), pltpu.VMEM((pair, TQ, KR * CBLOCK), F32)],
        ),
        out_shape=[jax.ShapeDtypeStruct((L, width), F32)] * 2,
        compiler_params=pltpu.CompilerParams(vmem_limit_bytes=60 * MIB),
        cost_estimate=pl.CostEstimate(flops=12 * area, bytes_accessed=30 * MIB, transcendentals=area // HD),
        name="attend",
    )(meta, qkv, qkv, qkv, own_k, own_v)


def attend_other(meta, qkv, fetched, partial, lse, pair=4):
    width = qkv.shape[1] // 3
    heads = width // HD
    wide = pair * HD
    row = pl.BlockSpec((TQ, wide), lambda h, i, meta: (i, h))
    specs = attention_specs(heads, pair)
    return pl.pallas_call(
        functools.partial(attend_other_kernel, pair=pair),
        grid_spec=pltpu.PrefetchScalarGridSpec(
            num_scalar_prefetch=1,
            grid=(heads // pair, L // TQ),
            in_specs=[specs[0], specs[5], specs[6], row, row],
            out_specs=[row, row],
            scratch_shapes=[pltpu.VMEM((TQ // QBLOCK, KR * CBLOCK, wide), BF16)] * 2,
        ),
        out_shape=[jax.ShapeDtypeStruct((L, width), BF16), jax.ShapeDtypeStruct((L, width), F32)],
        compiler_params=pltpu.CompilerParams(vmem_limit_bytes=60 * MIB),
        cost_estimate=pl.CostEstimate(
            flops=4 * L * 256 * width, bytes_accessed=30 * MIB, transcendentals=L * 256 * heads
        ),
        name="attend_other",
    )(meta, qkv, fetched, fetched, partial, lse)


def attend_back(meta, qkv, own_k, own_v, fetched, grad_context, context, lse, pair=4):
    width = context.shape[1]
    heads = width // HD
    wide = pair * HD
    row = pl.BlockSpec((TQ, wide), lambda h, i, meta: (i, h))
    col = pl.BlockSpec((L, wide), lambda h, i, meta: (0, h))
    area = L * 1900 * width
    return pl.pallas_call(
        functools.partial(attend_back_kernel, pair=pair),
        grid_spec=pltpu.PrefetchScalarGridSpec(
            num_scalar_prefetch=1,
            grid=(heads // pair, L // TQ),
            in_specs=attention_specs(heads, pair) + [row, row, row],
            out_specs=[row, col, col],
            scratch_shapes=[pltpu.VMEM((TQ // QBLOCK, 2 * KR * CBLOCK, wide), BF16)] * 2
            + [pltpu.VMEM((L, wide), F32)] * 2,
        ),
        out_shape=[jax.ShapeDtypeStruct((L, width), BF16)] * 3,
        compiler_params=pltpu.CompilerParams(vmem_limit_bytes=60 * MIB),
        cost_estimate=pl.CostEstimate(flops=12 * area, bytes_accessed=40 * MIB, transcendentals=area // HD),
        name="attend_back",
    )(meta, qkv, qkv, qkv, own_k, own_v, fetched, fetched, grad_context, context, lse)


def project_kernel(x_ref, gain_ref, w_ref, normed_ref, qkv_ref):
    rows = x_ref[...].astype(F32)
    scale = lax.rsqrt(jnp.mean(rows * rows, axis=1, keepdims=True) + EPS)
    normed_ref[...] = (rows * scale * gain_ref[...]).astype(BF16)
    left = normed_ref[...]

    def chunk(c, carry):
        cs = pl.ds(pl.multiple_of(c * 512, 512), 512)
        qkv_ref[:, cs] = mm(left, w_ref[:, cs]).astype(BF16)
        return carry

    lax.fori_loop(0, qkv_ref.shape[1] // 512, chunk, 0)


def project(x, gain, weights):
    width = x.shape[1]
    cols = 3 * width
    row = lambda n: pl.BlockSpec((ROWS, n), lambda i: (i, 0))
    whole = lambda n: pl.BlockSpec((width, n), lambda i: (0, 0))
    return pl.pallas_call(
        project_kernel,
        grid=(L // ROWS,),
        in_specs=[row(width), pl.BlockSpec((1, width), lambda i: (0, 0)), whole(cols)],
        out_specs=[row(width), row(cols)],
        out_shape=[jax.ShapeDtypeStruct((L, width), BF16), jax.ShapeDtypeStruct((L, cols), BF16)],
        compiler_params=pltpu.CompilerParams(vmem_limit_bytes=60 * MIB),
        cost_estimate=pl.CostEstimate(flops=2 * L * width * cols, bytes_accessed=26 * MIB, transcendentals=0),
        name="project",
    )(x, gain, weights)


def mix_kernel(x_ref, ctx_ref, gain_ref, w_ref, mixed_ref, normed_ref):
    mixed = x_ref[...].astype(F32) + mm(ctx_ref[...], w_ref[...], NT)
    mixed_ref[...] = mixed
    scale = lax.rsqrt(jnp.mean(mixed * mixed, axis=1, keepdims=True) + EPS)
    normed_ref[...] = (mixed * scale * gain_ref[...]).astype(BF16)


def mix(x, context, gain, weights):
    width = x.shape[1]
    row = pl.BlockSpec((ROWS, width), lambda i: (i, 0))
    return pl.pallas_call(
        mix_kernel,
        grid=(L // ROWS,),
        in_specs=[row, row, pl.BlockSpec((1, width), lambda i: (0, 0)), pl.BlockSpec((width, width), lambda i: (0, 0))],
        out_specs=[row, row],
        out_shape=[jax.ShapeDtypeStruct((L, width), F32), jax.ShapeDtypeStruct((L, width), BF16)],
        compiler_params=pltpu.CompilerParams(vmem_limit_bytes=60 * MIB),
        cost_estimate=pl.CostEstimate(flops=2 * L * width * width, bytes_accessed=22 * MIB, transcendentals=0),
        name="mix",
    )(x, context, gain, weights)


RING = 8


def ring_place(p):
    y = p // 4
    return (p + y * (7 - 2 * p)) * 2 + y


def meet(devices, me, spot):
    barrier = pltpu.get_barrier_semaphore()
    for d in range(1, devices):
        pl.semaphore_signal(
            barrier, inc=1, device_id=((me + d) % devices, spot), device_id_type=pl.DeviceIdType.MESH
        )
    pl.semaphore_signal(barrier, inc=1, device_id=(me, 1 - spot), device_id_type=pl.DeviceIdType.MESH)
    pl.semaphore_wait(barrier, devices)


def remote(src, dst, send, recv, device):
    return pltpu.make_async_remote_copy(
        src_ref=src, dst_ref=dst, send_sem=send, recv_sem=recv, device_id=device, device_id_type=pl.DeviceIdType.MESH
    )


UT = 256


def ffn_kernel(
    n_ref, g_ref, wg0, wg1, wu0, wu1, wd0, wd1, gain_ref, mixed_ref, wo_ref,
    share_ref, gg_ref, out_ref, gm_ref, br_ref, gc_ref,
    acc, gn, hid, duo, part, got, passed, keep, land,
    wo_buf, mixed_buf, out_buf, br_buf, gc_buf,
    pair_send, pair_recv, x_send, x_recv, wo_sem, mixed_sem, done_sem, *, devices,
):
    tile = pl.program_id(0)
    tiles = pl.num_programs(0)
    me = lax.axis_index("dp")
    spot = lax.axis_index("tensor")
    core = me % 2
    pair = (me + 1 - 2 * core, spot)
    peer = (me, 1 - spot)
    side = HT // 2
    width = n_ref.shape[1]
    wo_copy = pltpu.make_async_copy(wo_ref.at[:, pl.ds(0, width)], wo_buf, wo_sem)

    @pl.when(tile == 0)
    def _():
        barrier = pltpu.get_barrier_semaphore()
        for device in (pair, peer):
            pl.semaphore_signal(barrier, inc=1, device_id=device, device_id_type=pl.DeviceIdType.MESH)
        pl.semaphore_wait(barrier, 2)
        acc[...] = jnp.zeros_like(acc)
        gn[...] = jnp.zeros_like(gn)

    def to_pair(k):
        return remote(part.at[k % 2, :, 1 - core], got.at[k % 2], pair_send.at[k % 2], pair_recv.at[k % 2], pair)

    def to_peer(k):
        return remote(passed.at[k % 2], land.at[k % 4], x_send.at[k % 2], x_recv.at[k % 4], peer)

    def join(k):
        slot = (k + 2) % 2
        total = (got[slot].astype(F32) + part[slot, :, core].astype(F32)).astype(BF16)
        for m in range(3):
            passed[slot, :, :, m * side : (m + 1) * side] = total[:, :, m * HT + side : (m + 1) * HT]
            keep[(k + 4) % 4, :, :, m * side : (m + 1) * side] = total[:, :, m * HT : m * HT + side]

    def settle(k):
        slot = (jnp.maximum(k, -1) + 4) % 4
        total = (keep[slot].astype(F32) + land[slot].astype(F32)).astype(BF16)
        total = total.reshape(share_ref.shape[0], 3 * side)
        for m in range(3):
            place = pl.multiple_of((m * tiles + jnp.maximum(k, 0)) * side, side)
            share_ref[:, pl.ds(place, side)] = total[:, m * side : (m + 1) * side]

    wgu = jnp.concatenate([wg0[...], wg1[...], wu0[...], wu1[...]], axis=1)
    wd = jnp.concatenate([wd0[...], wd1[...]], axis=1)

    def chunk(r):
        rs = pl.ds(r * ROWS, ROWS)
        both = mm(n_ref[rs, :], wgu)
        grad_hidden = mm(g_ref[rs, :], wd)
        gate, up = both[:, :HT], both[:, HT:]
        sigma = 1.0 / (1.0 + jnp.exp(-gate))
        silu = gate * sigma
        hidden = (silu * up).astype(BF16)
        grad_gate = grad_hidden * up * (sigma * (1.0 + gate * (1.0 - sigma)))
        grads = jnp.concatenate([grad_gate.astype(BF16), (grad_hidden * silu).astype(BF16)], axis=1)
        acc[rs, :] += mm(hidden, wd, NT)
        gn[rs, :] += mm(grads, wgu, NT)
        hid[rs, :] = hidden
        duo[rs, :] = grads

    @pl.when(tile > 2)
    def _():
        to_peer(tile - 3).wait()

    settle(tile - 3)
    for r in range(L // ROWS):
        chunk(r)

    @pl.when(tile > 0)
    def _():
        to_pair(tile - 1).wait()

    join(tile - 1)
    slot = tile % 2
    shape = part.shape[1:4]
    part[slot, :, :, :, : 2 * HT] = mm(n_ref[...], duo[...], TN).astype(BF16).reshape(shape + (2 * HT,))
    part[slot, :, :, :, 2 * HT :] = mm(g_ref[...], hid[...], TN).astype(BF16).reshape(shape + (HT,))
    to_pair(tile).start()

    @pl.when(tile > 0)
    def _():
        to_peer(tile - 1).start()

    def rows_of(t):
        return pl.ds(pl.multiple_of(t * UT, UT), UT)

    def fetch(t):
        return pltpu.make_async_copy(mixed_ref.at[rows_of(t), :], mixed_buf.at[t % 2], mixed_sem.at[t % 2])

    def write(t):
        sources = [out_buf.at[t % 2], gn.at[rows_of(t), :], br_buf.at[t % 2], gc_buf.at[t % 2]]
        return [
            pltpu.make_async_copy(source, ref.at[rows_of(t), :], done_sem.at[i, t % 2])
            for i, (source, ref) in enumerate(zip(sources, [out_ref, gm_ref, br_ref, gc_ref]))
        ]

    def unmix(t, carry):
        @pl.when(t < L // UT - 1)
        def _():
            fetch(t + 1).start()

        fetch(t).wait()

        @pl.when(t > 1)
        def _():
            for copy in write(t - 2):
                copy.wait()

        rs = rows_of(t)
        now = t % 2
        mixed = mixed_buf[now]
        grad = gn[rs, :]
        scale = lax.rsqrt(jnp.mean(mixed * mixed, axis=1, keepdims=True) + EPS)
        unit = mixed * scale
        inner = grad * gain_ref[...]
        back = scale * (inner - unit * jnp.mean(inner * unit, axis=1, keepdims=True))
        grad_mixed = g_ref[rs, :].astype(F32) + back
        out_buf[now] = (mixed + acc[rs, :]).astype(BF16)
        gn[rs, :] = grad_mixed
        branch = grad_mixed.astype(BF16)
        br_buf[now] = branch
        gc_buf[now] = mm(branch, wo_buf[...]).astype(BF16)
        gg_ref[...] += jnp.sum(grad * unit, axis=0, keepdims=True)
        for copy in write(t):
            copy.start()
        return carry

    @pl.when(tile == tiles - 1)
    def _():
        wo_copy.start()
        fetch(0).start()
        gg_ref[...] = jnp.zeros_like(gg_ref)
        to_peer(tile - 2).wait()
        settle(tile - 2)
        wo_copy.wait()
        lax.fori_loop(0, 4, unmix, 0)
        to_pair(tile).wait()
        join(tile)
        to_peer(tile).start()
        lax.fori_loop(4, L // UT, unmix, 0)
        to_peer(tile - 1).wait()
        settle(tile - 1)
        to_peer(tile).wait()
        settle(tile)
        for t in (L // UT - 2, L // UT - 1):
            for copy in write(t):
                copy.wait()


def ffn(normed, cotangent, weights, gain, mixed, width, hidden, devices):
    once = pl.Buffered(1)
    tiles = hidden // HT
    side = HT // 2
    rows = width // devices
    chips = devices // 2
    lead = width // side
    part = lambda k: pl.BlockSpec((width, side), lambda j: (0, lead + k * tiles + j))
    whole = pl.BlockSpec((L, width), lambda j: (0, 0), pipeline_mode=once)
    fixed = lambda shape: pl.BlockSpec(shape, lambda j: (0, 0), pipeline_mode=once)
    hbm = pl.BlockSpec(memory_space=pltpu.HBM)
    dma = pltpu.SemaphoreType.DMA
    tile = lambda kind: pltpu.VMEM((2, UT, width), kind)
    return pl.pallas_call(
        functools.partial(ffn_kernel, devices=devices),
        grid=(tiles,),
        in_specs=[whole, whole] + [part(k) for k in range(6)] + [fixed((1, width)), hbm, hbm],
        out_specs=[fixed((width // 2, 3 * hidden // 2)), fixed((1, width)), hbm, hbm, hbm, hbm],
        out_shape=[
            jax.ShapeDtypeStruct((width // 2, 3 * hidden // 2), BF16),
            jax.ShapeDtypeStruct((1, width), F32),
            jax.ShapeDtypeStruct((L, width), BF16),
            jax.ShapeDtypeStruct((L, width), F32),
            jax.ShapeDtypeStruct((L, width), BF16),
            jax.ShapeDtypeStruct((L, width), BF16),
        ],
        scratch_shapes=[
            pltpu.VMEM((L, width), F32), pltpu.VMEM((L, width), F32),
            pltpu.VMEM((L, HT), BF16), pltpu.VMEM((L, 2 * HT), BF16),
            pltpu.VMEM((2, chips, 2, rows, 3 * HT), BF16),
            pltpu.VMEM((2, chips, rows, 3 * HT), BF16),
            pltpu.VMEM((2, chips, rows, 3 * side), BF16),
            pltpu.VMEM((4, chips, rows, 3 * side), BF16),
            pltpu.VMEM((4, chips, rows, 3 * side), BF16),
            pltpu.VMEM((width, width), BF16), tile(F32), tile(BF16), tile(BF16), tile(BF16),
            dma((2,)), dma((2,)), dma((2,)), dma((4,)), dma, dma((2,)), dma((4, 2)),
        ],
        compiler_params=pltpu.CompilerParams(collective_id=2, has_side_effects=True, vmem_limit_bytes=61 * MIB),
        cost_estimate=pl.CostEstimate(
            flops=18 * L * width * hidden, bytes_accessed=60 * MIB, transcendentals=L * hidden
        ),
        name="ffn",
    )(normed, cotangent, *([weights] * 6), gain, mixed, weights)


FT = 256


def finish_kernel(
    x_ref, gm_ref, n_ref, ctx_ref, br_ref, dq_ref, dk_ref, dv_ref, w_ref, gain_ref, gain_two_ref,
    gt_ref, sums_ref, share_ref,
    n_buf, ctx_buf, br_buf, dq_buf, dk_buf, dv_buf, w_buf, x_buf, gm_buf, gt_buf,
    part, got, land, across, gains, gain_land,
    load_sem, x_sem, gm_sem, gt_sem, gt_recv, pair_send, pair_recv, ring_send, ring_recv, x_send, x_recv, g_send, g_recv,
    *, devices,
):
    me = lax.axis_index("dp")
    spot = lax.axis_index("tensor")
    core = me % 2
    z, y = me // 4, (me // 2) % 2
    place = z + y * (7 - 2 * z)
    width = n_buf.shape[1]
    half = width // 2
    rows = part.shape[2]
    loads = [
        pltpu.make_async_copy(src, dst, load_sem.at[i])
        for i, (src, dst) in enumerate(
            [
                (ctx_ref, ctx_buf), (br_ref, br_buf), (n_ref, n_buf), (dv_ref, dv_buf),
                (dk_ref, dk_buf), (dq_ref, dq_buf), (w_ref.at[:, pl.ds(0, 3 * width)], w_buf),
            ]
        )
    ]
    for copy in loads:
        copy.start()
    meet(devices, me, spot)

    def tile_in(t, slot):
        rs = pl.ds(pl.multiple_of(t * FT, FT), FT)
        return [
            pltpu.make_async_copy(x_ref.at[rs, :], x_buf.at[slot], x_sem.at[slot]),
            pltpu.make_async_copy(gm_ref.at[rs, :], gm_buf.at[slot], gm_sem.at[slot]),
        ]

    held = L // FT // 2

    def give(k, slot):
        rs = pl.ds(pl.multiple_of(k * FT, FT), FT)
        return remote(
            gt_buf.at[slot], gt_ref.at[spot, rs, :], gt_sem.at[slot], gt_recv.at[k], (me, 1 - spot)
        )

    def keep(k, slot):
        rs = pl.ds(pl.multiple_of(k * FT, FT), FT)
        return pltpu.make_async_copy(gt_buf.at[slot], gt_ref.at[spot, rs, :], gt_sem.at[slot])

    def tile_of(k):
        return (k + held * (1 - spot)) % (2 * held)

    for copy in tile_in(tile_of(0), 0):
        copy.start()

    pair = (me + 1 - 2 * core, spot)

    def column(m, h):
        return (m // 2) * 2 * width + h * width + (m % 2) * half

    def to_pair(m, h):
        cs = pl.ds(column(m, h), half)
        return remote(
            part.at[:, 1 - core, :, cs], got.at[:, :, cs], pair_send.at[m, h], pair_recv.at[m, h], pair
        )

    def product(m, left, right):
        for h in range(2):
            value = mm(left[...], right[:, h * half : (h + 1) * half], TN).astype(BF16)
            part[:, :, :, column(m, h) : column(m, h) + half] = value.reshape(part.shape[0], 2, rows, half)
            to_pair(m, h).start()

    def join(m, h):
        to_pair(m, h).wait_recv()
        cs = pl.ds(column(m, h), half)
        got[:, :, cs] = (got[:, :, cs].astype(F32) + part[:, core, :, cs].astype(F32)).astype(BF16)

    neighbours = [(place + 1) % RING, (place + RING - 1) % RING]

    def held_block(g, direction, s):
        p = (place + 2 * RING - 1 - s) % RING if direction == 0 else (place + 1 + s) % RING
        return got.at[ring_place(p), :, pl.ds((2 * g + direction) * width, width)]

    def hop(g, direction, s):
        to = ring_place(neighbours[direction]) * 2 + core
        return remote(
            held_block(g, direction, s), land.at[g, direction, s],
            ring_send.at[g, direction, s], ring_recv.at[g, direction, s], (to, spot),
        )

    def advance(g, s, more=True):
        for direction in range(2):
            hop(g, direction, s).wait_recv()
            block = held_block(g, direction, s + 1)
            block[...] = (block[...].astype(F32) + land[g, direction, s].astype(F32)).astype(BF16)
            if more:
                hop(g, direction, s + 1).start()

    def launch(g):
        for h in range(2):
            join(2 * g, h)
            join(2 * g + 1, h)
            hop(g, h, 0).start()

    def finish_rows(t, slot, k):
        for copy in tile_in(t, slot):
            copy.wait()
        rs = pl.ds(pl.multiple_of(t * FT, FT), FT)
        grad = mm(dq_buf[rs, :], w_buf[:, :width], NT)
        grad += mm(dk_buf[rs, :], w_buf[:, width : 2 * width], NT)
        grad += mm(dv_buf[rs, :], w_buf[:, 2 * width :], NT)
        values = x_buf[slot].astype(F32)
        scale = lax.rsqrt(jnp.mean(values * values, axis=1, keepdims=True) + EPS)
        unit = values * scale
        inner = grad * gain_ref[...]
        back = scale * (inner - unit * jnp.mean(inner * unit, axis=1, keepdims=True))
        gt_buf[k] = (gm_buf[slot] + back).astype(BF16)
        gains[:1, :] += jnp.sum(grad * unit, axis=0, keepdims=True)

    def two_tiles(j, advances, give_away):
        for slot in (0, 1):
            k = 2 * j + slot
            if slot == 0 or give_away:
                for copy in tile_in(tile_of(k + 1), 1 - slot):
                    copy.start()
            else:

                @pl.when(j < held - 1)
                def _():
                    for copy in tile_in(tile_of(k + 1), 0):
                        copy.start()

            finish_rows(tile_of(k), slot, k)
            if give_away:
                give(k, k).start()
            else:
                keep(k - held, k).start()
        for g, s in advances:
            advance(g, s)

    gains[:1, :] = jnp.zeros((1, width), F32)
    gains[1:, :] = gain_two_ref[...]
    for i in (0, 1):
        loads[i].wait()
    product(0, br_buf, ctx_buf)
    for i in (2, 3):
        loads[i].wait()
    product(1, n_buf, dv_buf)
    launch(0)
    for i in (4, 5, 6):
        loads[i].wait()

    def theirs(j, carry):
        two_tiles(j, [(0, j)], True)
        return carry

    def ours(j, carry):
        two_tiles(j, [(0, j + 2), (1, j - 2)], False)
        return carry

    lax.fori_loop(0, held // 2, theirs, 0)
    product(2, n_buf, dk_buf)
    advance(0, 2)
    product(3, n_buf, dq_buf)
    advance(0, 3)
    launch(1)
    lax.fori_loop(held // 2, held, ours, 0)

    partners = [
        (me + 1 - 2 * core, spot),
        (me + 2 - 4 * y, spot),
        (me + 4 - 8 * (z % 2), spot),
        (me + 8 - 16 * (z // 2), spot),
        (me, 1 - spot),
    ]

    def add_gains(r):
        return remote(gains, gain_land.at[r], g_send.at[r], g_recv.at[r], partners[r])

    def gain_round(r):
        add_gains(r).wait()
        gains[...] = gains[...] + gain_land[r]
        if r < 4:
            add_gains(r + 1).start()

    own = ring_place(place)
    peer = (me, 1 - spot)

    def over(g):
        return remote(
            got.at[own, :, pl.ds((2 * g + 1) * width, width)], across.at[:, pl.ds(g * width, width)],
            x_send.at[g], x_recv.at[g], peer,
        )

    add_gains(0).start()
    advance(0, 6, False)
    over(0).start()
    advance(1, 2)
    gain_round(0)
    advance(1, 3)
    gain_round(1)
    advance(1, 4)
    gain_round(2)
    advance(1, 5)
    gain_round(3)
    advance(1, 6, False)
    over(1).start()
    gain_round(4)
    sums_ref[...] = gains[...]
    for g in range(2):
        over(g).wait_recv()
        cs = pl.ds(g * width, width)
        share_ref[:, cs] = got[own, :, pl.ds(2 * g * width, width)].astype(F32) + across[:, cs].astype(F32)
    for g in range(2):
        over(g).wait_send()
        for direction in range(2):
            for s in range(RING - 1):
                hop(g, direction, s).wait_send()
    for m in range(4):
        for h in range(2):
            to_pair(m, h).wait_send()
    for k in range(held):
        give(k, k).wait()
        keep(k, k + held).wait()


def finish(x, grad_mixed, normed, context, branch, dq, dk, dv, weights, gain, gain_two_part, devices):
    width = x.shape[1]
    rows = width // devices
    anywhere = pl.BlockSpec(memory_space=pltpu.HBM)
    vmem = pl.BlockSpec(memory_space=pltpu.VMEM)
    dma = pltpu.SemaphoreType.DMA
    whole = pltpu.VMEM((L, width), BF16)
    return pl.pallas_call(
        functools.partial(finish_kernel, devices=devices),
        in_specs=[anywhere] * 9 + [vmem] * 2,
        out_specs=[anywhere, vmem, vmem],
        out_shape=[
            jax.ShapeDtypeStruct((2, L // 2, width), BF16),
            jax.ShapeDtypeStruct((2, width), F32),
            jax.ShapeDtypeStruct((rows, 2 * width), F32),
        ],
        scratch_shapes=[
            whole, whole, whole, whole, whole, whole, pltpu.VMEM((width, 3 * width), BF16),
            pltpu.VMEM((2, FT, width), BF16), pltpu.VMEM((2, FT, width), F32), pltpu.VMEM((L // FT, FT, width), BF16),
            pltpu.VMEM((RING, 2, rows, 4 * width), BF16),
            pltpu.VMEM((RING, rows, 4 * width), BF16),
            pltpu.VMEM((2, 2, RING - 1, rows, width), BF16),
            pltpu.VMEM((rows, 2 * width), BF16),
            pltpu.VMEM((2, width), F32), pltpu.VMEM((5, 2, width), F32),
            dma((7,)), dma((2,)), dma((2,)), dma((2 * (L // FT // 2),)), dma((L // FT // 2,)), dma((4, 2)), dma((4, 2)),
            dma((2, 2, RING - 1)), dma((2, 2, RING - 1)), dma((2,)), dma((2,)), dma((5,)), dma((5,)),
        ],
        compiler_params=pltpu.CompilerParams(collective_id=1, has_side_effects=True, vmem_limit_bytes=60 * MIB),
        cost_estimate=pl.CostEstimate(flops=14 * L * width * width, bytes_accessed=80 * MIB, transcendentals=0),
        name="finish",
    )(x, grad_mixed, normed, context, branch, dq, dk, dv, weights, gain, gain_two_part)


def pick_kernel(table, held_ref, sent_ref, sems):
    def copy(i):
        return pltpu.make_async_copy(held_ref.at[table[i]], sent_ref.at[i], sems.at[i])

    for i in range(sent_ref.shape[0]):
        copy(i).start()
    for i in range(sent_ref.shape[0]):
        copy(i).wait()


def pick_rows(table, held):
    count = held.shape[0]
    return pl.pallas_call(
        pick_kernel,
        grid_spec=pltpu.PrefetchScalarGridSpec(
            num_scalar_prefetch=1,
            grid=(),
            in_specs=[pl.BlockSpec(memory_space=pl.ANY)],
            out_specs=pl.BlockSpec(memory_space=pltpu.VMEM),
            scratch_shapes=[pltpu.SemaphoreType.DMA((count,))],
        ),
        out_shape=jax.ShapeDtypeStruct(held.shape, held.dtype),
        compiler_params=pltpu.CompilerParams(vmem_limit_bytes=60 * MIB),
        cost_estimate=pl.CostEstimate(flops=0, bytes_accessed=2 * held.size * 2, transcendentals=0),
        name="pick_rows",
    )(table, held)


def spread_kernel(
    tok_ref, ck_ref, cv_ref, small_ref, extra_ref, big_ref,
    x_ref, ok_ref, ov_ref, held_ref, first_ref, second_ref,
    tok_buf, k_buf, v_buf, local_sem, x_send, x_recv, all_send, all_recv, ring_send, ring_recv, line_send, line_recv, pair_send, pair_recv,
):
    me = lax.axis_index("dp")
    spot = lax.axis_index("tensor")
    peer = 1 - spot
    devices = held_ref.shape[0]
    rows, cols = small_ref.shape[0], small_ref.shape[1] // 3
    core = me % 2
    z, y = me // 4, (me // 2) % 2

    def target(dp, tensor):
        return (dp, tensor)

    barrier = pltpu.get_barrier_semaphore()
    for d in range(1, devices):
        pl.semaphore_signal(barrier, inc=1, device_id=target((me + d) % devices, spot), device_id_type=pl.DeviceIdType.MESH)
    pl.semaphore_signal(barrier, inc=1, device_id=target(me, peer), device_id_type=pl.DeviceIdType.MESH)
    pl.semaphore_wait(barrier, devices)

    def remote(src, dst, send, recv, device):
        return pltpu.make_async_remote_copy(
            src_ref=src, dst_ref=dst, send_sem=send, recv_sem=recv,
            device_id=device, device_id_type=pl.DeviceIdType.MESH,
        )

    mine = pl.multiple_of(me * rows, rows)
    across = target(me, peer)
    weight_copies = []
    for i in range(3):
        weight_copies.append(
            remote(
                small_ref.at[:, pl.ds(i * cols, cols)],
                first_ref.at[pl.ds(mine, rows), pl.ds((2 * i + 1) * cols, cols)],
                x_send.at[i], x_recv.at[i], across,
            )
        )
    for copy in weight_copies:
        copy.start()
    for i in range(3):
        first_ref[pl.ds(mine, rows), pl.ds(2 * i * cols, cols)] = small_ref[:, pl.ds(i * cols, cols)]
    first_ref[pl.ds(mine, rows), pl.ds(6 * cols, HD)] = extra_ref[...]

    loads = [
        pltpu.make_async_copy(tok_ref.at[spot], tok_buf, local_sem.at[0]),
        pltpu.make_async_copy(ck_ref.at[spot], k_buf, local_sem.at[1]),
        pltpu.make_async_copy(cv_ref.at[spot], v_buf, local_sem.at[2]),
    ]
    stores = [
        pltpu.make_async_copy(tok_buf, x_ref.at[spot], local_sem.at[3]),
        pltpu.make_async_copy(k_buf, ok_ref.at[spot], local_sem.at[4]),
        pltpu.make_async_copy(v_buf, ov_ref.at[spot], local_sem.at[5]),
    ]
    for copy in loads:
        copy.start()

    x_copies = [remote(tok_ref.at[peer], x_ref.at[spot], x_send.at[3], x_recv.at[3], across)]
    wide = big_ref.shape[1]
    hidden = (wide - cols) // 3
    starts = [(0, cols)] + [(cols + i * hidden, hidden) for i in range(3)]
    own_cols = []
    for i, (start, size) in enumerate(starts):
        base = 2 * start
        own_cols.append(pltpu.make_async_copy(
            big_ref.at[:, pl.ds(start, size)], second_ref.at[:, pl.ds(base, size)], local_sem.at[6 + i]))
        x_copies.append(remote(
            big_ref.at[:, pl.ds(start, size)], second_ref.at[:, pl.ds(base + size, size)],
            x_send.at[4 + i], x_recv.at[4 + i], across))
    x_copies.append(remote(ck_ref.at[peer], ok_ref.at[spot], x_send.at[8], x_recv.at[8], across))
    x_copies.append(remote(cv_ref.at[peer], ov_ref.at[spot], x_send.at[9], x_recv.at[9], across))
    for copy in x_copies + own_cols:
        copy.start()

    def to_device(d, dst_dp):
        chunk = pl.ds(pl.multiple_of(dst_dp * CBLOCK, CBLOCK), CBLOCK)
        dst = target(dst_dp, spot)
        return [
            remote(ck_ref.at[:, chunk, :], held_ref.at[me, :, 0], all_send.at[0, d], all_recv.at[0, d], dst),
            remote(cv_ref.at[:, chunk, :], held_ref.at[me, :, 1], all_send.at[1, d], all_recv.at[1, d], dst),
        ]

    for copy in weight_copies:
        copy.wait_recv()

    def block(zz, yy, c):
        return first_ref.at[pl.ds(pl.multiple_of((zz * 4 + yy * 2 + c) * rows, rows), rows), :]

    def along(s, direction):
        zz = z - (s - 1) if direction == 0 else z + (s - 1)
        to = z + 1 if direction == 0 else z - 1
        k = (s - 1) * 2 + direction
        held = block(zz, y, core)
        return remote(held, held, ring_send.at[k], ring_recv.at[k], target(to * 4 + y * 2 + core, spot))

    def sends(s, direction):
        return (z < 3) & (z - (s - 1) >= 0) if direction == 0 else (z > 0) & (z + (s - 1) <= 3)

    def gets(s, direction):
        return z - s >= 0 if direction == 0 else z + s <= 3

    def to_line(zz):
        held = block(zz, y, core)
        return remote(held, held, line_send.at[zz], line_recv.at[zz], target(z * 4 + (1 - y) * 2 + core, spot))

    def to_pair(zz, yy):
        held = block(zz, yy, core)
        k = zz * 2 + yy
        return remote(held, held, pair_send.at[k], pair_recv.at[k], target(me + 1 - 2 * core, spot))

    for direction in range(2):

        @pl.when(sends(1, direction))
        def _():
            along(1, direction).start()

    to_line(z).start()
    to_pair(z, y).start()
    copies = []
    order = [8, 4, 12, 6, 10, 2, 14, 9, 5, 13, 1, 7, 11, 3, 15]
    assert sorted(order) == list(range(1, devices))

    def some(count):
        for d in order[:count]:
            for copy in to_device(d, (me + d) % devices):
                copy.start()
                copies.append(copy)
        del order[:count]

    some(3)
    chunk = pl.ds(pl.multiple_of(me * CBLOCK, CBLOCK), CBLOCK)
    kept = [
        pltpu.make_async_copy(ck_ref.at[:, chunk, :], held_ref.at[me, :, 0], local_sem.at[10]),
        pltpu.make_async_copy(cv_ref.at[:, chunk, :], held_ref.at[me, :, 1], local_sem.at[11]),
    ]
    for copy in kept:
        copy.start()
    for load, store in zip(loads, stores):
        load.wait()
        store.start()
    for s in range(1, 4):
        for direction in range(2):

            @pl.when(gets(s, direction))
            def _():
                along(s, direction).wait_recv()
                zz = z - s if direction == 0 else z + s
                if s < 3:

                    @pl.when(sends(s + 1, direction))
                    def _():
                        along(s + 1, direction).start()

                to_line(zz).start()
                to_pair(zz, y).start()

        some(2)
    for zz in range(4):
        to_line(zz).wait_recv()
        to_pair(zz, 1 - y).start()
        some(1)
    some(devices)
    for s in range(1, 4):
        for direction in range(2):

            @pl.when(sends(s, direction))
            def _():
                along(s, direction).wait_send()

    for zz in range(4):
        to_line(zz).wait_send()
        for yy in range(2):
            to_pair(zz, yy).wait()
    for copy in weight_copies:
        copy.wait_send()
    for copy in x_copies + copies:
        copy.wait()
    for copy in stores + own_cols + kept:
        copy.wait()


def spread(tokens, cache_keys, cache_values, small, extra, big, devices):
    micro, shard_len, width = tokens.shape
    rows, cols = small.shape[0], small.shape[1] // 3
    anywhere = pl.BlockSpec(memory_space=pltpu.HBM)
    vmem = pl.BlockSpec(memory_space=pltpu.VMEM)
    dma = pltpu.SemaphoreType.DMA
    return pl.pallas_call(
        spread_kernel,
        in_specs=[anywhere, anywhere, anywhere, vmem, vmem, vmem],
        out_specs=[anywhere, anywhere, anywhere, anywhere, vmem, anywhere],
        out_shape=[
            jax.ShapeDtypeStruct((2, shard_len, width), BF16),
            jax.ShapeDtypeStruct((2, CACHE_LEN, cols), BF16),
            jax.ShapeDtypeStruct((2, CACHE_LEN, cols), BF16),
            jax.ShapeDtypeStruct((devices, micro, 2, CBLOCK, cols), BF16),
            jax.ShapeDtypeStruct((rows * devices, 6 * cols + HD), BF16),
            jax.ShapeDtypeStruct((rows, 2 * big.shape[1]), BF16),
        ],
        scratch_shapes=[
            pltpu.VMEM((shard_len, width), BF16),
            pltpu.VMEM((CACHE_LEN, cols), BF16),
            pltpu.VMEM((CACHE_LEN, cols), BF16),
            dma((12,)), dma((10,)), dma((10,)), dma((2, devices)), dma((2, devices)),
            dma((6,)), dma((6,)), dma((4,)), dma((4,)), dma((8,)), dma((8,)),
        ],
        compiler_params=pltpu.CompilerParams(collective_id=0, has_side_effects=True, vmem_limit_bytes=60 * MIB),
        cost_estimate=pl.CostEstimate(flops=0, bytes_accessed=300 * MIB, transcendentals=0),
        name="spread",
    )(tokens, cache_keys, cache_values, small, extra, big)


def swap(values):
    return lax.ppermute(values, "tensor", [(0, 1), (1, 0)])


def sequence_body(
    tokens, gain_attn, w_query, w_key, w_value, w_out, gain_ffn, w_gate, w_up, w_down,
    cache_keys, cache_values, prefix, partner, own_blocks, partner_blocks, grad_out,
):
    micro, shard_len, width = tokens.shape
    devices = lax.axis_size("dp")
    seqs = micro * devices
    rows_held, cols = w_query.shape
    hidden_held = w_gate.shape[1]
    hidden = 2 * hidden_held
    spot = lax.axis_index("tensor")
    exchange = functools.partial(lax.all_to_all, axis_name="tensor", split_axis=0, concat_axis=0, tiled=True)
    chunks = CACHE_LEN // CBLOCK

    small = jnp.concatenate([w_query, w_key, w_value], axis=1)
    partner_column = jnp.zeros((rows_held, 1), BF16).at[:micro, 0].set(partner.astype(BF16))
    extra = jnp.concatenate(
        [gain_attn[:, None], gain_ffn[:, None], partner_column, jnp.zeros((rows_held, HD - 3), BF16)], axis=1
    )
    big = jnp.concatenate([w_out.T, w_gate, w_up, w_down.T], axis=1)
    x, own_k, own_v, held, first_all, second_rows = spread(
        tokens, cache_keys, cache_values, small, extra, big, devices
    )
    x = x.reshape(L, width)
    theirs = swap(lax.dynamic_index_in_dim(grad_out, 1 - spot, 0, keepdims=False))
    mine = lax.dynamic_index_in_dim(grad_out, spot, 0, keepdims=False)
    cotangent = jnp.where(spot == 0, jnp.concatenate([mine, theirs], 0), jnp.concatenate([theirs, mine], 0))
    second_all = lax.all_gather(second_rows, "dp", axis=0, tiled=True)

    tail = lax.optimization_barrier(first_all[:, 3 * width :])
    gains = mm((jnp.arange(2)[:, None] == jnp.arange(HD)[None, :]).astype(BF16), tail, NT)
    gain_one, gain_two = gains[:1], gains[1:]
    table = tail[:, 2].reshape(devices, rows_held)[:, :micro].reshape(seqs).astype(jnp.int32)
    sent = pick_rows(table, held.reshape(seqs, 2 * CBLOCK, cols))
    fetched = lax.all_to_all(sent, ("dp", "tensor"), split_axis=0, concat_axis=0, tiled=True)
    fetched = fetched.reshape(chunks, 2, 2, CBLOCK, cols)

    meta = jnp.concatenate(
        [
            prefix[spot][None], spot[None].astype(jnp.int32),
            own_blocks[spot].reshape(-1), partner_blocks[spot].reshape(-1),
        ]
    )
    normed, qkv = project(x, gain_one, first_all)
    partial, partial_lse = attend(meta, qkv, own_k, own_v)
    context, lse = attend_other(meta, qkv, fetched, partial, partial_lse)
    mixed, normed_two = mix(x, context, gain_two, second_all)
    ffn_grads, gain_part_two, out, grad_mixed, branch, grad_context = ffn(
        normed_two, cotangent, second_all, gain_two, mixed, width, hidden, devices
    )
    ffn_share = lax.psum_scatter(
        ffn_grads, "dp", scatter_dimension=0, tiled=True,
        axis_index_groups=[list(range(c, devices, 2)) for c in range(2)],
    )
    out = exchange(out.reshape(2, shard_len, width))
    dq, dk, dv = attend_back(meta, qkv, own_k, own_v, fetched, grad_context, context, lse)
    dq, out = lax.optimization_barrier((dq, out))
    grad_tokens, gain_sums, attn_share = finish(
        x, grad_mixed, normed, context, branch, dq, dk, dv, first_all, gain_one, gain_part_two, devices
    )
    grad_tokens = grad_tokens.astype(F32)
    g_out, g_value, g_key, g_query = jnp.split(attn_share, 4, axis=1)
    g_gate, g_up, g_down = [
        ffn_share[:, i * hidden_held : (i + 1) * hidden_held].astype(F32) for i in range(3)
    ]
    return (
        out, grad_tokens, gain_sums[0], g_query, g_key, g_value, g_out.T, gain_sums[1], g_gate, g_up, g_down.T,
    )


def solution(mesh):
    in_specs = (
        P("dp", "tensor", None),
        P("dp"),
        P("dp", "tensor"),
        P("dp", "tensor"),
        P("dp", "tensor"),
        P("tensor", "dp"),
        P("dp"),
        P("dp", "tensor"),
        P("dp", "tensor"),
        P("tensor", "dp"),
        P("dp", None, "tensor"),
        P("dp", None, "tensor"),
        P("dp"),
        P("dp"),
        P("dp", None, None),
        P("dp", None, None),
        P("dp", "tensor", None),
    )
    out_specs = (
        P("dp", "tensor", None),
        P("dp", "tensor", None),
        P(),
        P("dp", "tensor"),
        P("dp", "tensor"),
        P("dp", "tensor"),
        P("tensor", "dp"),
        P(),
        P("dp", "tensor"),
        P("dp", "tensor"),
        P("tensor", "dp"),
    )
    whole = mesh.shape["tensor"] == 2 and mesh.shape["dp"] == CACHE_LEN // CBLOCK
    body = sequence_body if whole else tensor_body
    return jax.shard_map(body, mesh=mesh, in_specs=in_specs, out_specs=out_specs, check_vma=False)
```

```python
import functools

import jax
import jax.numpy as jnp
from jax import lax
from jax.experimental import pallas as pl
from jax.experimental.pallas import tpu as pltpu
from jax.sharding import PartitionSpec as P

HD = 128
L = 2048
CACHE_LEN = 1024
QBLOCK = 128
CBLOCK = 64
KR = 4
QROWS = 512


EPS = 1e-05
NEGATIVE = -1e30


def norm_rows(values, gain):
    scale_rows = lax.rsqrt(jnp.mean(values * values, axis=-1, keepdims=True) + EPS)
    return (values * scale_rows * gain, scale_rows)


def norm_back(grad_normed, values, scale_rows, gain):
    unit = values * scale_rows
    grad_unit = grad_normed * gain
    grad_values = scale_rows * (
        grad_unit - unit * jnp.mean(grad_unit * unit, axis=-1, keepdims=True)
    )
    return (grad_values, jnp.sum(grad_normed * unit, axis=0))


def inner_rows(left, right):
    return lax.dot_general(
        left, right, (((0,), (0,)), ((), ())), preferred_element_type=jnp.float32
    )


def outer_cols(left, right):
    return lax.dot_general(
        left, right, (((1,), (1,)), ((), ())), preferred_element_type=jnp.float32
    )


def memory_rows(cache_one, chosen, width):
    shaped = cache_one.reshape(CACHE_LEN // CBLOCK, CBLOCK, width)
    return jnp.take(shaped, chosen, axis=0)


def block_scores(query_block, keys_part, mem_part, first_row, limit):
    rows_here, heads_here, size = query_block.shape
    extent = keys_part.shape[0]
    local = jnp.einsum(
        "qhd,khd->hqk", query_block, keys_part, preferred_element_type=jnp.float32
    ) * size ** (-0.5)
    row_ids = first_row + jnp.arange(rows_here, dtype=jnp.int32)[:, None]
    key_ids = jnp.arange(extent, dtype=jnp.int32)[None, :]
    allowed = (key_ids <= row_ids) | (row_ids < limit) & (key_ids < limit)
    local = jnp.where(allowed[None], local, NEGATIVE)
    groups = mem_part.shape[0]
    grouped = query_block.reshape(groups, rows_here // groups, heads_here, size)
    remote = jnp.einsum(
        "bqhd,bkhd->hbqk", grouped, mem_part, preferred_element_type=jnp.float32
    ) * size ** (-0.5)
    return (local, remote.reshape(heads_here, rows_here, -1))


def attention_forward(query, keys, values, mem_keys, mem_values, limit):
    groups = QROWS // QBLOCK
    heads_here = query.shape[1]
    context_parts = []
    lse_parts = []
    for index in range(L // QROWS):
        first = index * QROWS
        extent = max(first + QROWS, L // 2)
        query_block = query[first : first + QROWS]
        mem_k = mem_keys[index * groups : (index + 1) * groups]
        mem_v = mem_values[index * groups : (index + 1) * groups]
        local, remote = block_scores(query_block, keys[:extent], mem_k, first, limit)
        top = jnp.maximum(jnp.max(local, axis=-1), jnp.max(remote, axis=-1))
        e_local = jnp.exp(local - top[..., None])
        e_remote = jnp.exp(remote - top[..., None])
        total = jnp.sum(e_local, axis=-1) + jnp.sum(e_remote, axis=-1)
        p_local = (e_local / total[..., None]).astype(jnp.bfloat16)
        p_remote = (
            (e_remote / total[..., None])
            .astype(jnp.bfloat16)
            .reshape(heads_here, groups, QBLOCK, -1)
        )
        part = jnp.einsum(
            "hqk,khd->qhd", p_local, values[:extent], preferred_element_type=jnp.float32
        )
        extra = jnp.einsum("hbqk,bkhd->bqhd", p_remote, mem_v, preferred_element_type=jnp.float32)
        context_parts.append(part + extra.reshape(part.shape))
        lse_parts.append(top + jnp.log(total))
    return (jnp.concatenate(context_parts, axis=0), lse_parts)


def attention_backward(query, keys, values, mem_keys, mem_values, limit, lse_parts, grad_context):
    groups = QROWS // QBLOCK
    length, heads_here, size = query.shape
    scale = size ** (-0.5)
    grad_query_parts = []
    grad_keys = jnp.zeros(query.shape, jnp.float32)
    grad_values = jnp.zeros(query.shape, jnp.float32)
    for index in range(L // QROWS):
        first = index * QROWS
        extent = max(first + QROWS, L // 2)
        query_block = query[first : first + QROWS]
        mem_k = mem_keys[index * groups : (index + 1) * groups]
        mem_v = mem_values[index * groups : (index + 1) * groups]
        local, remote = block_scores(query_block, keys[:extent], mem_k, first, limit)
        lse_block = lse_parts[index][..., None]
        p_local = jnp.exp(local - lse_block)
        p_remote = jnp.exp(remote - lse_block)
        grad_block = grad_context[first : first + QROWS]
        grouped_grad = grad_block.reshape(groups, QBLOCK, heads_here, size)
        dp_local = jnp.einsum(
            "qhd,khd->hqk", grad_block, values[:extent], preferred_element_type=jnp.float32
        )
        dp_remote = jnp.einsum(
            "bqhd,bkhd->hbqk", grouped_grad, mem_v, preferred_element_type=jnp.float32
        )
        dp_remote = dp_remote.reshape(heads_here, QROWS, -1)
        delta = jnp.sum(p_local * dp_local, axis=-1) + jnp.sum(p_remote * dp_remote, axis=-1)
        ds_local = (p_local * (dp_local - delta[..., None])).astype(jnp.bfloat16)
        ds_remote = (p_remote * (dp_remote - delta[..., None])).astype(jnp.bfloat16)
        ds_remote = ds_remote.reshape(heads_here, groups, QBLOCK, -1)
        dq_block = jnp.einsum(
            "hqk,khd->qhd", ds_local, keys[:extent], preferred_element_type=jnp.float32
        )
        dq_extra = jnp.einsum(
            "hbqk,bkhd->bqhd", ds_remote, mem_k, preferred_element_type=jnp.float32
        )
        grad_query_parts.append((dq_block + dq_extra.reshape(dq_block.shape)) * scale)
        dk_part = (
            jnp.einsum("hqk,qhd->khd", ds_local, query_block, preferred_element_type=jnp.float32)
            * scale
        )
        dv_part = jnp.einsum(
            "hqk,qhd->khd",
            p_local.astype(jnp.bfloat16),
            grad_block,
            preferred_element_type=jnp.float32,
        )
        grad_keys = grad_keys.at[:extent].add(dk_part)
        grad_values = grad_values.at[:extent].add(dv_part)
    return (jnp.concatenate(grad_query_parts, axis=0), grad_keys, grad_values)


def tensor_body(
    tokens,
    gain_attn,
    w_query,
    w_key,
    w_value,
    w_out,
    gain_ffn,
    w_gate,
    w_up,
    w_down,
    cache_keys,
    cache_values,
    prefix,
    partner,
    own_blocks,
    partner_blocks,
    grad_out,
):
    micro, shard_len, width = tokens.shape
    cols = w_query.shape[1]
    heads_local = cols // HD
    qblocks = L // QBLOCK
    mem_len = 2 * KR * CBLOCK
    piece_keys = lax.all_gather(cache_keys, "dp", axis=0, tiled=True)
    piece_values = lax.all_gather(cache_values, "dp", axis=0, tiled=True)
    count = piece_keys.shape[0]
    onehot = (partner[:, None] == jnp.arange(count, dtype=jnp.int32)[None, :]).astype(jnp.bfloat16)
    add_keys = jnp.einsum("mn,nkc->mkc", onehot, piece_keys, preferred_element_type=jnp.float32)
    add_values = jnp.einsum("mn,nkc->mkc", onehot, piece_values, preferred_element_type=jnp.float32)
    fetched_keys = add_keys.astype(jnp.bfloat16)
    fetched_values = add_values.astype(jnp.bfloat16)
    totals = (
        jnp.zeros((width, cols), jnp.float32),
        jnp.zeros((width, cols), jnp.float32),
        jnp.zeros((width, cols), jnp.float32),
        jnp.zeros((cols, width), jnp.float32),
        jnp.zeros((width, w_gate.shape[1]), jnp.float32),
        jnp.zeros((width, w_gate.shape[1]), jnp.float32),
        jnp.zeros((w_gate.shape[1], width), jnp.float32),
    )
    shares = tuple(
        (
            jnp.zeros(w.shape, jnp.float32)
            for w in (w_query, w_key, w_value, w_out, w_gate, w_up, w_down)
        )
    )
    gain_total_attn = jnp.zeros((width,), jnp.float32)
    gain_total_ffn = jnp.zeros((width,), jnp.float32)
    out_rows = []
    grad_rows = []
    for step in range(micro):
        fwd = (
            lax.all_gather(gain_attn, "dp", axis=0, tiled=True),
            lax.all_gather(w_query, "dp", axis=0, tiled=True),
            lax.all_gather(w_key, "dp", axis=0, tiled=True),
            lax.all_gather(w_value, "dp", axis=0, tiled=True),
            lax.all_gather(w_out, "dp", axis=1, tiled=True),
            lax.all_gather(gain_ffn, "dp", axis=0, tiled=True),
            lax.all_gather(w_gate, "dp", axis=0, tiled=True),
            lax.all_gather(w_up, "dp", axis=0, tiled=True),
            lax.all_gather(w_down, "dp", axis=1, tiled=True),
        )
        g_attn, wq_full, wk_full, wv_full, wo_full, g_ffn, wg_full, wu_full, wd_full = fwd
        limit = prefix[step]
        own_k = memory_rows(cache_keys[step], own_blocks[step], cols)
        par_k = memory_rows(fetched_keys[step], partner_blocks[step], cols)
        own_v = memory_rows(cache_values[step], own_blocks[step], cols)
        par_v = memory_rows(fetched_values[step], partner_blocks[step], cols)
        mem_keys = jnp.concatenate([own_k, par_k], axis=1).reshape(
            qblocks, mem_len, heads_local, HD
        )
        mem_values = jnp.concatenate([own_v, par_v], axis=1).reshape(
            qblocks, mem_len, heads_local, HD
        )
        token_rows = tokens[step].astype(jnp.float32)
        normed, scale_one = norm_rows(token_rows, g_attn.astype(jnp.float32))
        normed_all = lax.all_gather(normed.astype(jnp.bfloat16), "tensor", axis=0, tiled=True)
        query = (
            jnp.dot(normed_all, wq_full, preferred_element_type=jnp.float32)
            .astype(jnp.bfloat16)
            .reshape(L, heads_local, HD)
        )
        keys = (
            jnp.dot(normed_all, wk_full, preferred_element_type=jnp.float32)
            .astype(jnp.bfloat16)
            .reshape(L, heads_local, HD)
        )
        values = (
            jnp.dot(normed_all, wv_full, preferred_element_type=jnp.float32)
            .astype(jnp.bfloat16)
            .reshape(L, heads_local, HD)
        )
        context_full, lse_parts = attention_forward(
            query, keys, values, mem_keys, mem_values, limit
        )
        context = context_full.reshape(L, cols).astype(jnp.bfloat16)
        mixed = token_rows + lax.psum_scatter(
            jnp.dot(context, wo_full, preferred_element_type=jnp.float32),
            "tensor",
            scatter_dimension=0,
            tiled=True,
        )
        normed_two, scale_two = norm_rows(mixed, g_ffn.astype(jnp.float32))
        normed_two_all = lax.all_gather(
            normed_two.astype(jnp.bfloat16), "tensor", axis=0, tiled=True
        )
        gate = jnp.dot(normed_two_all, wg_full, preferred_element_type=jnp.float32)
        upward = jnp.dot(normed_two_all, wu_full, preferred_element_type=jnp.float32)
        sigma = jax.nn.sigmoid(gate)
        silu_gate = gate * sigma
        hidden = (silu_gate * upward).astype(jnp.bfloat16)
        out_rows.append(
            (
                mixed
                + lax.psum_scatter(
                    jnp.dot(hidden, wd_full, preferred_element_type=jnp.float32).astype(
                        jnp.bfloat16
                    ),
                    "tensor",
                    scatter_dimension=0,
                    tiled=True,
                ).astype(jnp.float32)
            ).astype(jnp.bfloat16)
        )
        bwd = (
            lax.all_gather(gain_attn, "dp", axis=0, tiled=True),
            lax.all_gather(w_query, "dp", axis=0, tiled=True),
            lax.all_gather(w_key, "dp", axis=0, tiled=True),
            lax.all_gather(w_value, "dp", axis=0, tiled=True),
            lax.all_gather(w_out, "dp", axis=1, tiled=True),
            lax.all_gather(gain_ffn, "dp", axis=0, tiled=True),
            lax.all_gather(w_gate, "dp", axis=0, tiled=True),
            lax.all_gather(w_up, "dp", axis=0, tiled=True),
            lax.all_gather(w_down, "dp", axis=1, tiled=True),
        )
        g_attn, wq_full, wk_full, wv_full, wo_full, g_ffn, wg_full, wu_full, wd_full = bwd
        grad_here = grad_out[step]
        grad_all = lax.all_gather(grad_here, "tensor", axis=0, tiled=True)
        d_down = inner_rows(hidden, grad_all)
        grad_hidden = outer_cols(grad_all, wd_full)
        grad_gate = (grad_hidden * upward * sigma * (1.0 + gate * (1.0 - sigma))).astype(
            jnp.bfloat16
        )
        grad_up = (grad_hidden * silu_gate).astype(jnp.bfloat16)
        d_gate = inner_rows(normed_two_all, grad_gate)
        d_up = inner_rows(normed_two_all, grad_up)
        grad_normed_two = lax.psum_scatter(
            outer_cols(grad_gate, wg_full) + outer_cols(grad_up, wu_full),
            "tensor",
            scatter_dimension=0,
            tiled=True,
        )
        grad_mixed_norm, gain_part_ffn = norm_back(
            grad_normed_two, mixed, scale_two, g_ffn.astype(jnp.float32)
        )
        grad_mixed = grad_here.astype(jnp.float32) + grad_mixed_norm
        branch_all = lax.all_gather(grad_mixed.astype(jnp.bfloat16), "tensor", axis=0, tiled=True)
        d_out = inner_rows(context, branch_all)
        grad_context = (
            outer_cols(branch_all, wo_full).astype(jnp.bfloat16).reshape(L, heads_local, HD)
        )
        grad_query, grad_keys, grad_values = attention_backward(
            query, keys, values, mem_keys, mem_values, limit, lse_parts, grad_context
        )
        grad_query = grad_query.reshape(L, cols).astype(jnp.bfloat16)
        grad_keys = grad_keys.reshape(L, cols).astype(jnp.bfloat16)
        grad_values = grad_values.reshape(L, cols).astype(jnp.bfloat16)
        d_query = inner_rows(normed_all, grad_query)
        d_key = inner_rows(normed_all, grad_keys)
        d_value = inner_rows(normed_all, grad_values)
        grad_normed = lax.psum_scatter(
            (
                outer_cols(grad_query, wq_full)
                + outer_cols(grad_keys, wk_full)
                + outer_cols(grad_values, wv_full)
            ).astype(jnp.bfloat16),
            "tensor",
            scatter_dimension=0,
            tiled=True,
        ).astype(jnp.float32)
        grad_token_norm, gain_part_attn = norm_back(
            grad_normed, token_rows, scale_one, g_attn.astype(jnp.float32)
        )
        grad_rows.append(grad_mixed + grad_token_norm)
        gain_total_attn = gain_total_attn + gain_part_attn
        gain_total_ffn = gain_total_ffn + gain_part_ffn
        totals = tuple(
            (
                held + fresh
                for held, fresh in zip(
                    totals, (d_query, d_key, d_value, d_out, d_gate, d_up, d_down)
                )
            )
        )
    shares = (
        lax.psum_scatter(
            totals[0].astype(jnp.bfloat16), "dp", scatter_dimension=0, tiled=True
        ).astype(jnp.float32),
        lax.psum_scatter(
            totals[1].astype(jnp.bfloat16), "dp", scatter_dimension=0, tiled=True
        ).astype(jnp.float32),
        lax.psum_scatter(
            totals[2].astype(jnp.bfloat16), "dp", scatter_dimension=0, tiled=True
        ).astype(jnp.float32),
        lax.psum_scatter(
            totals[3].astype(jnp.bfloat16), "dp", scatter_dimension=1, tiled=True
        ).astype(jnp.float32),
        lax.psum_scatter(
            totals[4].astype(jnp.bfloat16), "dp", scatter_dimension=0, tiled=True
        ).astype(jnp.float32),
        lax.psum_scatter(
            totals[5].astype(jnp.bfloat16), "dp", scatter_dimension=0, tiled=True
        ).astype(jnp.float32),
        lax.psum_scatter(
            totals[6].astype(jnp.bfloat16), "dp", scatter_dimension=1, tiled=True
        ).astype(jnp.float32),
    )
    gain_attn_sum, gain_ffn_sum = lax.psum((gain_total_attn, gain_total_ffn), ("dp", "tensor"))
    return (
        jnp.stack(out_rows, axis=0),
        jnp.stack(grad_rows, axis=0),
        gain_attn_sum,
        shares[0],
        shares[1],
        shares[2],
        shares[3],
        gain_ffn_sum,
        shares[4],
        shares[5],
        shares[6],
    )


TQ = 512
TK = 512
ROWS = 512
HT = 256
SCALE = HD**-0.5
EXP_SCALE = SCALE * 1.4426950408889634
LOG2E = 1.4426950408889634
NT = (((1,), (1,)), ((), ()))
TN = (((0,), (0,)), ((), ()))
F32 = jnp.float32
BF16 = jnp.bfloat16
MIB = 1 << 20


def mm(left, right, dims=(((1,), (0,)), ((), ()))):
    return lax.dot_general(left, right, dims, preferred_element_type=F32)


def fold_max(values):
    best = values[:, :HD]
    for i in range(1, values.shape[1] // HD):
        best = jnp.maximum(best, values[:, i * HD : (i + 1) * HD])
    return best


def fold_sum(values):
    total = values[:, :HD]
    for i in range(1, values.shape[1] // HD):
        total = total + values[:, i * HD : (i + 1) * HD]
    return total


def reach_mask(first, tile, limit):
    rows = first + lax.broadcasted_iota(jnp.int32, (TQ, 1), 0)
    keys = tile * TK + lax.broadcasted_iota(jnp.int32, (1, TK), 1)
    reach = jnp.where(rows < limit, jnp.maximum(rows, limit - 1), rows)
    return keys <= reach


def pick_own(meta, block, own, buf):
    for i in range(KR):
        c = meta[2 + block * KR + i]
        buf[pl.ds(i * CBLOCK, CBLOCK), :] = own[0, pl.ds(pl.multiple_of(c * CBLOCK, CBLOCK), CBLOCK), :]


def pick_other(meta, block, other, buf, start=0):
    for i in range(KR):
        d = meta[2 + (L // QBLOCK) * KR + block * KR + i]
        buf[pl.ds(start + i * CBLOCK, CBLOCK), :] = other[d, 0, 0]


def pick_blocks(meta, block, own, other, buf):
    pick_own(meta, block, own, buf)
    pick_other(meta, block, other, buf, KR * CBLOCK)


def attend_kernel(
    meta, q_ref, k_ref, v_ref, ok_ref, ov_ref, ctx_ref, lse_ref, kbuf, vbuf, sbuf, smem, *, pair
):
    step = pl.program_id(1)
    limit = meta[0]
    first = step * TQ
    free = jnp.where(first < limit, (limit + TK - 1) // TK, 0)
    tiles = jnp.maximum(step + 1, free)
    blocks = TQ // QBLOCK
    for b in range(blocks):
        pick_own(meta, step * blocks + b, ok_ref, kbuf.at[b])
        pick_own(meta, step * blocks + b, ov_ref, vbuf.at[b])
    state = []
    for h in range(pair):
        cs = pl.ds(h * HD, HD)
        best = []
        for b in range(blocks):
            s = mm(q_ref[pl.ds(b * QBLOCK, QBLOCK), cs], kbuf[b, :, cs], NT)
            smem[h, pl.ds(b * QBLOCK, QBLOCK), :] = s
            best.append(fold_max(s))
        state.append(jnp.concatenate(best, 0))

    def scores(tile, state, masked):
        ks = pl.ds(pl.multiple_of(tile * TK, TK), TK)
        if masked:
            allowed = reach_mask(first, tile, limit)
        new = []
        for h in range(pair):
            cs = pl.ds(h * HD, HD)
            s = mm(q_ref[:, cs], k_ref[ks, cs], NT)
            if masked:
                s = jnp.where(allowed, s, NEGATIVE)
            sbuf[h, tile] = s
            new.append(jnp.maximum(state[h], fold_max(s)))
        return tuple(new)

    state = lax.fori_loop(0, step, lambda tile, s: scores(tile, s, False), tuple(state))
    state = lax.fori_loop(step, tiles, lambda tile, s: scores(tile, s, True), state)
    tops = [jnp.max(s, axis=1, keepdims=True) for s in state]
    state = []
    for h in range(pair):
        cs = pl.ds(h * HD, HD)
        p = jnp.exp2((smem[h] - tops[h]) * EXP_SCALE)
        low = p.astype(BF16)
        parts = [mm(low[b * QBLOCK : (b + 1) * QBLOCK], vbuf[b, :, cs]) for b in range(blocks)]
        state.append((fold_sum(p), jnp.concatenate(parts, 0)))

    def weigh(tile, state):
        ks = pl.ds(pl.multiple_of(tile * TK, TK), TK)
        new = []
        for h in range(pair):
            total, acc = state[h]
            p = jnp.exp2((sbuf[h, tile] - tops[h]) * EXP_SCALE)
            new.append((total + fold_sum(p), acc + mm(p.astype(BF16), v_ref[ks, pl.ds(h * HD, HD)])))
        return tuple(new)

    state = lax.fori_loop(0, tiles, weigh, tuple(state))
    for h in range(pair):
        cs = pl.ds(h * HD, HD)
        total = jnp.sum(state[h][0], axis=1, keepdims=True)
        ctx_ref[:, cs] = state[h][1] / total
        lse_ref[:, cs] = jnp.broadcast_to(tops[h] * SCALE + jnp.log(total), (TQ, HD))


def attend_other_kernel(meta, q_ref, pk_ref, pv_ref, part_ref, plse_ref, ctx_ref, lse_ref, kbuf, vbuf, *, pair):
    step = pl.program_id(1)
    blocks = TQ // QBLOCK
    for b in range(blocks):
        pick_other(meta, step * blocks + b, pk_ref, kbuf.at[b])
        pick_other(meta, step * blocks + b, pv_ref, vbuf.at[b])
    for h in range(pair):
        cs = pl.ds(h * HD, HD)
        rows = [pl.ds(b * QBLOCK, QBLOCK) for b in range(blocks)]
        s = jnp.concatenate([mm(q_ref[rows[b], cs], kbuf[b, :, cs], NT) for b in range(blocks)], 0)
        before = plse_ref[:, cs]
        top = jnp.maximum(before, jnp.max(fold_max(s), axis=1, keepdims=True) * SCALE)
        keep = jnp.exp(before - top)
        p = jnp.exp2(s * EXP_SCALE - top[:, :1] * LOG2E)
        low = p.astype(BF16)
        more = jnp.concatenate(
            [mm(low[b * QBLOCK : (b + 1) * QBLOCK], vbuf[b, :, cs]) for b in range(blocks)], 0
        )
        total = keep + jnp.sum(fold_sum(p), axis=1, keepdims=True)
        ctx_ref[:, cs] = ((part_ref[:, cs] * keep + more) / total).astype(BF16)
        lse_ref[:, cs] = top + jnp.log(total)


def attend_back_kernel(
    meta, q_ref, k_ref, v_ref, ok_ref, ov_ref, pk_ref, pv_ref, do_ref, ctx_ref, lse_ref,
    dq_ref, dk_ref, dv_ref, kbuf, vbuf, dks, dvs, *, pair
):
    step = pl.program_id(1)
    limit = meta[0]
    first = step * TQ
    free = jnp.where(first < limit, (limit + TK - 1) // TK, 0)
    tiles = jnp.maximum(step + 1, free)
    blocks = TQ // QBLOCK

    @pl.when(step == 0)
    def _():
        dks[...] = jnp.zeros_like(dks)
        dvs[...] = jnp.zeros_like(dvs)

    for b in range(blocks):
        pick_blocks(meta, step * blocks + b, ok_ref, pk_ref, kbuf.at[b])
        pick_blocks(meta, step * blocks + b, ov_ref, pv_ref, vbuf.at[b])
    state = []
    aux = []
    for h in range(pair):
        cs = pl.ds(h * HD, HD)
        delta = jnp.sum(do_ref[:, cs].astype(F32) * ctx_ref[:, cs].astype(F32), axis=1, keepdims=True)
        lse2 = lse_ref[:, cs][:, :1] * LOG2E
        aux.append((lse2, delta))
        parts = []
        for b in range(blocks):
            rs = pl.ds(b * QBLOCK, QBLOCK)
            s = mm(q_ref[rs, cs], kbuf[b, :, cs], NT)
            p = jnp.exp2(s * EXP_SCALE - lse2[b * QBLOCK : (b + 1) * QBLOCK])
            dp = mm(do_ref[rs, cs], vbuf[b, :, cs], NT)
            ds = (p * (dp - delta[b * QBLOCK : (b + 1) * QBLOCK])).astype(BF16)
            parts.append(mm(ds, kbuf[b, :, cs]))
        state.append(jnp.concatenate(parts, 0))

    def grads(tile, state, masked):
        ks = pl.ds(pl.multiple_of(tile * TK, TK), TK)
        if masked:
            allowed = reach_mask(first, tile, limit)
        new = []
        for h in range(pair):
            cs = pl.ds(h * HD, HD)
            lse2, delta = aux[h]
            s = mm(q_ref[:, cs], k_ref[ks, cs], NT)
            p = jnp.exp2(s * EXP_SCALE - lse2)
            if masked:
                p = jnp.where(allowed, p, 0.0)
            dp = mm(do_ref[:, cs], v_ref[ks, cs], NT)
            ds = (p * (dp - delta)).astype(BF16)
            dvs[ks, cs] += mm(p.astype(BF16), do_ref[:, cs], TN)
            dks[ks, cs] += mm(ds, q_ref[:, cs], TN)
            new.append(state[h] + mm(ds, k_ref[ks, cs]))
        return tuple(new)

    state = lax.fori_loop(0, step, lambda tile, s: grads(tile, s, False), tuple(state))
    state = lax.fori_loop(step, tiles, lambda tile, s: grads(tile, s, True), state)
    for h in range(pair):
        dq_ref[:, pl.ds(h * HD, HD)] = (state[h] * SCALE).astype(BF16)

    @pl.when(step == L // TQ - 1)
    def _():
        dk_ref[...] = (dks[...] * SCALE).astype(BF16)
        dv_ref[...] = dvs[...].astype(BF16)


def attention_specs(heads, pair):
    wide = pair * HD
    per = heads // 2 // pair
    groups = heads // pair
    return [
        pl.BlockSpec((TQ, wide), lambda h, i, meta: (i, h)),
        pl.BlockSpec((L, wide), lambda h, i, meta: (0, groups + h)),
        pl.BlockSpec((L, wide), lambda h, i, meta: (0, 2 * groups + h)),
        pl.BlockSpec((1, CACHE_LEN, wide), lambda h, i, meta: ((h // per) ^ meta[1], 0, h % per)),
        pl.BlockSpec((1, CACHE_LEN, wide), lambda h, i, meta: ((h // per) ^ meta[1], 0, h % per)),
        pl.BlockSpec(
            (CACHE_LEN // CBLOCK, 1, 1, CBLOCK, wide),
            lambda h, i, meta: (0, (h // per) ^ meta[1], 0, 0, h % per),
        ),
        pl.BlockSpec(
            (CACHE_LEN // CBLOCK, 1, 1, CBLOCK, wide),
            lambda h, i, meta: (0, (h // per) ^ meta[1], 1, 0, h % per),
        ),
    ]


def attend(meta, qkv, own_k, own_v, pair=4):
    width = qkv.shape[1] // 3
    heads = width // HD
    wide = pair * HD
    row = pl.BlockSpec((TQ, wide), lambda h, i, meta: (i, h))
    area = L * 1600 * width
    return pl.pallas_call(
        functools.partial(attend_kernel, pair=pair),
        grid_spec=pltpu.PrefetchScalarGridSpec(
            num_scalar_prefetch=1,
            grid=(heads // pair, L // TQ),
            in_specs=attention_specs(heads, pair)[:5],
            out_specs=[row, row],
            scratch_shapes=[pltpu.VMEM((TQ // QBLOCK, KR * CBLOCK, wide), BF16)] * 2
            + [pltpu.VMEM((pair, L // TK, TQ, TK), F32), pltpu.VMEM((pair, TQ, KR * CBLOCK), F32)],
        ),
        out_shape=[jax.ShapeDtypeStruct((L, width), F32)] * 2,
        compiler_params=pltpu.CompilerParams(vmem_limit_bytes=60 * MIB),
        cost_estimate=pl.CostEstimate(flops=12 * area, bytes_accessed=30 * MIB, transcendentals=area // HD),
        name="attend",
    )(meta, qkv, qkv, qkv, own_k, own_v)


def attend_other(meta, qkv, fetched, partial, lse, pair=4):
    width = qkv.shape[1] // 3
    heads = width // HD
    wide = pair * HD
    row = pl.BlockSpec((TQ, wide), lambda h, i, meta: (i, h))
    specs = attention_specs(heads, pair)
    return pl.pallas_call(
        functools.partial(attend_other_kernel, pair=pair),
        grid_spec=pltpu.PrefetchScalarGridSpec(
            num_scalar_prefetch=1,
            grid=(heads // pair, L // TQ),
            in_specs=[specs[0], specs[5], specs[6], row, row],
            out_specs=[row, row],
            scratch_shapes=[pltpu.VMEM((TQ // QBLOCK, KR * CBLOCK, wide), BF16)] * 2,
        ),
        out_shape=[jax.ShapeDtypeStruct((L, width), BF16), jax.ShapeDtypeStruct((L, width), F32)],
        compiler_params=pltpu.CompilerParams(vmem_limit_bytes=60 * MIB),
        cost_estimate=pl.CostEstimate(
            flops=4 * L * 256 * width, bytes_accessed=30 * MIB, transcendentals=L * 256 * heads
        ),
        name="attend_other",
    )(meta, qkv, fetched, fetched, partial, lse)


def attend_back(meta, qkv, own_k, own_v, fetched, grad_context, context, lse, pair=4):
    width = context.shape[1]
    heads = width // HD
    wide = pair * HD
    row = pl.BlockSpec((TQ, wide), lambda h, i, meta: (i, h))
    col = pl.BlockSpec((L, wide), lambda h, i, meta: (0, h))
    area = L * 1900 * width
    return pl.pallas_call(
        functools.partial(attend_back_kernel, pair=pair),
        grid_spec=pltpu.PrefetchScalarGridSpec(
            num_scalar_prefetch=1,
            grid=(heads // pair, L // TQ),
            in_specs=attention_specs(heads, pair) + [row, row, row],
            out_specs=[row, col, col],
            scratch_shapes=[pltpu.VMEM((TQ // QBLOCK, 2 * KR * CBLOCK, wide), BF16)] * 2
            + [pltpu.VMEM((L, wide), F32)] * 2,
        ),
        out_shape=[jax.ShapeDtypeStruct((L, width), BF16)] * 3,
        compiler_params=pltpu.CompilerParams(vmem_limit_bytes=60 * MIB),
        cost_estimate=pl.CostEstimate(flops=12 * area, bytes_accessed=40 * MIB, transcendentals=area // HD),
        name="attend_back",
    )(meta, qkv, qkv, qkv, own_k, own_v, fetched, fetched, grad_context, context, lse)


def project_kernel(x_ref, gain_ref, w_ref, normed_ref, qkv_ref):
    rows = x_ref[...].astype(F32)
    scale = lax.rsqrt(jnp.mean(rows * rows, axis=1, keepdims=True) + EPS)
    normed_ref[...] = (rows * scale * gain_ref[...]).astype(BF16)
    left = normed_ref[...]

    def chunk(c, carry):
        cs = pl.ds(pl.multiple_of(c * 512, 512), 512)
        qkv_ref[:, cs] = mm(left, w_ref[:, cs]).astype(BF16)
        return carry

    lax.fori_loop(0, qkv_ref.shape[1] // 512, chunk, 0)


def project(x, gain, weights):
    width = x.shape[1]
    cols = 3 * width
    row = lambda n: pl.BlockSpec((ROWS, n), lambda i: (i, 0))
    whole = lambda n: pl.BlockSpec((width, n), lambda i: (0, 0))
    return pl.pallas_call(
        project_kernel,
        grid=(L // ROWS,),
        in_specs=[row(width), pl.BlockSpec((1, width), lambda i: (0, 0)), whole(cols)],
        out_specs=[row(width), row(cols)],
        out_shape=[jax.ShapeDtypeStruct((L, width), BF16), jax.ShapeDtypeStruct((L, cols), BF16)],
        compiler_params=pltpu.CompilerParams(vmem_limit_bytes=60 * MIB),
        cost_estimate=pl.CostEstimate(flops=2 * L * width * cols, bytes_accessed=26 * MIB, transcendentals=0),
        name="project",
    )(x, gain, weights)


def mix_kernel(x_ref, ctx_ref, gain_ref, w_ref, mixed_ref, normed_ref):
    mixed = x_ref[...].astype(F32) + mm(ctx_ref[...], w_ref[...], NT)
    mixed_ref[...] = mixed
    scale = lax.rsqrt(jnp.mean(mixed * mixed, axis=1, keepdims=True) + EPS)
    normed_ref[...] = (mixed * scale * gain_ref[...]).astype(BF16)


def mix(x, context, gain, weights):
    width = x.shape[1]
    row = pl.BlockSpec((ROWS, width), lambda i: (i, 0))
    return pl.pallas_call(
        mix_kernel,
        grid=(L // ROWS,),
        in_specs=[row, row, pl.BlockSpec((1, width), lambda i: (0, 0)), pl.BlockSpec((width, width), lambda i: (0, 0))],
        out_specs=[row, row],
        out_shape=[jax.ShapeDtypeStruct((L, width), F32), jax.ShapeDtypeStruct((L, width), BF16)],
        compiler_params=pltpu.CompilerParams(vmem_limit_bytes=60 * MIB),
        cost_estimate=pl.CostEstimate(flops=2 * L * width * width, bytes_accessed=22 * MIB, transcendentals=0),
        name="mix",
    )(x, context, gain, weights)


RING = 8


def ring_place(p):
    y = p // 4
    return (p + y * (7 - 2 * p)) * 2 + y


def meet(devices, me, spot):
    barrier = pltpu.get_barrier_semaphore()
    for d in range(1, devices):
        pl.semaphore_signal(
            barrier, inc=1, device_id=((me + d) % devices, spot), device_id_type=pl.DeviceIdType.MESH
        )
    pl.semaphore_signal(barrier, inc=1, device_id=(me, 1 - spot), device_id_type=pl.DeviceIdType.MESH)
    pl.semaphore_wait(barrier, devices)


def remote(src, dst, send, recv, device):
    return pltpu.make_async_remote_copy(
        src_ref=src, dst_ref=dst, send_sem=send, recv_sem=recv, device_id=device, device_id_type=pl.DeviceIdType.MESH
    )


UT = 256


def ffn_kernel(
    n_ref, g_ref, wg0, wg1, wu0, wu1, wd0, wd1, gain_ref, mixed_ref, wo_ref,
    share_ref, gg_ref, out_ref, gm_ref, br_ref, gc_ref,
    acc, gn, hid, duo, part, got, passed, keep, land,
    wo_buf, mixed_buf, out_buf, br_buf, gc_buf,
    pair_send, pair_recv, x_send, x_recv, wo_sem, mixed_sem, done_sem, *, devices,
):
    tile = pl.program_id(0)
    tiles = pl.num_programs(0)
    me = lax.axis_index("dp")
    spot = lax.axis_index("tensor")
    core = me % 2
    pair = (me + 1 - 2 * core, spot)
    peer = (me, 1 - spot)
    side = HT // 2
    width = n_ref.shape[1]
    wo_copy = pltpu.make_async_copy(wo_ref.at[:, pl.ds(0, width)], wo_buf, wo_sem)

    @pl.when(tile == 0)
    def _():
        barrier = pltpu.get_barrier_semaphore()
        for device in (pair, peer):
            pl.semaphore_signal(barrier, inc=1, device_id=device, device_id_type=pl.DeviceIdType.MESH)
        pl.semaphore_wait(barrier, 2)
        acc[...] = jnp.zeros_like(acc)
        gn[...] = jnp.zeros_like(gn)

    def to_pair(k):
        return remote(part.at[k % 2, :, 1 - core], got.at[k % 2], pair_send.at[k % 2], pair_recv.at[k % 2], pair)

    def to_peer(k):
        return remote(passed.at[k % 2], land.at[k % 4], x_send.at[k % 2], x_recv.at[k % 4], peer)

    def join(k):
        slot = (k + 2) % 2
        total = (got[slot].astype(F32) + part[slot, :, core].astype(F32)).astype(BF16)
        for m in range(3):
            passed[slot, :, :, m * side : (m + 1) * side] = total[:, :, m * HT + side : (m + 1) * HT]
            keep[(k + 4) % 4, :, :, m * side : (m + 1) * side] = total[:, :, m * HT : m * HT + side]

    def settle(k):
        slot = (jnp.maximum(k, -1) + 4) % 4
        total = (keep[slot].astype(F32) + land[slot].astype(F32)).astype(BF16)
        total = total.reshape(share_ref.shape[0], 3 * side)
        for m in range(3):
            place = pl.multiple_of((m * tiles + jnp.maximum(k, 0)) * side, side)
            share_ref[:, pl.ds(place, side)] = total[:, m * side : (m + 1) * side]

    wgu = jnp.concatenate([wg0[...], wg1[...], wu0[...], wu1[...]], axis=1)
    wd = jnp.concatenate([wd0[...], wd1[...]], axis=1)

    def chunk(r):
        rs = pl.ds(r * ROWS, ROWS)
        both = mm(n_ref[rs, :], wgu)
        grad_hidden = mm(g_ref[rs, :], wd)
        gate, up = both[:, :HT], both[:, HT:]
        sigma = 1.0 / (1.0 + jnp.exp(-gate))
        silu = gate * sigma
        hidden = (silu * up).astype(BF16)
        grad_gate = grad_hidden * up * (sigma * (1.0 + gate * (1.0 - sigma)))
        grads = jnp.concatenate([grad_gate.astype(BF16), (grad_hidden * silu).astype(BF16)], axis=1)
        acc[rs, :] += mm(hidden, wd, NT)
        gn[rs, :] += mm(grads, wgu, NT)
        hid[rs, :] = hidden
        duo[rs, :] = grads

    @pl.when(tile > 2)
    def _():
        to_peer(tile - 3).wait()

    settle(tile - 3)
    for r in range(L // ROWS):
        chunk(r)

    @pl.when(tile > 0)
    def _():
        to_pair(tile - 1).wait()

    join(tile - 1)
    slot = tile % 2
    shape = part.shape[1:4]
    part[slot, :, :, :, : 2 * HT] = mm(n_ref[...], duo[...], TN).astype(BF16).reshape(shape + (2 * HT,))
    part[slot, :, :, :, 2 * HT :] = mm(g_ref[...], hid[...], TN).astype(BF16).reshape(shape + (HT,))
    to_pair(tile).start()

    @pl.when(tile > 0)
    def _():
        to_peer(tile - 1).start()

    def rows_of(t):
        return pl.ds(pl.multiple_of(t * UT, UT), UT)

    def fetch(t):
        return pltpu.make_async_copy(mixed_ref.at[rows_of(t), :], mixed_buf.at[t % 2], mixed_sem.at[t % 2])

    def write(t):
        sources = [out_buf.at[t % 2], gn.at[rows_of(t), :], br_buf.at[t % 2], gc_buf.at[t % 2]]
        return [
            pltpu.make_async_copy(source, ref.at[rows_of(t), :], done_sem.at[i, t % 2])
            for i, (source, ref) in enumerate(zip(sources, [out_ref, gm_ref, br_ref, gc_ref]))
        ]

    def unmix(t, carry):
        @pl.when(t < L // UT - 1)
        def _():
            fetch(t + 1).start()

        fetch(t).wait()

        @pl.when(t > 1)
        def _():
            for copy in write(t - 2):
                copy.wait()

        rs = rows_of(t)
        now = t % 2
        mixed = mixed_buf[now]
        grad = gn[rs, :]
        scale = lax.rsqrt(jnp.mean(mixed * mixed, axis=1, keepdims=True) + EPS)
        unit = mixed * scale
        inner = grad * gain_ref[...]
        back = scale * (inner - unit * jnp.mean(inner * unit, axis=1, keepdims=True))
        grad_mixed = g_ref[rs, :].astype(F32) + back
        out_buf[now] = (mixed + acc[rs, :]).astype(BF16)
        gn[rs, :] = grad_mixed
        branch = grad_mixed.astype(BF16)
        br_buf[now] = branch
        gc_buf[now] = mm(branch, wo_buf[...]).astype(BF16)
        gg_ref[...] += jnp.sum(grad * unit, axis=0, keepdims=True)
        for copy in write(t):
            copy.start()
        return carry

    @pl.when(tile == tiles - 2)
    def _():
        wo_copy.start()
        fetch(0).start()

    @pl.when(tile == tiles - 1)
    def _():
        gg_ref[...] = jnp.zeros_like(gg_ref)
        to_peer(tile - 2).wait()
        settle(tile - 2)
        wo_copy.wait()
        lax.fori_loop(0, 3, unmix, 0)
        to_pair(tile).wait()
        join(tile)
        to_peer(tile).start()
        lax.fori_loop(3, L // UT, unmix, 0)
        to_peer(tile - 1).wait()
        settle(tile - 1)
        to_peer(tile).wait()
        settle(tile)
        for t in (L // UT - 2, L // UT - 1):
            for copy in write(t):
                copy.wait()


def ffn(normed, cotangent, weights, gain, mixed, width, hidden, devices):
    once = pl.Buffered(1)
    tiles = hidden // HT
    side = HT // 2
    rows = width // devices
    chips = devices // 2
    lead = width // side
    part = lambda k: pl.BlockSpec((width, side), lambda j: (0, lead + k * tiles + j))
    whole = pl.BlockSpec((L, width), lambda j: (0, 0), pipeline_mode=once)
    fixed = lambda shape: pl.BlockSpec(shape, lambda j: (0, 0), pipeline_mode=once)
    hbm = pl.BlockSpec(memory_space=pltpu.HBM)
    dma = pltpu.SemaphoreType.DMA
    tile = lambda kind: pltpu.VMEM((2, UT, width), kind)
    return pl.pallas_call(
        functools.partial(ffn_kernel, devices=devices),
        grid=(tiles,),
        in_specs=[whole, whole] + [part(k) for k in range(6)] + [fixed((1, width)), hbm, hbm],
        out_specs=[fixed((width // 2, 3 * hidden // 2)), fixed((1, width)), hbm, hbm, hbm, hbm],
        out_shape=[
            jax.ShapeDtypeStruct((width // 2, 3 * hidden // 2), BF16),
            jax.ShapeDtypeStruct((1, width), F32),
            jax.ShapeDtypeStruct((L, width), BF16),
            jax.ShapeDtypeStruct((L, width), F32),
            jax.ShapeDtypeStruct((L, width), BF16),
            jax.ShapeDtypeStruct((L, width), BF16),
        ],
        scratch_shapes=[
            pltpu.VMEM((L, width), F32), pltpu.VMEM((L, width), F32),
            pltpu.VMEM((L, HT), BF16), pltpu.VMEM((L, 2 * HT), BF16),
            pltpu.VMEM((2, chips, 2, rows, 3 * HT), BF16),
            pltpu.VMEM((2, chips, rows, 3 * HT), BF16),
            pltpu.VMEM((2, chips, rows, 3 * side), BF16),
            pltpu.VMEM((4, chips, rows, 3 * side), BF16),
            pltpu.VMEM((4, chips, rows, 3 * side), BF16),
            pltpu.VMEM((width, width), BF16), tile(F32), tile(BF16), tile(BF16), tile(BF16),
            dma((2,)), dma((2,)), dma((2,)), dma((4,)), dma, dma((2,)), dma((4, 2)),
        ],
        compiler_params=pltpu.CompilerParams(collective_id=2, has_side_effects=True, vmem_limit_bytes=61 * MIB),
        cost_estimate=pl.CostEstimate(
            flops=18 * L * width * hidden, bytes_accessed=60 * MIB, transcendentals=L * hidden
        ),
        name="ffn",
    )(normed, cotangent, *([weights] * 6), gain, mixed, weights)


FT = 256


def finish_kernel(
    x_ref, gm_ref, n_ref, ctx_ref, br_ref, dq_ref, dk_ref, dv_ref, w_ref, gain_ref, gain_two_ref,
    gt_ref, sums_ref, share_ref,
    n_buf, ctx_buf, br_buf, dq_buf, dk_buf, dv_buf, w_buf, x_buf, gm_buf, gt_buf,
    part, got, land, across, gains, gain_land,
    load_sem, x_sem, gm_sem, gt_sem, gt_recv, pair_send, pair_recv, ring_send, ring_recv, x_send, x_recv, g_send, g_recv,
    *, devices,
):
    me = lax.axis_index("dp")
    spot = lax.axis_index("tensor")
    core = me % 2
    z, y = me // 4, (me // 2) % 2
    place = z + y * (7 - 2 * z)
    width = n_buf.shape[1]
    half = width // 2
    rows = part.shape[2]
    loads = [
        pltpu.make_async_copy(src, dst, load_sem.at[i])
        for i, (src, dst) in enumerate(
            [
                (ctx_ref, ctx_buf), (br_ref, br_buf), (n_ref, n_buf), (dv_ref, dv_buf),
                (dk_ref, dk_buf), (dq_ref, dq_buf), (w_ref.at[:, pl.ds(0, 3 * width)], w_buf),
            ]
        )
    ]
    for copy in loads:
        copy.start()
    meet(devices, me, spot)

    def tile_in(t, slot):
        rs = pl.ds(pl.multiple_of(t * FT, FT), FT)
        return [
            pltpu.make_async_copy(x_ref.at[rs, :], x_buf.at[slot], x_sem.at[slot]),
            pltpu.make_async_copy(gm_ref.at[rs, :], gm_buf.at[slot], gm_sem.at[slot]),
        ]

    held = L // FT // 2

    def give(k, slot):
        rs = pl.ds(pl.multiple_of(k * FT, FT), FT)
        return remote(
            gt_buf.at[slot], gt_ref.at[spot, rs, :], gt_sem.at[slot], gt_recv.at[k], (me, 1 - spot)
        )

    def keep(k, slot):
        rs = pl.ds(pl.multiple_of(k * FT, FT), FT)
        return pltpu.make_async_copy(gt_buf.at[slot], gt_ref.at[spot, rs, :], gt_sem.at[slot])

    def tile_of(k):
        return (k + held * (1 - spot)) % (2 * held)

    for copy in tile_in(tile_of(0), 0):
        copy.start()

    pair = (me + 1 - 2 * core, spot)

    def column(m, h):
        return (m // 2) * 2 * width + h * width + (m % 2) * half

    def to_pair(m, h):
        cs = pl.ds(column(m, h), half)
        return remote(
            part.at[:, 1 - core, :, cs], got.at[:, :, cs], pair_send.at[m, h], pair_recv.at[m, h], pair
        )

    def product(m, left, right):
        for h in range(2):
            value = mm(left[...], right[:, h * half : (h + 1) * half], TN).astype(BF16)
            part[:, :, :, column(m, h) : column(m, h) + half] = value.reshape(part.shape[0], 2, rows, half)
            to_pair(m, h).start()

    def join(m, h):
        to_pair(m, h).wait_recv()
        cs = pl.ds(column(m, h), half)
        got[:, :, cs] = (got[:, :, cs].astype(F32) + part[:, core, :, cs].astype(F32)).astype(BF16)

    neighbours = [(place + 1) % RING, (place + RING - 1) % RING]

    def held_block(g, direction, s):
        p = (place + 2 * RING - 1 - s) % RING if direction == 0 else (place + 1 + s) % RING
        return got.at[ring_place(p), :, pl.ds((2 * g + direction) * width, width)]

    def hop(g, direction, s):
        to = ring_place(neighbours[direction]) * 2 + core
        return remote(
            held_block(g, direction, s), land.at[g, direction, s],
            ring_send.at[g, direction, s], ring_recv.at[g, direction, s], (to, spot),
        )

    def advance(g, s, more=True):
        for direction in range(2):
            hop(g, direction, s).wait_recv()
            block = held_block(g, direction, s + 1)
            block[...] = (block[...].astype(F32) + land[g, direction, s].astype(F32)).astype(BF16)
            if more:
                hop(g, direction, s + 1).start()

    def launch(g):
        for h in range(2):
            join(2 * g, h)
            join(2 * g + 1, h)
            hop(g, h, 0).start()

    def finish_rows(t, slot, k):
        for copy in tile_in(t, slot):
            copy.wait()
        rs = pl.ds(pl.multiple_of(t * FT, FT), FT)
        grad = mm(dq_buf[rs, :], w_buf[:, :width], NT)
        grad += mm(dk_buf[rs, :], w_buf[:, width : 2 * width], NT)
        grad += mm(dv_buf[rs, :], w_buf[:, 2 * width :], NT)
        values = x_buf[slot].astype(F32)
        scale = lax.rsqrt(jnp.mean(values * values, axis=1, keepdims=True) + EPS)
        unit = values * scale
        inner = grad * gain_ref[...]
        back = scale * (inner - unit * jnp.mean(inner * unit, axis=1, keepdims=True))
        gt_buf[k] = (gm_buf[slot] + back).astype(BF16)
        gains[:1, :] += jnp.sum(grad * unit, axis=0, keepdims=True)

    def two_tiles(j, advances, give_away):
        for slot in (0, 1):
            k = 2 * j + slot
            if slot == 0 or give_away:
                for copy in tile_in(tile_of(k + 1), 1 - slot):
                    copy.start()
            else:

                @pl.when(j < held - 1)
                def _():
                    for copy in tile_in(tile_of(k + 1), 0):
                        copy.start()

            finish_rows(tile_of(k), slot, k)
            if give_away:
                give(k, k).start()
            else:
                keep(k - held, k).start()
        for g, s in advances:
            advance(g, s)

    gains[:1, :] = jnp.zeros((1, width), F32)
    gains[1:, :] = gain_two_ref[...]
    for i in (0, 1):
        loads[i].wait()
    product(0, br_buf, ctx_buf)
    for i in (2, 3):
        loads[i].wait()
    product(1, n_buf, dv_buf)
    launch(0)
    for i in (4, 5, 6):
        loads[i].wait()

    def theirs(j, carry):
        two_tiles(j, [(0, j)], True)
        return carry

    def ours(j, carry):
        two_tiles(j, [(0, j + 2), (1, j - 2)], False)
        return carry

    lax.fori_loop(0, held // 2, theirs, 0)
    product(2, n_buf, dk_buf)
    advance(0, 2)
    product(3, n_buf, dq_buf)
    advance(0, 3)
    launch(1)
    lax.fori_loop(held // 2, held, ours, 0)

    partners = [
        (me + 1 - 2 * core, spot),
        (me + 2 - 4 * y, spot),
        (me + 4 - 8 * (z % 2), spot),
        (me + 8 - 16 * (z // 2), spot),
        (me, 1 - spot),
    ]

    def add_gains(r):
        return remote(gains, gain_land.at[r], g_send.at[r], g_recv.at[r], partners[r])

    def gain_round(r):
        add_gains(r).wait()
        gains[...] = gains[...] + gain_land[r]
        if r < 4:
            add_gains(r + 1).start()

    own = ring_place(place)
    peer = (me, 1 - spot)

    def over(g):
        return remote(
            got.at[own, :, pl.ds((2 * g + 1) * width, width)], across.at[:, pl.ds(g * width, width)],
            x_send.at[g], x_recv.at[g], peer,
        )

    add_gains(0).start()
    advance(0, 6, False)
    over(0).start()
    advance(1, 2)
    gain_round(0)
    advance(1, 3)
    gain_round(1)
    advance(1, 4)
    gain_round(2)
    advance(1, 5)
    gain_round(3)
    advance(1, 6, False)
    over(1).start()
    gain_round(4)
    sums_ref[...] = gains[...]
    for g in range(2):
        over(g).wait_recv()
        cs = pl.ds(g * width, width)
        share_ref[:, cs] = got[own, :, pl.ds(2 * g * width, width)].astype(F32) + across[:, cs].astype(F32)
    for g in range(2):
        over(g).wait_send()
        for direction in range(2):
            for s in range(RING - 1):
                hop(g, direction, s).wait_send()
    for m in range(4):
        for h in range(2):
            to_pair(m, h).wait_send()
    for k in range(held):
        give(k, k).wait()
        keep(k, k + held).wait()


def finish(x, grad_mixed, normed, context, branch, dq, dk, dv, weights, gain, gain_two_part, devices):
    width = x.shape[1]
    rows = width // devices
    anywhere = pl.BlockSpec(memory_space=pltpu.HBM)
    vmem = pl.BlockSpec(memory_space=pltpu.VMEM)
    dma = pltpu.SemaphoreType.DMA
    whole = pltpu.VMEM((L, width), BF16)
    return pl.pallas_call(
        functools.partial(finish_kernel, devices=devices),
        in_specs=[anywhere] * 9 + [vmem] * 2,
        out_specs=[anywhere, vmem, vmem],
        out_shape=[
            jax.ShapeDtypeStruct((2, L // 2, width), BF16),
            jax.ShapeDtypeStruct((2, width), F32),
            jax.ShapeDtypeStruct((rows, 2 * width), F32),
        ],
        scratch_shapes=[
            whole, whole, whole, whole, whole, whole, pltpu.VMEM((width, 3 * width), BF16),
            pltpu.VMEM((2, FT, width), BF16), pltpu.VMEM((2, FT, width), F32), pltpu.VMEM((L // FT, FT, width), BF16),
            pltpu.VMEM((RING, 2, rows, 4 * width), BF16),
            pltpu.VMEM((RING, rows, 4 * width), BF16),
            pltpu.VMEM((2, 2, RING - 1, rows, width), BF16),
            pltpu.VMEM((rows, 2 * width), BF16),
            pltpu.VMEM((2, width), F32), pltpu.VMEM((5, 2, width), F32),
            dma((7,)), dma((2,)), dma((2,)), dma((2 * (L // FT // 2),)), dma((L // FT // 2,)), dma((4, 2)), dma((4, 2)),
            dma((2, 2, RING - 1)), dma((2, 2, RING - 1)), dma((2,)), dma((2,)), dma((5,)), dma((5,)),
        ],
        compiler_params=pltpu.CompilerParams(collective_id=1, has_side_effects=True, vmem_limit_bytes=60 * MIB),
        cost_estimate=pl.CostEstimate(flops=14 * L * width * width, bytes_accessed=80 * MIB, transcendentals=0),
        name="finish",
    )(x, grad_mixed, normed, context, branch, dq, dk, dv, weights, gain, gain_two_part)


def pick_kernel(table, held_ref, sent_ref, sems):
    def copy(i):
        return pltpu.make_async_copy(held_ref.at[table[i]], sent_ref.at[i], sems.at[i])

    for i in range(sent_ref.shape[0]):
        copy(i).start()
    for i in range(sent_ref.shape[0]):
        copy(i).wait()


def pick_rows(table, held):
    count = held.shape[0]
    return pl.pallas_call(
        pick_kernel,
        grid_spec=pltpu.PrefetchScalarGridSpec(
            num_scalar_prefetch=1,
            grid=(),
            in_specs=[pl.BlockSpec(memory_space=pl.ANY)],
            out_specs=pl.BlockSpec(memory_space=pltpu.VMEM),
            scratch_shapes=[pltpu.SemaphoreType.DMA((count,))],
        ),
        out_shape=jax.ShapeDtypeStruct(held.shape, held.dtype),
        compiler_params=pltpu.CompilerParams(vmem_limit_bytes=60 * MIB),
        cost_estimate=pl.CostEstimate(flops=0, bytes_accessed=2 * held.size * 2, transcendentals=0),
        name="pick_rows",
    )(table, held)


def spread_kernel(
    tok_ref, ck_ref, cv_ref, small_ref, extra_ref, big_ref,
    x_ref, ok_ref, ov_ref, held_ref, first_ref, second_ref,
    tok_buf, k_buf, v_buf, local_sem, x_send, x_recv, all_send, all_recv, ring_send, ring_recv, line_send, line_recv, pair_send, pair_recv,
):
    me = lax.axis_index("dp")
    spot = lax.axis_index("tensor")
    peer = 1 - spot
    devices = held_ref.shape[0]
    rows, cols = small_ref.shape[0], small_ref.shape[1] // 3
    core = me % 2
    z, y = me // 4, (me // 2) % 2

    def target(dp, tensor):
        return (dp, tensor)

    barrier = pltpu.get_barrier_semaphore()
    for d in range(1, devices):
        pl.semaphore_signal(barrier, inc=1, device_id=target((me + d) % devices, spot), device_id_type=pl.DeviceIdType.MESH)
    pl.semaphore_signal(barrier, inc=1, device_id=target(me, peer), device_id_type=pl.DeviceIdType.MESH)
    pl.semaphore_wait(barrier, devices)

    def remote(src, dst, send, recv, device):
        return pltpu.make_async_remote_copy(
            src_ref=src, dst_ref=dst, send_sem=send, recv_sem=recv,
            device_id=device, device_id_type=pl.DeviceIdType.MESH,
        )

    mine = pl.multiple_of(me * rows, rows)
    across = target(me, peer)
    weight_copies = []
    for i in range(3):
        weight_copies.append(
            remote(
                small_ref.at[:, pl.ds(i * cols, cols)],
                first_ref.at[pl.ds(mine, rows), pl.ds((2 * i + 1) * cols, cols)],
                x_send.at[i], x_recv.at[i], across,
            )
        )
    for copy in weight_copies:
        copy.start()
    for i in range(3):
        first_ref[pl.ds(mine, rows), pl.ds(2 * i * cols, cols)] = small_ref[:, pl.ds(i * cols, cols)]
    first_ref[pl.ds(mine, rows), pl.ds(6 * cols, HD)] = extra_ref[...]

    loads = [
        pltpu.make_async_copy(tok_ref.at[spot], tok_buf, local_sem.at[0]),
        pltpu.make_async_copy(ck_ref.at[spot], k_buf, local_sem.at[1]),
        pltpu.make_async_copy(cv_ref.at[spot], v_buf, local_sem.at[2]),
    ]
    stores = [
        pltpu.make_async_copy(tok_buf, x_ref.at[spot], local_sem.at[3]),
        pltpu.make_async_copy(k_buf, ok_ref.at[spot], local_sem.at[4]),
        pltpu.make_async_copy(v_buf, ov_ref.at[spot], local_sem.at[5]),
    ]
    for copy in loads:
        copy.start()

    x_copies = [remote(tok_ref.at[peer], x_ref.at[spot], x_send.at[3], x_recv.at[3], across)]
    wide = big_ref.shape[1]
    hidden = (wide - cols) // 3
    starts = [(0, cols)] + [(cols + i * hidden, hidden) for i in range(3)]
    own_cols = []
    for i, (start, size) in enumerate(starts):
        base = 2 * start
        own_cols.append(pltpu.make_async_copy(
            big_ref.at[:, pl.ds(start, size)], second_ref.at[:, pl.ds(base, size)], local_sem.at[6 + i]))
        x_copies.append(remote(
            big_ref.at[:, pl.ds(start, size)], second_ref.at[:, pl.ds(base + size, size)],
            x_send.at[4 + i], x_recv.at[4 + i], across))
    x_copies.append(remote(ck_ref.at[peer], ok_ref.at[spot], x_send.at[8], x_recv.at[8], across))
    x_copies.append(remote(cv_ref.at[peer], ov_ref.at[spot], x_send.at[9], x_recv.at[9], across))
    for copy in x_copies + own_cols:
        copy.start()

    def to_device(d, dst_dp):
        chunk = pl.ds(pl.multiple_of(dst_dp * CBLOCK, CBLOCK), CBLOCK)
        dst = target(dst_dp, spot)
        return [
            remote(ck_ref.at[:, chunk, :], held_ref.at[me, :, 0], all_send.at[0, d], all_recv.at[0, d], dst),
            remote(cv_ref.at[:, chunk, :], held_ref.at[me, :, 1], all_send.at[1, d], all_recv.at[1, d], dst),
        ]

    for copy in weight_copies:
        copy.wait_recv()

    def block(zz, yy, c):
        return first_ref.at[pl.ds(pl.multiple_of((zz * 4 + yy * 2 + c) * rows, rows), rows), :]

    def along(s, direction):
        zz = z - (s - 1) if direction == 0 else z + (s - 1)
        to = z + 1 if direction == 0 else z - 1
        k = (s - 1) * 2 + direction
        held = block(zz, y, core)
        return remote(held, held, ring_send.at[k], ring_recv.at[k], target(to * 4 + y * 2 + core, spot))

    def sends(s, direction):
        return (z < 3) & (z - (s - 1) >= 0) if direction == 0 else (z > 0) & (z + (s - 1) <= 3)

    def gets(s, direction):
        return z - s >= 0 if direction == 0 else z + s <= 3

    def to_line(zz):
        held = block(zz, y, core)
        return remote(held, held, line_send.at[zz], line_recv.at[zz], target(z * 4 + (1 - y) * 2 + core, spot))

    def to_pair(zz, yy):
        held = block(zz, yy, core)
        k = zz * 2 + yy
        return remote(held, held, pair_send.at[k], pair_recv.at[k], target(me + 1 - 2 * core, spot))

    for direction in range(2):

        @pl.when(sends(1, direction))
        def _():
            along(1, direction).start()

    to_line(z).start()
    to_pair(z, y).start()
    copies = []
    order = [8, 4, 12, 6, 10, 2, 14, 9, 5, 13, 1, 7, 11, 3, 15]
    assert sorted(order) == list(range(1, devices))

    def some(count):
        for d in order[:count]:
            for copy in to_device(d, (me + d) % devices):
                copy.start()
                copies.append(copy)
        del order[:count]

    some(3)
    chunk = pl.ds(pl.multiple_of(me * CBLOCK, CBLOCK), CBLOCK)
    kept = [
        pltpu.make_async_copy(ck_ref.at[:, chunk, :], held_ref.at[me, :, 0], local_sem.at[10]),
        pltpu.make_async_copy(cv_ref.at[:, chunk, :], held_ref.at[me, :, 1], local_sem.at[11]),
    ]
    for copy in kept:
        copy.start()
    for load, store in zip(loads, stores):
        load.wait()
        store.start()
    for s in range(1, 4):
        for direction in range(2):

            @pl.when(gets(s, direction))
            def _():
                along(s, direction).wait_recv()
                zz = z - s if direction == 0 else z + s
                if s < 3:

                    @pl.when(sends(s + 1, direction))
                    def _():
                        along(s + 1, direction).start()

                to_line(zz).start()
                to_pair(zz, y).start()

        some(3)
    for zz in range(4):
        to_line(zz).wait_recv()
        to_pair(zz, 1 - y).start()
        some(1)
    some(devices)
    for s in range(1, 4):
        for direction in range(2):

            @pl.when(sends(s, direction))
            def _():
                along(s, direction).wait_send()

    for zz in range(4):
        to_line(zz).wait_send()
        for yy in range(2):
            to_pair(zz, yy).wait()
    for copy in weight_copies:
        copy.wait_send()
    for copy in x_copies + copies:
        copy.wait()
    for copy in stores + own_cols + kept:
        copy.wait()


def spread(tokens, cache_keys, cache_values, small, extra, big, devices):
    micro, shard_len, width = tokens.shape
    rows, cols = small.shape[0], small.shape[1] // 3
    anywhere = pl.BlockSpec(memory_space=pltpu.HBM)
    vmem = pl.BlockSpec(memory_space=pltpu.VMEM)
    dma = pltpu.SemaphoreType.DMA
    return pl.pallas_call(
        spread_kernel,
        in_specs=[anywhere, anywhere, anywhere, vmem, vmem, vmem],
        out_specs=[anywhere, anywhere, anywhere, anywhere, vmem, anywhere],
        out_shape=[
            jax.ShapeDtypeStruct((2, shard_len, width), BF16),
            jax.ShapeDtypeStruct((2, CACHE_LEN, cols), BF16),
            jax.ShapeDtypeStruct((2, CACHE_LEN, cols), BF16),
            jax.ShapeDtypeStruct((devices, micro, 2, CBLOCK, cols), BF16),
            jax.ShapeDtypeStruct((rows * devices, 6 * cols + HD), BF16),
            jax.ShapeDtypeStruct((rows, 2 * big.shape[1]), BF16),
        ],
        scratch_shapes=[
            pltpu.VMEM((shard_len, width), BF16),
            pltpu.VMEM((CACHE_LEN, cols), BF16),
            pltpu.VMEM((CACHE_LEN, cols), BF16),
            dma((12,)), dma((10,)), dma((10,)), dma((2, devices)), dma((2, devices)),
            dma((6,)), dma((6,)), dma((4,)), dma((4,)), dma((8,)), dma((8,)),
        ],
        compiler_params=pltpu.CompilerParams(collective_id=0, has_side_effects=True, vmem_limit_bytes=60 * MIB),
        cost_estimate=pl.CostEstimate(flops=0, bytes_accessed=300 * MIB, transcendentals=0),
        name="spread",
    )(tokens, cache_keys, cache_values, small, extra, big)


def swap(values):
    return lax.ppermute(values, "tensor", [(0, 1), (1, 0)])


def sequence_body(
    tokens, gain_attn, w_query, w_key, w_value, w_out, gain_ffn, w_gate, w_up, w_down,
    cache_keys, cache_values, prefix, partner, own_blocks, partner_blocks, grad_out,
):
    micro, shard_len, width = tokens.shape
    devices = lax.axis_size("dp")
    seqs = micro * devices
    rows_held, cols = w_query.shape
    hidden_held = w_gate.shape[1]
    hidden = 2 * hidden_held
    spot = lax.axis_index("tensor")
    exchange = functools.partial(lax.all_to_all, axis_name="tensor", split_axis=0, concat_axis=0, tiled=True)
    chunks = CACHE_LEN // CBLOCK

    small = jnp.concatenate([w_query, w_key, w_value], axis=1)
    partner_column = jnp.zeros((rows_held, 1), BF16).at[:micro, 0].set(partner.astype(BF16))
    extra = jnp.concatenate(
        [gain_attn[:, None], gain_ffn[:, None], partner_column, jnp.zeros((rows_held, HD - 3), BF16)], axis=1
    )
    big = jnp.concatenate([w_out.T, w_gate, w_up, w_down.T], axis=1)
    x, own_k, own_v, held, first_all, second_rows = spread(
        tokens, cache_keys, cache_values, small, extra, big, devices
    )
    x = x.reshape(L, width)
    theirs = swap(lax.dynamic_index_in_dim(grad_out, 1 - spot, 0, keepdims=False))
    mine = lax.dynamic_index_in_dim(grad_out, spot, 0, keepdims=False)
    cotangent = jnp.where(spot == 0, jnp.concatenate([mine, theirs], 0), jnp.concatenate([theirs, mine], 0))
    second_all = lax.all_gather(second_rows, "dp", axis=0, tiled=True)

    tail = lax.optimization_barrier(first_all[:, 3 * width :])
    gains = mm((jnp.arange(2)[:, None] == jnp.arange(HD)[None, :]).astype(BF16), tail, NT)
    gain_one, gain_two = gains[:1], gains[1:]
    table = tail[:, 2].reshape(devices, rows_held)[:, :micro].reshape(seqs).astype(jnp.int32)
    sent = pick_rows(table, held.reshape(seqs, 2 * CBLOCK, cols))
    fetched = lax.all_to_all(sent, ("dp", "tensor"), split_axis=0, concat_axis=0, tiled=True)
    fetched = fetched.reshape(chunks, 2, 2, CBLOCK, cols)

    meta = jnp.concatenate(
        [
            prefix[spot][None], spot[None].astype(jnp.int32),
            own_blocks[spot].reshape(-1), partner_blocks[spot].reshape(-1),
        ]
    )
    normed, qkv = project(x, gain_one, first_all)
    partial, partial_lse = attend(meta, qkv, own_k, own_v)
    context, lse = attend_other(meta, qkv, fetched, partial, partial_lse)
    mixed, normed_two = mix(x, context, gain_two, second_all)
    ffn_grads, gain_part_two, out, grad_mixed, branch, grad_context = ffn(
        normed_two, cotangent, second_all, gain_two, mixed, width, hidden, devices
    )
    ffn_share = lax.psum_scatter(
        ffn_grads, "dp", scatter_dimension=0, tiled=True,
        axis_index_groups=[list(range(c, devices, 2)) for c in range(2)],
    )
    out = exchange(out.reshape(2, shard_len, width))
    dq, dk, dv = attend_back(meta, qkv, own_k, own_v, fetched, grad_context, context, lse)
    dq, out = lax.optimization_barrier((dq, out))
    grad_tokens, gain_sums, attn_share = finish(
        x, grad_mixed, normed, context, branch, dq, dk, dv, first_all, gain_one, gain_part_two, devices
    )
    grad_tokens = grad_tokens.astype(F32)
    g_out, g_value, g_key, g_query = jnp.split(attn_share, 4, axis=1)
    g_gate, g_up, g_down = [
        ffn_share[:, i * hidden_held : (i + 1) * hidden_held].astype(F32) for i in range(3)
    ]
    return (
        out, grad_tokens, gain_sums[0], g_query, g_key, g_value, g_out.T, gain_sums[1], g_gate, g_up, g_down.T,
    )


def solution(mesh):
    in_specs = (
        P("dp", "tensor", None),
        P("dp"),
        P("dp", "tensor"),
        P("dp", "tensor"),
        P("dp", "tensor"),
        P("tensor", "dp"),
        P("dp"),
        P("dp", "tensor"),
        P("dp", "tensor"),
        P("tensor", "dp"),
        P("dp", None, "tensor"),
        P("dp", None, "tensor"),
        P("dp"),
        P("dp"),
        P("dp", None, None),
        P("dp", None, None),
        P("dp", "tensor", None),
    )
    out_specs = (
        P("dp", "tensor", None),
        P("dp", "tensor", None),
        P(),
        P("dp", "tensor"),
        P("dp", "tensor"),
        P("dp", "tensor"),
        P("tensor", "dp"),
        P(),
        P("dp", "tensor"),
        P("dp", "tensor"),
        P("tensor", "dp"),
    )
    whole = mesh.shape["tensor"] == 2 and mesh.shape["dp"] == CACHE_LEN // CBLOCK
    body = sequence_body if whole else tensor_body
    return jax.shard_map(body, mesh=mesh, in_specs=in_specs, out_specs=out_specs, check_vma=False)
```

```python
import functools

import jax
import jax.numpy as jnp
from jax import lax
from jax.experimental import pallas as pl
from jax.experimental.pallas import tpu as pltpu
from jax.sharding import PartitionSpec as P

HD = 128
L = 2048
CACHE_LEN = 1024
QBLOCK = 128
CBLOCK = 64
KR = 4
QROWS = 512


EPS = 1e-05
NEGATIVE = -1e30


def norm_rows(values, gain):
    scale_rows = lax.rsqrt(jnp.mean(values * values, axis=-1, keepdims=True) + EPS)
    return (values * scale_rows * gain, scale_rows)


def norm_back(grad_normed, values, scale_rows, gain):
    unit = values * scale_rows
    grad_unit = grad_normed * gain
    grad_values = scale_rows * (
        grad_unit - unit * jnp.mean(grad_unit * unit, axis=-1, keepdims=True)
    )
    return (grad_values, jnp.sum(grad_normed * unit, axis=0))


def inner_rows(left, right):
    return lax.dot_general(
        left, right, (((0,), (0,)), ((), ())), preferred_element_type=jnp.float32
    )


def outer_cols(left, right):
    return lax.dot_general(
        left, right, (((1,), (1,)), ((), ())), preferred_element_type=jnp.float32
    )


def memory_rows(cache_one, chosen, width):
    shaped = cache_one.reshape(CACHE_LEN // CBLOCK, CBLOCK, width)
    return jnp.take(shaped, chosen, axis=0)


def block_scores(query_block, keys_part, mem_part, first_row, limit):
    rows_here, heads_here, size = query_block.shape
    extent = keys_part.shape[0]
    local = jnp.einsum(
        "qhd,khd->hqk", query_block, keys_part, preferred_element_type=jnp.float32
    ) * size ** (-0.5)
    row_ids = first_row + jnp.arange(rows_here, dtype=jnp.int32)[:, None]
    key_ids = jnp.arange(extent, dtype=jnp.int32)[None, :]
    allowed = (key_ids <= row_ids) | (row_ids < limit) & (key_ids < limit)
    local = jnp.where(allowed[None], local, NEGATIVE)
    groups = mem_part.shape[0]
    grouped = query_block.reshape(groups, rows_here // groups, heads_here, size)
    remote = jnp.einsum(
        "bqhd,bkhd->hbqk", grouped, mem_part, preferred_element_type=jnp.float32
    ) * size ** (-0.5)
    return (local, remote.reshape(heads_here, rows_here, -1))


def attention_forward(query, keys, values, mem_keys, mem_values, limit):
    groups = QROWS // QBLOCK
    heads_here = query.shape[1]
    context_parts = []
    lse_parts = []
    for index in range(L // QROWS):
        first = index * QROWS
        extent = max(first + QROWS, L // 2)
        query_block = query[first : first + QROWS]
        mem_k = mem_keys[index * groups : (index + 1) * groups]
        mem_v = mem_values[index * groups : (index + 1) * groups]
        local, remote = block_scores(query_block, keys[:extent], mem_k, first, limit)
        top = jnp.maximum(jnp.max(local, axis=-1), jnp.max(remote, axis=-1))
        e_local = jnp.exp(local - top[..., None])
        e_remote = jnp.exp(remote - top[..., None])
        total = jnp.sum(e_local, axis=-1) + jnp.sum(e_remote, axis=-1)
        p_local = (e_local / total[..., None]).astype(jnp.bfloat16)
        p_remote = (
            (e_remote / total[..., None])
            .astype(jnp.bfloat16)
            .reshape(heads_here, groups, QBLOCK, -1)
        )
        part = jnp.einsum(
            "hqk,khd->qhd", p_local, values[:extent], preferred_element_type=jnp.float32
        )
        extra = jnp.einsum("hbqk,bkhd->bqhd", p_remote, mem_v, preferred_element_type=jnp.float32)
        context_parts.append(part + extra.reshape(part.shape))
        lse_parts.append(top + jnp.log(total))
    return (jnp.concatenate(context_parts, axis=0), lse_parts)


def attention_backward(query, keys, values, mem_keys, mem_values, limit, lse_parts, grad_context):
    groups = QROWS // QBLOCK
    length, heads_here, size = query.shape
    scale = size ** (-0.5)
    grad_query_parts = []
    grad_keys = jnp.zeros(query.shape, jnp.float32)
    grad_values = jnp.zeros(query.shape, jnp.float32)
    for index in range(L // QROWS):
        first = index * QROWS
        extent = max(first + QROWS, L // 2)
        query_block = query[first : first + QROWS]
        mem_k = mem_keys[index * groups : (index + 1) * groups]
        mem_v = mem_values[index * groups : (index + 1) * groups]
        local, remote = block_scores(query_block, keys[:extent], mem_k, first, limit)
        lse_block = lse_parts[index][..., None]
        p_local = jnp.exp(local - lse_block)
        p_remote = jnp.exp(remote - lse_block)
        grad_block = grad_context[first : first + QROWS]
        grouped_grad = grad_block.reshape(groups, QBLOCK, heads_here, size)
        dp_local = jnp.einsum(
            "qhd,khd->hqk", grad_block, values[:extent], preferred_element_type=jnp.float32
        )
        dp_remote = jnp.einsum(
            "bqhd,bkhd->hbqk", grouped_grad, mem_v, preferred_element_type=jnp.float32
        )
        dp_remote = dp_remote.reshape(heads_here, QROWS, -1)
        delta = jnp.sum(p_local * dp_local, axis=-1) + jnp.sum(p_remote * dp_remote, axis=-1)
        ds_local = (p_local * (dp_local - delta[..., None])).astype(jnp.bfloat16)
        ds_remote = (p_remote * (dp_remote - delta[..., None])).astype(jnp.bfloat16)
        ds_remote = ds_remote.reshape(heads_here, groups, QBLOCK, -1)
        dq_block = jnp.einsum(
            "hqk,khd->qhd", ds_local, keys[:extent], preferred_element_type=jnp.float32
        )
        dq_extra = jnp.einsum(
            "hbqk,bkhd->bqhd", ds_remote, mem_k, preferred_element_type=jnp.float32
        )
        grad_query_parts.append((dq_block + dq_extra.reshape(dq_block.shape)) * scale)
        dk_part = (
            jnp.einsum("hqk,qhd->khd", ds_local, query_block, preferred_element_type=jnp.float32)
            * scale
        )
        dv_part = jnp.einsum(
            "hqk,qhd->khd",
            p_local.astype(jnp.bfloat16),
            grad_block,
            preferred_element_type=jnp.float32,
        )
        grad_keys = grad_keys.at[:extent].add(dk_part)
        grad_values = grad_values.at[:extent].add(dv_part)
    return (jnp.concatenate(grad_query_parts, axis=0), grad_keys, grad_values)


def tensor_body(
    tokens,
    gain_attn,
    w_query,
    w_key,
    w_value,
    w_out,
    gain_ffn,
    w_gate,
    w_up,
    w_down,
    cache_keys,
    cache_values,
    prefix,
    partner,
    own_blocks,
    partner_blocks,
    grad_out,
):
    micro, shard_len, width = tokens.shape
    cols = w_query.shape[1]
    heads_local = cols // HD
    qblocks = L // QBLOCK
    mem_len = 2 * KR * CBLOCK
    piece_keys = lax.all_gather(cache_keys, "dp", axis=0, tiled=True)
    piece_values = lax.all_gather(cache_values, "dp", axis=0, tiled=True)
    count = piece_keys.shape[0]
    onehot = (partner[:, None] == jnp.arange(count, dtype=jnp.int32)[None, :]).astype(jnp.bfloat16)
    add_keys = jnp.einsum("mn,nkc->mkc", onehot, piece_keys, preferred_element_type=jnp.float32)
    add_values = jnp.einsum("mn,nkc->mkc", onehot, piece_values, preferred_element_type=jnp.float32)
    fetched_keys = add_keys.astype(jnp.bfloat16)
    fetched_values = add_values.astype(jnp.bfloat16)
    totals = (
        jnp.zeros((width, cols), jnp.float32),
        jnp.zeros((width, cols), jnp.float32),
        jnp.zeros((width, cols), jnp.float32),
        jnp.zeros((cols, width), jnp.float32),
        jnp.zeros((width, w_gate.shape[1]), jnp.float32),
        jnp.zeros((width, w_gate.shape[1]), jnp.float32),
        jnp.zeros((w_gate.shape[1], width), jnp.float32),
    )
    shares = tuple(
        (
            jnp.zeros(w.shape, jnp.float32)
            for w in (w_query, w_key, w_value, w_out, w_gate, w_up, w_down)
        )
    )
    gain_total_attn = jnp.zeros((width,), jnp.float32)
    gain_total_ffn = jnp.zeros((width,), jnp.float32)
    out_rows = []
    grad_rows = []
    for step in range(micro):
        fwd = (
            lax.all_gather(gain_attn, "dp", axis=0, tiled=True),
            lax.all_gather(w_query, "dp", axis=0, tiled=True),
            lax.all_gather(w_key, "dp", axis=0, tiled=True),
            lax.all_gather(w_value, "dp", axis=0, tiled=True),
            lax.all_gather(w_out, "dp", axis=1, tiled=True),
            lax.all_gather(gain_ffn, "dp", axis=0, tiled=True),
            lax.all_gather(w_gate, "dp", axis=0, tiled=True),
            lax.all_gather(w_up, "dp", axis=0, tiled=True),
            lax.all_gather(w_down, "dp", axis=1, tiled=True),
        )
        g_attn, wq_full, wk_full, wv_full, wo_full, g_ffn, wg_full, wu_full, wd_full = fwd
        limit = prefix[step]
        own_k = memory_rows(cache_keys[step], own_blocks[step], cols)
        par_k = memory_rows(fetched_keys[step], partner_blocks[step], cols)
        own_v = memory_rows(cache_values[step], own_blocks[step], cols)
        par_v = memory_rows(fetched_values[step], partner_blocks[step], cols)
        mem_keys = jnp.concatenate([own_k, par_k], axis=1).reshape(
            qblocks, mem_len, heads_local, HD
        )
        mem_values = jnp.concatenate([own_v, par_v], axis=1).reshape(
            qblocks, mem_len, heads_local, HD
        )
        token_rows = tokens[step].astype(jnp.float32)
        normed, scale_one = norm_rows(token_rows, g_attn.astype(jnp.float32))
        normed_all = lax.all_gather(normed.astype(jnp.bfloat16), "tensor", axis=0, tiled=True)
        query = (
            jnp.dot(normed_all, wq_full, preferred_element_type=jnp.float32)
            .astype(jnp.bfloat16)
            .reshape(L, heads_local, HD)
        )
        keys = (
            jnp.dot(normed_all, wk_full, preferred_element_type=jnp.float32)
            .astype(jnp.bfloat16)
            .reshape(L, heads_local, HD)
        )
        values = (
            jnp.dot(normed_all, wv_full, preferred_element_type=jnp.float32)
            .astype(jnp.bfloat16)
            .reshape(L, heads_local, HD)
        )
        context_full, lse_parts = attention_forward(
            query, keys, values, mem_keys, mem_values, limit
        )
        context = context_full.reshape(L, cols).astype(jnp.bfloat16)
        mixed = token_rows + lax.psum_scatter(
            jnp.dot(context, wo_full, preferred_element_type=jnp.float32),
            "tensor",
            scatter_dimension=0,
            tiled=True,
        )
        normed_two, scale_two = norm_rows(mixed, g_ffn.astype(jnp.float32))
        normed_two_all = lax.all_gather(
            normed_two.astype(jnp.bfloat16), "tensor", axis=0, tiled=True
        )
        gate = jnp.dot(normed_two_all, wg_full, preferred_element_type=jnp.float32)
        upward = jnp.dot(normed_two_all, wu_full, preferred_element_type=jnp.float32)
        sigma = jax.nn.sigmoid(gate)
        silu_gate = gate * sigma
        hidden = (silu_gate * upward).astype(jnp.bfloat16)
        out_rows.append(
            (
                mixed
                + lax.psum_scatter(
                    jnp.dot(hidden, wd_full, preferred_element_type=jnp.float32).astype(
                        jnp.bfloat16
                    ),
                    "tensor",
                    scatter_dimension=0,
                    tiled=True,
                ).astype(jnp.float32)
            ).astype(jnp.bfloat16)
        )
        bwd = (
            lax.all_gather(gain_attn, "dp", axis=0, tiled=True),
            lax.all_gather(w_query, "dp", axis=0, tiled=True),
            lax.all_gather(w_key, "dp", axis=0, tiled=True),
            lax.all_gather(w_value, "dp", axis=0, tiled=True),
            lax.all_gather(w_out, "dp", axis=1, tiled=True),
            lax.all_gather(gain_ffn, "dp", axis=0, tiled=True),
            lax.all_gather(w_gate, "dp", axis=0, tiled=True),
            lax.all_gather(w_up, "dp", axis=0, tiled=True),
            lax.all_gather(w_down, "dp", axis=1, tiled=True),
        )
        g_attn, wq_full, wk_full, wv_full, wo_full, g_ffn, wg_full, wu_full, wd_full = bwd
        grad_here = grad_out[step]
        grad_all = lax.all_gather(grad_here, "tensor", axis=0, tiled=True)
        d_down = inner_rows(hidden, grad_all)
        grad_hidden = outer_cols(grad_all, wd_full)
        grad_gate = (grad_hidden * upward * sigma * (1.0 + gate * (1.0 - sigma))).astype(
            jnp.bfloat16
        )
        grad_up = (grad_hidden * silu_gate).astype(jnp.bfloat16)
        d_gate = inner_rows(normed_two_all, grad_gate)
        d_up = inner_rows(normed_two_all, grad_up)
        grad_normed_two = lax.psum_scatter(
            outer_cols(grad_gate, wg_full) + outer_cols(grad_up, wu_full),
            "tensor",
            scatter_dimension=0,
            tiled=True,
        )
        grad_mixed_norm, gain_part_ffn = norm_back(
            grad_normed_two, mixed, scale_two, g_ffn.astype(jnp.float32)
        )
        grad_mixed = grad_here.astype(jnp.float32) + grad_mixed_norm
        branch_all = lax.all_gather(grad_mixed.astype(jnp.bfloat16), "tensor", axis=0, tiled=True)
        d_out = inner_rows(context, branch_all)
        grad_context = (
            outer_cols(branch_all, wo_full).astype(jnp.bfloat16).reshape(L, heads_local, HD)
        )
        grad_query, grad_keys, grad_values = attention_backward(
            query, keys, values, mem_keys, mem_values, limit, lse_parts, grad_context
        )
        grad_query = grad_query.reshape(L, cols).astype(jnp.bfloat16)
        grad_keys = grad_keys.reshape(L, cols).astype(jnp.bfloat16)
        grad_values = grad_values.reshape(L, cols).astype(jnp.bfloat16)
        d_query = inner_rows(normed_all, grad_query)
        d_key = inner_rows(normed_all, grad_keys)
        d_value = inner_rows(normed_all, grad_values)
        grad_normed = lax.psum_scatter(
            (
                outer_cols(grad_query, wq_full)
                + outer_cols(grad_keys, wk_full)
                + outer_cols(grad_values, wv_full)
            ).astype(jnp.bfloat16),
            "tensor",
            scatter_dimension=0,
            tiled=True,
        ).astype(jnp.float32)
        grad_token_norm, gain_part_attn = norm_back(
            grad_normed, token_rows, scale_one, g_attn.astype(jnp.float32)
        )
        grad_rows.append(grad_mixed + grad_token_norm)
        gain_total_attn = gain_total_attn + gain_part_attn
        gain_total_ffn = gain_total_ffn + gain_part_ffn
        totals = tuple(
            (
                held + fresh
                for held, fresh in zip(
                    totals, (d_query, d_key, d_value, d_out, d_gate, d_up, d_down)
                )
            )
        )
    shares = (
        lax.psum_scatter(
            totals[0].astype(jnp.bfloat16), "dp", scatter_dimension=0, tiled=True
        ).astype(jnp.float32),
        lax.psum_scatter(
            totals[1].astype(jnp.bfloat16), "dp", scatter_dimension=0, tiled=True
        ).astype(jnp.float32),
        lax.psum_scatter(
            totals[2].astype(jnp.bfloat16), "dp", scatter_dimension=0, tiled=True
        ).astype(jnp.float32),
        lax.psum_scatter(
            totals[3].astype(jnp.bfloat16), "dp", scatter_dimension=1, tiled=True
        ).astype(jnp.float32),
        lax.psum_scatter(
            totals[4].astype(jnp.bfloat16), "dp", scatter_dimension=0, tiled=True
        ).astype(jnp.float32),
        lax.psum_scatter(
            totals[5].astype(jnp.bfloat16), "dp", scatter_dimension=0, tiled=True
        ).astype(jnp.float32),
        lax.psum_scatter(
            totals[6].astype(jnp.bfloat16), "dp", scatter_dimension=1, tiled=True
        ).astype(jnp.float32),
    )
    gain_attn_sum, gain_ffn_sum = lax.psum((gain_total_attn, gain_total_ffn), ("dp", "tensor"))
    return (
        jnp.stack(out_rows, axis=0),
        jnp.stack(grad_rows, axis=0),
        gain_attn_sum,
        shares[0],
        shares[1],
        shares[2],
        shares[3],
        gain_ffn_sum,
        shares[4],
        shares[5],
        shares[6],
    )


TQ = 512
TK = 512
ROWS = 512
HT = 256
SCALE = HD**-0.5
EXP_SCALE = SCALE * 1.4426950408889634
LOG2E = 1.4426950408889634
NT = (((1,), (1,)), ((), ()))
TN = (((0,), (0,)), ((), ()))
F32 = jnp.float32
BF16 = jnp.bfloat16
MIB = 1 << 20


def mm(left, right, dims=(((1,), (0,)), ((), ()))):
    return lax.dot_general(left, right, dims, preferred_element_type=F32)


def fold_max(values):
    best = values[:, :HD]
    for i in range(1, values.shape[1] // HD):
        best = jnp.maximum(best, values[:, i * HD : (i + 1) * HD])
    return best


def fold_sum(values):
    total = values[:, :HD]
    for i in range(1, values.shape[1] // HD):
        total = total + values[:, i * HD : (i + 1) * HD]
    return total


def reach_mask(first, tile, limit):
    rows = first + lax.broadcasted_iota(jnp.int32, (TQ, 1), 0)
    keys = tile * TK + lax.broadcasted_iota(jnp.int32, (1, TK), 1)
    reach = jnp.where(rows < limit, jnp.maximum(rows, limit - 1), rows)
    return keys <= reach


def pick_own(meta, block, own, buf):
    for i in range(KR):
        c = meta[2 + block * KR + i]
        buf[pl.ds(i * CBLOCK, CBLOCK), :] = own[0, pl.ds(pl.multiple_of(c * CBLOCK, CBLOCK), CBLOCK), :]


def pick_other(meta, block, other, buf, start=0):
    for i in range(KR):
        d = meta[2 + (L // QBLOCK) * KR + block * KR + i]
        buf[pl.ds(start + i * CBLOCK, CBLOCK), :] = other[d, 0, 0]


def pick_blocks(meta, block, own, other, buf):
    pick_own(meta, block, own, buf)
    pick_other(meta, block, other, buf, KR * CBLOCK)


def attend_kernel(
    meta, q_ref, k_ref, v_ref, ok_ref, ov_ref, ctx_ref, lse_ref, kbuf, vbuf, sbuf, smem, *, pair
):
    step = pl.program_id(1)
    limit = meta[0]
    first = step * TQ
    free = jnp.where(first < limit, (limit + TK - 1) // TK, 0)
    tiles = jnp.maximum(step + 1, free)
    blocks = TQ // QBLOCK
    for b in range(blocks):
        pick_own(meta, step * blocks + b, ok_ref, kbuf.at[b])
        pick_own(meta, step * blocks + b, ov_ref, vbuf.at[b])
    state = []
    for h in range(pair):
        cs = pl.ds(h * HD, HD)
        best = []
        for b in range(blocks):
            s = mm(q_ref[pl.ds(b * QBLOCK, QBLOCK), cs], kbuf[b, :, cs], NT)
            smem[h, pl.ds(b * QBLOCK, QBLOCK), :] = s
            best.append(fold_max(s))
        state.append(jnp.concatenate(best, 0))

    def scores(tile, state, masked):
        ks = pl.ds(pl.multiple_of(tile * TK, TK), TK)
        if masked:
            allowed = reach_mask(first, tile, limit)
        new = []
        for h in range(pair):
            cs = pl.ds(h * HD, HD)
            s = mm(q_ref[:, cs], k_ref[ks, cs], NT)
            if masked:
                s = jnp.where(allowed, s, NEGATIVE)
            sbuf[h, tile] = s
            new.append(jnp.maximum(state[h], fold_max(s)))
        return tuple(new)

    state = lax.fori_loop(0, step, lambda tile, s: scores(tile, s, False), tuple(state))
    state = lax.fori_loop(step, tiles, lambda tile, s: scores(tile, s, True), state)
    tops = [jnp.max(s, axis=1, keepdims=True) for s in state]
    state = []
    for h in range(pair):
        cs = pl.ds(h * HD, HD)
        p = jnp.exp2((smem[h] - tops[h]) * EXP_SCALE)
        low = p.astype(BF16)
        parts = [mm(low[b * QBLOCK : (b + 1) * QBLOCK], vbuf[b, :, cs]) for b in range(blocks)]
        state.append((fold_sum(p), jnp.concatenate(parts, 0)))

    def weigh(tile, state):
        ks = pl.ds(pl.multiple_of(tile * TK, TK), TK)
        new = []
        for h in range(pair):
            total, acc = state[h]
            p = jnp.exp2((sbuf[h, tile] - tops[h]) * EXP_SCALE)
            new.append((total + fold_sum(p), acc + mm(p.astype(BF16), v_ref[ks, pl.ds(h * HD, HD)])))
        return tuple(new)

    state = lax.fori_loop(0, tiles, weigh, tuple(state))
    for h in range(pair):
        cs = pl.ds(h * HD, HD)
        total = jnp.sum(state[h][0], axis=1, keepdims=True)
        ctx_ref[:, cs] = state[h][1] / total
        lse_ref[:, cs] = jnp.broadcast_to(tops[h] * SCALE + jnp.log(total), (TQ, HD))


def attend_other_kernel(meta, q_ref, pk_ref, pv_ref, part_ref, plse_ref, ctx_ref, lse_ref, kbuf, vbuf, *, pair):
    step = pl.program_id(1)
    blocks = TQ // QBLOCK
    for b in range(blocks):
        pick_other(meta, step * blocks + b, pk_ref, kbuf.at[b])
        pick_other(meta, step * blocks + b, pv_ref, vbuf.at[b])
    for h in range(pair):
        cs = pl.ds(h * HD, HD)
        rows = [pl.ds(b * QBLOCK, QBLOCK) for b in range(blocks)]
        s = jnp.concatenate([mm(q_ref[rows[b], cs], kbuf[b, :, cs], NT) for b in range(blocks)], 0)
        before = plse_ref[:, cs]
        top = jnp.maximum(before, jnp.max(fold_max(s), axis=1, keepdims=True) * SCALE)
        keep = jnp.exp(before - top)
        p = jnp.exp2(s * EXP_SCALE - top[:, :1] * LOG2E)
        low = p.astype(BF16)
        more = jnp.concatenate(
            [mm(low[b * QBLOCK : (b + 1) * QBLOCK], vbuf[b, :, cs]) for b in range(blocks)], 0
        )
        total = keep + jnp.sum(fold_sum(p), axis=1, keepdims=True)
        ctx_ref[:, cs] = ((part_ref[:, cs] * keep + more) / total).astype(BF16)
        lse_ref[:, cs] = top + jnp.log(total)


def attend_back_kernel(
    meta, q_ref, k_ref, v_ref, ok_ref, ov_ref, pk_ref, pv_ref, do_ref, ctx_ref, lse_ref,
    dq_ref, dk_ref, dv_ref, kbuf, vbuf, dks, dvs, *, pair
):
    step = pl.program_id(1)
    limit = meta[0]
    first = step * TQ
    free = jnp.where(first < limit, (limit + TK - 1) // TK, 0)
    tiles = jnp.maximum(step + 1, free)
    blocks = TQ // QBLOCK

    @pl.when(step == 0)
    def _():
        dks[...] = jnp.zeros_like(dks)
        dvs[...] = jnp.zeros_like(dvs)

    for b in range(blocks):
        pick_blocks(meta, step * blocks + b, ok_ref, pk_ref, kbuf.at[b])
        pick_blocks(meta, step * blocks + b, ov_ref, pv_ref, vbuf.at[b])
    state = []
    aux = []
    for h in range(pair):
        cs = pl.ds(h * HD, HD)
        delta = jnp.sum(do_ref[:, cs].astype(F32) * ctx_ref[:, cs].astype(F32), axis=1, keepdims=True)
        lse2 = lse_ref[:, cs][:, :1] * LOG2E
        aux.append((lse2, delta))
        parts = []
        for b in range(blocks):
            rs = pl.ds(b * QBLOCK, QBLOCK)
            s = mm(q_ref[rs, cs], kbuf[b, :, cs], NT)
            p = jnp.exp2(s * EXP_SCALE - lse2[b * QBLOCK : (b + 1) * QBLOCK])
            dp = mm(do_ref[rs, cs], vbuf[b, :, cs], NT)
            ds = (p * (dp - delta[b * QBLOCK : (b + 1) * QBLOCK])).astype(BF16)
            parts.append(mm(ds, kbuf[b, :, cs]))
        state.append(jnp.concatenate(parts, 0))

    def grads(tile, state, masked):
        ks = pl.ds(pl.multiple_of(tile * TK, TK), TK)
        if masked:
            allowed = reach_mask(first, tile, limit)
        new = []
        for h in range(pair):
            cs = pl.ds(h * HD, HD)
            lse2, delta = aux[h]
            s = mm(q_ref[:, cs], k_ref[ks, cs], NT)
            p = jnp.exp2(s * EXP_SCALE - lse2)
            if masked:
                p = jnp.where(allowed, p, 0.0)
            dp = mm(do_ref[:, cs], v_ref[ks, cs], NT)
            ds = (p * (dp - delta)).astype(BF16)
            dvs[ks, cs] += mm(p.astype(BF16), do_ref[:, cs], TN)
            dks[ks, cs] += mm(ds, q_ref[:, cs], TN)
            new.append(state[h] + mm(ds, k_ref[ks, cs]))
        return tuple(new)

    state = lax.fori_loop(0, step, lambda tile, s: grads(tile, s, False), tuple(state))
    state = lax.fori_loop(step, tiles, lambda tile, s: grads(tile, s, True), state)
    for h in range(pair):
        dq_ref[:, pl.ds(h * HD, HD)] = (state[h] * SCALE).astype(BF16)

    @pl.when(step == L // TQ - 1)
    def _():
        dk_ref[...] = (dks[...] * SCALE).astype(BF16)
        dv_ref[...] = dvs[...].astype(BF16)


def attention_specs(heads, pair):
    wide = pair * HD
    per = heads // 2 // pair
    groups = heads // pair
    return [
        pl.BlockSpec((TQ, wide), lambda h, i, meta: (i, h)),
        pl.BlockSpec((L, wide), lambda h, i, meta: (0, groups + h)),
        pl.BlockSpec((L, wide), lambda h, i, meta: (0, 2 * groups + h)),
        pl.BlockSpec((1, CACHE_LEN, wide), lambda h, i, meta: ((h // per) ^ meta[1], 0, h % per)),
        pl.BlockSpec((1, CACHE_LEN, wide), lambda h, i, meta: ((h // per) ^ meta[1], 0, h % per)),
        pl.BlockSpec(
            (CACHE_LEN // CBLOCK, 1, 1, CBLOCK, wide),
            lambda h, i, meta: (0, (h // per) ^ meta[1], 0, 0, h % per),
        ),
        pl.BlockSpec(
            (CACHE_LEN // CBLOCK, 1, 1, CBLOCK, wide),
            lambda h, i, meta: (0, (h // per) ^ meta[1], 1, 0, h % per),
        ),
    ]


def attend(meta, qkv, own_k, own_v, pair=4):
    width = qkv.shape[1] // 3
    heads = width // HD
    wide = pair * HD
    row = pl.BlockSpec((TQ, wide), lambda h, i, meta: (i, h))
    area = L * 1600 * width
    return pl.pallas_call(
        functools.partial(attend_kernel, pair=pair),
        grid_spec=pltpu.PrefetchScalarGridSpec(
            num_scalar_prefetch=1,
            grid=(heads // pair, L // TQ),
            in_specs=attention_specs(heads, pair)[:5],
            out_specs=[row, row],
            scratch_shapes=[pltpu.VMEM((TQ // QBLOCK, KR * CBLOCK, wide), BF16)] * 2
            + [pltpu.VMEM((pair, L // TK, TQ, TK), F32), pltpu.VMEM((pair, TQ, KR * CBLOCK), F32)],
        ),
        out_shape=[jax.ShapeDtypeStruct((L, width), F32)] * 2,
        compiler_params=pltpu.CompilerParams(vmem_limit_bytes=60 * MIB),
        cost_estimate=pl.CostEstimate(flops=12 * area, bytes_accessed=30 * MIB, transcendentals=area // HD),
        name="attend",
    )(meta, qkv, qkv, qkv, own_k, own_v)


def attend_other(meta, qkv, fetched, partial, lse, pair=4):
    width = qkv.shape[1] // 3
    heads = width // HD
    wide = pair * HD
    row = pl.BlockSpec((TQ, wide), lambda h, i, meta: (i, h))
    specs = attention_specs(heads, pair)
    return pl.pallas_call(
        functools.partial(attend_other_kernel, pair=pair),
        grid_spec=pltpu.PrefetchScalarGridSpec(
            num_scalar_prefetch=1,
            grid=(heads // pair, L // TQ),
            in_specs=[specs[0], specs[5], specs[6], row, row],
            out_specs=[row, row],
            scratch_shapes=[pltpu.VMEM((TQ // QBLOCK, KR * CBLOCK, wide), BF16)] * 2,
        ),
        out_shape=[jax.ShapeDtypeStruct((L, width), BF16), jax.ShapeDtypeStruct((L, width), F32)],
        compiler_params=pltpu.CompilerParams(vmem_limit_bytes=60 * MIB),
        cost_estimate=pl.CostEstimate(
            flops=4 * L * 256 * width, bytes_accessed=30 * MIB, transcendentals=L * 256 * heads
        ),
        name="attend_other",
    )(meta, qkv, fetched, fetched, partial, lse)


def attend_back(meta, qkv, own_k, own_v, fetched, grad_context, context, lse, pair=4):
    width = context.shape[1]
    heads = width // HD
    wide = pair * HD
    row = pl.BlockSpec((TQ, wide), lambda h, i, meta: (i, h))
    col = pl.BlockSpec((L, wide), lambda h, i, meta: (0, h))
    area = L * 1900 * width
    return pl.pallas_call(
        functools.partial(attend_back_kernel, pair=pair),
        grid_spec=pltpu.PrefetchScalarGridSpec(
            num_scalar_prefetch=1,
            grid=(heads // pair, L // TQ),
            in_specs=attention_specs(heads, pair) + [row, row, row],
            out_specs=[row, col, col],
            scratch_shapes=[pltpu.VMEM((TQ // QBLOCK, 2 * KR * CBLOCK, wide), BF16)] * 2
            + [pltpu.VMEM((L, wide), F32)] * 2,
        ),
        out_shape=[jax.ShapeDtypeStruct((L, width), BF16)] * 3,
        compiler_params=pltpu.CompilerParams(vmem_limit_bytes=60 * MIB),
        cost_estimate=pl.CostEstimate(flops=12 * area, bytes_accessed=40 * MIB, transcendentals=area // HD),
        name="attend_back",
    )(meta, qkv, qkv, qkv, own_k, own_v, fetched, fetched, grad_context, context, lse)


def project_kernel(x_ref, gain_ref, w_ref, normed_ref, qkv_ref):
    rows = x_ref[...].astype(F32)
    scale = lax.rsqrt(jnp.mean(rows * rows, axis=1, keepdims=True) + EPS)
    normed_ref[...] = (rows * scale * gain_ref[...]).astype(BF16)
    left = normed_ref[...]

    def chunk(c, carry):
        cs = pl.ds(pl.multiple_of(c * 512, 512), 512)
        qkv_ref[:, cs] = mm(left, w_ref[:, cs]).astype(BF16)
        return carry

    lax.fori_loop(0, qkv_ref.shape[1] // 512, chunk, 0)


def project(x, gain, weights):
    width = x.shape[1]
    cols = 3 * width
    row = lambda n: pl.BlockSpec((ROWS, n), lambda i: (i, 0))
    whole = lambda n: pl.BlockSpec((width, n), lambda i: (0, 0))
    return pl.pallas_call(
        project_kernel,
        grid=(L // ROWS,),
        in_specs=[row(width), pl.BlockSpec((1, width), lambda i: (0, 0)), whole(cols)],
        out_specs=[row(width), row(cols)],
        out_shape=[jax.ShapeDtypeStruct((L, width), BF16), jax.ShapeDtypeStruct((L, cols), BF16)],
        compiler_params=pltpu.CompilerParams(vmem_limit_bytes=60 * MIB),
        cost_estimate=pl.CostEstimate(flops=2 * L * width * cols, bytes_accessed=26 * MIB, transcendentals=0),
        name="project",
    )(x, gain, weights)


def mix_kernel(x_ref, ctx_ref, gain_ref, w_ref, mixed_ref, normed_ref):
    mixed = x_ref[...].astype(F32) + mm(ctx_ref[...], w_ref[...], NT)
    mixed_ref[...] = mixed
    scale = lax.rsqrt(jnp.mean(mixed * mixed, axis=1, keepdims=True) + EPS)
    normed_ref[...] = (mixed * scale * gain_ref[...]).astype(BF16)


def mix(x, context, gain, weights):
    width = x.shape[1]
    rows = ROWS // 2
    row = pl.BlockSpec((rows, width), lambda i: (i, 0))
    return pl.pallas_call(
        mix_kernel,
        grid=(L // rows,),
        in_specs=[row, row, pl.BlockSpec((1, width), lambda i: (0, 0)), pl.BlockSpec((width, width), lambda i: (0, 0))],
        out_specs=[row, row],
        out_shape=[jax.ShapeDtypeStruct((L, width), F32), jax.ShapeDtypeStruct((L, width), BF16)],
        compiler_params=pltpu.CompilerParams(vmem_limit_bytes=60 * MIB),
        cost_estimate=pl.CostEstimate(flops=2 * L * width * width, bytes_accessed=22 * MIB, transcendentals=0),
        name="mix",
    )(x, context, gain, weights)


RING = 8


def ring_place(p):
    y = p // 4
    return (p + y * (7 - 2 * p)) * 2 + y


def meet(devices, me, spot):
    barrier = pltpu.get_barrier_semaphore()
    for d in range(1, devices):
        pl.semaphore_signal(
            barrier, inc=1, device_id=((me + d) % devices, spot), device_id_type=pl.DeviceIdType.MESH
        )
    pl.semaphore_signal(barrier, inc=1, device_id=(me, 1 - spot), device_id_type=pl.DeviceIdType.MESH)
    pl.semaphore_wait(barrier, devices)


def remote(src, dst, send, recv, device):
    return pltpu.make_async_remote_copy(
        src_ref=src, dst_ref=dst, send_sem=send, recv_sem=recv, device_id=device, device_id_type=pl.DeviceIdType.MESH
    )


UT = 256


def ffn_kernel(
    n_ref, g_ref, wg0, wg1, wu0, wu1, wd0, wd1, gain_ref, mixed_ref, wo_ref,
    share_ref, gg_ref, out_ref, gm_ref, br_ref, gc_ref,
    acc, gn, hid, duo, part, got, passed, keep, land,
    wo_buf, mixed_buf, out_buf, br_buf, gc_buf,
    pair_send, pair_recv, x_send, x_recv, wo_sem, mixed_sem, done_sem, *, devices,
):
    tile = pl.program_id(0)
    tiles = pl.num_programs(0)
    me = lax.axis_index("dp")
    spot = lax.axis_index("tensor")
    core = me % 2
    pair = (me + 1 - 2 * core, spot)
    peer = (me, 1 - spot)
    side = HT // 2
    width = n_ref.shape[1]
    wo_copy = pltpu.make_async_copy(wo_ref.at[:, pl.ds(0, width)], wo_buf, wo_sem)

    @pl.when(tile == 0)
    def _():
        barrier = pltpu.get_barrier_semaphore()
        for device in (pair, peer):
            pl.semaphore_signal(barrier, inc=1, device_id=device, device_id_type=pl.DeviceIdType.MESH)
        pl.semaphore_wait(barrier, 2)
        acc[...] = jnp.zeros_like(acc)
        gn[...] = jnp.zeros_like(gn)

    def to_pair(k):
        return remote(part.at[k % 2, :, 1 - core], got.at[k % 2], pair_send.at[k % 2], pair_recv.at[k % 2], pair)

    def to_peer(k):
        return remote(passed.at[k % 2], land.at[k % 4], x_send.at[k % 2], x_recv.at[k % 4], peer)

    def join(k):
        slot = (k + 2) % 2
        total = (got[slot].astype(F32) + part[slot, :, core].astype(F32)).astype(BF16)
        for m in range(3):
            passed[slot, :, :, m * side : (m + 1) * side] = total[:, :, m * HT + side : (m + 1) * HT]
            keep[(k + 4) % 4, :, :, m * side : (m + 1) * side] = total[:, :, m * HT : m * HT + side]

    def settle(k):
        slot = (jnp.maximum(k, -1) + 4) % 4
        total = (keep[slot].astype(F32) + land[slot].astype(F32)).astype(BF16)
        total = total.reshape(share_ref.shape[0], 3 * side)
        for m in range(3):
            place = pl.multiple_of((m * tiles + jnp.maximum(k, 0)) * side, side)
            share_ref[:, pl.ds(place, side)] = total[:, m * side : (m + 1) * side]

    wgu = jnp.concatenate([wg0[...], wg1[...], wu0[...], wu1[...]], axis=1)
    wd = jnp.concatenate([wd0[...], wd1[...]], axis=1)

    def chunk(r):
        rs = pl.ds(r * ROWS, ROWS)
        both = mm(n_ref[rs, :], wgu)
        grad_hidden = mm(g_ref[rs, :], wd)
        gate, up = both[:, :HT], both[:, HT:]
        sigma = 1.0 / (1.0 + jnp.exp(-gate))
        silu = gate * sigma
        hidden = (silu * up).astype(BF16)
        grad_gate = grad_hidden * up * (sigma * (1.0 + gate * (1.0 - sigma)))
        grads = jnp.concatenate([grad_gate.astype(BF16), (grad_hidden * silu).astype(BF16)], axis=1)
        acc[rs, :] += mm(hidden, wd, NT)
        gn[rs, :] += mm(grads, wgu, NT)
        hid[rs, :] = hidden
        duo[rs, :] = grads

    @pl.when(tile > 2)
    def _():
        to_peer(tile - 3).wait()

    settle(tile - 3)
    for r in range(L // ROWS):
        chunk(r)

    @pl.when(tile > 0)
    def _():
        to_pair(tile - 1).wait()

    join(tile - 1)
    slot = tile % 2
    shape = part.shape[1:4]
    part[slot, :, :, :, : 2 * HT] = mm(n_ref[...], duo[...], TN).astype(BF16).reshape(shape + (2 * HT,))
    part[slot, :, :, :, 2 * HT :] = mm(g_ref[...], hid[...], TN).astype(BF16).reshape(shape + (HT,))
    to_pair(tile).start()

    @pl.when(tile > 0)
    def _():
        to_peer(tile - 1).start()

    def rows_of(t):
        return pl.ds(pl.multiple_of(t * UT, UT), UT)

    def fetch(t):
        return pltpu.make_async_copy(mixed_ref.at[rows_of(t), :], mixed_buf.at[t % 2], mixed_sem.at[t % 2])

    def write(t):
        sources = [out_buf.at[t % 2], gn.at[rows_of(t), :], br_buf.at[t % 2], gc_buf.at[t % 2]]
        return [
            pltpu.make_async_copy(source, ref.at[rows_of(t), :], done_sem.at[i, t % 2])
            for i, (source, ref) in enumerate(zip(sources, [out_ref, gm_ref, br_ref, gc_ref]))
        ]

    def unmix(t, carry):
        @pl.when(t < L // UT - 1)
        def _():
            fetch(t + 1).start()

        fetch(t).wait()

        @pl.when(t > 1)
        def _():
            for copy in write(t - 2):
                copy.wait()

        rs = rows_of(t)
        now = t % 2
        mixed = mixed_buf[now]
        grad = gn[rs, :]
        scale = lax.rsqrt(jnp.mean(mixed * mixed, axis=1, keepdims=True) + EPS)
        unit = mixed * scale
        inner = grad * gain_ref[...]
        back = scale * (inner - unit * jnp.mean(inner * unit, axis=1, keepdims=True))
        grad_mixed = g_ref[rs, :].astype(F32) + back
        out_buf[now] = (mixed + acc[rs, :]).astype(BF16)
        gn[rs, :] = grad_mixed
        branch = grad_mixed.astype(BF16)
        br_buf[now] = branch
        gc_buf[now] = mm(branch, wo_buf[...]).astype(BF16)
        gg_ref[...] += jnp.sum(grad * unit, axis=0, keepdims=True)
        for copy in write(t):
            copy.start()
        return carry

    @pl.when(tile == tiles - 2)
    def _():
        wo_copy.start()
        fetch(0).start()

    @pl.when(tile == tiles - 1)
    def _():
        gg_ref[...] = jnp.zeros_like(gg_ref)
        to_peer(tile - 2).wait()
        settle(tile - 2)
        wo_copy.wait()
        lax.fori_loop(0, 3, unmix, 0)
        to_pair(tile).wait()
        join(tile)
        to_peer(tile).start()
        lax.fori_loop(3, L // UT, unmix, 0)
        to_peer(tile - 1).wait()
        settle(tile - 1)
        to_peer(tile).wait()
        settle(tile)
        for t in (L // UT - 2, L // UT - 1):
            for copy in write(t):
                copy.wait()


def ffn(normed, cotangent, weights, gain, mixed, width, hidden, devices):
    once = pl.Buffered(1)
    tiles = hidden // HT
    side = HT // 2
    rows = width // devices
    chips = devices // 2
    lead = width // side
    part = lambda k: pl.BlockSpec((width, side), lambda j: (0, lead + k * tiles + j))
    whole = pl.BlockSpec((L, width), lambda j: (0, 0), pipeline_mode=once)
    fixed = lambda shape: pl.BlockSpec(shape, lambda j: (0, 0), pipeline_mode=once)
    hbm = pl.BlockSpec(memory_space=pltpu.HBM)
    dma = pltpu.SemaphoreType.DMA
    tile = lambda kind: pltpu.VMEM((2, UT, width), kind)
    return pl.pallas_call(
        functools.partial(ffn_kernel, devices=devices),
        grid=(tiles,),
        in_specs=[whole, whole] + [part(k) for k in range(6)] + [fixed((1, width)), hbm, hbm],
        out_specs=[fixed((width // 2, 3 * hidden // 2)), fixed((1, width)), hbm, hbm, hbm, hbm],
        out_shape=[
            jax.ShapeDtypeStruct((width // 2, 3 * hidden // 2), BF16),
            jax.ShapeDtypeStruct((1, width), F32),
            jax.ShapeDtypeStruct((L, width), BF16),
            jax.ShapeDtypeStruct((L, width), F32),
            jax.ShapeDtypeStruct((L, width), BF16),
            jax.ShapeDtypeStruct((L, width), BF16),
        ],
        scratch_shapes=[
            pltpu.VMEM((L, width), F32), pltpu.VMEM((L, width), F32),
            pltpu.VMEM((L, HT), BF16), pltpu.VMEM((L, 2 * HT), BF16),
            pltpu.VMEM((2, chips, 2, rows, 3 * HT), BF16),
            pltpu.VMEM((2, chips, rows, 3 * HT), BF16),
            pltpu.VMEM((2, chips, rows, 3 * side), BF16),
            pltpu.VMEM((4, chips, rows, 3 * side), BF16),
            pltpu.VMEM((4, chips, rows, 3 * side), BF16),
            pltpu.VMEM((width, width), BF16), tile(F32), tile(BF16), tile(BF16), tile(BF16),
            dma((2,)), dma((2,)), dma((2,)), dma((4,)), dma, dma((2,)), dma((4, 2)),
        ],
        compiler_params=pltpu.CompilerParams(collective_id=2, has_side_effects=True, vmem_limit_bytes=61 * MIB),
        cost_estimate=pl.CostEstimate(
            flops=18 * L * width * hidden, bytes_accessed=60 * MIB, transcendentals=L * hidden
        ),
        name="ffn",
    )(normed, cotangent, *([weights] * 6), gain, mixed, weights)


FT = 256


def finish_kernel(
    x_ref, gm_ref, n_ref, ctx_ref, br_ref, dq_ref, dk_ref, dv_ref, w_ref, gain_ref, gain_two_ref,
    gt_ref, sums_ref, share_ref,
    n_buf, ctx_buf, br_buf, dq_buf, dk_buf, dv_buf, w_buf, x_buf, gm_buf, gt_buf,
    part, got, land, across, gains, gain_land,
    load_sem, x_sem, gm_sem, gt_sem, gt_recv, pair_send, pair_recv, ring_send, ring_recv, x_send, x_recv, g_send, g_recv,
    *, devices,
):
    me = lax.axis_index("dp")
    spot = lax.axis_index("tensor")
    core = me % 2
    z, y = me // 4, (me // 2) % 2
    place = z + y * (7 - 2 * z)
    width = n_buf.shape[1]
    half = width // 2
    rows = part.shape[2]
    loads = [
        pltpu.make_async_copy(src, dst, load_sem.at[i])
        for i, (src, dst) in enumerate(
            [
                (ctx_ref, ctx_buf), (br_ref, br_buf), (n_ref, n_buf), (dv_ref, dv_buf),
                (dk_ref, dk_buf), (dq_ref, dq_buf), (w_ref.at[:, pl.ds(0, 3 * width)], w_buf),
            ]
        )
    ]
    for copy in loads:
        copy.start()
    meet(devices, me, spot)

    def tile_in(t, slot):
        rs = pl.ds(pl.multiple_of(t * FT, FT), FT)
        return [
            pltpu.make_async_copy(x_ref.at[rs, :], x_buf.at[slot], x_sem.at[slot]),
            pltpu.make_async_copy(gm_ref.at[rs, :], gm_buf.at[slot], gm_sem.at[slot]),
        ]

    held = L // FT // 2

    def give(k, slot):
        rs = pl.ds(pl.multiple_of(k * FT, FT), FT)
        return remote(
            gt_buf.at[slot], gt_ref.at[spot, rs, :], gt_sem.at[slot], gt_recv.at[k], (me, 1 - spot)
        )

    def keep(k, slot):
        rs = pl.ds(pl.multiple_of(k * FT, FT), FT)
        return pltpu.make_async_copy(gt_buf.at[slot], gt_ref.at[spot, rs, :], gt_sem.at[slot])

    def tile_of(k):
        return (k + held * (1 - spot)) % (2 * held)

    for copy in tile_in(tile_of(0), 0):
        copy.start()

    pair = (me + 1 - 2 * core, spot)

    def column(m, h):
        return (m // 2) * 2 * width + h * width + (m % 2) * half

    def to_pair(m, h):
        cs = pl.ds(column(m, h), half)
        return remote(
            part.at[:, 1 - core, :, cs], got.at[:, :, cs], pair_send.at[m, h], pair_recv.at[m, h], pair
        )

    def product(m, left, right):
        for h in range(2):
            value = mm(left[...], right[:, h * half : (h + 1) * half], TN).astype(BF16)
            part[:, :, :, column(m, h) : column(m, h) + half] = value.reshape(part.shape[0], 2, rows, half)
            to_pair(m, h).start()

    def join(m, h):
        to_pair(m, h).wait_recv()
        cs = pl.ds(column(m, h), half)
        got[:, :, cs] = (got[:, :, cs].astype(F32) + part[:, core, :, cs].astype(F32)).astype(BF16)

    neighbours = [(place + 1) % RING, (place + RING - 1) % RING]

    def held_block(g, direction, s):
        p = (place + 2 * RING - 1 - s) % RING if direction == 0 else (place + 1 + s) % RING
        return got.at[ring_place(p), :, pl.ds((2 * g + direction) * width, width)]

    def hop(g, direction, s):
        to = ring_place(neighbours[direction]) * 2 + core
        return remote(
            held_block(g, direction, s), land.at[g, direction, s],
            ring_send.at[g, direction, s], ring_recv.at[g, direction, s], (to, spot),
        )

    def advance(g, s, more=True):
        for direction in range(2):
            hop(g, direction, s).wait_recv()
            block = held_block(g, direction, s + 1)
            block[...] = (block[...].astype(F32) + land[g, direction, s].astype(F32)).astype(BF16)
            if more:
                hop(g, direction, s + 1).start()

    def launch(g):
        for h in range(2):
            join(2 * g, h)
            join(2 * g + 1, h)
            hop(g, h, 0).start()

    def finish_rows(t, slot, k):
        for copy in tile_in(t, slot):
            copy.wait()
        rs = pl.ds(pl.multiple_of(t * FT, FT), FT)
        grad = mm(dq_buf[rs, :], w_buf[:, :width], NT)
        grad += mm(dk_buf[rs, :], w_buf[:, width : 2 * width], NT)
        grad += mm(dv_buf[rs, :], w_buf[:, 2 * width :], NT)
        values = x_buf[slot].astype(F32)
        scale = lax.rsqrt(jnp.mean(values * values, axis=1, keepdims=True) + EPS)
        unit = values * scale
        inner = grad * gain_ref[...]
        back = scale * (inner - unit * jnp.mean(inner * unit, axis=1, keepdims=True))
        gt_buf[k] = (gm_buf[slot] + back).astype(BF16)
        gains[:1, :] += jnp.sum(grad * unit, axis=0, keepdims=True)

    def two_tiles(j, advances, give_away):
        for slot in (0, 1):
            k = 2 * j + slot
            if slot == 0 or give_away:
                for copy in tile_in(tile_of(k + 1), 1 - slot):
                    copy.start()
            else:

                @pl.when(j < held - 1)
                def _():
                    for copy in tile_in(tile_of(k + 1), 0):
                        copy.start()

            finish_rows(tile_of(k), slot, k)
            if give_away:
                give(k, k).start()
            else:
                keep(k - held, k).start()
        for g, s in advances:
            advance(g, s)

    gains[:1, :] = jnp.zeros((1, width), F32)
    gains[1:, :] = gain_two_ref[...]
    for i in (0, 1):
        loads[i].wait()
    product(0, br_buf, ctx_buf)
    for i in (2, 3):
        loads[i].wait()
    product(1, n_buf, dv_buf)
    launch(0)
    for i in (4, 5, 6):
        loads[i].wait()

    def theirs(j, carry):
        two_tiles(j, [(0, j)], True)
        return carry

    def ours(j, carry):
        two_tiles(j, [(0, j + 2), (1, j - 2)], False)
        return carry

    lax.fori_loop(0, held // 2, theirs, 0)
    product(2, n_buf, dk_buf)
    advance(0, 2)
    product(3, n_buf, dq_buf)
    advance(0, 3)
    launch(1)
    lax.fori_loop(held // 2, held, ours, 0)

    partners = [
        (me + 1 - 2 * core, spot),
        (me + 2 - 4 * y, spot),
        (me + 4 - 8 * (z % 2), spot),
        (me + 8 - 16 * (z // 2), spot),
        (me, 1 - spot),
    ]

    def add_gains(r):
        return remote(gains, gain_land.at[r], g_send.at[r], g_recv.at[r], partners[r])

    def gain_round(r):
        add_gains(r).wait()
        gains[...] = gains[...] + gain_land[r]
        if r < 4:
            add_gains(r + 1).start()

    own = ring_place(place)
    peer = (me, 1 - spot)

    def over(g):
        return remote(
            got.at[own, :, pl.ds((2 * g + 1) * width, width)], across.at[:, pl.ds(g * width, width)],
            x_send.at[g], x_recv.at[g], peer,
        )

    add_gains(0).start()
    advance(0, 6, False)
    over(0).start()
    advance(1, 2)
    gain_round(0)
    advance(1, 3)
    gain_round(1)
    advance(1, 4)
    gain_round(2)
    advance(1, 5)
    gain_round(3)
    advance(1, 6, False)
    over(1).start()
    gain_round(4)
    sums_ref[...] = gains[...]
    for g in range(2):
        over(g).wait_recv()
        cs = pl.ds(g * width, width)
        share_ref[:, cs] = got[own, :, pl.ds(2 * g * width, width)].astype(F32) + across[:, cs].astype(F32)
    for g in range(2):
        over(g).wait_send()
        for direction in range(2):
            for s in range(RING - 1):
                hop(g, direction, s).wait_send()
    for m in range(4):
        for h in range(2):
            to_pair(m, h).wait_send()
    for k in range(held):
        give(k, k).wait()
        keep(k, k + held).wait()


def finish(x, grad_mixed, normed, context, branch, dq, dk, dv, weights, gain, gain_two_part, devices):
    width = x.shape[1]
    rows = width // devices
    anywhere = pl.BlockSpec(memory_space=pltpu.HBM)
    vmem = pl.BlockSpec(memory_space=pltpu.VMEM)
    dma = pltpu.SemaphoreType.DMA
    whole = pltpu.VMEM((L, width), BF16)
    return pl.pallas_call(
        functools.partial(finish_kernel, devices=devices),
        in_specs=[anywhere] * 9 + [vmem] * 2,
        out_specs=[anywhere, vmem, vmem],
        out_shape=[
            jax.ShapeDtypeStruct((2, L // 2, width), BF16),
            jax.ShapeDtypeStruct((2, width), F32),
            jax.ShapeDtypeStruct((rows, 2 * width), F32),
        ],
        scratch_shapes=[
            whole, whole, whole, whole, whole, whole, pltpu.VMEM((width, 3 * width), BF16),
            pltpu.VMEM((2, FT, width), BF16), pltpu.VMEM((2, FT, width), F32), pltpu.VMEM((L // FT, FT, width), BF16),
            pltpu.VMEM((RING, 2, rows, 4 * width), BF16),
            pltpu.VMEM((RING, rows, 4 * width), BF16),
            pltpu.VMEM((2, 2, RING - 1, rows, width), BF16),
            pltpu.VMEM((rows, 2 * width), BF16),
            pltpu.VMEM((2, width), F32), pltpu.VMEM((5, 2, width), F32),
            dma((7,)), dma((2,)), dma((2,)), dma((2 * (L // FT // 2),)), dma((L // FT // 2,)), dma((4, 2)), dma((4, 2)),
            dma((2, 2, RING - 1)), dma((2, 2, RING - 1)), dma((2,)), dma((2,)), dma((5,)), dma((5,)),
        ],
        compiler_params=pltpu.CompilerParams(collective_id=1, has_side_effects=True, vmem_limit_bytes=60 * MIB),
        cost_estimate=pl.CostEstimate(flops=14 * L * width * width, bytes_accessed=80 * MIB, transcendentals=0),
        name="finish",
    )(x, grad_mixed, normed, context, branch, dq, dk, dv, weights, gain, gain_two_part)


def pick_kernel(table, held_ref, sent_ref, sems):
    def copy(i):
        return pltpu.make_async_copy(held_ref.at[table[i]], sent_ref.at[i], sems.at[i])

    for i in range(sent_ref.shape[0]):
        copy(i).start()
    for i in range(sent_ref.shape[0]):
        copy(i).wait()


def pick_rows(table, held):
    count = held.shape[0]
    return pl.pallas_call(
        pick_kernel,
        grid_spec=pltpu.PrefetchScalarGridSpec(
            num_scalar_prefetch=1,
            grid=(),
            in_specs=[pl.BlockSpec(memory_space=pl.ANY)],
            out_specs=pl.BlockSpec(memory_space=pltpu.VMEM),
            scratch_shapes=[pltpu.SemaphoreType.DMA((count,))],
        ),
        out_shape=jax.ShapeDtypeStruct(held.shape, held.dtype),
        compiler_params=pltpu.CompilerParams(vmem_limit_bytes=60 * MIB),
        cost_estimate=pl.CostEstimate(flops=0, bytes_accessed=2 * held.size * 2, transcendentals=0),
        name="pick_rows",
    )(table, held)


def spread_kernel(
    tok_ref, ck_ref, cv_ref, small_ref, extra_ref, big_ref,
    x_ref, ok_ref, ov_ref, held_ref, first_ref, second_ref,
    tok_buf, k_buf, v_buf, local_sem, x_send, x_recv, all_send, all_recv, ring_send, ring_recv, line_send, line_recv, pair_send, pair_recv,
):
    me = lax.axis_index("dp")
    spot = lax.axis_index("tensor")
    peer = 1 - spot
    devices = held_ref.shape[0]
    rows, cols = small_ref.shape[0], small_ref.shape[1] // 3
    core = me % 2
    z, y = me // 4, (me // 2) % 2

    def target(dp, tensor):
        return (dp, tensor)

    barrier = pltpu.get_barrier_semaphore()
    for d in range(1, devices):
        pl.semaphore_signal(barrier, inc=1, device_id=target((me + d) % devices, spot), device_id_type=pl.DeviceIdType.MESH)
    pl.semaphore_signal(barrier, inc=1, device_id=target(me, peer), device_id_type=pl.DeviceIdType.MESH)
    pl.semaphore_wait(barrier, devices)

    def remote(src, dst, send, recv, device):
        return pltpu.make_async_remote_copy(
            src_ref=src, dst_ref=dst, send_sem=send, recv_sem=recv,
            device_id=device, device_id_type=pl.DeviceIdType.MESH,
        )

    mine = pl.multiple_of(me * rows, rows)
    across = target(me, peer)
    weight_copies = []
    for i in range(3):
        weight_copies.append(
            remote(
                small_ref.at[:, pl.ds(i * cols, cols)],
                first_ref.at[pl.ds(mine, rows), pl.ds((2 * i + 1) * cols, cols)],
                x_send.at[i], x_recv.at[i], across,
            )
        )
    for copy in weight_copies:
        copy.start()
    for i in range(3):
        first_ref[pl.ds(mine, rows), pl.ds(2 * i * cols, cols)] = small_ref[:, pl.ds(i * cols, cols)]
    first_ref[pl.ds(mine, rows), pl.ds(6 * cols, HD)] = extra_ref[...]

    loads = [
        pltpu.make_async_copy(tok_ref.at[spot], tok_buf, local_sem.at[0]),
        pltpu.make_async_copy(ck_ref.at[spot], k_buf, local_sem.at[1]),
        pltpu.make_async_copy(cv_ref.at[spot], v_buf, local_sem.at[2]),
    ]
    stores = [
        pltpu.make_async_copy(tok_buf, x_ref.at[spot], local_sem.at[3]),
        pltpu.make_async_copy(k_buf, ok_ref.at[spot], local_sem.at[4]),
        pltpu.make_async_copy(v_buf, ov_ref.at[spot], local_sem.at[5]),
    ]
    for copy in loads:
        copy.start()

    x_copies = [remote(tok_ref.at[peer], x_ref.at[spot], x_send.at[3], x_recv.at[3], across)]
    wide = big_ref.shape[1]
    hidden = (wide - cols) // 3
    starts = [(0, cols)] + [(cols + i * hidden, hidden) for i in range(3)]
    own_cols = []
    for i, (start, size) in enumerate(starts):
        base = 2 * start
        own_cols.append(pltpu.make_async_copy(
            big_ref.at[:, pl.ds(start, size)], second_ref.at[:, pl.ds(base, size)], local_sem.at[6 + i]))
        x_copies.append(remote(
            big_ref.at[:, pl.ds(start, size)], second_ref.at[:, pl.ds(base + size, size)],
            x_send.at[4 + i], x_recv.at[4 + i], across))
    x_copies.append(remote(ck_ref.at[peer], ok_ref.at[spot], x_send.at[8], x_recv.at[8], across))
    x_copies.append(remote(cv_ref.at[peer], ov_ref.at[spot], x_send.at[9], x_recv.at[9], across))
    for copy in x_copies + own_cols:
        copy.start()

    def to_device(d, dst_dp):
        chunk = pl.ds(pl.multiple_of(dst_dp * CBLOCK, CBLOCK), CBLOCK)
        dst = target(dst_dp, spot)
        return [
            remote(ck_ref.at[:, chunk, :], held_ref.at[me, :, 0], all_send.at[0, d], all_recv.at[0, d], dst),
            remote(cv_ref.at[:, chunk, :], held_ref.at[me, :, 1], all_send.at[1, d], all_recv.at[1, d], dst),
        ]

    for copy in weight_copies:
        copy.wait_recv()

    def block(zz, yy, c):
        return first_ref.at[pl.ds(pl.multiple_of((zz * 4 + yy * 2 + c) * rows, rows), rows), :]

    def along(s, direction):
        zz = z - (s - 1) if direction == 0 else z + (s - 1)
        to = z + 1 if direction == 0 else z - 1
        k = (s - 1) * 2 + direction
        held = block(zz, y, core)
        return remote(held, held, ring_send.at[k], ring_recv.at[k], target(to * 4 + y * 2 + core, spot))

    def sends(s, direction):
        return (z < 3) & (z - (s - 1) >= 0) if direction == 0 else (z > 0) & (z + (s - 1) <= 3)

    def gets(s, direction):
        return z - s >= 0 if direction == 0 else z + s <= 3

    def to_line(zz):
        held = block(zz, y, core)
        return remote(held, held, line_send.at[zz], line_recv.at[zz], target(z * 4 + (1 - y) * 2 + core, spot))

    def to_pair(zz, yy):
        held = block(zz, yy, core)
        k = zz * 2 + yy
        return remote(held, held, pair_send.at[k], pair_recv.at[k], target(me + 1 - 2 * core, spot))

    for direction in range(2):

        @pl.when(sends(1, direction))
        def _():
            along(1, direction).start()

    to_line(z).start()
    to_pair(z, y).start()
    copies = []
    order = [8, 4, 12, 6, 10, 2, 14, 9, 5, 13, 1, 7, 11, 3, 15]
    assert sorted(order) == list(range(1, devices))

    def some(count):
        for d in order[:count]:
            for copy in to_device(d, (me + d) % devices):
                copy.start()
                copies.append(copy)
        del order[:count]

    some(3)
    chunk = pl.ds(pl.multiple_of(me * CBLOCK, CBLOCK), CBLOCK)
    kept = [
        pltpu.make_async_copy(ck_ref.at[:, chunk, :], held_ref.at[me, :, 0], local_sem.at[10]),
        pltpu.make_async_copy(cv_ref.at[:, chunk, :], held_ref.at[me, :, 1], local_sem.at[11]),
    ]
    for copy in kept:
        copy.start()
    for load, store in zip(loads, stores):
        load.wait()
        store.start()
    for s in range(1, 4):
        for direction in range(2):

            @pl.when(gets(s, direction))
            def _():
                along(s, direction).wait_recv()
                zz = z - s if direction == 0 else z + s
                if s < 3:

                    @pl.when(sends(s + 1, direction))
                    def _():
                        along(s + 1, direction).start()

                to_line(zz).start()
                to_pair(zz, y).start()

        some(3)
    for zz in range(4):
        to_line(zz).wait_recv()
        to_pair(zz, 1 - y).start()
        some(1)
    some(devices)
    for s in range(1, 4):
        for direction in range(2):

            @pl.when(sends(s, direction))
            def _():
                along(s, direction).wait_send()

    for zz in range(4):
        to_line(zz).wait_send()
        for yy in range(2):
            to_pair(zz, yy).wait()
    for copy in weight_copies:
        copy.wait_send()
    for copy in x_copies + copies:
        copy.wait()
    for copy in stores + own_cols + kept:
        copy.wait()


def spread(tokens, cache_keys, cache_values, small, extra, big, devices):
    micro, shard_len, width = tokens.shape
    rows, cols = small.shape[0], small.shape[1] // 3
    anywhere = pl.BlockSpec(memory_space=pltpu.HBM)
    vmem = pl.BlockSpec(memory_space=pltpu.VMEM)
    dma = pltpu.SemaphoreType.DMA
    return pl.pallas_call(
        spread_kernel,
        in_specs=[anywhere, anywhere, anywhere, vmem, vmem, vmem],
        out_specs=[anywhere, anywhere, anywhere, anywhere, vmem, anywhere],
        out_shape=[
            jax.ShapeDtypeStruct((2, shard_len, width), BF16),
            jax.ShapeDtypeStruct((2, CACHE_LEN, cols), BF16),
            jax.ShapeDtypeStruct((2, CACHE_LEN, cols), BF16),
            jax.ShapeDtypeStruct((devices, micro, 2, CBLOCK, cols), BF16),
            jax.ShapeDtypeStruct((rows * devices, 6 * cols + HD), BF16),
            jax.ShapeDtypeStruct((rows, 2 * big.shape[1]), BF16),
        ],
        scratch_shapes=[
            pltpu.VMEM((shard_len, width), BF16),
            pltpu.VMEM((CACHE_LEN, cols), BF16),
            pltpu.VMEM((CACHE_LEN, cols), BF16),
            dma((12,)), dma((10,)), dma((10,)), dma((2, devices)), dma((2, devices)),
            dma((6,)), dma((6,)), dma((4,)), dma((4,)), dma((8,)), dma((8,)),
        ],
        compiler_params=pltpu.CompilerParams(collective_id=0, has_side_effects=True, vmem_limit_bytes=60 * MIB),
        cost_estimate=pl.CostEstimate(flops=0, bytes_accessed=300 * MIB, transcendentals=0),
        name="spread",
    )(tokens, cache_keys, cache_values, small, extra, big)


def swap(values):
    return lax.ppermute(values, "tensor", [(0, 1), (1, 0)])


def sequence_body(
    tokens, gain_attn, w_query, w_key, w_value, w_out, gain_ffn, w_gate, w_up, w_down,
    cache_keys, cache_values, prefix, partner, own_blocks, partner_blocks, grad_out,
):
    micro, shard_len, width = tokens.shape
    devices = lax.axis_size("dp")
    seqs = micro * devices
    rows_held, cols = w_query.shape
    hidden_held = w_gate.shape[1]
    hidden = 2 * hidden_held
    spot = lax.axis_index("tensor")
    exchange = functools.partial(lax.all_to_all, axis_name="tensor", split_axis=0, concat_axis=0, tiled=True)
    chunks = CACHE_LEN // CBLOCK

    small = jnp.concatenate([w_query, w_key, w_value], axis=1)
    partner_column = jnp.zeros((rows_held, 1), BF16).at[:micro, 0].set(partner.astype(BF16))
    extra = jnp.concatenate(
        [gain_attn[:, None], gain_ffn[:, None], partner_column, jnp.zeros((rows_held, HD - 3), BF16)], axis=1
    )
    big = jnp.concatenate([w_out.T, w_gate, w_up, w_down.T], axis=1)
    x, own_k, own_v, held, first_all, second_rows = spread(
        tokens, cache_keys, cache_values, small, extra, big, devices
    )
    x = x.reshape(L, width)
    theirs = swap(lax.dynamic_index_in_dim(grad_out, 1 - spot, 0, keepdims=False))
    mine = lax.dynamic_index_in_dim(grad_out, spot, 0, keepdims=False)
    cotangent = jnp.where(spot == 0, jnp.concatenate([mine, theirs], 0), jnp.concatenate([theirs, mine], 0))
    second_all = lax.all_gather(second_rows, "dp", axis=0, tiled=True)

    tail = lax.optimization_barrier(first_all[:, 3 * width :])
    gains = mm((jnp.arange(2)[:, None] == jnp.arange(HD)[None, :]).astype(BF16), tail, NT)
    gain_one, gain_two = gains[:1], gains[1:]
    table = tail[:, 2].reshape(devices, rows_held)[:, :micro].reshape(seqs).astype(jnp.int32)
    sent = pick_rows(table, held.reshape(seqs, 2 * CBLOCK, cols))
    fetched = lax.all_to_all(sent, ("dp", "tensor"), split_axis=0, concat_axis=0, tiled=True)
    fetched = fetched.reshape(chunks, 2, 2, CBLOCK, cols)

    meta = jnp.concatenate(
        [
            prefix[spot][None], spot[None].astype(jnp.int32),
            own_blocks[spot].reshape(-1), partner_blocks[spot].reshape(-1),
        ]
    )
    normed, qkv = project(x, gain_one, first_all)
    partial, partial_lse = attend(meta, qkv, own_k, own_v)
    context, lse = attend_other(meta, qkv, fetched, partial, partial_lse)
    mixed, normed_two = mix(x, context, gain_two, second_all)
    ffn_grads, gain_part_two, out, grad_mixed, branch, grad_context = ffn(
        normed_two, cotangent, second_all, gain_two, mixed, width, hidden, devices
    )
    ffn_share = lax.psum_scatter(
        ffn_grads, "dp", scatter_dimension=0, tiled=True,
        axis_index_groups=[list(range(c, devices, 2)) for c in range(2)],
    )
    out = exchange(out.reshape(2, shard_len, width))
    dq, dk, dv = attend_back(meta, qkv, own_k, own_v, fetched, grad_context, context, lse)
    dq, out = lax.optimization_barrier((dq, out))
    grad_tokens, gain_sums, attn_share = finish(
        x, grad_mixed, normed, context, branch, dq, dk, dv, first_all, gain_one, gain_part_two, devices
    )
    grad_tokens = grad_tokens.astype(F32)
    g_out, g_value, g_key, g_query = jnp.split(attn_share, 4, axis=1)
    g_gate, g_up, g_down = [
        ffn_share[:, i * hidden_held : (i + 1) * hidden_held].astype(F32) for i in range(3)
    ]
    return (
        out, grad_tokens, gain_sums[0], g_query, g_key, g_value, g_out.T, gain_sums[1], g_gate, g_up, g_down.T,
    )


def solution(mesh):
    in_specs = (
        P("dp", "tensor", None),
        P("dp"),
        P("dp", "tensor"),
        P("dp", "tensor"),
        P("dp", "tensor"),
        P("tensor", "dp"),
        P("dp"),
        P("dp", "tensor"),
        P("dp", "tensor"),
        P("tensor", "dp"),
        P("dp", None, "tensor"),
        P("dp", None, "tensor"),
        P("dp"),
        P("dp"),
        P("dp", None, None),
        P("dp", None, None),
        P("dp", "tensor", None),
    )
    out_specs = (
        P("dp", "tensor", None),
        P("dp", "tensor", None),
        P(),
        P("dp", "tensor"),
        P("dp", "tensor"),
        P("dp", "tensor"),
        P("tensor", "dp"),
        P(),
        P("dp", "tensor"),
        P("dp", "tensor"),
        P("tensor", "dp"),
    )
    whole = mesh.shape["tensor"] == 2 and mesh.shape["dp"] == CACHE_LEN // CBLOCK
    body = sequence_body if whole else tensor_body
    return jax.shard_map(body, mesh=mesh, in_specs=in_specs, out_specs=out_specs, check_vma=False)
```
